32 devices in a mesh: section: 2 (over y), dp: 16 (over z, x, core).
Axes of the slice: x: 2, y: 2, z: 4, core: 2. Of those that a mesh axis runs over, the one named last changes fastest.
Arguments:
- inputs: bfloat16 [16384, 768], P('dp'), may hold values from -6 to 6
- cotangent: bfloat16 [16384, 768], P('dp'), may hold values from -6 to 6
- segments: int32 [16384], P('dp'), may hold values from 0 to 511, as said below
- valid_flags: int32 [16384], P('dp'), may hold values from 0 to 1, as said below
- first_gain: bfloat16 [2, 768], P('section'), may hold values from 0.5 to 1.5
- first_shift: bfloat16 [2, 768], P('section'), may hold values from -1.75 to 1.75
- project_weight: bfloat16 [2, 768, 2304], P('section'), may hold values from -0.21875 to 0.21875
- query_bias: bfloat16 [2, 768], P('section'), may hold values from -1.75 to 1.75
- value_bias: bfloat16 [2, 768], P('section'), may hold values from -1.75 to 1.75
- out_weight: bfloat16 [2, 768, 768], P('section'), may hold values from -0.875 to 0.875
- out_bias: bfloat16 [2, 768], P('section'), may hold values from -1.75 to 1.75
- second_gain: bfloat16 [2, 768], P('section'), may hold values from 0.5 to 1.5
- second_shift: bfloat16 [2, 768], P('section'), may hold values from -1.75 to 1.75
- up_weight: bfloat16 [2, 768, 3072], P('section'), may hold values from -0.21875 to 0.21875
- up_bias: bfloat16 [2, 3072], P('section'), may hold values from -1.75 to 1.75
- down_weight: bfloat16 [2, 3072, 768], P('section'), may hold values from -0.109375 to 0.109375
- down_bias: bfloat16 [2, 768], P('section'), may hold values from -1.75 to 1.75
Outputs:
- layer_out: bfloat16 [2, 16384, 768], P('section', 'dp')
- input_grad: float32 [2, 16384, 768], P('section', 'dp')
- first_gain_grad: float32 [2, 768], P('section', 'dp')
- first_shift_grad: float32 [2, 768], P('section', 'dp')
- project_weight_grad: float32 [2, 768, 2304], P('section', None, 'dp')
- query_bias_grad: float32 [2, 768], P('section', 'dp')
- value_bias_grad: float32 [2, 768], P('section', 'dp')
- out_weight_grad: float32 [2, 768, 768], P('section', None, 'dp')
- out_bias_grad: float32 [2, 768], P('section', 'dp')
- second_gain_grad: float32 [2, 768], P('section', 'dp')
- second_shift_grad: float32 [2, 768], P('section', 'dp')
- up_weight_grad: float32 [2, 768, 3072], P('section', None, 'dp')
- up_bias_grad: float32 [2, 3072], P('section', 'dp')
- down_weight_grad: float32 [2, 3072, 768], P('section', None, 'dp')
- down_bias_grad: float32 [2, 768], P('section', 'dp')
The draws below stay inside these ranges and needn't reach their ends.
Inputs may be any that keep to these rules, and one draw needn't show every extreme that they name: `segments`: within each pack of 512 consecutive rows, segment numbers start at 0 and never fall, each number covering one run of rows; rows with flag 0 come after all rows with flag 1 in their pack and carry the segment number 512 - 1, which no row with flag 1 carries. `valid_flags`: each pack of 512 rows begins with a row of flag 1 and ends with a row of flag 0.
All inputs are finite; a program needn't handle non-finite values.
Results may differ from the reference program's by a relative error of at most 0.015.
Values may be sent and summed in bfloat16 or wider, within the bound.
A program may use at most 256 MiB of HBM per device.

```python
import jax
import jax.numpy as jnp
import numpy as np
from jax import lax

D = 768
HEADS = 12
HEAD_DIM = 64
FF = 3072
SEQ = 512
LAYERS = 2
TOKENS = 16384


PATCH_COUNTS = np.array([900, 576, 400, 256, 225, 144, 100, 64, 36, 25], dtype=np.int32)


def pack_layout(key):
    image_count = SEQ // 16 + 48
    pack_count = TOKENS // SEQ
    picked = jax.random.randint(jax.random.fold_in(key, 11), (pack_count, image_count), 0, 10)
    run_table = jnp.maximum(2, jnp.asarray(PATCH_COUNTS, dtype=jnp.int32) * SEQ // 1024)
    lengths = run_table[picked]
    run_ends = jnp.cumsum(lengths, axis=1)
    positions = jnp.arange(SEQ, dtype=jnp.int32)
    segment_ids = jnp.sum((run_ends[:, None, :] <= positions[None, :, None]).astype(jnp.int32), axis=2)
    last_end = jnp.max(jnp.where(run_ends <= SEQ, run_ends, 0), axis=1)
    live_end = jnp.minimum(last_end, SEQ - 1)
    flag_rows = (positions[None, :] < live_end[:, None]).astype(jnp.int32)
    segment_ids = jnp.where(flag_rows == 1, segment_ids, SEQ - 1)
    return (segment_ids.reshape(-1).astype(jnp.int32), flag_rows.reshape(-1).astype(jnp.int32))


def draw_segments(key, part):
    return pack_layout(key)[0]


def draw_valid_flags(key, part):
    return pack_layout(key)[1]


def with_spikes(result, stream_key, source, target, parts, factor):
    owner, partner = [(jnp.arange(result.shape[axis_at]) // (result.shape[axis_at] // parts)).reshape([-1 if axis == axis_at else 1 for axis in range(result.ndim)]) for axis_at in (source, target)]
    chosen = jax.random.permutation(stream_key, parts)[partner]
    strong = (owner == chosen) | (owner == (partner + parts // 2) % parts)
    return jnp.where(strong, factor * result, result)


def block_scale(stream_key, dims, split, least, largest):
    level, own = 1.0, jax.random.fold_in(stream_key, 6)
    for position, blocks in split:
        steps = jnp.exp(jax.random.uniform(jax.random.fold_in(own, position), (blocks,), jnp.float32, least / len(split), largest / len(split)))
        level = level * jnp.repeat(steps, dims[position] // blocks).reshape([-1 if axis == position else 1 for axis in range(len(dims))])
    return level


def scatter_about(rng, extent, width, limit, split=(), held_as=jnp.bfloat16):
    entries = width * jax.random.normal(rng, extent, jnp.float32)
    if split:
        entries = entries * block_scale(rng, extent, split, -0.22, 0.18)
    return jnp.clip(entries, -limit, limit).astype(held_as)


def gaussian_with(rng, shape, scale, bound, shards, heavy, kind=jnp.bfloat16):
    values = scale * jax.random.normal(rng, shape, jnp.float32)
    if shards:
        values = values * block_scale(rng, shape, shards, -0.22, 0.18)
    return jnp.clip(with_spikes(values, jax.random.fold_in(rng, 3), *heavy), -bound, bound).astype(kind)


def setup_inputs(seed: int = 0) -> dict:
    streams_of = jax.random.split(jax.random.key(seed), 18)
    return {
        "inputs": scatter_about(streams_of[0], (TOKENS, D), 1.0, 6.0, ((0, 16),)),
        "cotangent": gaussian_with(streams_of[1], (TOKENS, D), 1.0, 6.0, ((0, 16),), (0, 1, 16, 2.0)),
        "segments": draw_segments(jax.random.fold_in(streams_of[17], 71), 0),
        "valid_flags": draw_valid_flags(jax.random.fold_in(streams_of[17], 71), 0),
        "first_gain": jnp.clip(1.0 + 0.1 * jax.random.normal(streams_of[4], (LAYERS, D), jnp.float32), 0.5, 1.5).astype(jnp.bfloat16),
        "first_shift": scatter_about(streams_of[5], (LAYERS, D), 0.3, 1.75, ((0, 2),)),
        "project_weight": scatter_about(streams_of[6], (LAYERS, D, 3 * D), D ** -0.5, 0.21875, ((0, 2),)),
        "query_bias": scatter_about(streams_of[7], (LAYERS, D), 0.3, 1.75, ((0, 2),)),
        "value_bias": scatter_about(streams_of[8], (LAYERS, D), 0.3, 1.75, ((0, 2),)),
        "out_weight": scatter_about(streams_of[9], (LAYERS, D, D), (D // 16) ** -0.5, 0.875, ((0, 2),)),
        "out_bias": scatter_about(streams_of[10], (LAYERS, D), 0.3, 1.75, ((0, 2),)),
        "second_gain": jnp.clip(1.0 + 0.1 * jax.random.normal(streams_of[11], (LAYERS, D), jnp.float32), 0.5, 1.5).astype(jnp.bfloat16),
        "second_shift": scatter_about(streams_of[12], (LAYERS, D), 0.3, 1.75, ((0, 2),)),
        "up_weight": scatter_about(streams_of[13], (LAYERS, D, FF), D ** -0.5, 0.21875, ((0, 2),)),
        "up_bias": scatter_about(streams_of[14], (LAYERS, FF), 0.3, 1.75, ((0, 2),)),
        "down_weight": scatter_about(streams_of[15], (LAYERS, FF, D), FF ** -0.5, 0.109375, ((0, 2),)),
        "down_bias": scatter_about(streams_of[16], (LAYERS, D), 0.3, 1.75, ((0, 2),)),
    }


EPSILON = 1e-06
SCORE_SCALE = 0.125
FULL_PRECISION = lax.Precision.HIGHEST

@jax.custom_vjp
def low(v):
    return lax.optimization_barrier(v.astype(jnp.bfloat16)).astype(jnp.float32)

@jax.custom_vjp
def low_back(v):
    return v

def low_keep(v):
    return (low(v), None)

def low_pass(kept, grad):
    return (grad,)

def back_keep(v):
    return (v, None)

def back_low(kept, grad):
    return (low(grad),)
low.defvjp(low_keep, low_pass)
low_back.defvjp(back_keep, back_low)

def product_high(left, right):
    return jnp.dot(left, right, precision=FULL_PRECISION, preferred_element_type=jnp.float32)

def norm_rows(values, gain, shift):
    average = lax.optimization_barrier(jnp.mean(values, axis=-1, keepdims=True))
    centred = values - average
    inv_scale = lax.rsqrt(lax.optimization_barrier(jnp.mean(centred * centred, axis=-1, keepdims=True)) + EPSILON)
    return centred * inv_scale * gain + shift

def attend(query_rows, key_rows, value_rows, segment, validity):
    length = query_rows.shape[0]
    query_heads = query_rows.reshape(length, HEADS, HEAD_DIM)
    key_heads = key_rows.reshape(length, HEADS, HEAD_DIM)
    value_heads = value_rows.reshape(length, HEADS, HEAD_DIM)
    scores = low_back(jnp.einsum('qhd,khd->hqk', query_heads, key_heads, precision=FULL_PRECISION) * SCORE_SCALE)
    places = jnp.arange(length)
    allowed = (segment[:, None] == segment[None, :]) & (validity[None, :] == 1) | (places[:, None] == places[None, :])
    scores = jnp.where(allowed[None], scores, -1e+30)
    row_max = lax.optimization_barrier(jnp.max(scores, axis=-1, keepdims=True))
    exponent = jnp.exp(scores - row_max)
    attention = low(exponent / lax.optimization_barrier(jnp.sum(exponent, axis=-1, keepdims=True)))
    mixed_heads = jnp.einsum('hqk,khd->qhd', attention, value_heads, precision=FULL_PRECISION)
    return mixed_heads.reshape(length, HEADS * HEAD_DIM)

def attend_bundle(bundle):
    return attend(bundle[0], bundle[1], bundle[2], bundle[3], bundle[4])

def layer(params, rows_in, segments, valid_flags):
    first_gain, first_shift, project_weight, query_bias, value_bias, out_weight, out_bias, second_gain, second_shift, up_weight, up_bias, down_weight, down_bias = params
    normed = low(norm_rows(rows_in, first_gain, first_shift))
    combined = product_high(normed, project_weight)
    query_rows = low_back(low(combined[:, :D] + query_bias))
    key_rows = low_back(low(combined[:, D:2 * D]))
    value_rows = low_back(low(combined[:, 2 * D:] + value_bias))
    pack_total = rows_in.shape[0] // SEQ
    attended = lax.map(jax.checkpoint(attend_bundle), (query_rows.reshape(pack_total, SEQ, D), key_rows.reshape(pack_total, SEQ, D), value_rows.reshape(pack_total, SEQ, D), segments.reshape(pack_total, SEQ), valid_flags.reshape(pack_total, SEQ))).reshape(pack_total * SEQ, D)
    attended = low_back(low(attended))
    middle = rows_in + low_back(product_high(attended, out_weight) + out_bias)
    second_normed = low(norm_rows(middle, second_gain, second_shift))
    upper = low_back(product_high(second_normed, up_weight) + up_bias)
    hidden = low_back(low(jax.nn.gelu(upper, approximate=False)))
    return middle + low_back(product_high(hidden, down_weight) + down_bias)

def reference(inputs, cotangent, segments, valid_flags, first_gain, first_shift, project_weight, query_bias, value_bias, out_weight, out_bias, second_gain, second_shift, up_weight, up_bias, down_weight, down_bias):
    stacks = (first_gain, first_shift, project_weight, query_bias, value_bias, out_weight, out_bias, second_gain, second_shift, up_weight, up_bias, down_weight, down_bias)
    carried = inputs.astype(jnp.float32)
    layer_results = []
    pullbacks = []
    for layer_index in range(LAYERS):
        params = tuple((member[layer_index].astype(jnp.float32) for member in stacks))
        layer_result, pullback = jax.vjp(lambda params_in, state_in: layer(params_in, state_in, segments, valid_flags), params, carried)
        layer_results.append(layer_result.astype(jnp.bfloat16))
        pullbacks.append(pullback)
        carried = low(layer_result)
    gradient = cotangent.astype(jnp.float32)
    state_grads = [None] * LAYERS
    param_grads = [None] * LAYERS
    for layer_index in reversed(range(LAYERS)):
        param_part, state_grad = pullbacks[layer_index](gradient)
        state_grads[layer_index] = state_grad
        param_grads[layer_index] = param_part
        gradient = low(state_grad)
    stacked = [jnp.stack([param_grads[layer_index][member] for layer_index in range(LAYERS)]) for member in range(13)]
    return (jnp.stack(layer_results), jnp.stack(state_grads), stacked[0], stacked[1], stacked[2], stacked[3], stacked[4], stacked[5], stacked[6], stacked[7], stacked[8], stacked[9], stacked[10], stacked[11], stacked[12])
```

```python
from functools import partial

import jax
import jax.numpy as jnp
from jax import lax
from jax.sharding import PartitionSpec as P

HEADS = 12
HEAD_DIM = 64
SEQ = 512
MICRO = 2


EPSILON = 1e-06
SCORE_SCALE = 0.125


def from_behind(value, axis, by):
    devices = lax.axis_size(axis)
    pairs = [(i, i + by) for i in range(devices) if 0 <= i + by < devices]
    return lax.ppermute(value, axis, pairs)


def norm_rows(values):
    average = jnp.mean(values, axis=-1, keepdims=True)
    centred = values - average
    inv_scale = lax.rsqrt(jnp.mean(centred * centred, axis=-1, keepdims=True) + EPSILON)
    return (centred * inv_scale, inv_scale)


def norm_back(normed_grad, whitened, inv_scale, gain_vec):
    scaled = normed_grad * gain_vec.astype(jnp.float32)
    return inv_scale * (
        scaled
        - jnp.mean(scaled, axis=-1, keepdims=True)
        - whitened * jnp.mean(scaled * whitened, axis=-1, keepdims=True)
    )


def contract_rows(left, right):
    return lax.dot_general(
        left, right, (((0,), (0,)), ((), ())), preferred_element_type=jnp.float32
    )


def times_transpose(left, right):
    return lax.dot_general(
        left, right, (((1,), (1,)), ((), ())), preferred_element_type=jnp.float32
    )


def pair_mask(segment, validity, block_rows):
    length = segment.shape[0]
    row_place = lax.broadcasted_iota(jnp.int32, (block_rows, length), 0)
    col_place = lax.broadcasted_iota(jnp.int32, (block_rows, length), 1)
    return (segment[:, None] == segment[None, :]) & (validity[None, :] == 1) | (
        row_place == col_place
    )


def attend_pack(query_rows, key_rows, value_rows, segment, validity):
    length = query_rows.shape[0]
    block_rows = min(512, length)
    key_heads = key_rows.reshape(length, HEADS, HEAD_DIM)
    value_heads = value_rows.reshape(length, HEADS, HEAD_DIM)
    query_block = query_rows.reshape(block_rows, HEADS, HEAD_DIM)
    scores = (
        jnp.einsum("qhd,khd->hqk", query_block, key_heads, preferred_element_type=jnp.float32)
        * SCORE_SCALE
    )
    scores = jnp.where(pair_mask(segment, validity, block_rows)[None], scores, -1e30)
    row_max = jnp.max(scores, axis=-1, keepdims=True)
    exponent = jnp.exp(scores - row_max)
    row_sum = jnp.sum(exponent, axis=-1, keepdims=True)
    attention_low = (exponent / row_sum).astype(jnp.bfloat16)
    combined = jnp.einsum(
        "hqk,khd->qhd", attention_low, value_heads, preferred_element_type=jnp.float32
    )
    out_parts = [combined.reshape(block_rows, HEADS * HEAD_DIM).astype(jnp.bfloat16)]
    log_parts = [(row_max + jnp.log(row_sum))[:, :, 0]]
    return (jnp.concatenate(out_parts, axis=0), jnp.concatenate(log_parts, axis=1))


def attend_back(query_rows, key_rows, value_rows, log_sums, attended_low, segment, validity):
    length = query_rows.shape[0]
    block_rows = min(512, length)
    key_heads = key_rows.reshape(length, HEADS, HEAD_DIM)
    value_heads = value_rows.reshape(length, HEADS, HEAD_DIM)
    query_block = query_rows.reshape(block_rows, HEADS, HEAD_DIM)
    upstream = attended_low.reshape(block_rows, HEADS, HEAD_DIM)
    scores = (
        jnp.einsum("qhd,khd->hqk", query_block, key_heads, preferred_element_type=jnp.float32)
        * SCORE_SCALE
    )
    scores = jnp.where(pair_mask(segment, validity, block_rows)[None], scores, -1e30)
    attention = jnp.exp(scores - log_sums[:, 0:block_rows, None])
    attention_low = attention.astype(jnp.bfloat16)
    value_grad = jnp.einsum(
        "hqk,qhd->khd", attention_low, upstream, preferred_element_type=jnp.float32
    )
    attention_grad = jnp.einsum(
        "qhd,khd->hqk", upstream, value_heads, preferred_element_type=jnp.float32
    )
    inner = jnp.sum(attention * attention_grad, axis=-1, keepdims=True)
    score_low = (attention * (attention_grad - inner)).astype(jnp.bfloat16)
    query_grad = (
        jnp.einsum("hqk,khd->qhd", score_low, key_heads, preferred_element_type=jnp.float32)
        * SCORE_SCALE
    )
    query_parts = [query_grad.reshape(block_rows, HEADS * HEAD_DIM).astype(jnp.bfloat16)]
    key_grad = (
        jnp.einsum("hqk,qhd->khd", score_low, query_block, preferred_element_type=jnp.float32)
        * SCORE_SCALE
    )
    return (
        jnp.concatenate(query_parts, axis=0),
        key_grad.reshape(length, HEADS * HEAD_DIM).astype(jnp.bfloat16),
        value_grad.reshape(length, HEADS * HEAD_DIM).astype(jnp.bfloat16),
    )


def stash_zeros(micro_count, micro_rows, width, hidden_width):
    plain = jnp.zeros((micro_count, micro_rows, width), jnp.bfloat16)
    log_zero = jnp.zeros((micro_count, micro_rows // SEQ, HEADS, SEQ), jnp.float32)
    middle_zero = jnp.zeros((micro_count, micro_rows, width), jnp.float32)
    zeros_all = (plain, plain, plain, plain, plain, log_zero, plain, middle_zero, plain)
    zeros_all = zeros_all + (jnp.zeros((micro_count, micro_rows, hidden_width), jnp.float32),)
    return zeros_all


def layer_forward(weights, layer_in, segment, validity):
    (
        first_gain,
        first_shift,
        project_weight,
        query_bias,
        value_bias,
        out_weight,
        out_bias,
        second_gain,
        second_shift,
        up_weight,
        up_bias,
        down_weight,
        down_bias,
    ) = weights
    width = layer_in.shape[1]
    widened = layer_in.astype(jnp.float32)
    whitened, inv_scale = norm_rows(widened)
    normed = (whitened * first_gain + first_shift).astype(jnp.bfloat16)
    combined = jnp.dot(normed, project_weight, preferred_element_type=jnp.float32)
    query_rows = (combined[:, :width] + query_bias).astype(jnp.bfloat16)
    key_rows = combined[:, width : 2 * width].astype(jnp.bfloat16)
    value_rows = (combined[:, 2 * width :] + value_bias).astype(jnp.bfloat16)
    attended_piece, log_piece = attend_pack(query_rows, key_rows, value_rows, segment, validity)
    attended_parts = [attended_piece]
    log_parts = [log_piece]
    attended = jnp.concatenate(attended_parts, axis=0)
    log_sums = jnp.stack(log_parts)
    middle = widened + (
        jnp.dot(attended, out_weight, preferred_element_type=jnp.float32) + out_bias
    )
    second_white, second_scale = norm_rows(middle)
    second_normed = (second_white * second_gain + second_shift).astype(jnp.bfloat16)
    upper = jnp.dot(second_normed, up_weight, preferred_element_type=jnp.float32) + up_bias
    hidden = jax.nn.gelu(upper, approximate=False).astype(jnp.bfloat16)
    layer_result = middle + (
        jnp.dot(hidden, down_weight, preferred_element_type=jnp.float32) + down_bias
    )
    stash = (
        layer_in,
        normed,
        query_rows,
        key_rows,
        value_rows,
        log_sums,
        attended,
        middle,
        second_normed,
    )
    stash = stash + (upper,)
    return (layer_result, stash)


def layer_backward(weights, stash, gradient, segment, validity):
    (
        first_gain,
        first_shift,
        project_weight,
        query_bias,
        value_bias,
        out_weight,
        out_bias,
        second_gain,
        second_shift,
        up_weight,
        up_bias,
        down_weight,
        down_bias,
    ) = weights
    (
        layer_in,
        normed,
        query_rows,
        key_rows,
        value_rows,
        log_sums,
        attended,
        middle,
        second_normed,
    ) = stash[:9]
    upper = stash[9]
    hidden = jax.nn.gelu(upper, approximate=False).astype(jnp.bfloat16)
    output_low = gradient.astype(jnp.bfloat16)
    hidden_low = times_transpose(output_low, down_weight).astype(jnp.bfloat16)
    unused, gelu_back = jax.vjp(partial(jax.nn.gelu, approximate=False), upper)
    upper_low = gelu_back(hidden_low.astype(jnp.float32))[0].astype(jnp.bfloat16)
    second_grad = times_transpose(upper_low, up_weight)
    second_white, second_scale = norm_rows(middle)
    middle_grad = gradient + norm_back(second_grad, second_white, second_scale, second_gain)
    branch_low = middle_grad.astype(jnp.bfloat16)
    attended_low = times_transpose(branch_low, out_weight).astype(jnp.bfloat16)
    query_grad, key_grad, value_grad = attend_back(
        query_rows, key_rows, value_rows, log_sums[0], attended_low, segment, validity
    )
    query_parts = [query_grad]
    key_parts = [key_grad]
    value_parts = [value_grad]
    mixed_low = jnp.concatenate(
        [
            jnp.concatenate(query_parts, axis=0),
            jnp.concatenate(key_parts, axis=0),
            jnp.concatenate(value_parts, axis=0),
        ],
        axis=1,
    )
    first_grad = times_transpose(mixed_low, project_weight)
    whitened, inv_scale = norm_rows(layer_in.astype(jnp.float32))
    input_grad = middle_grad + norm_back(first_grad, whitened, inv_scale, first_gain)
    norm_terms = (
        jnp.sum(first_grad * whitened, axis=0),
        jnp.sum(first_grad, axis=0),
        jnp.sum(second_grad * second_white, axis=0),
        jnp.sum(second_grad, axis=0),
    )
    parts = (output_low, branch_low, upper_low, mixed_low, hidden, normed, attended, second_normed)
    return (input_grad, parts, norm_terms)


def weight_terms(parts):
    output_low, branch_low, upper_low, mixed_low, hidden, normed, attended, second_normed = parts
    width = output_low.shape[1]
    return (
        contract_rows(mixed_low, normed),
        jnp.sum(mixed_low[:, :width], axis=0, dtype=jnp.float32),
        jnp.sum(mixed_low[:, 2 * width :], axis=0, dtype=jnp.float32),
        contract_rows(branch_low, attended),
        jnp.sum(branch_low, axis=0, dtype=jnp.float32),
        contract_rows(upper_low, second_normed),
        jnp.sum(upper_low, axis=0, dtype=jnp.float32),
        contract_rows(output_low, hidden),
        jnp.sum(output_low, axis=0, dtype=jnp.float32),
    )


def on_device(
    inputs,
    cotangent,
    segments,
    valid_flags,
    first_gain,
    first_shift,
    project_weight,
    query_bias,
    value_bias,
    out_weight,
    out_bias,
    second_gain,
    second_shift,
    up_weight,
    up_bias,
    down_weight,
    down_bias,
):
    section_index = lax.axis_index("section")
    section_count = lax.axis_size("section")
    weights = tuple(
        (
            member[0]
            for member in (
                first_gain,
                first_shift,
                project_weight,
                query_bias,
                value_bias,
                out_weight,
                out_bias,
                second_gain,
                second_shift,
                up_weight,
                up_bias,
                down_weight,
                down_bias,
            )
        )
    )
    width = inputs.shape[1]
    hidden_width = up_weight.shape[2]
    micro_rows = inputs.shape[0] // MICRO
    buffers = stash_zeros(MICRO, micro_rows, width, hidden_width)
    layer_outs = jnp.zeros((MICRO, micro_rows, width), jnp.bfloat16)
    arrived = jnp.zeros((micro_rows, width), jnp.bfloat16)
    tick_total = MICRO + section_count - 1
    for tick_index in range(tick_total):
        micro_index = tick_index - section_index
        active = (micro_index >= 0) & (micro_index < MICRO)
        mb_slot = jnp.clip(micro_index, 0, MICRO - 1)
        row_start = mb_slot * micro_rows

        def run_tick(carried):
            buffers_in, outs_in, arrived_in = carried
            fresh = lax.dynamic_slice_in_dim(inputs, row_start, micro_rows, 0)
            layer_in = jnp.where(section_index == 0, fresh, arrived_in)
            segment = lax.dynamic_slice_in_dim(segments, row_start, micro_rows, 0)
            validity = lax.dynamic_slice_in_dim(valid_flags, row_start, micro_rows, 0)
            layer_result, stash = layer_forward(weights, layer_in, segment, validity)
            stash = stash[: len(buffers_in)]
            buffers_out = tuple(
                (
                    lax.dynamic_update_index_in_dim(buffer, member, mb_slot, 0)
                    for buffer, member in zip(buffers_in, stash)
                )
            )
            outs_out = lax.dynamic_update_index_in_dim(
                outs_in, layer_result.astype(jnp.bfloat16), mb_slot, 0
            )
            return (buffers_out, outs_out)

        def skip_tick(carried):
            return (carried[0], carried[1])

        buffers, layer_outs = lax.cond(active, run_tick, skip_tick, (buffers, layer_outs, arrived))
        if tick_index + 1 < tick_total:
            outgoing = lax.dynamic_index_in_dim(layer_outs, mb_slot, 0, keepdims=False)
            arrived = from_behind(outgoing, "section", 1)
    input_grads = jnp.zeros((MICRO, micro_rows, width), jnp.float32)
    weight_parts = (
        jnp.zeros((3 * width, width), jnp.float32),
        jnp.zeros((width,), jnp.float32),
        jnp.zeros((width,), jnp.float32),
        jnp.zeros((width, width), jnp.float32),
        jnp.zeros((width,), jnp.float32),
        jnp.zeros((hidden_width, width), jnp.float32),
        jnp.zeros((hidden_width,), jnp.float32),
        jnp.zeros((width, hidden_width), jnp.float32),
        jnp.zeros((width,), jnp.float32),
    )
    norm_sums = tuple((jnp.zeros((width,), jnp.float32) for unused in range(4)))
    coming = jnp.zeros((micro_rows, width), jnp.bfloat16)
    for tick_index in range(tick_total):
        back_order = tick_index - (section_count - 1 - section_index)
        active = (back_order >= 0) & (back_order < MICRO)
        mb_slot = jnp.clip(MICRO - 1 - back_order, 0, MICRO - 1)
        row_start = mb_slot * micro_rows

        def back_tick(carried):
            grads_in, parts_in, sums_in, coming_in = carried
            last_rows = lax.dynamic_slice_in_dim(cotangent, row_start, micro_rows, 0)
            gradient = jnp.where(section_index == section_count - 1, last_rows, coming_in).astype(
                jnp.float32
            )
            segment = lax.dynamic_slice_in_dim(segments, row_start, micro_rows, 0)
            validity = lax.dynamic_slice_in_dim(valid_flags, row_start, micro_rows, 0)
            stash = tuple(
                (lax.dynamic_index_in_dim(buffer, mb_slot, 0, keepdims=False) for buffer in buffers)
            )
            input_grad, parts, norm_terms = layer_backward(
                weights, stash, gradient, segment, validity
            )
            grads_out = lax.dynamic_update_index_in_dim(grads_in, input_grad, mb_slot, 0)
            parts_out = tuple(
                (running + addend for running, addend in zip(parts_in, weight_terms(parts)))
            )
            sums_out = tuple((running + addend for running, addend in zip(sums_in, norm_terms)))
            return (grads_out, parts_out, sums_out)

        def rest_tick(carried):
            return (carried[0], carried[1], carried[2])

        input_grads, weight_parts, norm_sums = lax.cond(
            active, back_tick, rest_tick, (input_grads, weight_parts, norm_sums, coming)
        )
        if tick_index + 1 < tick_total:
            outgoing = lax.dynamic_index_in_dim(input_grads, mb_slot, 0, keepdims=False).astype(
                jnp.bfloat16
            )
            coming = from_behind(outgoing, "section", -1)
    all_rows = MICRO * micro_rows
    (
        project_term,
        query_bias_term,
        value_bias_term,
        out_weight_term,
        out_bias_term,
        up_weight_term,
        up_bias_term,
        down_weight_term,
        down_bias_term,
    ) = weight_parts
    shards = lax.axis_size("dp")
    vectors = (
        norm_sums[0],
        norm_sums[1],
        query_bias_term,
        value_bias_term,
        out_bias_term,
        norm_sums[2],
        norm_sums[3],
        up_bias_term,
        down_bias_term,
    )
    sizes = [vector.shape[0] // shards for vector in vectors]
    packed = jnp.concatenate([vector.reshape(shards, -1) for vector in vectors], axis=1)
    packed = lax.psum_scatter(packed, "dp", scatter_dimension=0, tiled=True)[0]
    small = []
    start = 0
    for size in sizes:
        small.append(packed[start : start + size][None])
        start += size

    def reduce_rows(term):
        piece = lax.psum_scatter(
            term.astype(jnp.bfloat16), "dp", scatter_dimension=0, tiled=True
        )
        return piece.astype(jnp.float32).T[None]

    return (
        layer_outs.reshape(1, all_rows, width),
        input_grads.reshape(1, all_rows, width),
        small[0],
        small[1],
        reduce_rows(project_term),
        small[2],
        small[3],
        reduce_rows(out_weight_term),
        small[4],
        small[5],
        small[6],
        reduce_rows(up_weight_term),
        small[7],
        reduce_rows(down_weight_term),
        small[8],
    )


def solution(mesh):
    in_specs = (
        P("dp", None),
        P("dp", None),
        P("dp"),
        P("dp"),
        P("section", None),
        P("section", None),
        P("section", None, None),
        P("section", None),
        P("section", None),
        P("section", None, None),
        P("section", None),
        P("section", None),
        P("section", None),
        P("section", None, None),
        P("section", None),
        P("section", None, None),
        P("section", None),
    )
    out_specs = (
        P("section", "dp", None),
        P("section", "dp", None),
        P("section", "dp"),
        P("section", "dp"),
        P("section", None, "dp"),
        P("section", "dp"),
        P("section", "dp"),
        P("section", None, "dp"),
        P("section", "dp"),
        P("section", "dp"),
        P("section", "dp"),
        P("section", None, "dp"),
        P("section", "dp"),
        P("section", None, "dp"),
        P("section", "dp"),
    )
    return jax.shard_map(
        on_device, mesh=mesh, in_specs=in_specs, out_specs=out_specs, check_vma=False
    )
```

```python
import jax
import jax.numpy as jnp
from jax import lax
from jax.experimental import pallas as pl
from jax.experimental.pallas import tpu as pltpu
from jax.sharding import PartitionSpec as P

HEADS = 12
HEAD_DIM = 64
SEQ = 512
PAIR = 2 * HEAD_DIM
PAIRS = HEADS // 2
TILE = 256
ROWS = 128
EPSILON = 1e-06
SCORE_SCALE = 0.125
FAR = -1e30
F32 = jnp.float32
LOW = jnp.bfloat16
MESH = pl.DeviceIdType.MESH


def times(left, right):
    return lax.dot_general(left, right, (((1,), (0,)), ((), ())), preferred_element_type=F32)


def times_t(left, right):
    return lax.dot_general(left, right, (((1,), (1,)), ((), ())), preferred_element_type=F32)


def loop(count, body):
    def step(index, carry):
        body(index)
        return carry

    lax.fori_loop(0, count, step, 0)


def part(index, size):
    return pl.ds(pl.multiple_of(index * size, size), size)


def norm_rows(values):
    average = jnp.mean(values, axis=-1, keepdims=True)
    centred = values - average
    inv_scale = lax.rsqrt(jnp.mean(centred * centred, axis=-1, keepdims=True) + EPSILON)
    return centred * inv_scale, inv_scale


def norm_back(normed_grad, whitened, inv_scale, gain):
    scaled = normed_grad * gain
    return inv_scale * (
        scaled
        - jnp.mean(scaled, axis=-1, keepdims=True)
        - whitened * jnp.mean(scaled * whitened, axis=-1, keepdims=True)
    )


def fold_rows(values):
    rows, width = values.shape
    return jnp.sum(values.reshape(rows // 8, 8, width), axis=0)


def fill_bias(code_row, bias):
    across = jnp.transpose(jnp.broadcast_to(code_row, (128, SEQ)))
    for block in range(SEQ // 128):
        lanes = slice(block * 128, (block + 1) * 128)
        bias[:, lanes] = jnp.where(across == code_row[:, lanes], 0.0, FAR)


def gelu_both(upper):
    cumulative = 0.5 * (1.0 + lax.erf(upper * (0.5**0.5)))
    density = jnp.exp(-0.5 * (upper * upper)) * 0.3989422804014327
    return upper * cumulative, cumulative + upper * density


def relay_kernel(
    x_hbm,
    cot_hbm,
    code_ref,
    first_gain,
    first_shift,
    project_hbm,
    query_bias,
    value_bias,
    out_hbm,
    out_bias,
    second_gain,
    second_shift,
    up_hbm,
    up_bias,
    down_hbm,
    down_bias,
    result_hbm,
    input_grad_hbm,
    sums_ref,
    up_sums_ref,
    normed_hbm,
    attended_hbm,
    second_hbm,
    hidden_hbm,
    mixed_hbm,
    branch_hbm,
    upper_hbm,
    output_hbm,
    project,
    out_weight,
    up_weight,
    down_weight,
    x_in,
    g_in,
    normed,
    mixed,
    attended,
    middle,
    second_normed,
    hidden,
    slope,
    result,
    branch,
    attended_low,
    wide,
    input_grad,
    grad_low,
    bias,
    lse_cols,
    lse_rows,
    delta_rows,
    sums,
    up_sums,
    weight_sem,
    x_sem,
    g_sem,
    send_sem,
    out_sem,
):
    section = lax.axis_index("section")
    width = x_in.shape[2]
    hidden_width = hidden.shape[2]
    packs = x_in.shape[0]
    last = lax.axis_size("section") - 1
    partner = {"section": 1 - section}

    def rows_of(ref, pack):
        return ref.at[pl.ds(pl.multiple_of(pack * SEQ, SEQ), SEQ)]

    weights = (
        pltpu.make_async_copy(project_hbm.at[0], project, weight_sem.at[0]),
        pltpu.make_async_copy(out_hbm.at[0], out_weight, weight_sem.at[1]),
        pltpu.make_async_copy(up_hbm.at[0], up_weight, weight_sem.at[2]),
        pltpu.make_async_copy(down_hbm.at[0], down_weight, weight_sem.at[3]),
    )

    @pl.when(section == 0)
    def _():
        for pack in range(packs):
            pltpu.make_async_copy(rows_of(x_hbm, pack), x_in.at[pack], x_sem.at[pack]).start()

    for copy in weights:
        copy.start()

    @pl.when(section == last)
    def _():
        for pack in range(packs):
            pltpu.make_async_copy(rows_of(cot_hbm, pack), g_in.at[pack], g_sem.at[pack]).start()

    barrier = pltpu.get_barrier_semaphore()
    pl.semaphore_signal(barrier, inc=1, device_id=partner, device_id_type=MESH)
    pl.semaphore_wait(barrier, 1)

    sums[...] = jnp.zeros_like(sums)
    up_sums[...] = jnp.zeros_like(up_sums)

    def hop_forward(pack):
        return pltpu.make_async_remote_copy(
            src_ref=result.at[pack],
            dst_ref=x_in.at[pack],
            send_sem=send_sem.at[0, pack],
            recv_sem=x_sem.at[pack],
            device_id=partner,
            device_id_type=MESH,
        )

    def hop_backward(pack):
        return pltpu.make_async_remote_copy(
            src_ref=grad_low.at[pack],
            dst_ref=g_in.at[pack],
            send_sem=send_sem.at[1, pack],
            recv_sem=g_sem.at[pack],
            device_id=partner,
            device_id_type=MESH,
        )

    kept = (
        (result, result_hbm),
        (normed, normed_hbm),
        (attended, attended_hbm),
        (second_normed, second_hbm),
        (hidden, hidden_hbm),
        (mixed, mixed_hbm),
        (branch, branch_hbm),
        (slope, upper_hbm),
        (g_in, output_hbm),
        (input_grad, input_grad_hbm),
    )

    def store(index, pack):
        source, target = kept[index]
        return pltpu.make_async_copy(source.at[pack], rows_of(target, pack), out_sem.at[index, pack])

    lane = lax.broadcasted_iota(jnp.int32, (SEQ, PAIR), 1)

    def forward(pack):
        first = pack == 0

        @pl.when(section == 0)
        def _():
            pltpu.make_async_copy(rows_of(x_hbm, pack), x_in.at[pack], x_sem.at[pack]).wait()

        @pl.when(section == last)
        def _():
            hop_forward(pack).wait_recv()

        gain = first_gain[...].astype(F32)
        shift = first_shift[...].astype(F32)

        def norm_step(block):
            rows = part(block, ROWS)
            white, _ = norm_rows(x_in[pack, rows].astype(F32))
            normed[pack, rows] = (white * gain + shift).astype(LOW)

        loop(SEQ // ROWS, norm_step)
        fill_bias(code_ref[pack], bias)

        @pl.when(first)
        def _():
            weights[0].wait()

        for third, offset_ref in enumerate((query_bias, None, value_bias)):

            def project_step(tile, third=third, offset_ref=offset_ref):
                here = part(tile, TILE)
                there = pl.ds(pl.multiple_of(third * width + tile * TILE, TILE), TILE)
                value = times(normed[pack], project[:, there])
                if offset_ref is not None:
                    value = value + offset_ref[:, here].astype(F32)
                mixed[pack, :, there] = value.astype(LOW)

            loop(width // TILE, project_step)

        def attend_step(pair):
            here = part(pair, PAIR)
            query = mixed[pack, :, here]
            key = mixed[pack, :, pl.ds(pl.multiple_of(width + pair * PAIR, PAIR), PAIR)]
            value = mixed[pack, :, pl.ds(pl.multiple_of(2 * width + pair * PAIR, PAIR), PAIR)]
            for block in range(SEQ // TILE):
                rows = slice(block * TILE, (block + 1) * TILE)
                outs = []
                for side in range(2):
                    own = (lane[rows] < HEAD_DIM) == (side == 0)
                    one = jnp.where(own, query[rows] * SCORE_SCALE, 0.0).astype(LOW)
                    scores = times_t(one, key) + bias[rows]
                    row_max = jnp.max(scores, axis=-1, keepdims=True)
                    exponent = jnp.exp(scores - row_max)
                    row_sum = jnp.sum(exponent, axis=-1, keepdims=True)
                    outs.append(times(exponent.astype(LOW), value) * (1.0 / row_sum))
                    log_sum = row_max + jnp.log(row_sum)
                    lse_cols[rows] = jnp.where(lane[rows] == 2 * pair + side, log_sum, lse_cols[rows])
                attended[pack, rows, here] = jnp.where(lane[rows] < HEAD_DIM, outs[0], outs[1]).astype(LOW)

        loop(PAIRS, attend_step)
        lse_rows[pack] = jnp.transpose(lse_cols[...])[: lse_rows.shape[1]]

        @pl.when(first)
        def _():
            weights[1].wait()

        def out_step(tile):
            here = part(tile, TILE)
            middle[pack, :, here] = x_in[pack, :, here].astype(F32) + (
                times(attended[pack], out_weight[:, here]) + out_bias[:, here].astype(F32)
            )

        loop(width // TILE, out_step)
        gain2 = second_gain[...].astype(F32)
        shift2 = second_shift[...].astype(F32)

        def second_step(block):
            rows = part(block, ROWS)
            white, _ = norm_rows(middle[pack, rows])
            second_normed[pack, rows] = (white * gain2 + shift2).astype(LOW)

        loop(SEQ // ROWS, second_step)

        @pl.when(first)
        def _():
            weights[2].wait()

        def up_step(tile):
            here = part(tile, TILE)
            upper = times(second_normed[pack], up_weight[:, here]) + up_bias[:, here].astype(F32)
            act, act_slope = gelu_both(upper)
            hidden[pack, :, here] = act.astype(LOW)
            slope[pack, :, here] = act_slope.astype(LOW)

        loop(hidden_width // TILE, up_step)

        @pl.when(first)
        def _():
            weights[3].wait()

        def down_step(tile):
            here = part(tile, TILE)
            value = middle[pack, :, here] + (
                times(hidden[pack], down_weight[:, here]) + down_bias[:, here].astype(F32)
            )
            result[pack, :, here] = value.astype(LOW)

        loop(width // TILE, down_step)

        @pl.when(section == 0)
        def _():
            hop_forward(pack).start()

        for index in range(5):
            store(index, pack).start()

    def backward(order):
        pack = packs - 1 - order

        @pl.when(section == last)
        def _():
            pltpu.make_async_copy(rows_of(cot_hbm, pack), g_in.at[pack], g_sem.at[pack]).wait()

        @pl.when(section == 0)
        def _():
            hop_backward(pack).wait_recv()

        store(8, pack).start()
        fill_bias(code_ref[pack], bias)

        def fold_g(block):
            sums[7] += fold_rows(g_in[pack, part(block, ROWS)].astype(F32))

        loop(SEQ // ROWS, fold_g)

        def hidden_step(tile):
            here = part(tile, TILE)
            value = times_t(g_in[pack], down_weight[here]).astype(LOW).astype(F32)
            low = (value * slope[pack, :, here].astype(F32)).astype(LOW)
            slope[pack, :, here] = low
            up_sums[:, here] += fold_rows(low.astype(F32))

        loop(hidden_width // TILE, hidden_step)
        store(7, pack).start()

        def second_step(tile):
            here = part(tile, TILE)
            wide[:, here] = times_t(slope[pack], up_weight[here])

        loop(width // TILE, second_step)
        gain2 = second_gain[...].astype(F32)

        def second_back(block):
            rows = part(block, ROWS)
            grad = wide[rows]
            white, scale = norm_rows(middle[pack, rows])
            total = g_in[pack, rows].astype(F32) + norm_back(grad, white, scale, gain2)
            sums[5] += fold_rows(grad * white)
            sums[6] += fold_rows(grad)
            middle[pack, rows] = total
            low = total.astype(LOW)
            branch[pack, rows] = low
            sums[4] += fold_rows(low.astype(F32))

        loop(SEQ // ROWS, second_back)
        store(6, pack).start()

        def attended_step(tile):
            here = part(tile, TILE)
            attended_low[:, here] = times_t(branch[pack], out_weight[here]).astype(LOW)

        loop(width // TILE, attended_step)

        head_of = lax.broadcasted_iota(jnp.int32, (delta_rows.shape[0], width), 1) // HEAD_DIM
        pick = jnp.where(head_of == lax.broadcasted_iota(jnp.int32, head_of.shape, 0), 1.0, 0.0).astype(LOW)
        product = attended_low[...].astype(F32) * attended[pack].astype(F32)
        coarse = product.astype(LOW)
        fine = (product - coarse.astype(F32)).astype(LOW)
        delta_rows[...] = times_t(pick, coarse) + times_t(pick, fine)

        def attend_back(pair):
            here = part(pair, PAIR)
            key_part = pl.ds(pl.multiple_of(width + pair * PAIR, PAIR), PAIR)
            value_part = pl.ds(pl.multiple_of(2 * width + pair * PAIR, PAIR), PAIR)
            query = mixed[pack, :, here]
            key = mixed[pack, :, key_part]
            value = mixed[pack, :, value_part]
            upstream = attended_low[:, here]
            key_across = jnp.transpose(key)
            query_across = []
            key_grad = [0.0, 0.0]
            value_grad = [0.0, 0.0]
            for side in range(2):
                own = (lane < HEAD_DIM) == (side == 0)
                one_query = jnp.where(own, query * SCORE_SCALE, 0.0).astype(LOW)
                one_up = jnp.where(own, upstream, 0.0).astype(LOW)
                log_row = lse_rows[pack, pl.ds(2 * pair + side, 1)]
                delta_row = delta_rows[pl.ds(2 * pair + side, 1)]
                heads = slice(side * HEAD_DIM, (side + 1) * HEAD_DIM)
                across = 0.0
                for block in range(SEQ // TILE):
                    rows = slice(block * TILE, (block + 1) * TILE)
                    soft = jnp.exp(times_t(key[rows], one_query) + bias[rows] - log_row)
                    soft_grad = times_t(value[rows], one_up)
                    score_low = (soft * (soft_grad - delta_row)).astype(LOW)
                    value_grad[block] += times(soft.astype(LOW), one_up)
                    key_grad[block] += times(score_low, one_query)
                    across += times(key_across[heads, rows], score_low)
                query_across.append(across)
            query_grad = (jnp.transpose(jnp.concatenate(query_across, axis=0)) * SCORE_SCALE).astype(LOW)
            mixed[pack, :, here] = query_grad
            sums[2, :, here] += fold_rows(query_grad.astype(F32))
            for block in range(SEQ // TILE):
                rows = slice(block * TILE, (block + 1) * TILE)
                mixed[pack, rows, key_part] = key_grad[block].astype(LOW)
                low = value_grad[block].astype(LOW)
                mixed[pack, rows, value_part] = low
                sums[3, :, here] += fold_rows(low.astype(F32))

        loop(PAIRS, attend_back)
        store(5, pack).start()

        def first_step(tile):
            here = part(tile, TILE)
            wide[:, here] = times_t(mixed[pack], project[here])

        loop(width // TILE, first_step)
        gain = first_gain[...].astype(F32)

        def first_back(block):
            rows = part(block, ROWS)
            grad = wide[rows]
            white, scale = norm_rows(x_in[pack, rows].astype(F32))
            total = middle[pack, rows] + norm_back(grad, white, scale, gain)
            sums[0] += fold_rows(grad * white)
            sums[1] += fold_rows(grad)
            input_grad[pack, rows] = total
            grad_low[pack, rows] = total.astype(LOW)

        loop(SEQ // ROWS, first_back)

        @pl.when(section == last)
        def _():
            hop_backward(pack).start()

        store(9, pack).start()

    loop(packs, forward)
    loop(packs, backward)

    for index in range(sums.shape[0]):
        sums_ref[index : index + 1] = jnp.sum(sums[index], axis=0, keepdims=True)
    up_sums_ref[...] = jnp.sum(up_sums[...], axis=0, keepdims=True)

    for pack in range(packs):
        for index in range(len(kept)):
            store(index, pack).wait()

    @pl.when(section == 0)
    def _():
        for pack in range(packs):
            hop_forward(pack).wait_send()

    @pl.when(section == last)
    def _():
        for pack in range(packs):
            hop_backward(pack).wait_send()


def relay(arrays):
    inputs, cotangent, segments, valid_flags = arrays[:4]
    rows, width = inputs.shape
    hidden_width = arrays[13].shape[2]
    packs = rows // SEQ
    places = lax.broadcasted_iota(jnp.int32, (rows,), 0) + SEQ
    code = jnp.where(valid_flags == 1, segments, places).astype(F32).reshape(packs, 1, SEQ)
    anywhere = pl.BlockSpec(memory_space=pl.ANY)
    vmem = pl.BlockSpec(memory_space=pltpu.VMEM)

    def low(columns):
        return jax.ShapeDtypeStruct((rows, columns), LOW)

    outs = (
        low(width),
        jax.ShapeDtypeStruct((rows, width), F32),
        jax.ShapeDtypeStruct((8, width), F32),
        jax.ShapeDtypeStruct((1, hidden_width), F32),
        low(width),
        low(width),
        low(width),
        low(hidden_width),
        low(3 * width),
        low(width),
        low(hidden_width),
        low(width),
    )

    def held(columns, kind=LOW):
        return pltpu.VMEM((packs, SEQ, columns), kind)

    scratch = [
        pltpu.VMEM((width, 3 * width), LOW),
        pltpu.VMEM((width, width), LOW),
        pltpu.VMEM((width, hidden_width), LOW),
        pltpu.VMEM((hidden_width, width), LOW),
        held(width),
        held(width),
        held(width),
        held(3 * width),
        held(width),
        held(width, F32),
        held(width),
        held(hidden_width),
        held(hidden_width),
        held(width),
        held(width),
        pltpu.VMEM((SEQ, width), LOW),
        pltpu.VMEM((SEQ, width), F32),
        held(width, F32),
        held(width),
        pltpu.VMEM((SEQ, SEQ), F32),
        pltpu.VMEM((SEQ, 128), F32),
        pltpu.VMEM((packs, 16, SEQ), F32),
        pltpu.VMEM((16, SEQ), F32),
        pltpu.VMEM((8, 8, width), F32),
        pltpu.VMEM((8, hidden_width), F32),
        pltpu.SemaphoreType.DMA((4,)),
        pltpu.SemaphoreType.DMA((packs,)),
        pltpu.SemaphoreType.DMA((packs,)),
        pltpu.SemaphoreType.DMA((2, packs)),
        pltpu.SemaphoreType.DMA((10, packs)),
    ]
    return pl.pallas_call(
        relay_kernel,
        out_shape=outs,
        in_specs=[
            anywhere, anywhere, vmem,
            vmem, vmem, anywhere, vmem, vmem, anywhere, vmem,
            vmem, vmem, anywhere, vmem, anywhere, vmem,
        ],
        out_specs=[anywhere, anywhere, vmem, vmem] + [anywhere] * 8,
        scratch_shapes=scratch,
        name="relay",
        compiler_params=pltpu.CompilerParams(
            collective_id=0, has_side_effects=True, vmem_limit_bytes=66 * 2**20 - 2**21
        ),
    )(inputs, cotangent, code, *arrays[4:])


def contract_rows(left, right):
    return lax.dot_general(left, right, (((0,), (0,)), ((), ())), preferred_element_type=F32)


def on_device(*arrays):
    shards = lax.axis_size("dp")
    (
        result, input_grad, sums, up_sums,
        normed, attended, second_normed, hidden, mixed, branch, upper_low, output_low,
    ) = relay(arrays)

    def reduce_rows(left, right):
        term = contract_rows(left, right).astype(LOW)
        piece = lax.psum_scatter(term, "dp", scatter_dimension=0, tiled=True)
        return piece.astype(F32).T[None]

    packed = jnp.concatenate([sums.reshape(-1, shards, sums.shape[1] // shards).transpose(1, 0, 2).reshape(shards, -1), up_sums.reshape(shards, -1)], axis=1)
    packed = lax.psum_scatter(packed, "dp", scatter_dimension=0, tiled=True)
    size = sums.shape[1] // shards
    small = [packed[:, index * size : (index + 1) * size] for index in range(8)]
    up_small = packed[:, 8 * size :]
    return (
        result[None],
        input_grad[None],
        small[0],
        small[1],
        reduce_rows(mixed, normed),
        small[2],
        small[3],
        reduce_rows(branch, attended),
        small[4],
        small[5],
        small[6],
        reduce_rows(upper_low, second_normed),
        up_small,
        reduce_rows(output_low, hidden),
        small[7],
    )


def solution(mesh):
    stack1 = P("section", None)
    stack2 = P("section", None, None)
    in_specs = (
        P("dp", None), P("dp", None), P("dp"), P("dp"),
        stack1, stack1, stack2, stack1, stack1, stack2, stack1,
        stack1, stack1, stack2, stack1, stack2, stack1,
    )
    row = P("section", "dp")
    matrix = P("section", None, "dp")
    rows = P("section", "dp", None)
    out_specs = (
        rows, rows, row, row, matrix, row, row, matrix, row, row, row, matrix, row, matrix, row,
    )
    return jax.shard_map(
        on_device, mesh=mesh, in_specs=in_specs, out_specs=out_specs, check_vma=False
    )
```

```python
import jax
import jax.numpy as jnp
from jax import lax
from jax.experimental import pallas as pl
from jax.experimental.pallas import tpu as pltpu
from jax.sharding import PartitionSpec as P

HEADS = 12
HEAD_DIM = 64
SEQ = 512
PAIR = 2 * HEAD_DIM
PAIRS = HEADS // 2
TILE = 256
ROWS = 128
EPSILON = 1e-06
SCORE_SCALE = 0.125
FAR = -1e30
F32 = jnp.float32
LOW = jnp.bfloat16
MESH = pl.DeviceIdType.MESH


def times(left, right):
    return lax.dot_general(left, right, (((1,), (0,)), ((), ())), preferred_element_type=F32)


def times_t(left, right):
    return lax.dot_general(left, right, (((1,), (1,)), ((), ())), preferred_element_type=F32)


def loop(count, body):
    def step(index, carry):
        body(index)
        return carry

    lax.fori_loop(0, count, step, 0)


def part(index, size):
    return pl.ds(pl.multiple_of(index * size, size), size)


def norm_rows(values):
    average = jnp.mean(values, axis=-1, keepdims=True)
    centred = values - average
    inv_scale = lax.rsqrt(jnp.mean(centred * centred, axis=-1, keepdims=True) + EPSILON)
    return centred * inv_scale, inv_scale


def norm_back(normed_grad, whitened, inv_scale, gain):
    scaled = normed_grad * gain
    return inv_scale * (
        scaled
        - jnp.mean(scaled, axis=-1, keepdims=True)
        - whitened * jnp.mean(scaled * whitened, axis=-1, keepdims=True)
    )


def fold_rows(values):
    rows, width = values.shape
    return jnp.sum(values.reshape(rows // 8, 8, width), axis=0)


def fill_bias(code_row, bias):
    across = jnp.transpose(jnp.broadcast_to(code_row, (128, SEQ)))
    for block in range(SEQ // 128):
        lanes = slice(block * 128, (block + 1) * 128)
        bias[:, lanes] = jnp.where(across == code_row[:, lanes], 0.0, FAR)


def gelu_both(upper):
    cumulative = 0.5 * (1.0 + lax.erf(upper * (0.5**0.5)))
    density = jnp.exp(-0.5 * (upper * upper)) * 0.3989422804014327
    return upper * cumulative, cumulative + upper * density


def relay_kernel(
    x_hbm,
    cot_hbm,
    code_ref,
    first_gain,
    first_shift,
    project_hbm,
    query_bias,
    value_bias,
    out_hbm,
    out_bias,
    second_gain,
    second_shift,
    up_hbm,
    up_bias,
    down_hbm,
    down_bias,
    result_hbm,
    input_grad_hbm,
    vector_ref,
    normed_hbm,
    attended_hbm,
    second_hbm,
    hidden_hbm,
    mixed_hbm,
    branch_hbm,
    upper_hbm,
    output_hbm,
    project,
    out_weight,
    up_weight,
    down_weight,
    x_in,
    g_in,
    normed,
    mixed,
    attended,
    middle,
    second_normed,
    hidden,
    slope,
    result,
    branch,
    attended_low,
    wide,
    input_grad,
    grad_low,
    bias,
    lse_cols,
    lse_rows,
    soft_all,
    weighted_all,
    sums,
    up_sums,
    weight_sem,
    x_sem,
    g_sem,
    send_sem,
    out_sem,
):
    section = lax.axis_index("section")
    width = x_in.shape[2]
    hidden_width = hidden.shape[2]
    packs = x_in.shape[0]
    last = lax.axis_size("section") - 1
    partner = {"section": 1 - section}

    def rows_of(ref, pack):
        return ref.at[pl.ds(pl.multiple_of(pack * SEQ, SEQ), SEQ)]

    weights = (
        pltpu.make_async_copy(project_hbm.at[0], project, weight_sem.at[0]),
        pltpu.make_async_copy(out_hbm.at[0], out_weight, weight_sem.at[1]),
        pltpu.make_async_copy(up_hbm.at[0], up_weight, weight_sem.at[2]),
        pltpu.make_async_copy(down_hbm.at[0], down_weight, weight_sem.at[3]),
    )

    @pl.when(section == 0)
    def _():
        for pack in range(packs):
            pltpu.make_async_copy(rows_of(x_hbm, pack), x_in.at[pack], x_sem.at[pack]).start()

    for copy in weights:
        copy.start()

    @pl.when(section == last)
    def _():
        for pack in range(packs):
            pltpu.make_async_copy(rows_of(cot_hbm, pack), g_in.at[pack], g_sem.at[pack]).start()

    barrier = pltpu.get_barrier_semaphore()
    pl.semaphore_signal(barrier, inc=1, device_id=partner, device_id_type=MESH)
    pl.semaphore_wait(barrier, 1)

    sums[...] = jnp.zeros_like(sums)
    up_sums[...] = jnp.zeros_like(up_sums)

    def hop_forward(pack):
        return pltpu.make_async_remote_copy(
            src_ref=result.at[pack],
            dst_ref=x_in.at[pack],
            send_sem=send_sem.at[0, pack],
            recv_sem=x_sem.at[pack],
            device_id=partner,
            device_id_type=MESH,
        )

    def hop_backward(pack):
        return pltpu.make_async_remote_copy(
            src_ref=grad_low.at[pack],
            dst_ref=g_in.at[pack],
            send_sem=send_sem.at[1, pack],
            recv_sem=g_sem.at[pack],
            device_id=partner,
            device_id_type=MESH,
        )

    kept = (
        (result, result_hbm),
        (normed, normed_hbm),
        (attended, attended_hbm),
        (second_normed, second_hbm),
        (hidden, hidden_hbm),
        (mixed, mixed_hbm),
        (branch, branch_hbm),
        (slope, upper_hbm),
        (g_in, output_hbm),
        (input_grad, input_grad_hbm),
    )

    def store(index, pack):
        source, target = kept[index]
        return pltpu.make_async_copy(source.at[pack], rows_of(target, pack), out_sem.at[index, pack])

    lane = lax.broadcasted_iota(jnp.int32, (SEQ, PAIR), 1)

    def forward(pack):
        first = pack == 0

        @pl.when(section == 0)
        def _():
            pltpu.make_async_copy(rows_of(x_hbm, pack), x_in.at[pack], x_sem.at[pack]).wait()

        @pl.when(section == last)
        def _():
            hop_forward(pack).wait_recv()

        gain = first_gain[...].astype(F32)
        shift = first_shift[...].astype(F32)

        def norm_step(block):
            rows = part(block, ROWS)
            white, _ = norm_rows(x_in[pack, rows].astype(F32))
            normed[pack, rows] = (white * gain + shift).astype(LOW)

        loop(SEQ // ROWS, norm_step)
        fill_bias(code_ref[pack], bias)

        @pl.when(first)
        def _():
            weights[0].wait()

        for third, offset_ref in enumerate((query_bias, None, value_bias)):

            def project_step(tile, third=third, offset_ref=offset_ref):
                here = part(tile, TILE)
                there = pl.ds(pl.multiple_of(third * width + tile * TILE, TILE), TILE)
                value = times(normed[pack], project[:, there])
                if offset_ref is not None:
                    value = value + offset_ref[:, here].astype(F32)
                mixed[pack, :, there] = value.astype(LOW)

            loop(width // TILE, project_step)

        def attend_step(pair):
            here = part(pair, PAIR)
            query = mixed[pack, :, here]
            key = mixed[pack, :, pl.ds(pl.multiple_of(width + pair * PAIR, PAIR), PAIR)]
            value = mixed[pack, :, pl.ds(pl.multiple_of(2 * width + pair * PAIR, PAIR), PAIR)]
            for block in range(SEQ // TILE):
                rows = slice(block * TILE, (block + 1) * TILE)
                outs = []
                for side in range(2):
                    own = (lane[rows] < HEAD_DIM) == (side == 0)
                    one = jnp.where(own, query[rows] * SCORE_SCALE, 0.0).astype(LOW)
                    scores = times_t(one, key) + bias[rows]
                    row_max = jnp.max(scores, axis=-1, keepdims=True)
                    exponent = jnp.exp(scores - row_max)
                    row_sum = jnp.sum(exponent, axis=-1, keepdims=True)
                    outs.append(times(exponent.astype(LOW), value) * (1.0 / row_sum))
                    log_sum = row_max + jnp.log(row_sum)
                    lse_cols[rows] = jnp.where(lane[rows] == 2 * pair + side, log_sum, lse_cols[rows])
                attended[pack, rows, here] = jnp.where(lane[rows] < HEAD_DIM, outs[0], outs[1]).astype(LOW)

        loop(PAIRS, attend_step)
        lse_rows[pack] = jnp.transpose(lse_cols[...])[: lse_rows.shape[1]]

        @pl.when(first)
        def _():
            weights[1].wait()

        def out_step(tile):
            here = part(tile, TILE)
            middle[pack, :, here] = x_in[pack, :, here].astype(F32) + (
                times(attended[pack], out_weight[:, here]) + out_bias[:, here].astype(F32)
            )

        loop(width // TILE, out_step)
        gain2 = second_gain[...].astype(F32)
        shift2 = second_shift[...].astype(F32)

        def second_step(block):
            rows = part(block, ROWS)
            white, _ = norm_rows(middle[pack, rows])
            second_normed[pack, rows] = (white * gain2 + shift2).astype(LOW)

        loop(SEQ // ROWS, second_step)

        @pl.when(first)
        def _():
            weights[2].wait()

        def up_step(tile):
            here = part(tile, TILE)
            upper = times(second_normed[pack], up_weight[:, here]) + up_bias[:, here].astype(F32)
            act, act_slope = gelu_both(upper)
            hidden[pack, :, here] = act.astype(LOW)
            slope[pack, :, here] = act_slope.astype(LOW)

        loop(hidden_width // TILE, up_step)

        @pl.when(first)
        def _():
            weights[3].wait()

        def down_step(tile):
            here = part(tile, TILE)
            value = middle[pack, :, here] + (
                times(hidden[pack], down_weight[:, here]) + down_bias[:, here].astype(F32)
            )
            result[pack, :, here] = value.astype(LOW)

        loop(width // TILE, down_step)

        @pl.when(section == 0)
        def _():
            hop_forward(pack).start()

        for index in range(5):
            store(index, pack).start()

    def backward(order):
        pack = packs - 1 - order

        @pl.when(section == last)
        def _():
            pltpu.make_async_copy(rows_of(cot_hbm, pack), g_in.at[pack], g_sem.at[pack]).wait()

        @pl.when(section == 0)
        def _():
            hop_backward(pack).wait_recv()

        store(8, pack).start()
        fill_bias(code_ref[pack], bias)

        def fold_g(block):
            sums[7] += fold_rows(g_in[pack, part(block, ROWS)].astype(F32))

        loop(SEQ // ROWS, fold_g)

        def hidden_step(tile):
            here = part(tile, TILE)
            value = times_t(g_in[pack], down_weight[here]).astype(LOW).astype(F32)
            low = (value * slope[pack, :, here].astype(F32)).astype(LOW)
            slope[pack, :, here] = low
            up_sums[:, here] += fold_rows(low.astype(F32))

        loop(hidden_width // TILE, hidden_step)
        store(7, pack).start()

        def second_step(tile):
            here = part(tile, TILE)
            wide[:, here] = times_t(slope[pack], up_weight[here])

        loop(width // TILE, second_step)
        gain2 = second_gain[...].astype(F32)

        def second_back(block):
            rows = part(block, ROWS)
            grad = wide[rows]
            white, scale = norm_rows(middle[pack, rows])
            total = g_in[pack, rows].astype(F32) + norm_back(grad, white, scale, gain2)
            sums[5] += fold_rows(grad * white)
            sums[6] += fold_rows(grad)
            middle[pack, rows] = total
            low = total.astype(LOW)
            branch[pack, rows] = low
            sums[4] += fold_rows(low.astype(F32))

        loop(SEQ // ROWS, second_back)
        store(6, pack).start()

        def attended_step(tile):
            here = part(tile, TILE)
            attended_low[:, here] = times_t(branch[pack], out_weight[here]).astype(LOW)

        loop(width // TILE, attended_step)

        def attend_back(pair):
            here = part(pair, PAIR)
            key_part = pl.ds(pl.multiple_of(width + pair * PAIR, PAIR), PAIR)
            value_part = pl.ds(pl.multiple_of(2 * width + pair * PAIR, PAIR), PAIR)
            query = mixed[pack, :, here]
            key = mixed[pack, :, key_part]
            value = mixed[pack, :, value_part]
            upstream = attended_low[:, here]
            key_across = jnp.transpose(key)
            query_across = []
            key_grad = [0.0, 0.0]
            value_grad = [0.0, 0.0]
            for side in range(2):
                own = (lane < HEAD_DIM) == (side == 0)
                one_query = jnp.where(own, query * SCORE_SCALE, 0.0).astype(LOW)
                one_up = jnp.where(own, upstream, 0.0).astype(LOW)
                log_row = lse_rows[pack, pl.ds(2 * pair + side, 1)]
                heads = slice(side * HEAD_DIM, (side + 1) * HEAD_DIM)
                inner = 0.0
                for block in range(SEQ // TILE):
                    rows = slice(block * TILE, (block + 1) * TILE)
                    soft = jnp.exp(times_t(key[rows], one_query) + bias[rows] - log_row)
                    weighted = soft * times_t(value[rows], one_up)
                    value_grad[block] += times(soft.astype(LOW), one_up)
                    inner += jnp.sum(fold_rows(weighted), axis=0, keepdims=True)
                    soft_all[rows] = soft
                    weighted_all[rows] = weighted
                across = 0.0
                for block in range(SEQ // TILE):
                    rows = slice(block * TILE, (block + 1) * TILE)
                    score_low = (weighted_all[rows] - soft_all[rows] * inner).astype(LOW)
                    key_grad[block] += times(score_low, one_query)
                    across += times(key_across[heads, rows], score_low)
                query_across.append(across)
            query_grad = (jnp.transpose(jnp.concatenate(query_across, axis=0)) * SCORE_SCALE).astype(LOW)
            mixed[pack, :, here] = query_grad
            sums[2, :, here] += fold_rows(query_grad.astype(F32))
            for block in range(SEQ // TILE):
                rows = slice(block * TILE, (block + 1) * TILE)
                mixed[pack, rows, key_part] = key_grad[block].astype(LOW)
                low = value_grad[block].astype(LOW)
                mixed[pack, rows, value_part] = low
                sums[3, :, here] += fold_rows(low.astype(F32))

        loop(PAIRS, attend_back)
        store(5, pack).start()

        def first_step(tile):
            here = part(tile, TILE)
            wide[:, here] = times_t(mixed[pack], project[here])

        loop(width // TILE, first_step)
        gain = first_gain[...].astype(F32)

        def first_back(block):
            rows = part(block, ROWS)
            grad = wide[rows]
            white, scale = norm_rows(x_in[pack, rows].astype(F32))
            total = middle[pack, rows] + norm_back(grad, white, scale, gain)
            sums[0] += fold_rows(grad * white)
            sums[1] += fold_rows(grad)
            input_grad[pack, rows] = total
            grad_low[pack, rows] = total.astype(LOW)

        loop(SEQ // ROWS, first_back)

        @pl.when(section == last)
        def _():
            hop_backward(pack).start()

        store(9, pack).start()

    loop(packs, forward)
    loop(packs, backward)

    count = sums.shape[0]
    for index in range(count):
        vector_ref[index : index + 1] = jnp.sum(sums[index], axis=0, keepdims=True)
    for index in range(hidden_width // width):
        lanes = slice(index * width, (index + 1) * width)
        vector_ref[count + index : count + index + 1] = jnp.sum(up_sums[:, lanes], axis=0, keepdims=True)

    for pack in range(packs):
        for index in range(len(kept)):
            store(index, pack).wait()

    @pl.when(section == 0)
    def _():
        for pack in range(packs):
            hop_forward(pack).wait_send()

    @pl.when(section == last)
    def _():
        for pack in range(packs):
            hop_backward(pack).wait_send()


def relay(arrays):
    inputs, cotangent, segments, valid_flags = arrays[:4]
    rows, width = inputs.shape
    hidden_width = arrays[13].shape[2]
    packs = rows // SEQ
    places = lax.broadcasted_iota(jnp.int32, (rows,), 0) + SEQ
    code = jnp.where(valid_flags == 1, segments, places).astype(F32).reshape(packs, 1, SEQ)
    anywhere = pl.BlockSpec(memory_space=pl.ANY)
    vmem = pl.BlockSpec(memory_space=pltpu.VMEM)

    def low(columns):
        return jax.ShapeDtypeStruct((rows, columns), LOW)

    outs = (
        low(width),
        jax.ShapeDtypeStruct((rows, width), F32),
        jax.ShapeDtypeStruct((8 + hidden_width // width, width), F32),
        low(width),
        low(width),
        low(width),
        low(hidden_width),
        low(3 * width),
        low(width),
        low(hidden_width),
        low(width),
    )

    def held(columns, kind=LOW):
        return pltpu.VMEM((packs, SEQ, columns), kind)

    scratch = [
        pltpu.VMEM((width, 3 * width), LOW),
        pltpu.VMEM((width, width), LOW),
        pltpu.VMEM((width, hidden_width), LOW),
        pltpu.VMEM((hidden_width, width), LOW),
        held(width),
        held(width),
        held(width),
        held(3 * width),
        held(width),
        held(width, F32),
        held(width),
        held(hidden_width),
        held(hidden_width),
        held(width),
        held(width),
        pltpu.VMEM((SEQ, width), LOW),
        pltpu.VMEM((SEQ, width), F32),
        held(width, F32),
        held(width),
        pltpu.VMEM((SEQ, SEQ), F32),
        pltpu.VMEM((SEQ, 128), F32),
        pltpu.VMEM((packs, 16, SEQ), F32),
        pltpu.VMEM((SEQ, SEQ), F32),
        pltpu.VMEM((SEQ, SEQ), F32),
        pltpu.VMEM((8, 8, width), F32),
        pltpu.VMEM((8, hidden_width), F32),
        pltpu.SemaphoreType.DMA((4,)),
        pltpu.SemaphoreType.DMA((packs,)),
        pltpu.SemaphoreType.DMA((packs,)),
        pltpu.SemaphoreType.DMA((2, packs)),
        pltpu.SemaphoreType.DMA((10, packs)),
    ]
    return pl.pallas_call(
        relay_kernel,
        out_shape=outs,
        in_specs=[
            anywhere, anywhere, vmem,
            vmem, vmem, anywhere, vmem, vmem, anywhere, vmem,
            vmem, vmem, anywhere, vmem, anywhere, vmem,
        ],
        out_specs=[anywhere, anywhere, vmem] + [anywhere] * 8,
        scratch_shapes=scratch,
        name="relay",
        compiler_params=pltpu.CompilerParams(
            collective_id=0, has_side_effects=True, vmem_limit_bytes=66 * 2**20 - 2**21
        ),
    )(inputs, cotangent, code, *arrays[4:])


def reduce_kernel(
    vector_ref,
    branch_hbm,
    output_hbm,
    upper_hbm,
    mixed_hbm,
    attended_hbm,
    hidden_hbm,
    second_hbm,
    normed_hbm,
    total_ref,
    whole_ref,
    rights,
    loaded,
    lefts,
    send_core,
    take_core,
    send_x,
    take_x,
    send_z,
    take_z,
    own,
    vectors,
    take_vector,
    right_sem,
    load_sem,
    core_sems,
    x_sems,
    z_sems,
    vector_sems,
):
    units, unit, width = total_ref.shape
    rows = rights.shape[1]
    shards = lax.axis_size("dp")
    levels = shards // 4
    ups = upper_hbm.shape[1] // width
    me = lax.axis_index("dp")
    core, x, z = me % 2, (me // 2) % 2, me // 4
    sibling = {"dp": me + 1 - 2 * core}
    across = {"dp": me + 2 - 4 * x}

    def level_peer(step):
        return {"dp": ((z + step) % levels) * 4 + x * 2 + core}

    first_up = 1 + ups
    first_mixed = first_up + ups

    sources = (
        [attended_hbm]
        + [hidden_hbm.at[:, pl.ds(block * width, width)] for block in range(ups)]
        + [second_hbm, normed_hbm]
    )

    def right_copy(index):
        return pltpu.make_async_copy(sources[index], rights.at[index], right_sem.at[index])

    chunks = [(branch_hbm, 0), (output_hbm, 0)]
    chunks += [(upper_hbm, block) for block in range(ups)]
    chunks += [(mixed_hbm, block) for block in range(3)]

    def left_copy(index):
        source, block = chunks[index]
        return pltpu.make_async_copy(
            source.at[:, pl.ds(block * width, width)], loaded.at[index % 2], load_sem.at[index % 2]
        )

    left_copy(0).start()
    right_copy(0).start()
    left_copy(1).start()
    for index in range(1, len(sources)):
        right_copy(index).start()

    barrier = pltpu.get_barrier_semaphore()
    peers = [sibling, across] + [level_peer(step) for step in range(1, levels)]
    for peer in peers:
        pl.semaphore_signal(barrier, inc=1, device_id=peer, device_id_type=MESH)
    pl.semaphore_wait(barrier, len(peers))

    def send(source, target, sems, index, peer):
        return pltpu.make_async_remote_copy(
            src_ref=source,
            dst_ref=target,
            send_sem=sems.at[(0,) + index],
            recv_sem=sems.at[(1,) + index],
            device_id=peer,
            device_id_type=MESH,
        )

    def to_core(j):
        return send(send_core.at[j], take_core.at[j], core_sems, (j,), sibling)

    def to_x(j):
        return send(send_x.at[j], take_x.at[j], x_sems, (j,), across)

    def to_z(j, step):
        return send(send_z.at[j, step - 1], take_z.at[j, step - 1], z_sems, (j, step - 1), level_peer(step))

    def vector_hop(index):
        peer = (sibling, across)[index] if index < 2 else level_peer(index - 1)
        return send(vectors.at[min(index, 2)], take_vector.at[index], vector_sems, (index,), peer)

    vectors[0] = vector_ref[...]
    vector_hop(0).start()

    def turn(index, group, first_left):
        left_copy(index).wait()
        block = chunks[index][1]
        source = loaded.at[index % 2]
        pieces = unit // 16

        def step(lane_block):
            turned = jnp.transpose(source[:, part(lane_block, 128)])
            for piece in range(8):
                place = block * (width // 16) + lane_block * 8 + piece
                shard, inner = lax.div(place, group), lax.rem(place, group)
                order = (
                    2 * levels * (1 - lax.rem(shard + core, 2))
                    + levels * (1 - lax.rem(lax.div(shard, 2) + x, 2))
                    + lax.div(shard, 4)
                )
                row = pl.multiple_of(order * unit + lax.rem(inner, pieces) * 16, 16)
                lefts[first_left + lax.div(inner, pieces), pl.ds(row, 16)] = turned[piece * 16 : (piece + 1) * 16]

        loop(width // 128, step)
        if index + 2 < len(chunks):
            left_copy(index + 2).start()

    half = 2 * levels * unit
    quarter = levels * unit

    def left_of(j):
        return jnp.maximum(jnp.minimum(j, 1), j + 1 - ups)

    def right_of(j):
        return jnp.minimum(j, first_up) + jnp.where(j >= first_mixed, 1, 0)

    def product(j, start, count, tile):
        return times(lefts[left_of(j), start : start + count], rights[right_of(j), :, part(tile, TILE)])

    def stage_core(j):
        def step(tile):
            send_core[j, :, part(tile, TILE)] = product(j, 0, half, tile).astype(LOW)

        loop(width // TILE, step)
        to_core(j).start()

    def stage_x(j):
        to_core(j).wait_recv()

        def step(tile):
            here = part(tile, TILE)
            value = product(j, half, quarter, tile) + take_core[j, :quarter, here].astype(F32)
            send_x[j, :, here] = value.astype(LOW)

        loop(width // TILE, step)
        to_x(j).start()

    def stage_z(j):
        to_x(j).wait_recv()

        def step(tile):
            here = part(tile, TILE)
            value = (
                product(j, half + quarter, quarter, tile)
                + take_core[j, quarter:, here].astype(F32)
                + take_x[j, :, here].astype(F32)
            )
            own[:, :, here] = value.reshape(levels, unit, TILE)

        loop(width // TILE, step)
        for hop in range(1, levels):
            send_z[j, hop - 1] = own[(z + hop) % levels].astype(LOW)
            to_z(j, hop).start()
        total_ref[j] = own[z]

    def finish(j):
        value = total_ref[j]
        for hop in range(1, levels):
            to_z(j, hop).wait_recv()
            value = value + take_z[j, hop - 1].astype(F32)
        total_ref[j] = value

    def first_phase(start, stop):
        def step(index):
            j = index + start
            stage_core(j)

            @pl.when(j > 0)
            def _():
                stage_x(j - 1)

        loop(stop - start, step)

    turn(0, unit // 16, 0)
    right_copy(0).wait()
    first_phase(0, 1)
    turn(1, unit // 16, 1)
    for index in range(1, 1 + ups):
        right_copy(index).wait()
    first_phase(1, first_up)
    vector_hop(0).wait_recv()
    vectors[1] = vectors[0] + take_vector[0]
    vector_hop(1).start()
    for block in range(ups):
        turn(2 + block, ups * unit // 16, 2)
    right_copy(1 + ups).wait()
    first_phase(first_up, first_mixed)
    for block in range(3):
        turn(2 + ups + block, 3 * unit // 16, 2 + ups)
    right_copy(2 + ups).wait()
    first_phase(first_mixed, units)
    stage_x(units - 1)
    vector_hop(1).wait_recv()
    vectors[2] = vectors[1] + take_vector[1]
    for hop in range(1, levels):
        vector_hop(hop + 1).start()

    def second_phase(j):
        stage_z(j)

        @pl.when(j > 0)
        def _():
            finish(j - 1)

    loop(units, second_phase)
    finish(units - 1)
    whole = vectors[2]
    for hop in range(1, levels):
        vector_hop(hop + 1).wait_recv()
        whole = whole + take_vector[hop + 1]
    whole_ref[...] = whole

    def drain(j):
        to_core(j).wait_send()
        to_x(j).wait_send()
        for hop in range(1, levels):
            to_z(j, hop).wait_send()

    loop(units, drain)
    for hop in range(levels + 1):
        vector_hop(hop).wait_send()


def reduce_parts(vector, lefts, rights):
    shards = lax.axis_size("dp")
    branch, output_low, upper_low, mixed = lefts
    attended, hidden, second_normed, normed = rights
    rows, width = branch.shape
    ups = hidden.shape[1] // width
    unit, levels = width // shards, shards // 4
    units = 1 + 2 * ups + 3
    anywhere = pl.BlockSpec(memory_space=pl.ANY)
    vmem = pl.BlockSpec(memory_space=pltpu.VMEM)
    total, whole = pl.pallas_call(
        reduce_kernel,
        out_shape=(
            jax.ShapeDtypeStruct((units, unit, width), F32),
            jax.ShapeDtypeStruct(vector.shape, F32),
        ),
        in_specs=[vmem] + [anywhere] * 8,
        out_specs=[vmem, vmem],
        scratch_shapes=[
            pltpu.VMEM((3 + ups, rows, width), LOW),
            pltpu.VMEM((2, rows, width), LOW),
            pltpu.VMEM((5 + ups, width, rows), LOW),
            pltpu.VMEM((units, 2 * levels * unit, width), LOW),
            pltpu.VMEM((units, 2 * levels * unit, width), LOW),
            pltpu.VMEM((units, levels * unit, width), LOW),
            pltpu.VMEM((units, levels * unit, width), LOW),
            pltpu.VMEM((units, levels - 1, unit, width), LOW),
            pltpu.VMEM((units, levels - 1, unit, width), LOW),
            pltpu.VMEM((levels, unit, width), F32),
            pltpu.VMEM((3,) + vector.shape, F32),
            pltpu.VMEM((levels + 1,) + vector.shape, F32),
            pltpu.SemaphoreType.DMA((3 + ups,)),
            pltpu.SemaphoreType.DMA((2,)),
            pltpu.SemaphoreType.DMA((2, units)),
            pltpu.SemaphoreType.DMA((2, units)),
            pltpu.SemaphoreType.DMA((2, units, levels - 1)),
            pltpu.SemaphoreType.DMA((2, levels + 1)),
        ],
        name="reduce",
        compiler_params=pltpu.CompilerParams(
            collective_id=1, has_side_effects=True, vmem_limit_bytes=67043328
        ),
    )(vector, branch, output_low, upper_low, mixed, attended, hidden, second_normed, normed)
    first_up, first_mixed = 1 + ups, 1 + 2 * ups
    return (
        whole,
        total[first_mixed:].reshape(3 * unit, width).T,
        total[0].T,
        total[first_up:first_mixed].reshape(ups * unit, width).T,
        total[1:first_up].transpose(0, 2, 1).reshape(ups * width, unit),
    )


def contract_rows(left, right):
    return lax.dot_general(left, right, (((0,), (0,)), ((), ())), preferred_element_type=F32)


def scatter_parts(vector, lefts, rights):
    def reduce_rows(left, right):
        piece = lax.psum_scatter(contract_rows(left, right), "dp", scatter_dimension=0, tiled=True)
        return piece.T

    branch, output_low, upper_low, mixed = lefts
    attended, hidden, second_normed, normed = rights
    return (
        lax.psum(vector, "dp"),
        reduce_rows(mixed, normed),
        reduce_rows(branch, attended),
        reduce_rows(upper_low, second_normed),
        reduce_rows(output_low, hidden),
    )


def on_device(*arrays):
    shards = lax.axis_size("dp")
    me = lax.axis_index("dp")
    (
        result, input_grad, vector,
        normed, attended, second_normed, hidden, mixed, branch, upper_low, output_low,
    ) = relay(arrays)
    lefts = (branch, output_low, upper_low, mixed)
    rights = (attended, hidden, second_normed, normed)
    width = branch.shape[1]
    aligned = shards % 4 == 0 and width % (16 * shards) == 0
    combine = reduce_parts if aligned else scatter_parts
    whole, project_grad, out_grad, up_grad, down_grad = combine(vector, lefts, rights)
    size = width // shards
    small = lax.dynamic_slice_in_dim(whole[:8], me * size, size, 1)
    up_size = hidden.shape[1] // shards
    up_small = lax.dynamic_slice_in_dim(whole[8:].reshape(1, -1), me * up_size, up_size, 1)
    return (
        result[None],
        input_grad[None],
        small[0:1],
        small[1:2],
        project_grad[None],
        small[2:3],
        small[3:4],
        out_grad[None],
        small[4:5],
        small[5:6],
        small[6:7],
        up_grad[None],
        up_small,
        down_grad[None],
        small[7:8],
    )


def solution(mesh):
    stack1 = P("section", None)
    stack2 = P("section", None, None)
    in_specs = (
        P("dp", None), P("dp", None), P("dp"), P("dp"),
        stack1, stack1, stack2, stack1, stack1, stack2, stack1,
        stack1, stack1, stack2, stack1, stack2, stack1,
    )
    row = P("section", "dp")
    matrix = P("section", None, "dp")
    rows = P("section", "dp", None)
    out_specs = (
        rows, rows, row, row, matrix, row, row, matrix, row, row, row, matrix, row, matrix, row,
    )
    return jax.shard_map(
        on_device, mesh=mesh, in_specs=in_specs, out_specs=out_specs, check_vma=False
    )
```

```python
import jax
import jax.numpy as jnp
from jax import lax
from jax.experimental import pallas as pl
from jax.experimental.pallas import tpu as pltpu
from jax.sharding import PartitionSpec as P

HEADS = 12
HEAD_DIM = 64
SEQ = 512
PAIR = 2 * HEAD_DIM
PAIRS = HEADS // 2
TILE = 256
ROWS = 128
EPSILON = 1e-06
SCORE_SCALE = 0.125
FAR = -1e30
F32 = jnp.float32
LOW = jnp.bfloat16
MESH = pl.DeviceIdType.MESH


def times(left, right):
    return lax.dot_general(left, right, (((1,), (0,)), ((), ())), preferred_element_type=F32)


def times_t(left, right):
    return lax.dot_general(left, right, (((1,), (1,)), ((), ())), preferred_element_type=F32)


def loop(count, body):
    def step(index, carry):
        body(index)
        return carry

    lax.fori_loop(0, count, step, 0)


def part(index, size):
    return pl.ds(pl.multiple_of(index * size, size), size)


def norm_rows(values):
    average = jnp.mean(values, axis=-1, keepdims=True)
    centred = values - average
    inv_scale = lax.rsqrt(jnp.mean(centred * centred, axis=-1, keepdims=True) + EPSILON)
    return centred * inv_scale, inv_scale


def norm_back(normed_grad, whitened, inv_scale, gain):
    scaled = normed_grad * gain
    return inv_scale * (
        scaled
        - jnp.mean(scaled, axis=-1, keepdims=True)
        - whitened * jnp.mean(scaled * whitened, axis=-1, keepdims=True)
    )


def fold_rows(values):
    rows, width = values.shape
    return jnp.sum(values.reshape(rows // 8, 8, width), axis=0)


def fill_bias(code_row, bias):
    across = jnp.transpose(jnp.broadcast_to(code_row, (128, SEQ)))
    for block in range(SEQ // 128):
        lanes = slice(block * 128, (block + 1) * 128)
        bias[:, lanes] = jnp.where(across == code_row[:, lanes], 0.0, FAR)


def gelu_both(upper):
    cumulative = 0.5 * (1.0 + lax.erf(upper * (0.5**0.5)))
    density = jnp.exp(-0.5 * (upper * upper)) * 0.3989422804014327
    return upper * cumulative, cumulative + upper * density


def relay_kernel(
    x_hbm,
    cot_hbm,
    code_ref,
    first_gain,
    first_shift,
    project_hbm,
    query_bias,
    value_bias,
    out_hbm,
    out_bias,
    second_gain,
    second_shift,
    up_hbm,
    up_bias,
    down_hbm,
    down_bias,
    result_hbm,
    input_grad_hbm,
    vector_ref,
    normed_hbm,
    attended_hbm,
    second_hbm,
    hidden_hbm,
    mixed_hbm,
    branch_hbm,
    upper_hbm,
    output_hbm,
    project,
    out_weight,
    up_weight,
    down_weight,
    x_in,
    g_in,
    normed,
    mixed,
    attended,
    middle,
    second_normed,
    hidden,
    slope,
    result,
    branch,
    attended_low,
    wide,
    input_grad,
    grad_low,
    bias,
    lse_cols,
    lse_rows,
    soft_all,
    weighted_all,
    sums,
    up_sums,
    weight_sem,
    x_sem,
    g_sem,
    send_sem,
    out_sem,
):
    section = lax.axis_index("section")
    width = x_in.shape[2]
    hidden_width = hidden.shape[2]
    packs = x_in.shape[0]
    last = lax.axis_size("section") - 1
    partner = {"section": 1 - section}

    def rows_of(ref, pack):
        return ref.at[pl.ds(pl.multiple_of(pack * SEQ, SEQ), SEQ)]

    weights = (
        pltpu.make_async_copy(project_hbm.at[0], project, weight_sem.at[0]),
        pltpu.make_async_copy(out_hbm.at[0], out_weight, weight_sem.at[1]),
        pltpu.make_async_copy(up_hbm.at[0], up_weight, weight_sem.at[2]),
        pltpu.make_async_copy(down_hbm.at[0], down_weight, weight_sem.at[3]),
    )

    @pl.when(section == 0)
    def _():
        for pack in range(packs):
            pltpu.make_async_copy(rows_of(x_hbm, pack), x_in.at[pack], x_sem.at[pack]).start()

    for copy in weights:
        copy.start()

    @pl.when(section == last)
    def _():
        for pack in range(packs):
            pltpu.make_async_copy(rows_of(cot_hbm, pack), g_in.at[pack], g_sem.at[pack]).start()

    barrier = pltpu.get_barrier_semaphore()
    pl.semaphore_signal(barrier, inc=1, device_id=partner, device_id_type=MESH)
    pl.semaphore_wait(barrier, 1)

    sums[...] = jnp.zeros_like(sums)
    up_sums[...] = jnp.zeros_like(up_sums)

    def hop_forward(pack):
        return pltpu.make_async_remote_copy(
            src_ref=result.at[pack],
            dst_ref=x_in.at[pack],
            send_sem=send_sem.at[0, pack],
            recv_sem=x_sem.at[pack],
            device_id=partner,
            device_id_type=MESH,
        )

    def hop_backward(pack):
        return pltpu.make_async_remote_copy(
            src_ref=grad_low.at[pack],
            dst_ref=g_in.at[pack],
            send_sem=send_sem.at[1, pack],
            recv_sem=g_sem.at[pack],
            device_id=partner,
            device_id_type=MESH,
        )

    kept = (
        (result, result_hbm),
        (normed, normed_hbm),
        (attended, attended_hbm),
        (second_normed, second_hbm),
        (hidden, hidden_hbm),
        (mixed, mixed_hbm),
        (branch, branch_hbm),
        (slope, upper_hbm),
        (g_in, output_hbm),
        (input_grad, input_grad_hbm),
    )

    def store(index, pack):
        source, target = kept[index]
        return pltpu.make_async_copy(source.at[pack], rows_of(target, pack), out_sem.at[index, pack])

    lane = lax.broadcasted_iota(jnp.int32, (SEQ, PAIR), 1)

    def forward(pack):
        first = pack == 0

        @pl.when(section == 0)
        def _():
            pltpu.make_async_copy(rows_of(x_hbm, pack), x_in.at[pack], x_sem.at[pack]).wait()

        @pl.when(section == last)
        def _():
            hop_forward(pack).wait_recv()

        gain = first_gain[...].astype(F32)
        shift = first_shift[...].astype(F32)

        def norm_step(block):
            rows = part(block, ROWS)
            white, _ = norm_rows(x_in[pack, rows].astype(F32))
            normed[pack, rows] = (white * gain + shift).astype(LOW)

        loop(SEQ // ROWS, norm_step)
        fill_bias(code_ref[pack], bias)

        @pl.when(first)
        def _():
            weights[0].wait()

        for third, offset_ref in enumerate((query_bias, None, value_bias)):

            def project_step(tile, third=third, offset_ref=offset_ref):
                here = part(tile, TILE)
                there = pl.ds(pl.multiple_of(third * width + tile * TILE, TILE), TILE)
                value = times(normed[pack], project[:, there])
                if offset_ref is not None:
                    value = value + offset_ref[:, here].astype(F32)
                mixed[pack, :, there] = value.astype(LOW)

            loop(width // TILE, project_step)

        def attend_step(pair):
            here = part(pair, PAIR)
            query = mixed[pack, :, here]
            key = mixed[pack, :, pl.ds(pl.multiple_of(width + pair * PAIR, PAIR), PAIR)]
            value = mixed[pack, :, pl.ds(pl.multiple_of(2 * width + pair * PAIR, PAIR), PAIR)]
            for block in range(SEQ // TILE):
                rows = slice(block * TILE, (block + 1) * TILE)
                outs = []
                for side in range(2):
                    own = (lane[rows] < HEAD_DIM) == (side == 0)
                    one = jnp.where(own, query[rows] * SCORE_SCALE, 0.0).astype(LOW)
                    scores = times_t(one, key) + bias[rows]
                    row_max = jnp.max(scores, axis=-1, keepdims=True)
                    exponent = jnp.exp(scores - row_max)
                    row_sum = jnp.sum(exponent, axis=-1, keepdims=True)
                    outs.append(times(exponent.astype(LOW), value) * (1.0 / row_sum))
                    log_sum = row_max + jnp.log(row_sum)
                    lse_cols[rows] = jnp.where(lane[rows] == 2 * pair + side, log_sum, lse_cols[rows])
                attended[pack, rows, here] = jnp.where(lane[rows] < HEAD_DIM, outs[0], outs[1]).astype(LOW)

        loop(PAIRS, attend_step)
        lse_rows[pack] = jnp.transpose(lse_cols[...])[: lse_rows.shape[1]]

        @pl.when(first)
        def _():
            weights[1].wait()

        def out_step(tile):
            here = part(tile, TILE)
            middle[pack, :, here] = x_in[pack, :, here].astype(F32) + (
                times(attended[pack], out_weight[:, here]) + out_bias[:, here].astype(F32)
            )

        loop(width // TILE, out_step)
        gain2 = second_gain[...].astype(F32)
        shift2 = second_shift[...].astype(F32)

        def second_step(block):
            rows = part(block, ROWS)
            white, _ = norm_rows(middle[pack, rows])
            second_normed[pack, rows] = (white * gain2 + shift2).astype(LOW)

        loop(SEQ // ROWS, second_step)

        @pl.when(first)
        def _():
            weights[2].wait()

        def up_step(tile):
            here = part(tile, TILE)
            upper = times(second_normed[pack], up_weight[:, here]) + up_bias[:, here].astype(F32)
            act, act_slope = gelu_both(upper)
            hidden[pack, :, here] = act.astype(LOW)
            slope[pack, :, here] = act_slope.astype(LOW)

        loop(hidden_width // TILE, up_step)

        @pl.when(first)
        def _():
            weights[3].wait()

        def down_step(tile):
            here = part(tile, TILE)
            value = middle[pack, :, here] + (
                times(hidden[pack], down_weight[:, here]) + down_bias[:, here].astype(F32)
            )
            result[pack, :, here] = value.astype(LOW)

        loop(width // TILE, down_step)

        @pl.when(section == 0)
        def _():
            hop_forward(pack).start()

        for index in range(5):
            store(index, pack).start()

    def backward(order):
        pack = packs - 1 - order

        @pl.when(section == last)
        def _():
            pltpu.make_async_copy(rows_of(cot_hbm, pack), g_in.at[pack], g_sem.at[pack]).wait()

        @pl.when(section == 0)
        def _():
            hop_backward(pack).wait_recv()

        store(8, pack).start()
        fill_bias(code_ref[pack], bias)

        def fold_g(block):
            sums[7] += fold_rows(g_in[pack, part(block, ROWS)].astype(F32))

        loop(SEQ // ROWS, fold_g)

        def hidden_step(tile):
            here = part(tile, TILE)
            value = times_t(g_in[pack], down_weight[here]).astype(LOW).astype(F32)
            low = (value * slope[pack, :, here].astype(F32)).astype(LOW)
            slope[pack, :, here] = low
            up_sums[:, here] += fold_rows(low.astype(F32))

        loop(hidden_width // TILE, hidden_step)
        store(7, pack).start()

        def second_step(tile):
            here = part(tile, TILE)
            wide[:, here] = times_t(slope[pack], up_weight[here])

        loop(width // TILE, second_step)
        gain2 = second_gain[...].astype(F32)

        def second_back(block):
            rows = part(block, ROWS)
            grad = wide[rows]
            white, scale = norm_rows(middle[pack, rows])
            total = g_in[pack, rows].astype(F32) + norm_back(grad, white, scale, gain2)
            sums[5] += fold_rows(grad * white)
            sums[6] += fold_rows(grad)
            middle[pack, rows] = total
            low = total.astype(LOW)
            branch[pack, rows] = low
            sums[4] += fold_rows(low.astype(F32))

        loop(SEQ // ROWS, second_back)
        store(6, pack).start()

        def attended_step(tile):
            here = part(tile, TILE)
            attended_low[:, here] = times_t(branch[pack], out_weight[here]).astype(LOW)

        loop(width // TILE, attended_step)

        def attend_back(pair):
            here = part(pair, PAIR)
            key_part = pl.ds(pl.multiple_of(width + pair * PAIR, PAIR), PAIR)
            value_part = pl.ds(pl.multiple_of(2 * width + pair * PAIR, PAIR), PAIR)
            query = mixed[pack, :, here]
            key = mixed[pack, :, key_part]
            value = mixed[pack, :, value_part]
            upstream = attended_low[:, here]
            key_across = jnp.transpose(key)
            query_across = []
            key_grad = [0.0, 0.0]
            value_grad = [0.0, 0.0]
            for side in range(2):
                own = (lane < HEAD_DIM) == (side == 0)
                one_query = jnp.where(own, query * SCORE_SCALE, 0.0).astype(LOW)
                one_up = jnp.where(own, upstream, 0.0).astype(LOW)
                log_row = lse_rows[pack, pl.ds(2 * pair + side, 1)]
                heads = slice(side * HEAD_DIM, (side + 1) * HEAD_DIM)
                inner = 0.0
                for block in range(SEQ // TILE):
                    rows = slice(block * TILE, (block + 1) * TILE)
                    soft = jnp.exp(times_t(key[rows], one_query) + bias[rows] - log_row)
                    weighted = soft * times_t(value[rows], one_up)
                    value_grad[block] += times(soft.astype(LOW), one_up)
                    inner += jnp.sum(fold_rows(weighted), axis=0, keepdims=True)
                    soft_all[rows] = soft
                    weighted_all[rows] = weighted
                across = 0.0
                for block in range(SEQ // TILE):
                    rows = slice(block * TILE, (block + 1) * TILE)
                    score_low = (weighted_all[rows] - soft_all[rows] * inner).astype(LOW)
                    key_grad[block] += times(score_low, one_query)
                    across += times(key_across[heads, rows], score_low)
                query_across.append(across)
            query_grad = (jnp.transpose(jnp.concatenate(query_across, axis=0)) * SCORE_SCALE).astype(LOW)
            mixed[pack, :, here] = query_grad
            sums[2, :, here] += fold_rows(query_grad.astype(F32))
            for block in range(SEQ // TILE):
                rows = slice(block * TILE, (block + 1) * TILE)
                mixed[pack, rows, key_part] = key_grad[block].astype(LOW)
                low = value_grad[block].astype(LOW)
                mixed[pack, rows, value_part] = low
                sums[3, :, here] += fold_rows(low.astype(F32))

        loop(PAIRS, attend_back)
        store(5, pack).start()

        def first_step(tile):
            here = part(tile, TILE)
            wide[:, here] = times_t(mixed[pack], project[here])

        loop(width // TILE, first_step)
        gain = first_gain[...].astype(F32)

        def first_back(block):
            rows = part(block, ROWS)
            grad = wide[rows]
            white, scale = norm_rows(x_in[pack, rows].astype(F32))
            total = middle[pack, rows] + norm_back(grad, white, scale, gain)
            sums[0] += fold_rows(grad * white)
            sums[1] += fold_rows(grad)
            input_grad[pack, rows] = total
            grad_low[pack, rows] = total.astype(LOW)

        loop(SEQ // ROWS, first_back)

        @pl.when(section == last)
        def _():
            hop_backward(pack).start()

        store(9, pack).start()

    loop(packs, forward)
    loop(packs, backward)

    count = sums.shape[0]
    for index in range(count):
        vector_ref[index : index + 1] = jnp.sum(sums[index], axis=0, keepdims=True)
    for index in range(hidden_width // width):
        lanes = slice(index * width, (index + 1) * width)
        vector_ref[count + index : count + index + 1] = jnp.sum(up_sums[:, lanes], axis=0, keepdims=True)

    for pack in range(packs):
        for index in range(len(kept)):
            store(index, pack).wait()

    @pl.when(section == 0)
    def _():
        for pack in range(packs):
            hop_forward(pack).wait_send()

    @pl.when(section == last)
    def _():
        for pack in range(packs):
            hop_backward(pack).wait_send()


def relay(arrays):
    inputs, cotangent, segments, valid_flags = arrays[:4]
    rows, width = inputs.shape
    hidden_width = arrays[13].shape[2]
    packs = rows // SEQ
    places = lax.broadcasted_iota(jnp.int32, (rows,), 0) + SEQ
    code = jnp.where(valid_flags == 1, segments, places).astype(F32).reshape(packs, 1, SEQ)
    anywhere = pl.BlockSpec(memory_space=pl.ANY)
    vmem = pl.BlockSpec(memory_space=pltpu.VMEM)

    def low(columns):
        return jax.ShapeDtypeStruct((rows, columns), LOW)

    outs = (
        low(width),
        jax.ShapeDtypeStruct((rows, width), F32),
        jax.ShapeDtypeStruct((8 + hidden_width // width, width), F32),
        low(width),
        low(width),
        low(width),
        low(hidden_width),
        low(3 * width),
        low(width),
        low(hidden_width),
        low(width),
    )

    def held(columns, kind=LOW):
        return pltpu.VMEM((packs, SEQ, columns), kind)

    scratch = [
        pltpu.VMEM((width, 3 * width), LOW),
        pltpu.VMEM((width, width), LOW),
        pltpu.VMEM((width, hidden_width), LOW),
        pltpu.VMEM((hidden_width, width), LOW),
        held(width),
        held(width),
        held(width),
        held(3 * width),
        held(width),
        held(width, F32),
        held(width),
        held(hidden_width),
        held(hidden_width),
        held(width),
        held(width),
        pltpu.VMEM((SEQ, width), LOW),
        pltpu.VMEM((SEQ, width), F32),
        held(width, F32),
        held(width),
        pltpu.VMEM((SEQ, SEQ), F32),
        pltpu.VMEM((SEQ, 128), F32),
        pltpu.VMEM((packs, 16, SEQ), F32),
        pltpu.VMEM((SEQ, SEQ), F32),
        pltpu.VMEM((SEQ, SEQ), F32),
        pltpu.VMEM((8, 8, width), F32),
        pltpu.VMEM((8, hidden_width), F32),
        pltpu.SemaphoreType.DMA((4,)),
        pltpu.SemaphoreType.DMA((packs,)),
        pltpu.SemaphoreType.DMA((packs,)),
        pltpu.SemaphoreType.DMA((2, packs)),
        pltpu.SemaphoreType.DMA((10, packs)),
    ]
    return pl.pallas_call(
        relay_kernel,
        out_shape=outs,
        in_specs=[
            anywhere, anywhere, vmem,
            vmem, vmem, anywhere, vmem, vmem, anywhere, vmem,
            vmem, vmem, anywhere, vmem, anywhere, vmem,
        ],
        out_specs=[anywhere, anywhere, vmem] + [anywhere] * 8,
        scratch_shapes=scratch,
        name="relay",
        compiler_params=pltpu.CompilerParams(
            collective_id=0, has_side_effects=True, vmem_limit_bytes=66 * 2**20 - 2**21
        ),
    )(inputs, cotangent, code, *arrays[4:])


def reduce_kernel(
    vector_ref,
    branch_hbm,
    output_hbm,
    upper_hbm,
    mixed_hbm,
    attended_hbm,
    hidden_hbm,
    second_hbm,
    normed_hbm,
    total_ref,
    whole_ref,
    rights,
    loaded,
    lefts,
    send_core,
    take_core,
    send_x,
    take_x,
    send_z,
    take_z,
    own,
    vectors,
    take_vector,
    right_sem,
    load_sem,
    core_sems,
    x_sems,
    z_sems,
    vector_sems,
):
    units, unit, width = total_ref.shape
    rows = rights.shape[1]
    shards = lax.axis_size("dp")
    levels = shards // 4
    ups = upper_hbm.shape[1] // width
    me = lax.axis_index("dp")
    core, x, z = me % 2, (me // 2) % 2, me // 4
    sibling = {"dp": me + 1 - 2 * core}
    across = {"dp": me + 2 - 4 * x}

    def level_peer(step):
        return {"dp": ((z + step) % levels) * 4 + x * 2 + core}

    first_up = 1 + ups
    first_mixed = first_up + ups

    sources = (
        [attended_hbm]
        + [hidden_hbm.at[:, pl.ds(block * width, width)] for block in range(ups)]
        + [second_hbm, normed_hbm]
    )

    def right_copy(index):
        return pltpu.make_async_copy(sources[index], rights.at[index], right_sem.at[index])

    chunks = [(branch_hbm, 0), (output_hbm, 0)]
    chunks += [(upper_hbm, block) for block in range(ups)]
    chunks += [(mixed_hbm, block) for block in range(3)]

    def left_copy(index):
        source, block = chunks[index]
        return pltpu.make_async_copy(
            source.at[:, pl.ds(block * width, width)], loaded.at[index % 2], load_sem.at[index % 2]
        )

    left_copy(0).start()
    right_copy(0).start()
    left_copy(1).start()
    for index in range(1, len(sources)):
        right_copy(index).start()

    barrier = pltpu.get_barrier_semaphore()
    peers = [sibling, across] + [level_peer(step) for step in range(1, levels)]
    for peer in peers:
        pl.semaphore_signal(barrier, inc=1, device_id=peer, device_id_type=MESH)
    pl.semaphore_wait(barrier, len(peers))

    def send(source, target, sems, index, peer):
        return pltpu.make_async_remote_copy(
            src_ref=source,
            dst_ref=target,
            send_sem=sems.at[(0,) + index],
            recv_sem=sems.at[(1,) + index],
            device_id=peer,
            device_id_type=MESH,
        )

    def to_core(j):
        return send(send_core.at[j], take_core.at[j], core_sems, (j,), sibling)

    def to_x(j):
        return send(send_x.at[j], take_x.at[j], x_sems, (j,), across)

    def to_z(j, step):
        return send(send_z.at[j, step - 1], take_z.at[j, step - 1], z_sems, (j, step - 1), level_peer(step))

    def vector_hop(index):
        peer = (sibling, across)[index] if index < 2 else level_peer(index - 1)
        return send(vectors.at[min(index, 2)], take_vector.at[index], vector_sems, (index,), peer)

    vectors[0] = vector_ref[...]
    vector_hop(0).start()

    def turn(index, group, first_left):
        left_copy(index).wait()
        block = chunks[index][1]
        source = loaded.at[index % 2]
        pieces = unit // 16

        def step(lane_block):
            turned = jnp.transpose(source[:, part(lane_block, 128)])
            for piece in range(8):
                place = block * (width // 16) + lane_block * 8 + piece
                shard, inner = lax.div(place, group), lax.rem(place, group)
                order = (
                    2 * levels * (1 - lax.rem(shard + core, 2))
                    + levels * (1 - lax.rem(lax.div(shard, 2) + x, 2))
                    + lax.div(shard, 4)
                )
                row = pl.multiple_of(order * unit + lax.rem(inner, pieces) * 16, 16)
                lefts[first_left + lax.div(inner, pieces), pl.ds(row, 16)] = turned[piece * 16 : (piece + 1) * 16]

        loop(width // 128, step)
        if index + 2 < len(chunks):
            left_copy(index + 2).start()

    half = 2 * levels * unit
    quarter = levels * unit

    def left_of(j):
        return jnp.maximum(jnp.minimum(j, 1), j + 1 - ups)

    def right_of(j):
        return jnp.minimum(j, first_up) + jnp.where(j >= first_mixed, 1, 0)

    def product(j, start, count, tile):
        return times(lefts[left_of(j), start : start + count], rights[right_of(j), :, part(tile, TILE)])

    def stage_core(j):
        def step(tile):
            send_core[j, :, part(tile, TILE)] = product(j, 0, half, tile).astype(LOW)

        loop(width // TILE, step)
        to_core(j).start()

    def stage_x(j):
        to_core(j).wait_recv()

        def step(tile):
            here = part(tile, TILE)
            value = product(j, half, quarter, tile) + take_core[j, :quarter, here].astype(F32)
            send_x[j, :, here] = value.astype(LOW)

        loop(width // TILE, step)
        to_x(j).start()

    def stage_z(j):
        to_x(j).wait_recv()

        def step(tile):
            here = part(tile, TILE)
            value = (
                product(j, half + quarter, quarter, tile)
                + take_core[j, quarter:, here].astype(F32)
                + take_x[j, :, here].astype(F32)
            )
            own[:, :, here] = value.reshape(levels, unit, TILE)

        loop(width // TILE, step)
        for hop in range(1, levels):
            send_z[j, hop - 1] = own[(z + hop) % levels].astype(LOW)
            to_z(j, hop).start()
        total_ref[j] = own[z]

    def finish(j):
        value = total_ref[j]
        for hop in range(1, levels):
            to_z(j, hop).wait_recv()
            value = value + take_z[j, hop - 1].astype(F32)
        total_ref[j] = value

    def feed(j):
        @pl.when(j == 0)
        def _():
            turn(0, unit // 16, 0)
            right_copy(0).wait()

        @pl.when(j == 1)
        def _():
            turn(1, unit // 16, 1)
            for index in range(1, 1 + ups):
                right_copy(index).wait()

        @pl.when(j == first_up)
        def _():
            for block in range(ups):
                turn(2 + block, ups * unit // 16, 2)
            right_copy(1 + ups).wait()

        @pl.when(j == first_mixed)
        def _():
            for block in range(3):
                turn(2 + ups + block, 3 * unit // 16, 2 + ups)
            right_copy(2 + ups).wait()

    def advance(j):
        feed(j)

        @pl.when((j >= 1) & (j < units + 1))
        def _():
            stage_x(j - 1)

        @pl.when(j < units)
        def _():
            stage_core(j)

        @pl.when((j >= 3) & (j < units + 3))
        def _():
            stage_z(j - 3)

        @pl.when(j >= 5)
        def _():
            finish(j - 5)

        @pl.when(j == 2)
        def _():
            vector_hop(0).wait_recv()
            vectors[1] = vectors[0] + take_vector[0]
            vector_hop(1).start()

        @pl.when(j == 4)
        def _():
            vector_hop(1).wait_recv()
            vectors[2] = vectors[1] + take_vector[1]
            for hop in range(1, levels):
                vector_hop(hop + 1).start()

    loop(units + 5, advance)
    whole = vectors[2]
    for hop in range(1, levels):
        vector_hop(hop + 1).wait_recv()
        whole = whole + take_vector[hop + 1]
    whole_ref[...] = whole

    def drain(j):
        to_core(j).wait_send()
        to_x(j).wait_send()
        for hop in range(1, levels):
            to_z(j, hop).wait_send()

    loop(units, drain)
    for hop in range(levels + 1):
        vector_hop(hop).wait_send()


def reduce_parts(vector, lefts, rights):
    shards = lax.axis_size("dp")
    branch, output_low, upper_low, mixed = lefts
    attended, hidden, second_normed, normed = rights
    rows, width = branch.shape
    ups = hidden.shape[1] // width
    unit, levels = width // shards, shards // 4
    units = 1 + 2 * ups + 3
    anywhere = pl.BlockSpec(memory_space=pl.ANY)
    vmem = pl.BlockSpec(memory_space=pltpu.VMEM)
    total, whole = pl.pallas_call(
        reduce_kernel,
        out_shape=(
            jax.ShapeDtypeStruct((units, unit, width), F32),
            jax.ShapeDtypeStruct(vector.shape, F32),
        ),
        in_specs=[vmem] + [anywhere] * 8,
        out_specs=[vmem, vmem],
        scratch_shapes=[
            pltpu.VMEM((3 + ups, rows, width), LOW),
            pltpu.VMEM((2, rows, width), LOW),
            pltpu.VMEM((5 + ups, width, rows), LOW),
            pltpu.VMEM((units, 2 * levels * unit, width), LOW),
            pltpu.VMEM((units, 2 * levels * unit, width), LOW),
            pltpu.VMEM((units, levels * unit, width), LOW),
            pltpu.VMEM((units, levels * unit, width), LOW),
            pltpu.VMEM((units, levels - 1, unit, width), LOW),
            pltpu.VMEM((units, levels - 1, unit, width), LOW),
            pltpu.VMEM((levels, unit, width), F32),
            pltpu.VMEM((3,) + vector.shape, F32),
            pltpu.VMEM((levels + 1,) + vector.shape, F32),
            pltpu.SemaphoreType.DMA((3 + ups,)),
            pltpu.SemaphoreType.DMA((2,)),
            pltpu.SemaphoreType.DMA((2, units)),
            pltpu.SemaphoreType.DMA((2, units)),
            pltpu.SemaphoreType.DMA((2, units, levels - 1)),
            pltpu.SemaphoreType.DMA((2, levels + 1)),
        ],
        name="reduce",
        compiler_params=pltpu.CompilerParams(
            collective_id=1, has_side_effects=True, vmem_limit_bytes=67043328
        ),
    )(vector, branch, output_low, upper_low, mixed, attended, hidden, second_normed, normed)
    first_up, first_mixed = 1 + ups, 1 + 2 * ups
    return (
        whole,
        total[first_mixed:].reshape(3 * unit, width).T,
        total[0].T,
        total[first_up:first_mixed].reshape(ups * unit, width).T,
        total[1:first_up].transpose(0, 2, 1).reshape(ups * width, unit),
    )


def contract_rows(left, right):
    return lax.dot_general(left, right, (((0,), (0,)), ((), ())), preferred_element_type=F32)


def scatter_parts(vector, lefts, rights):
    def reduce_rows(left, right):
        piece = lax.psum_scatter(contract_rows(left, right), "dp", scatter_dimension=0, tiled=True)
        return piece.T

    branch, output_low, upper_low, mixed = lefts
    attended, hidden, second_normed, normed = rights
    return (
        lax.psum(vector, "dp"),
        reduce_rows(mixed, normed),
        reduce_rows(branch, attended),
        reduce_rows(upper_low, second_normed),
        reduce_rows(output_low, hidden),
    )


def on_device(*arrays):
    shards = lax.axis_size("dp")
    me = lax.axis_index("dp")
    (
        result, input_grad, vector,
        normed, attended, second_normed, hidden, mixed, branch, upper_low, output_low,
    ) = relay(arrays)
    lefts = (branch, output_low, upper_low, mixed)
    rights = (attended, hidden, second_normed, normed)
    width = branch.shape[1]
    aligned = shards % 4 == 0 and width % (16 * shards) == 0
    combine = reduce_parts if aligned else scatter_parts
    whole, project_grad, out_grad, up_grad, down_grad = combine(vector, lefts, rights)
    size = width // shards
    small = lax.dynamic_slice_in_dim(whole[:8], me * size, size, 1)
    up_size = hidden.shape[1] // shards
    up_small = lax.dynamic_slice_in_dim(whole[8:].reshape(1, -1), me * up_size, up_size, 1)
    return (
        result[None],
        input_grad[None],
        small[0:1],
        small[1:2],
        project_grad[None],
        small[2:3],
        small[3:4],
        out_grad[None],
        small[4:5],
        small[5:6],
        small[6:7],
        up_grad[None],
        up_small,
        down_grad[None],
        small[7:8],
    )


def solution(mesh):
    stack1 = P("section", None)
    stack2 = P("section", None, None)
    in_specs = (
        P("dp", None), P("dp", None), P("dp"), P("dp"),
        stack1, stack1, stack2, stack1, stack1, stack2, stack1,
        stack1, stack1, stack2, stack1, stack2, stack1,
    )
    row = P("section", "dp")
    matrix = P("section", None, "dp")
    rows = P("section", "dp", None)
    out_specs = (
        rows, rows, row, row, matrix, row, row, matrix, row, row, row, matrix, row, matrix, row,
    )
    return jax.shard_map(
        on_device, mesh=mesh, in_specs=in_specs, out_specs=out_specs, check_vma=False
    )
```

```python
import jax
import jax.numpy as jnp
from jax import lax
from jax.experimental import pallas as pl
from jax.experimental.pallas import tpu as pltpu
from jax.sharding import PartitionSpec as P

HEADS = 12
HEAD_DIM = 64
SEQ = 512
PAIR = 2 * HEAD_DIM
PAIRS = HEADS // 2
TILE = 256
WIDE = 1024
ROWS = 128
EPSILON = 1e-06
SCORE_SCALE = 0.125
FAR = -1e30
F32 = jnp.float32
LOW = jnp.bfloat16
MESH = pl.DeviceIdType.MESH


def times(left, right):
    return lax.dot_general(left, right, (((1,), (0,)), ((), ())), preferred_element_type=F32)


def times_t(left, right):
    return lax.dot_general(left, right, (((1,), (1,)), ((), ())), preferred_element_type=F32)


def loop(count, body):
    def step(index, carry):
        body(index)
        return carry

    lax.fori_loop(0, count, step, 0)


def part(index, size):
    return pl.ds(pl.multiple_of(index * size, size), size)


def norm_rows(values):
    average = jnp.mean(values, axis=-1, keepdims=True)
    centred = values - average
    inv_scale = lax.rsqrt(jnp.mean(centred * centred, axis=-1, keepdims=True) + EPSILON)
    return centred * inv_scale, inv_scale


def norm_back(normed_grad, whitened, inv_scale, gain):
    scaled = normed_grad * gain
    return inv_scale * (
        scaled
        - jnp.mean(scaled, axis=-1, keepdims=True)
        - whitened * jnp.mean(scaled * whitened, axis=-1, keepdims=True)
    )


def fold_rows(values):
    rows, width = values.shape
    return jnp.sum(values.reshape(rows // 8, 8, width), axis=0)


def fill_bias(code_row, bias):
    across = jnp.transpose(jnp.broadcast_to(code_row, (128, SEQ)))
    for block in range(SEQ // 128):
        lanes = slice(block * 128, (block + 1) * 128)
        bias[:, lanes] = jnp.where(across == code_row[:, lanes], 0.0, FAR)


def gelu_both(upper):
    cumulative = 0.5 * (1.0 + lax.erf(upper * (0.5**0.5)))
    density = jnp.exp(-0.5 * (upper * upper)) * 0.3989422804014327
    return upper * cumulative, cumulative + upper * density


def relay_kernel(
    x_hbm,
    cot_hbm,
    code_ref,
    first_gain,
    first_shift,
    project_hbm,
    query_bias,
    value_bias,
    out_hbm,
    out_bias,
    second_gain,
    second_shift,
    up_hbm,
    up_bias,
    down_hbm,
    down_bias,
    result_hbm,
    input_grad_hbm,
    vector_ref,
    normed_hbm,
    attended_hbm,
    second_hbm,
    hidden_hbm,
    mixed_hbm,
    branch_hbm,
    upper_hbm,
    output_hbm,
    project,
    out_weight,
    up_weight,
    down_weight,
    x_in,
    g_in,
    normed,
    mixed,
    attended,
    middle,
    second_normed,
    hidden,
    slope,
    result,
    branch,
    attended_low,
    wide,
    input_grad,
    grad_low,
    bias,
    log_sums,
    score_buf,
    soft_low,
    score_low,
    sums,
    up_sums,
    weight_sem,
    x_sem,
    g_sem,
    send_sem,
    out_sem,
):
    section = lax.axis_index("section")
    width = x_in.shape[2]
    hidden_width = hidden.shape[2]
    packs = x_in.shape[0]
    last = lax.axis_size("section") - 1
    partner = {"section": 1 - section}

    def rows_of(ref, pack):
        return ref.at[pl.ds(pl.multiple_of(pack * SEQ, SEQ), SEQ)]

    weights = (
        pltpu.make_async_copy(project_hbm.at[0], project, weight_sem.at[0]),
        pltpu.make_async_copy(out_hbm.at[0], out_weight, weight_sem.at[1]),
        pltpu.make_async_copy(up_hbm.at[0], up_weight, weight_sem.at[2]),
        pltpu.make_async_copy(down_hbm.at[0], down_weight, weight_sem.at[3]),
    )

    @pl.when(section == 0)
    def _():
        for pack in range(packs):
            pltpu.make_async_copy(rows_of(x_hbm, pack), x_in.at[pack], x_sem.at[pack]).start()

    for copy in weights:
        copy.start()

    @pl.when(section == last)
    def _():
        for pack in range(packs):
            pltpu.make_async_copy(rows_of(cot_hbm, pack), g_in.at[pack], g_sem.at[pack]).start()

    barrier = pltpu.get_barrier_semaphore()
    pl.semaphore_signal(barrier, inc=1, device_id=partner, device_id_type=MESH)
    pl.semaphore_wait(barrier, 1)

    sums[...] = jnp.zeros_like(sums)
    up_sums[...] = jnp.zeros_like(up_sums)

    def hop_forward(pack):
        return pltpu.make_async_remote_copy(
            src_ref=result.at[pack],
            dst_ref=x_in.at[pack],
            send_sem=send_sem.at[0, pack],
            recv_sem=x_sem.at[pack],
            device_id=partner,
            device_id_type=MESH,
        )

    def hop_backward(pack):
        return pltpu.make_async_remote_copy(
            src_ref=grad_low.at[pack],
            dst_ref=g_in.at[pack],
            send_sem=send_sem.at[1, pack],
            recv_sem=g_sem.at[pack],
            device_id=partner,
            device_id_type=MESH,
        )

    kept = (
        (result, result_hbm),
        (normed, normed_hbm),
        (attended, attended_hbm),
        (second_normed, second_hbm),
        (hidden, hidden_hbm),
        (mixed, mixed_hbm),
        (branch, branch_hbm),
        (slope, upper_hbm),
        (g_in, output_hbm),
        (input_grad, input_grad_hbm),
    )

    def store(index, pack):
        source, target = kept[index]
        return pltpu.make_async_copy(source.at[pack], rows_of(target, pack), out_sem.at[index, pack])

    lane = lax.broadcasted_iota(jnp.int32, (SEQ, PAIR), 1)

    def heads_of(pack, pair):
        start = pl.multiple_of(pair * PAIR, PAIR)
        return [mixed[pack, :, pl.ds(third * width + start, PAIR)] for third in range(3)]

    def forward(pack):
        first = pack == 0

        @pl.when(section == 0)
        def _():
            pltpu.make_async_copy(rows_of(x_hbm, pack), x_in.at[pack], x_sem.at[pack]).wait()

        @pl.when(section == last)
        def _():
            hop_forward(pack).wait_recv()

        gain = first_gain[...].astype(F32)
        shift = first_shift[...].astype(F32)

        def norm_step(block):
            rows = part(block, ROWS)
            white, _ = norm_rows(x_in[pack, rows].astype(F32))
            normed[pack, rows] = (white * gain + shift).astype(LOW)

        loop(SEQ // ROWS, norm_step)
        fill_bias(code_ref[pack], bias)

        @pl.when(first)
        def _():
            weights[0].wait()

        for third, offset_ref in enumerate((query_bias, None, value_bias)):
            there = slice(third * width, (third + 1) * width)
            value = times(normed[pack], project[:, there])
            if offset_ref is not None:
                value = value + offset_ref[...].astype(F32)
            mixed[pack, :, there] = value.astype(LOW)

        def scores_of(pair, slot):
            query, key, _ = heads_of(pack, pair)
            for side in range(2):
                own = (lane < HEAD_DIM) == (side == 0)
                one = jnp.where(own, query * SCORE_SCALE, 0.0).astype(LOW)
                score_buf[slot, side] = times_t(key, one) + bias[...]

        def attend(pair, slot):
            value_across = jnp.transpose(heads_of(pack, pair)[2])
            outs = []
            for side in range(2):
                heads = slice(side * HEAD_DIM, (side + 1) * HEAD_DIM)
                scores = score_buf[slot, side]
                key_max = jnp.max(scores, axis=0, keepdims=True)
                exponent = jnp.exp(scores - key_max)
                key_sum = jnp.sum(exponent, axis=0, keepdims=True)
                outs.append(times(value_across[heads], exponent.astype(LOW)) * (1.0 / key_sum))
                log_sum = key_max + jnp.log(key_sum)
                log_sums[pack, 2 * pair + side] = jnp.broadcast_to(log_sum, (8, SEQ))
            attended[pack, :, part(pair, PAIR)] = jnp.transpose(jnp.concatenate(outs, axis=0)).astype(LOW)

        scores_of(0, 0)

        def attend_step(index):
            for slot in range(2):
                pair = 2 * index + slot
                scores_of(jnp.minimum(pair + 1, PAIRS - 1), 1 - slot)
                attend(pair, slot)

        loop(PAIRS // 2, attend_step)

        @pl.when(first)
        def _():
            weights[1].wait()

        middle[pack] = x_in[pack].astype(F32) + (
            times(attended[pack], out_weight[...]) + out_bias[...].astype(F32)
        )
        gain2 = second_gain[...].astype(F32)
        shift2 = second_shift[...].astype(F32)

        def second_step(block):
            rows = part(block, ROWS)
            white, _ = norm_rows(middle[pack, rows])
            second_normed[pack, rows] = (white * gain2 + shift2).astype(LOW)

        loop(SEQ // ROWS, second_step)

        @pl.when(first)
        def _():
            weights[2].wait()

        def up_step(tile):
            here = part(tile, width)
            upper = times(second_normed[pack], up_weight[:, here]) + up_bias[:, here].astype(F32)
            act, act_slope = gelu_both(upper)
            hidden[pack, :, here] = act.astype(LOW)
            slope[pack, :, here] = act_slope.astype(LOW)

        loop(hidden_width // width, up_step)

        @pl.when(first)
        def _():
            weights[3].wait()

        value = middle[pack] + (times(hidden[pack], down_weight[...]) + down_bias[...].astype(F32))
        result[pack] = value.astype(LOW)

        @pl.when(section == 0)
        def _():
            hop_forward(pack).start()

        for index in range(5):
            store(index, pack).start()

    def backward(order):
        pack = packs - 1 - order

        @pl.when(section == last)
        def _():
            pltpu.make_async_copy(rows_of(cot_hbm, pack), g_in.at[pack], g_sem.at[pack]).wait()

        @pl.when(section == 0)
        def _():
            hop_backward(pack).wait_recv()

        store(8, pack).start()
        fill_bias(code_ref[pack], bias)

        def fold_g(block):
            sums[7] += fold_rows(g_in[pack, part(block, ROWS)].astype(F32))

        loop(SEQ // ROWS, fold_g)

        def hidden_step(tile):
            here = part(tile, WIDE)
            value = times_t(g_in[pack], down_weight[here]).astype(LOW).astype(F32)
            low = (value * slope[pack, :, here].astype(F32)).astype(LOW)
            slope[pack, :, here] = low
            up_sums[:, here] += fold_rows(low.astype(F32))

        loop(hidden_width // WIDE, hidden_step)
        store(7, pack).start()

        wide[...] = times_t(slope[pack], up_weight[...])
        gain2 = second_gain[...].astype(F32)

        def second_back(block):
            rows = part(block, ROWS)
            grad = wide[rows]
            white, scale = norm_rows(middle[pack, rows])
            total = g_in[pack, rows].astype(F32) + norm_back(grad, white, scale, gain2)
            sums[5] += fold_rows(grad * white)
            sums[6] += fold_rows(grad)
            middle[pack, rows] = total
            low = total.astype(LOW)
            branch[pack, rows] = low
            sums[4] += fold_rows(low.astype(F32))

        loop(SEQ // ROWS, second_back)
        store(6, pack).start()

        attended_low[...] = times_t(branch[pack], out_weight[...]).astype(LOW)

        def attend_back(pair):
            here = part(pair, PAIR)
            query, key, value = heads_of(pack, pair)
            upstream = attended_low[:, here]
            key_across, up_across = jnp.transpose(key), jnp.transpose(upstream)
            one_query = []
            for side in range(2):
                own = (lane < HEAD_DIM) == (side == 0)
                one_query.append(jnp.where(own, query * SCORE_SCALE, 0.0).astype(LOW))
                one_up = jnp.where(own, upstream, 0.0).astype(LOW)
                score_buf[0, side] = times_t(key, one_query[side]) + bias[...]
                score_buf[1, side] = times_t(value, one_up)
            for side in range(2):
                soft = jnp.exp(score_buf[0, side] - log_sums[pack, 2 * pair + side, 0:1])
                inner = jnp.sum(soft * score_buf[1, side], axis=0, keepdims=True)
                soft_low[side] = soft.astype(LOW)
                score_buf[0, side] = soft
                score_low[side] = (score_buf[0, side] * (score_buf[1, side] - inner)).astype(LOW)
            query_across, value_across, key_grad = [], [], 0.0
            for side in range(2):
                heads = slice(side * HEAD_DIM, (side + 1) * HEAD_DIM)
                value_across.append(times_t(up_across[heads], soft_low[side]))
                key_grad += times(score_low[side], one_query[side])
                query_across.append(times(key_across[heads], score_low[side]))
            query_grad = (jnp.transpose(jnp.concatenate(query_across, axis=0)) * SCORE_SCALE).astype(LOW)
            value_grad = jnp.transpose(jnp.concatenate(value_across, axis=0)).astype(LOW)
            sums[2, :, here] += fold_rows(query_grad.astype(F32))
            sums[3, :, here] += fold_rows(value_grad.astype(F32))
            for third, grad in enumerate((query_grad, key_grad.astype(LOW), value_grad)):
                start = pl.multiple_of(third * width + pair * PAIR, PAIR)
                mixed[pack, :, pl.ds(start, PAIR)] = grad

        loop(PAIRS, attend_back)
        store(5, pack).start()

        wide[...] = times_t(mixed[pack], project[...])
        gain = first_gain[...].astype(F32)

        def first_back(block):
            rows = part(block, ROWS)
            grad = wide[rows]
            white, scale = norm_rows(x_in[pack, rows].astype(F32))
            total = middle[pack, rows] + norm_back(grad, white, scale, gain)
            sums[0] += fold_rows(grad * white)
            sums[1] += fold_rows(grad)
            input_grad[pack, rows] = total
            grad_low[pack, rows] = total.astype(LOW)

        loop(SEQ // ROWS, first_back)

        @pl.when(section == last)
        def _():
            hop_backward(pack).start()

        store(9, pack).start()

    loop(packs, forward)
    loop(packs, backward)

    count = sums.shape[0]
    for index in range(count):
        vector_ref[index : index + 1] = jnp.sum(sums[index], axis=0, keepdims=True)
    for index in range(hidden_width // width):
        lanes = slice(index * width, (index + 1) * width)
        vector_ref[count + index : count + index + 1] = jnp.sum(up_sums[:, lanes], axis=0, keepdims=True)

    for pack in range(packs):
        for index in range(len(kept)):
            store(index, pack).wait()

    @pl.when(section == 0)
    def _():
        for pack in range(packs):
            hop_forward(pack).wait_send()

    @pl.when(section == last)
    def _():
        for pack in range(packs):
            hop_backward(pack).wait_send()


def relay(arrays):
    inputs, cotangent, segments, valid_flags = arrays[:4]
    rows, width = inputs.shape
    hidden_width = arrays[13].shape[2]
    packs = rows // SEQ
    places = lax.broadcasted_iota(jnp.int32, (rows,), 0) + SEQ
    code = jnp.where(valid_flags == 1, segments, places).astype(F32).reshape(packs, 1, SEQ)
    anywhere = pl.BlockSpec(memory_space=pl.ANY)
    vmem = pl.BlockSpec(memory_space=pltpu.VMEM)

    def low(columns):
        return jax.ShapeDtypeStruct((rows, columns), LOW)

    outs = (
        low(width),
        jax.ShapeDtypeStruct((rows, width), F32),
        jax.ShapeDtypeStruct((8 + hidden_width // width, width), F32),
        low(width),
        low(width),
        low(width),
        low(hidden_width),
        low(3 * width),
        low(width),
        low(hidden_width),
        low(width),
    )

    def held(columns, kind=LOW):
        return pltpu.VMEM((packs, SEQ, columns), kind)

    scratch = [
        pltpu.VMEM((width, 3 * width), LOW),
        pltpu.VMEM((width, width), LOW),
        pltpu.VMEM((width, hidden_width), LOW),
        pltpu.VMEM((hidden_width, width), LOW),
        held(width),
        held(width),
        held(width),
        held(3 * width),
        held(width),
        held(width, F32),
        held(width),
        held(hidden_width),
        held(hidden_width),
        held(width),
        held(width),
        pltpu.VMEM((SEQ, width), LOW),
        pltpu.VMEM((SEQ, width), F32),
        held(width, F32),
        held(width),
        pltpu.VMEM((SEQ, SEQ), F32),
        pltpu.VMEM((packs, HEADS, 8, SEQ), F32),
        pltpu.VMEM((2, 2, SEQ, SEQ), F32),
        pltpu.VMEM((2, SEQ, SEQ), LOW),
        pltpu.VMEM((2, SEQ, SEQ), LOW),
        pltpu.VMEM((8, 8, width), F32),
        pltpu.VMEM((8, hidden_width), F32),
        pltpu.SemaphoreType.DMA((4,)),
        pltpu.SemaphoreType.DMA((packs,)),
        pltpu.SemaphoreType.DMA((packs,)),
        pltpu.SemaphoreType.DMA((2, packs)),
        pltpu.SemaphoreType.DMA((10, packs)),
    ]
    return pl.pallas_call(
        relay_kernel,
        out_shape=outs,
        in_specs=[
            anywhere, anywhere, vmem,
            vmem, vmem, anywhere, vmem, vmem, anywhere, vmem,
            vmem, vmem, anywhere, vmem, anywhere, vmem,
        ],
        out_specs=[anywhere, anywhere, vmem] + [anywhere] * 8,
        scratch_shapes=scratch,
        name="relay",
        compiler_params=pltpu.CompilerParams(
            collective_id=0, has_side_effects=True, vmem_limit_bytes=66 * 2**20 - 2**21
        ),
    )(inputs, cotangent, code, *arrays[4:])


def reduce_kernel(
    vector_ref,
    branch_hbm,
    output_hbm,
    upper_hbm,
    mixed_hbm,
    attended_hbm,
    hidden_hbm,
    second_hbm,
    normed_hbm,
    total_ref,
    whole_ref,
    rights,
    loaded,
    lefts,
    send_core,
    take_core,
    send_x,
    take_x,
    send_z,
    take_z,
    own,
    vectors,
    take_vector,
    right_sem,
    load_sem,
    core_sems,
    x_sems,
    z_sems,
    vector_sems,
):
    units, unit, width = total_ref.shape
    rows = rights.shape[1]
    shards = lax.axis_size("dp")
    levels = shards // 4
    ups = upper_hbm.shape[1] // width
    me = lax.axis_index("dp")
    core, x, z = me % 2, (me // 2) % 2, me // 4
    sibling = {"dp": me + 1 - 2 * core}
    across = {"dp": me + 2 - 4 * x}

    def level_peer(step):
        return {"dp": ((z + step) % levels) * 4 + x * 2 + core}

    first_up = 1 + ups
    first_mixed = first_up + ups

    sources = (
        [attended_hbm]
        + [hidden_hbm.at[:, pl.ds(block * width, width)] for block in range(ups)]
        + [second_hbm, normed_hbm]
    )

    def right_copy(index):
        return pltpu.make_async_copy(sources[index], rights.at[index], right_sem.at[index])

    chunks = [(branch_hbm, 0), (output_hbm, 0)]
    chunks += [(upper_hbm, block) for block in range(ups)]
    chunks += [(mixed_hbm, block) for block in range(3)]

    def left_copy(index):
        source, block = chunks[index]
        return pltpu.make_async_copy(
            source.at[:, pl.ds(block * width, width)], loaded.at[index % 2], load_sem.at[index % 2]
        )

    left_copy(0).start()
    right_copy(0).start()
    left_copy(1).start()
    for index in range(1, len(sources)):
        right_copy(index).start()

    barrier = pltpu.get_barrier_semaphore()
    peers = [sibling, across] + [level_peer(step) for step in range(1, levels)]
    for peer in peers:
        pl.semaphore_signal(barrier, inc=1, device_id=peer, device_id_type=MESH)
    pl.semaphore_wait(barrier, len(peers))

    def send(source, target, sems, index, peer):
        return pltpu.make_async_remote_copy(
            src_ref=source,
            dst_ref=target,
            send_sem=sems.at[(0,) + index],
            recv_sem=sems.at[(1,) + index],
            device_id=peer,
            device_id_type=MESH,
        )

    def to_core(j):
        return send(send_core.at[j], take_core.at[j], core_sems, (j,), sibling)

    def to_x(j):
        return send(send_x.at[j], take_x.at[j], x_sems, (j,), across)

    def to_z(j, step):
        return send(send_z.at[j, step - 1], take_z.at[j, step - 1], z_sems, (j, step - 1), level_peer(step))

    def vector_hop(index):
        peer = (sibling, across)[index] if index < 2 else level_peer(index - 1)
        return send(vectors.at[min(index, 2)], take_vector.at[index], vector_sems, (index,), peer)

    vectors[0] = vector_ref[...]
    vector_hop(0).start()

    def turn(index, group, first_left):
        left_copy(index).wait()
        block = chunks[index][1]
        source = loaded.at[index % 2]
        pieces = unit // 16

        def step(lane_block):
            turned = jnp.transpose(source[:, part(lane_block, 128)])
            for piece in range(8):
                place = block * (width // 16) + lane_block * 8 + piece
                shard, inner = lax.div(place, group), lax.rem(place, group)
                order = (
                    2 * levels * (1 - lax.rem(shard + core, 2))
                    + levels * (1 - lax.rem(lax.div(shard, 2) + x, 2))
                    + lax.div(shard, 4)
                )
                row = pl.multiple_of(order * unit + lax.rem(inner, pieces) * 16, 16)
                lefts[first_left + lax.div(inner, pieces), pl.ds(row, 16)] = turned[piece * 16 : (piece + 1) * 16]

        loop(width // 128, step)
        if index + 2 < len(chunks):
            left_copy(index + 2).start()

    half = 2 * levels * unit
    quarter = levels * unit

    def left_of(j):
        return jnp.maximum(jnp.minimum(j, 1), j + 1 - ups)

    def right_of(j):
        return jnp.minimum(j, first_up) + jnp.where(j >= first_mixed, 1, 0)

    def product(j, start, count, tile):
        return times(lefts[left_of(j), start : start + count], rights[right_of(j), :, part(tile, width)])

    def stage_core(j):
        def step(tile):
            send_core[j, :, part(tile, width)] = product(j, 0, half, tile).astype(LOW)

        loop(1, step)
        to_core(j).start()

    def stage_x(j):
        to_core(j).wait_recv()

        def step(tile):
            here = part(tile, width)
            value = product(j, half, quarter, tile) + take_core[j, :quarter, here].astype(F32)
            send_x[j, :, here] = value.astype(LOW)

        loop(1, step)
        to_x(j).start()

    def stage_z(j):
        to_x(j).wait_recv()

        def step(tile):
            here = part(tile, width)
            value = (
                product(j, half + quarter, quarter, tile)
                + take_core[j, quarter:, here].astype(F32)
                + take_x[j, :, here].astype(F32)
            )
            own[:, :, here] = value.reshape(levels, unit, width)

        loop(1, step)
        for hop in range(1, levels):
            send_z[j, hop - 1] = own[(z + hop) % levels].astype(LOW)
            to_z(j, hop).start()
        total_ref[j] = own[z]

    def finish(j):
        value = total_ref[j]
        for hop in range(1, levels):
            to_z(j, hop).wait_recv()
            value = value + take_z[j, hop - 1].astype(F32)
        total_ref[j] = value

    def feed(j):
        @pl.when(j == 0)
        def _():
            turn(0, unit // 16, 0)
            right_copy(0).wait()

        @pl.when(j == 1)
        def _():
            turn(1, unit // 16, 1)
            for index in range(1, 1 + ups):
                right_copy(index).wait()

        @pl.when(j == first_up)
        def _():
            for block in range(ups):
                turn(2 + block, ups * unit // 16, 2)
            right_copy(1 + ups).wait()

        @pl.when(j == first_mixed)
        def _():
            for block in range(3):
                turn(2 + ups + block, 3 * unit // 16, 2 + ups)
            right_copy(2 + ups).wait()

    def advance(j):
        feed(j)

        @pl.when((j >= 1) & (j < units + 1))
        def _():
            stage_x(j - 1)

        @pl.when(j < units)
        def _():
            stage_core(j)

        @pl.when((j >= 3) & (j < units + 3))
        def _():
            stage_z(j - 3)

        @pl.when(j >= 5)
        def _():
            finish(j - 5)

        @pl.when(j == 2)
        def _():
            vector_hop(0).wait_recv()
            vectors[1] = vectors[0] + take_vector[0]
            vector_hop(1).start()

        @pl.when(j == 4)
        def _():
            vector_hop(1).wait_recv()
            vectors[2] = vectors[1] + take_vector[1]
            for hop in range(1, levels):
                vector_hop(hop + 1).start()

    loop(units + 5, advance)
    whole = vectors[2]
    for hop in range(1, levels):
        vector_hop(hop + 1).wait_recv()
        whole = whole + take_vector[hop + 1]
    whole_ref[...] = whole

    def drain(j):
        to_core(j).wait_send()
        to_x(j).wait_send()
        for hop in range(1, levels):
            to_z(j, hop).wait_send()

    loop(units, drain)
    for hop in range(levels + 1):
        vector_hop(hop).wait_send()


def reduce_parts(vector, lefts, rights):
    shards = lax.axis_size("dp")
    branch, output_low, upper_low, mixed = lefts
    attended, hidden, second_normed, normed = rights
    rows, width = branch.shape
    ups = hidden.shape[1] // width
    unit, levels = width // shards, shards // 4
    units = 1 + 2 * ups + 3
    anywhere = pl.BlockSpec(memory_space=pl.ANY)
    vmem = pl.BlockSpec(memory_space=pltpu.VMEM)
    total, whole = pl.pallas_call(
        reduce_kernel,
        out_shape=(
            jax.ShapeDtypeStruct((units, unit, width), F32),
            jax.ShapeDtypeStruct(vector.shape, F32),
        ),
        in_specs=[vmem] + [anywhere] * 8,
        out_specs=[vmem, vmem],
        scratch_shapes=[
            pltpu.VMEM((3 + ups, rows, width), LOW),
            pltpu.VMEM((2, rows, width), LOW),
            pltpu.VMEM((5 + ups, width, rows), LOW),
            pltpu.VMEM((units, 2 * levels * unit, width), LOW),
            pltpu.VMEM((units, 2 * levels * unit, width), LOW),
            pltpu.VMEM((units, levels * unit, width), LOW),
            pltpu.VMEM((units, levels * unit, width), LOW),
            pltpu.VMEM((units, levels - 1, unit, width), LOW),
            pltpu.VMEM((units, levels - 1, unit, width), LOW),
            pltpu.VMEM((levels, unit, width), F32),
            pltpu.VMEM((3,) + vector.shape, F32),
            pltpu.VMEM((levels + 1,) + vector.shape, F32),
            pltpu.SemaphoreType.DMA((3 + ups,)),
            pltpu.SemaphoreType.DMA((2,)),
            pltpu.SemaphoreType.DMA((2, units)),
            pltpu.SemaphoreType.DMA((2, units)),
            pltpu.SemaphoreType.DMA((2, units, levels - 1)),
            pltpu.SemaphoreType.DMA((2, levels + 1)),
        ],
        name="reduce",
        compiler_params=pltpu.CompilerParams(
            collective_id=1, has_side_effects=True, vmem_limit_bytes=67043328
        ),
    )(vector, branch, output_low, upper_low, mixed, attended, hidden, second_normed, normed)
    first_up, first_mixed = 1 + ups, 1 + 2 * ups
    return (
        whole,
        total[first_mixed:].reshape(3 * unit, width).T,
        total[0].T,
        total[first_up:first_mixed].reshape(ups * unit, width).T,
        total[1:first_up].transpose(0, 2, 1).reshape(ups * width, unit),
    )


def contract_rows(left, right):
    return lax.dot_general(left, right, (((0,), (0,)), ((), ())), preferred_element_type=F32)


def scatter_parts(vector, lefts, rights):
    def reduce_rows(left, right):
        piece = lax.psum_scatter(contract_rows(left, right), "dp", scatter_dimension=0, tiled=True)
        return piece.T

    branch, output_low, upper_low, mixed = lefts
    attended, hidden, second_normed, normed = rights
    return (
        lax.psum(vector, "dp"),
        reduce_rows(mixed, normed),
        reduce_rows(branch, attended),
        reduce_rows(upper_low, second_normed),
        reduce_rows(output_low, hidden),
    )


def on_device(*arrays):
    shards = lax.axis_size("dp")
    me = lax.axis_index("dp")
    (
        result, input_grad, vector,
        normed, attended, second_normed, hidden, mixed, branch, upper_low, output_low,
    ) = relay(arrays)
    lefts = (branch, output_low, upper_low, mixed)
    rights = (attended, hidden, second_normed, normed)
    width = branch.shape[1]
    aligned = shards % 4 == 0 and width % (16 * shards) == 0
    combine = reduce_parts if aligned else scatter_parts
    whole, project_grad, out_grad, up_grad, down_grad = combine(vector, lefts, rights)
    size = width // shards
    small = lax.dynamic_slice_in_dim(whole[:8], me * size, size, 1)
    up_size = hidden.shape[1] // shards
    up_small = lax.dynamic_slice_in_dim(whole[8:].reshape(1, -1), me * up_size, up_size, 1)
    return (
        result[None],
        input_grad[None],
        small[0:1],
        small[1:2],
        project_grad[None],
        small[2:3],
        small[3:4],
        out_grad[None],
        small[4:5],
        small[5:6],
        small[6:7],
        up_grad[None],
        up_small,
        down_grad[None],
        small[7:8],
    )


def solution(mesh):
    stack1 = P("section", None)
    stack2 = P("section", None, None)
    in_specs = (
        P("dp", None), P("dp", None), P("dp"), P("dp"),
        stack1, stack1, stack2, stack1, stack1, stack2, stack1,
        stack1, stack1, stack2, stack1, stack2, stack1,
    )
    row = P("section", "dp")
    matrix = P("section", None, "dp")
    rows = P("section", "dp", None)
    out_specs = (
        rows, rows, row, row, matrix, row, row, matrix, row, row, row, matrix, row, matrix, row,
    )
    return jax.shard_map(
        on_device, mesh=mesh, in_specs=in_specs, out_specs=out_specs, check_vma=False
    )
```

```python
import jax
import jax.numpy as jnp
from jax import lax
from jax.experimental import pallas as pl
from jax.experimental.pallas import tpu as pltpu
from jax.sharding import PartitionSpec as P

HEADS = 12
HEAD_DIM = 64
SEQ = 512
PAIR = 2 * HEAD_DIM
PAIRS = HEADS // 2
TILE = 256
WIDE = 1024
ROWS = 128
EPSILON = 1e-06
SCORE_SCALE = 0.125
FAR = -1e30
F32 = jnp.float32
LOW = jnp.bfloat16
MESH = pl.DeviceIdType.MESH


def times(left, right):
    return lax.dot_general(left, right, (((1,), (0,)), ((), ())), preferred_element_type=F32)


def times_t(left, right):
    return lax.dot_general(left, right, (((1,), (1,)), ((), ())), preferred_element_type=F32)


def loop(count, body):
    def step(index, carry):
        body(index)
        return carry

    lax.fori_loop(0, count, step, 0)


def part(index, size):
    return pl.ds(pl.multiple_of(index * size, size), size)


def norm_rows(values):
    average = jnp.mean(values, axis=-1, keepdims=True)
    centred = values - average
    inv_scale = lax.rsqrt(jnp.mean(centred * centred, axis=-1, keepdims=True) + EPSILON)
    return centred * inv_scale, inv_scale


def norm_back(normed_grad, whitened, inv_scale, gain):
    scaled = normed_grad * gain
    return inv_scale * (
        scaled
        - jnp.mean(scaled, axis=-1, keepdims=True)
        - whitened * jnp.mean(scaled * whitened, axis=-1, keepdims=True)
    )


def fold_rows(values):
    rows, width = values.shape
    return jnp.sum(values.reshape(rows // 8, 8, width), axis=0)


def fill_bias(code_row, bias):
    across = jnp.transpose(jnp.broadcast_to(code_row, (128, SEQ)))
    for block in range(SEQ // 128):
        lanes = slice(block * 128, (block + 1) * 128)
        bias[:, lanes] = jnp.where(across == code_row[:, lanes], 0.0, FAR)


def gelu_both(upper):
    cumulative = 0.5 * (1.0 + lax.erf(upper * (0.5**0.5)))
    density = jnp.exp2((upper * upper) * -0.7213475204444817) * 0.3989422804014327
    return upper * cumulative, cumulative + upper * density


def relay_kernel(
    x_hbm,
    cot_hbm,
    segment_ref,
    valid_ref,
    first_gain,
    first_shift,
    project_hbm,
    query_bias,
    value_bias,
    out_hbm,
    out_bias,
    second_gain,
    second_shift,
    up_hbm,
    up_bias,
    down_hbm,
    down_bias,
    result_hbm,
    input_grad_hbm,
    vector_ref,
    normed_hbm,
    attended_hbm,
    second_hbm,
    hidden_hbm,
    mixed_hbm,
    branch_hbm,
    upper_hbm,
    output_hbm,
    project,
    out_weight,
    up_weight,
    down_weight,
    x_in,
    g_in,
    normed,
    mixed,
    attended,
    middle,
    second_normed,
    hidden,
    slope,
    result,
    wide,
    grad_low,
    bias,
    inv_sums,
    score_buf,
    score_low,
    exponents,
    outputs_across,
    sums,
    up_sums,
    weight_sem,
    x_sem,
    g_sem,
    send_sem,
    out_sem,
):
    section = lax.axis_index("section")
    width = x_in.shape[2]
    hidden_width = hidden.shape[1]
    packs = x_in.shape[0]
    last = lax.axis_size("section") - 1
    partner = {"section": 1 - section}
    branch, attended_low, input_grad = normed, attended, wide

    def rows_of(ref, pack):
        return ref.at[pl.ds(pl.multiple_of(pack * SEQ, SEQ), SEQ)]

    weights = (
        pltpu.make_async_copy(project_hbm.at[0], project, weight_sem.at[0]),
        pltpu.make_async_copy(out_hbm.at[0], out_weight, weight_sem.at[1]),
        pltpu.make_async_copy(up_hbm.at[0], up_weight, weight_sem.at[2]),
        pltpu.make_async_copy(down_hbm.at[0], down_weight, weight_sem.at[3]),
    )

    @pl.when(section == 0)
    def _():
        for pack in range(packs):
            pltpu.make_async_copy(rows_of(x_hbm, pack), x_in.at[pack], x_sem.at[pack]).start()

    for copy in weights:
        copy.start()

    @pl.when(section == last)
    def _():
        for pack in range(packs):
            pltpu.make_async_copy(rows_of(cot_hbm, pack), g_in.at[pack], g_sem.at[pack]).start()

    barrier = pltpu.get_barrier_semaphore()
    pl.semaphore_signal(barrier, inc=1, device_id=partner, device_id_type=MESH)
    pl.semaphore_wait(barrier, 1)

    sums[...] = jnp.zeros_like(sums)
    up_sums[...] = jnp.zeros_like(up_sums)

    def hop_forward(pack):
        return pltpu.make_async_remote_copy(
            src_ref=result,
            dst_ref=x_in.at[pack],
            send_sem=send_sem.at[0, pack],
            recv_sem=x_sem.at[pack],
            device_id=partner,
            device_id_type=MESH,
        )

    def hop_backward(pack):
        return pltpu.make_async_remote_copy(
            src_ref=grad_low,
            dst_ref=g_in.at[pack],
            send_sem=send_sem.at[1, pack],
            recv_sem=g_sem.at[pack],
            device_id=partner,
            device_id_type=MESH,
        )

    kept = (
        (result, result_hbm),
        (normed, normed_hbm),
        (attended, attended_hbm),
        (second_normed, second_hbm),
        (hidden, hidden_hbm),
        (mixed, mixed_hbm),
        (branch, branch_hbm),
        (slope, upper_hbm),
        (g_in, output_hbm),
        (input_grad, input_grad_hbm),
    )

    def store(index, pack):
        source, target = kept[index]
        source = source if len(source.shape) == 2 else source.at[pack]
        return pltpu.make_async_copy(source, rows_of(target, pack), out_sem.at[index, pack])

    lane = lax.broadcasted_iota(jnp.int32, (SEQ, PAIR), 1)

    def heads_of(pack, pair):
        start = pl.multiple_of(pair * PAIR, PAIR)
        return [mixed[pack, :, pl.ds(third * width + start, PAIR)] for third in range(3)]

    def forward(pack):
        first = pack == 0

        @pl.when(section == 0)
        def _():
            pltpu.make_async_copy(rows_of(x_hbm, pack), x_in.at[pack], x_sem.at[pack]).wait()

        @pl.when(section == last)
        def _():
            hop_forward(pack).wait_recv()

        gain = first_gain[...].astype(F32)
        shift = first_shift[...].astype(F32)

        @pl.when(pack > 0)
        def _():
            store(1, pack - 1).wait()

        def norm_step(block):
            rows = part(block, ROWS)
            white, _ = norm_rows(x_in[pack, rows].astype(F32))
            normed[rows] = (white * gain + shift).astype(LOW)

        loop(SEQ // ROWS, norm_step)
        store(1, pack).start()
        places = lax.broadcasted_iota(jnp.int32, (1, SEQ), 1) + SEQ
        fill_bias(jnp.where(valid_ref[pack] == 1, segment_ref[pack], places).astype(F32), bias)

        @pl.when(first)
        def _():
            weights[0].wait()

        for third, offset_ref in enumerate((query_bias, None, value_bias)):
            there = slice(third * width, (third + 1) * width)
            value = times(normed[...], project[:, there])
            if offset_ref is not None:
                value = value + offset_ref[...].astype(F32)
            mixed[pack, :, there] = value.astype(LOW)

        def scores_of(pair, slot):
            query, key, _ = heads_of(pack, pair)
            for side in range(2):
                own = (lane < HEAD_DIM) == (side == 0)
                one = jnp.where(own, query * SCORE_SCALE, 0.0).astype(LOW)
                score_buf[slot, side] = times_t(key, one) + bias[...]

        def attend(pair, slot):
            value_across = jnp.transpose(heads_of(pack, pair)[2])
            ones = jnp.ones((16, SEQ), LOW)
            outs = []
            for side in range(2):
                heads = slice(side * HEAD_DIM, (side + 1) * HEAD_DIM)
                scores = score_buf[slot, side]
                key_max = jnp.max(scores, axis=0, keepdims=True)
                exponent = jnp.exp(scores - key_max).astype(LOW)
                exponents[pack, 2 * pair + side] = exponent
                sums_too = times(jnp.concatenate([value_across[heads], ones], axis=0), exponent)
                inverse = 1.0 / sums_too[HEAD_DIM : HEAD_DIM + 1]
                inv_sums[pack, 2 * pair + side] = jnp.broadcast_to(inverse, (8, SEQ))
                outs.append(sums_too[:HEAD_DIM] * inverse)
                outputs_across[pack, 2 * pair + side] = outs[side]
            attended[:, part(pair, PAIR)] = jnp.transpose(jnp.concatenate(outs, axis=0)).astype(LOW)

        @pl.when(pack > 0)
        def _():
            store(2, pack - 1).wait()

        scores_of(0, 0)

        def attend_step(index):
            for slot in range(2):
                pair = 2 * index + slot
                scores_of(jnp.minimum(pair + 1, PAIRS - 1), 1 - slot)
                attend(pair, slot)

        loop(PAIRS // 2, attend_step)
        store(2, pack).start()

        @pl.when(first)
        def _():
            weights[1].wait()

        middle[pack] = x_in[pack].astype(F32) + (
            times(attended[...], out_weight[...]) + out_bias[...].astype(F32)
        )
        gain2 = second_gain[...].astype(F32)
        shift2 = second_shift[...].astype(F32)

        @pl.when(pack > 0)
        def _():
            store(3, pack - 1).wait()
            store(4, pack - 1).wait()

        def second_step(block):
            rows = part(block, ROWS)
            white, _ = norm_rows(middle[pack, rows])
            second_normed[rows] = (white * gain2 + shift2).astype(LOW)

        loop(SEQ // ROWS, second_step)
        store(3, pack).start()

        @pl.when(first)
        def _():
            weights[2].wait()

        def up_step(tile):
            here = part(tile, width)
            upper = times(second_normed[...], up_weight[:, here]) + up_bias[:, here].astype(F32)
            act, act_slope = gelu_both(upper)
            hidden[:, here] = act.astype(LOW)
            slope[pack, :, here] = act_slope.astype(LOW)

        loop(hidden_width // width, up_step)
        store(4, pack).start()

        @pl.when(first)
        def _():
            weights[3].wait()

        @pl.when(pack > 0)
        def _():
            store(0, pack - 1).wait()

        @pl.when((pack > 0) & (section == 0))
        def _():
            hop_forward(pack - 1).wait_send()

        value = middle[pack] + (times(hidden[...], down_weight[...]) + down_bias[...].astype(F32))
        result[...] = value.astype(LOW)

        @pl.when(section == 0)
        def _():
            hop_forward(pack).start()

        store(0, pack).start()

    def backward(order):
        pack = packs - 1 - order

        @pl.when(section == last)
        def _():
            pltpu.make_async_copy(rows_of(cot_hbm, pack), g_in.at[pack], g_sem.at[pack]).wait()

        @pl.when(section == 0)
        def _():
            hop_backward(pack).wait_recv()

        store(8, pack).start()

        def fold_g(block):
            sums[7] += fold_rows(g_in[pack, part(block, ROWS)].astype(F32))

        loop(SEQ // ROWS, fold_g)

        def hidden_step(tile):
            here = part(tile, WIDE)
            value = times_t(g_in[pack], down_weight[here]).astype(LOW).astype(F32)
            low = (value * slope[pack, :, here].astype(F32)).astype(LOW)
            slope[pack, :, here] = low
            up_sums[:, here] += fold_rows(low.astype(F32))

        loop(hidden_width // WIDE, hidden_step)
        store(7, pack).start()

        @pl.when(order > 0)
        def _():
            store(9, pack + 1).wait()
            store(6, pack + 1).wait()

        @pl.when(order == 0)
        def _():
            store(1, pack).wait()
            store(2, pack).wait()

        wide[...] = times_t(slope[pack], up_weight[...])
        gain2 = second_gain[...].astype(F32)

        def second_back(block):
            rows = part(block, ROWS)
            grad = wide[rows]
            white, scale = norm_rows(middle[pack, rows])
            total = g_in[pack, rows].astype(F32) + norm_back(grad, white, scale, gain2)
            sums[5] += fold_rows(grad * white)
            sums[6] += fold_rows(grad)
            middle[pack, rows] = total
            low = total.astype(LOW)
            branch[rows] = low
            sums[4] += fold_rows(low.astype(F32))

        loop(SEQ // ROWS, second_back)
        store(6, pack).start()

        attended_low[...] = times_t(branch[...], out_weight[...]).astype(LOW)

        def attend_back(pair):
            here = part(pair, PAIR)
            query, key, value = heads_of(pack, pair)
            key_across, up_across = jnp.transpose(key), jnp.transpose(attended_low[:, here])
            empty = jnp.zeros((HEAD_DIM, SEQ), LOW)
            query_across, value_across, key_grad = [], [], 0.0
            for side in range(2):
                head = 2 * pair + side
                heads = slice(side * HEAD_DIM, (side + 1) * HEAD_DIM)
                own = (lane < HEAD_DIM) == (side == 0)
                one_query = jnp.where(own, query * SCORE_SCALE, 0.0).astype(LOW)
                one_up = (up_across[heads].astype(F32) * inv_sums[pack, head, 0:1]).astype(LOW)
                inner = jnp.sum(one_up.astype(F32) * outputs_across[pack, head], axis=0, keepdims=True)
                soft_grad = times(value, jnp.concatenate([one_up, empty][:: 1 - 2 * side], axis=0))
                score_low[side] = (exponents[pack, head].astype(F32) * (soft_grad - inner)).astype(LOW)
                value_across.append(times_t(one_up, exponents[pack, head]))
                key_grad += times(score_low[side], one_query)
                query_across.append(times(key_across[heads], score_low[side]))
            query_grad = (jnp.transpose(jnp.concatenate(query_across, axis=0)) * SCORE_SCALE).astype(LOW)
            value_grad = jnp.transpose(jnp.concatenate(value_across, axis=0)).astype(LOW)
            sums[2, :, here] += fold_rows(query_grad.astype(F32))
            sums[3, :, here] += fold_rows(value_grad.astype(F32))
            for third, grad in enumerate((query_grad, key_grad.astype(LOW), value_grad)):
                start = pl.multiple_of(third * width + pair * PAIR, PAIR)
                mixed[pack, :, pl.ds(start, PAIR)] = grad

        loop(PAIRS, attend_back)
        store(5, pack).start()

        wide[...] = times_t(mixed[pack], project[...])
        @pl.when((order > 0) & (section == last))
        def _():
            hop_backward(pack + 1).wait_send()

        gain = first_gain[...].astype(F32)

        def first_back(block):
            rows = part(block, ROWS)
            grad = wide[rows]
            white, scale = norm_rows(x_in[pack, rows].astype(F32))
            total = middle[pack, rows] + norm_back(grad, white, scale, gain)
            sums[0] += fold_rows(grad * white)
            sums[1] += fold_rows(grad)
            input_grad[rows] = total
            grad_low[rows] = total.astype(LOW)

        loop(SEQ // ROWS, first_back)

        @pl.when(section == last)
        def _():
            hop_backward(pack).start()

        store(9, pack).start()

    loop(packs, forward)
    loop(packs, backward)

    count = sums.shape[0]
    vector_ref[count:] = jnp.zeros((vector_ref.shape[0] - count, width), F32)
    for index in range(count):
        vector_ref[index : index + 1] = jnp.sum(sums[index], axis=0, keepdims=True)
    for index in range(hidden_width // width):
        lanes = slice(index * width, (index + 1) * width)
        vector_ref[count + index : count + index + 1] = jnp.sum(up_sums[:, lanes], axis=0, keepdims=True)

    for index in (0, 3, 4):
        store(index, packs - 1).wait()
    for index in (6, 9):
        store(index, 0).wait()
    for pack in range(packs):
        for index in (5, 7, 8):
            store(index, pack).wait()

    @pl.when(section == 0)
    def _():
        hop_forward(packs - 1).wait_send()

    @pl.when(section == last)
    def _():
        hop_backward(0).wait_send()


def relay(arrays):
    inputs, cotangent, segments, valid_flags = arrays[:4]
    rows, width = inputs.shape
    hidden_width = arrays[13].shape[2]
    packs = rows // SEQ
    anywhere = pl.BlockSpec(memory_space=pl.ANY)
    vmem = pl.BlockSpec(memory_space=pltpu.VMEM)

    def low(columns):
        return jax.ShapeDtypeStruct((rows, columns), LOW)

    outs = (
        low(width),
        jax.ShapeDtypeStruct((rows, width), F32),
        jax.ShapeDtypeStruct((16, width), F32),
        low(width),
        low(width),
        low(width),
        low(hidden_width),
        low(3 * width),
        low(width),
        low(hidden_width),
        low(width),
    )

    def held(columns, kind=LOW):
        return pltpu.VMEM((packs, SEQ, columns), kind)

    scratch = [
        pltpu.VMEM((width, 3 * width), LOW),
        pltpu.VMEM((width, width), LOW),
        pltpu.VMEM((width, hidden_width), LOW),
        pltpu.VMEM((hidden_width, width), LOW),
        held(width),
        held(width),
        pltpu.VMEM((SEQ, width), LOW),
        held(3 * width),
        pltpu.VMEM((SEQ, width), LOW),
        held(width, F32),
        pltpu.VMEM((SEQ, width), LOW),
        pltpu.VMEM((SEQ, hidden_width), LOW),
        held(hidden_width),
        pltpu.VMEM((SEQ, width), LOW),
        pltpu.VMEM((SEQ, width), F32),
        pltpu.VMEM((SEQ, width), LOW),
        pltpu.VMEM((SEQ, SEQ), F32),
        pltpu.VMEM((packs, HEADS, 8, SEQ), F32),
        pltpu.VMEM((2, 2, SEQ, SEQ), F32),
        pltpu.VMEM((2, SEQ, SEQ), LOW),
        pltpu.VMEM((packs, HEADS, SEQ, SEQ), LOW),
        pltpu.VMEM((packs, HEADS, HEAD_DIM, SEQ), F32),
        pltpu.VMEM((8, 8, width), F32),
        pltpu.VMEM((8, hidden_width), F32),
        pltpu.SemaphoreType.DMA((4,)),
        pltpu.SemaphoreType.DMA((packs,)),
        pltpu.SemaphoreType.DMA((packs,)),
        pltpu.SemaphoreType.DMA((2, packs)),
        pltpu.SemaphoreType.DMA((10, packs)),
    ]
    return pl.pallas_call(
        relay_kernel,
        out_shape=outs,
        in_specs=[
            anywhere, anywhere, vmem, vmem,
            vmem, vmem, anywhere, vmem, vmem, anywhere, vmem,
            vmem, vmem, anywhere, vmem, anywhere, vmem,
        ],
        out_specs=[anywhere, anywhere, vmem] + [anywhere] * 8,
        scratch_shapes=scratch,
        name="relay",
        compiler_params=pltpu.CompilerParams(
            collective_id=0, has_side_effects=True, vmem_limit_bytes=67043328
        ),
    )(
        inputs,
        cotangent,
        segments.reshape(packs, 1, SEQ),
        valid_flags.reshape(packs, 1, SEQ),
        *arrays[4:],
    )


def reduce_kernel(
    vector_ref,
    branch_hbm,
    output_hbm,
    upper_hbm,
    mixed_hbm,
    attended_hbm,
    hidden_hbm,
    second_hbm,
    normed_hbm,
    total_ref,
    whole_ref,
    rights,
    loaded,
    lefts,
    send_core,
    take_core,
    send_x,
    take_x,
    send_z,
    take_z,
    own,
    vectors,
    take_vector,
    right_sem,
    load_sem,
    core_sems,
    x_sems,
    z_sems,
    vector_sems,
):
    units, unit, width = total_ref.shape
    rows = rights.shape[1]
    shards = lax.axis_size("dp")
    levels = shards // 4
    ups = upper_hbm.shape[1] // width
    me = lax.axis_index("dp")
    core, x, z = me % 2, (me // 2) % 2, me // 4
    sibling = {"dp": me + 1 - 2 * core}
    across = {"dp": me + 2 - 4 * x}

    def level_peer(step):
        return {"dp": ((z + step) % levels) * 4 + x * 2 + core}

    first_up = 1 + ups
    first_mixed = first_up + ups

    sources = (
        [attended_hbm]
        + [hidden_hbm.at[:, pl.ds(block * width, width)] for block in range(ups)]
        + [second_hbm, normed_hbm]
    )

    def right_copy(index):
        return pltpu.make_async_copy(sources[index], rights.at[index], right_sem.at[index])

    chunks = [(branch_hbm, 0), (output_hbm, 0)]
    chunks += [(upper_hbm, block) for block in range(ups)]
    chunks += [(mixed_hbm, block) for block in range(3)]

    def left_copy(index):
        source, block = chunks[index]
        return pltpu.make_async_copy(
            source.at[:, pl.ds(block * width, width)], loaded.at[index % 2], load_sem.at[index % 2]
        )

    left_copy(0).start()
    right_copy(0).start()
    left_copy(1).start()
    for index in range(1, len(sources)):
        right_copy(index).start()

    barrier = pltpu.get_barrier_semaphore()
    peers = [sibling, across] + [level_peer(step) for step in range(1, levels)]
    for peer in peers:
        pl.semaphore_signal(barrier, inc=1, device_id=peer, device_id_type=MESH)
    pl.semaphore_wait(barrier, len(peers))

    def send(source, target, sems, index, peer):
        return pltpu.make_async_remote_copy(
            src_ref=source,
            dst_ref=target,
            send_sem=sems.at[(0,) + index],
            recv_sem=sems.at[(1,) + index],
            device_id=peer,
            device_id_type=MESH,
        )

    def to_core(j):
        return send(send_core.at[j], take_core.at[j], core_sems, (j,), sibling)

    def to_x(j):
        return send(send_x.at[j], take_x.at[j], x_sems, (j,), across)

    def to_z(j, step):
        return send(send_z.at[j, step - 1], take_z.at[j, step - 1], z_sems, (j, step - 1), level_peer(step))

    def vector_hop(index):
        peer = (sibling, across)[index] if index < 2 else level_peer(index - 1)
        return send(vectors.at[min(index, 2)], take_vector.at[index], vector_sems, (index,), peer)

    vectors[0] = vector_ref[...]
    vector_hop(0).start()

    def turn(index, group, first_left):
        left_copy(index).wait()
        block = chunks[index][1]
        source = loaded.at[index % 2]
        pieces = unit // 16

        def step(lane_block):
            turned = jnp.transpose(source[:, part(lane_block, 128)])
            for piece in range(8):
                place = block * (width // 16) + lane_block * 8 + piece
                shard, inner = lax.div(place, group), lax.rem(place, group)
                order = (
                    2 * levels * (1 - lax.rem(shard + core, 2))
                    + levels * (1 - lax.rem(lax.div(shard, 2) + x, 2))
                    + lax.div(shard, 4)
                )
                row = pl.multiple_of(order * unit + lax.rem(inner, pieces) * 16, 16)
                lefts[first_left + lax.div(inner, pieces), pl.ds(row, 16)] = turned[piece * 16 : (piece + 1) * 16]

        loop(width // 128, step)
        if index + 2 < len(chunks):
            left_copy(index + 2).start()

    half = 2 * levels * unit
    quarter = levels * unit

    def left_of(j):
        return jnp.maximum(jnp.minimum(j, 1), j + 1 - ups)

    def right_of(j):
        return jnp.minimum(j, first_up) + jnp.where(j >= first_mixed, 1, 0)

    def product(j, start, count, tile):
        return times(lefts[left_of(j), start : start + count], rights[right_of(j), :, part(tile, width)])

    def stage_core(j):
        def step(tile):
            send_core[j, :, part(tile, width)] = product(j, 0, half, tile).astype(LOW)

        loop(1, step)
        to_core(j).start()

    def stage_x(j):
        to_core(j).wait_recv()

        def step(tile):
            here = part(tile, width)
            value = product(j, half, quarter, tile) + take_core[j, :quarter, here].astype(F32)
            send_x[j, :, here] = value.astype(LOW)

        loop(1, step)
        to_x(j).start()

    def stage_z(j):
        to_x(j).wait_recv()

        def step(tile):
            here = part(tile, width)
            value = (
                product(j, half + quarter, quarter, tile)
                + take_core[j, quarter:, here].astype(F32)
                + take_x[j, :, here].astype(F32)
            )
            own[:, :, here] = value.reshape(levels, unit, width)

        loop(1, step)
        for hop in range(1, levels):
            send_z[j, hop - 1] = own[(z + hop) % levels].astype(LOW)
            to_z(j, hop).start()
        total_ref[j] = own[z]

    def finish(j):
        value = total_ref[j]
        for hop in range(1, levels):
            to_z(j, hop).wait_recv()
            value = value + take_z[j, hop - 1].astype(F32)
        total_ref[j] = value

    def feed(j):
        @pl.when(j == 0)
        def _():
            turn(0, unit // 16, 0)
            right_copy(0).wait()

        @pl.when(j == 1)
        def _():
            turn(1, unit // 16, 1)
            for index in range(1, 1 + ups):
                right_copy(index).wait()

        @pl.when(j == first_up)
        def _():
            for block in range(ups):
                turn(2 + block, ups * unit // 16, 2)
            right_copy(1 + ups).wait()

        @pl.when(j == first_mixed)
        def _():
            for block in range(3):
                turn(2 + ups + block, 3 * unit // 16, 2 + ups)
            right_copy(2 + ups).wait()

    def advance(j):
        feed(j)

        @pl.when((j >= 1) & (j < units + 1))
        def _():
            stage_x(j - 1)

        @pl.when(j < units)
        def _():
            stage_core(j)

        @pl.when((j >= 3) & (j < units + 3))
        def _():
            stage_z(j - 3)

        @pl.when(j >= 5)
        def _():
            finish(j - 5)

        @pl.when(j == 2)
        def _():
            vector_hop(0).wait_recv()
            vectors[1] = vectors[0] + take_vector[0]
            vector_hop(1).start()

        @pl.when(j == 4)
        def _():
            vector_hop(1).wait_recv()
            vectors[2] = vectors[1] + take_vector[1]
            for hop in range(1, levels):
                vector_hop(hop + 1).start()

    loop(units + 5, advance)
    whole = vectors[2]
    for hop in range(1, levels):
        vector_hop(hop + 1).wait_recv()
        whole = whole + take_vector[hop + 1]
    whole_ref[...] = whole

    def drain(j):
        to_core(j).wait_send()
        to_x(j).wait_send()
        for hop in range(1, levels):
            to_z(j, hop).wait_send()

    loop(units, drain)
    for hop in range(levels + 1):
        vector_hop(hop).wait_send()


def reduce_parts(vector, lefts, rights):
    shards = lax.axis_size("dp")
    branch, output_low, upper_low, mixed = lefts
    attended, hidden, second_normed, normed = rights
    rows, width = branch.shape
    ups = hidden.shape[1] // width
    unit, levels = width // shards, shards // 4
    units = 1 + 2 * ups + 3
    anywhere = pl.BlockSpec(memory_space=pl.ANY)
    vmem = pl.BlockSpec(memory_space=pltpu.VMEM)
    total, whole = pl.pallas_call(
        reduce_kernel,
        out_shape=(
            jax.ShapeDtypeStruct((units, unit, width), F32),
            jax.ShapeDtypeStruct(vector.shape, F32),
        ),
        in_specs=[vmem] + [anywhere] * 8,
        out_specs=[vmem, vmem],
        scratch_shapes=[
            pltpu.VMEM((3 + ups, rows, width), LOW),
            pltpu.VMEM((2, rows, width), LOW),
            pltpu.VMEM((5 + ups, width, rows), LOW),
            pltpu.VMEM((units, 2 * levels * unit, width), LOW),
            pltpu.VMEM((units, 2 * levels * unit, width), LOW),
            pltpu.VMEM((units, levels * unit, width), LOW),
            pltpu.VMEM((units, levels * unit, width), LOW),
            pltpu.VMEM((units, levels - 1, unit, width), LOW),
            pltpu.VMEM((units, levels - 1, unit, width), LOW),
            pltpu.VMEM((levels, unit, width), F32),
            pltpu.VMEM((3,) + vector.shape, F32),
            pltpu.VMEM((levels + 1,) + vector.shape, F32),
            pltpu.SemaphoreType.DMA((3 + ups,)),
            pltpu.SemaphoreType.DMA((2,)),
            pltpu.SemaphoreType.DMA((2, units)),
            pltpu.SemaphoreType.DMA((2, units)),
            pltpu.SemaphoreType.DMA((2, units, levels - 1)),
            pltpu.SemaphoreType.DMA((2, levels + 1)),
        ],
        name="reduce",
        compiler_params=pltpu.CompilerParams(
            collective_id=1, has_side_effects=True, vmem_limit_bytes=67043328
        ),
    )(vector, branch, output_low, upper_low, mixed, attended, hidden, second_normed, normed)
    return whole, total


def finish_kernel(
    whole_ref,
    total_hbm,
    result_hbm,
    input_grad_hbm,
    result_out,
    input_grad_out,
    first_gain_out,
    first_shift_out,
    project_out,
    query_bias_out,
    value_bias_out,
    out_weight_out,
    out_bias_out,
    second_gain_out,
    second_shift_out,
    up_out,
    up_bias_out,
    down_out,
    down_bias_out,
    total,
    rows_low,
    rows_wide,
    in_sem,
    out_sem,
):
    units, unit, width = total.shape
    ups = down_out.shape[1] // width
    blocks = rows_low.shape[0]
    me = lax.axis_index("dp")
    shards = lax.axis_size("dp")
    first_up, first_mixed = 1 + ups, 1 + 2 * ups
    take = pltpu.make_async_copy(total_hbm, total, in_sem.at[2 * blocks])
    take.start()

    def block_of(ref, block):
        size = rows_low.shape[1]
        return ref.at[pl.ds(block * size, size)]

    pairs = []
    for block in range(blocks):
        for index, (source, middle, target) in enumerate(
            ((result_hbm, rows_low, result_out), (input_grad_hbm, rows_wide, input_grad_out))
        ):
            slot = 2 * block + index
            load = pltpu.make_async_copy(block_of(source, block), middle.at[block], in_sem.at[slot])
            save = pltpu.make_async_copy(middle.at[block], block_of(target, block), out_sem.at[slot])
            load.start()
            pairs.append((load, save))

    pieces = [(0, out_weight_out)]
    pieces += [(1 + block, down_out.at[:, pl.ds(block * width, width)]) for block in range(ups)]
    pieces += [(first_up + block, up_out.at[pl.ds(block * unit, unit)]) for block in range(ups)]
    pieces += [(first_mixed + block, project_out.at[pl.ds(block * unit, unit)]) for block in range(3)]
    take.wait()
    for index, (source, target) in enumerate(pieces):
        save = pltpu.make_async_copy(total.at[source], target, out_sem.at[2 * blocks + index])
        save.start()
        pieces[index] = save
    for load, save in pairs:
        load.wait()
        save.start()
    rolled = pltpu.roll(whole_ref[:8], lax.rem(shards - me, shards) * unit, 1)
    small_outs = (
        first_gain_out, first_shift_out, query_bias_out, value_bias_out,
        out_bias_out, second_gain_out, second_shift_out, down_bias_out,
    )
    for index, small in enumerate(small_outs):
        small[...] = rolled[index : index + 1, :unit]
    span = ups * unit
    inner = width // span
    wide_rolled = pltpu.roll(whole_ref[8:16], lax.rem(inner - lax.rem(me, inner), inner) * span, 1)
    mine = lax.broadcasted_iota(jnp.int32, (8, width), 0) == lax.div(me, inner)
    up_bias_out[...] = jnp.sum(jnp.where(mine, wide_rolled, 0.0), axis=0, keepdims=True)[:, :span]
    for _, save in pairs:
        save.wait()
    for save in pieces:
        save.wait()


def finish(whole, total, result, input_grad, ups):
    units, unit, width = total.shape
    rows = result.shape[0]
    anywhere = pl.BlockSpec(memory_space=pl.ANY)
    vmem = pl.BlockSpec(memory_space=pltpu.VMEM)

    def wide(*shape):
        return jax.ShapeDtypeStruct(shape, F32)

    small, matrix = wide(1, unit), wide(unit, width)
    blocks = 4
    outs = pl.pallas_call(
        finish_kernel,
        out_shape=(
            jax.ShapeDtypeStruct(result.shape, LOW), wide(rows, width), small, small,
            wide(3 * unit, width), small, small, matrix, small, small, small,
            wide(ups * unit, width), wide(1, ups * unit), wide(unit, ups * width), small,
        ),
        in_specs=[vmem] + [anywhere] * 3,
        out_specs=[
            anywhere, anywhere, vmem, vmem, anywhere, vmem, vmem, anywhere,
            vmem, vmem, vmem, anywhere, vmem, anywhere, vmem,
        ],
        scratch_shapes=[
            pltpu.VMEM(total.shape, F32),
            pltpu.VMEM((blocks, rows // blocks, width), LOW),
            pltpu.VMEM((blocks, rows // blocks, width), F32),
            pltpu.SemaphoreType.DMA((2 * blocks + 1,)),
            pltpu.SemaphoreType.DMA((2 * blocks + units,)),
        ],
        name="finish",
        compiler_params=pltpu.CompilerParams(vmem_limit_bytes=67043328),
    )(whole, total, result, input_grad)
    result, input_grad = outs[0][None], outs[1][None]
    turned = [outs[index].T[None] for index in (4, 7, 11, 13)]
    return (
        result, input_grad, outs[2], outs[3], turned[0], outs[5], outs[6], turned[1],
        outs[8], outs[9], outs[10], turned[2], outs[12], turned[3], outs[14],
    )


def contract_rows(left, right):
    return lax.dot_general(left, right, (((0,), (0,)), ((), ())), preferred_element_type=F32)


def scatter_parts(vector, lefts, rights):
    def reduce_rows(left, right):
        piece = lax.psum_scatter(contract_rows(left, right), "dp", scatter_dimension=0, tiled=True)
        return piece.T

    branch, output_low, upper_low, mixed = lefts
    attended, hidden, second_normed, normed = rights
    return (
        lax.psum(vector, "dp"),
        reduce_rows(mixed, normed),
        reduce_rows(branch, attended),
        reduce_rows(upper_low, second_normed),
        reduce_rows(output_low, hidden),
    )


def on_device(*arrays):
    shards = lax.axis_size("dp")
    me = lax.axis_index("dp")
    (
        result, input_grad, vector,
        normed, attended, second_normed, hidden, mixed, branch, upper_low, output_low,
    ) = relay(arrays)
    lefts = (branch, output_low, upper_low, mixed)
    rights = (attended, hidden, second_normed, normed)
    width = branch.shape[1]
    if shards % 4 == 0 and width % (16 * shards) == 0:
        whole, total = reduce_parts(vector, lefts, rights)
        return finish(whole, total, result, input_grad, hidden.shape[1] // width)
    whole, project_grad, out_grad, up_grad, down_grad = scatter_parts(vector, lefts, rights)
    size = width // shards
    small = lax.dynamic_slice_in_dim(whole[:8], me * size, size, 1)
    up_size = hidden.shape[1] // shards
    up_small = lax.dynamic_slice_in_dim(whole[8:].reshape(1, -1), me * up_size, up_size, 1)
    return (
        result[None],
        input_grad[None],
        small[0:1],
        small[1:2],
        project_grad[None],
        small[2:3],
        small[3:4],
        out_grad[None],
        small[4:5],
        small[5:6],
        small[6:7],
        up_grad[None],
        up_small,
        down_grad[None],
        small[7:8],
    )


def solution(mesh):
    stack1 = P("section", None)
    stack2 = P("section", None, None)
    in_specs = (
        P("dp", None), P("dp", None), P("dp"), P("dp"),
        stack1, stack1, stack2, stack1, stack1, stack2, stack1,
        stack1, stack1, stack2, stack1, stack2, stack1,
    )
    row = P("section", "dp")
    matrix = P("section", None, "dp")
    rows = P("section", "dp", None)
    out_specs = (
        rows, rows, row, row, matrix, row, row, matrix, row, row, row, matrix, row, matrix, row,
    )
    return jax.shard_map(
        on_device, mesh=mesh, in_specs=in_specs, out_specs=out_specs, check_vma=False
    )
```

```python
import jax
import jax.numpy as jnp
from jax import lax
from jax.experimental import pallas as pl
from jax.experimental.pallas import tpu as pltpu
from jax.sharding import PartitionSpec as P

HEADS = 12
HEAD_DIM = 64
SEQ = 512
PAIR = 2 * HEAD_DIM
PAIRS = HEADS // 2
TILE = 256
WIDE = 1024
HALF = 256
CUT = 2
LAG = 3
ROWS = 128
EPSILON = 1e-06
SCORE_SCALE = 0.125
FAR = -1e30
F32 = jnp.float32
LOW = jnp.bfloat16
MESH = pl.DeviceIdType.MESH


def times(left, right):
    return lax.dot_general(left, right, (((1,), (0,)), ((), ())), preferred_element_type=F32)


def times_t(left, right):
    return lax.dot_general(left, right, (((1,), (1,)), ((), ())), preferred_element_type=F32)


def loop(count, body):
    def step(index, carry):
        body(index)
        return carry

    lax.fori_loop(0, count, step, 0)


def part(index, size):
    return pl.ds(pl.multiple_of(index * size, size), size)


def norm_rows(values):
    average = jnp.mean(values, axis=-1, keepdims=True)
    centred = values - average
    inv_scale = lax.rsqrt(jnp.mean(centred * centred, axis=-1, keepdims=True) + EPSILON)
    return centred * inv_scale, inv_scale


def norm_back(normed_grad, whitened, inv_scale, gain):
    scaled = normed_grad * gain
    return inv_scale * (
        scaled
        - jnp.mean(scaled, axis=-1, keepdims=True)
        - whitened * jnp.mean(scaled * whitened, axis=-1, keepdims=True)
    )


def fold_rows(values):
    rows, width = values.shape
    return jnp.sum(values.reshape(rows // 8, 8, width), axis=0)


def fill_bias(code_row, bias):
    across = jnp.transpose(jnp.broadcast_to(code_row, (128, SEQ)))
    for block in range(SEQ // 128):
        lanes = slice(block * 128, (block + 1) * 128)
        bias[:, lanes] = jnp.where(across == code_row[:, lanes], 0.0, FAR)


def gelu_both(upper):
    cumulative = 0.5 * (1.0 + lax.erf(upper * (0.5**0.5)))
    density = jnp.exp2((upper * upper) * -0.7213475204444817) * 0.3989422804014327
    return upper * cumulative, cumulative + upper * density


def relay_kernel(
    x_hbm,
    cot_hbm,
    segment_ref,
    valid_ref,
    first_gain,
    first_shift,
    project_hbm,
    query_bias,
    value_bias,
    out_hbm,
    out_bias,
    second_gain,
    second_shift,
    up_hbm,
    up_bias,
    down_hbm,
    down_bias,
    result_hbm,
    input_grad_hbm,
    vector_ref,
    normed_hbm,
    attended_hbm,
    second_hbm,
    hidden_hbm,
    mixed_hbm,
    branch_hbm,
    upper_hbm,
    output_hbm,
    project,
    out_weight,
    up_weight,
    down_weight,
    x_in,
    g_in,
    normed,
    mixed,
    attended,
    middle,
    second_normed,
    hidden,
    slope,
    result,
    wide,
    grad_low,
    bias,
    inv_sums,
    score_buf,
    score_low,
    exponents,
    outputs_across,
    sums,
    up_sums,
    weight_sem,
    x_sem,
    g_sem,
    send_sem,
    out_sem,
):
    section = lax.axis_index("section")
    width = x_in.shape[2]
    hidden_width = hidden.shape[1]
    packs = x_in.shape[0]
    last = lax.axis_size("section") - 1
    partner = {"section": 1 - section}
    branch, attended_low, input_grad = normed, attended, wide

    def rows_of(ref, pack):
        return ref.at[pl.ds(pl.multiple_of(pack * SEQ, SEQ), SEQ)]

    def half_of(half):
        return pl.ds(pl.multiple_of(half * HALF, HALF), HALF)

    def local_rows(source, target, sems, pack, half):
        there = pl.ds(pl.multiple_of(pack * SEQ + half * HALF, HALF), HALF)
        return pltpu.make_async_copy(source.at[there], target.at[pack, half_of(half)], sems.at[pack, half])

    def local_x(pack, half):
        return local_rows(x_hbm, x_in, x_sem, pack, half)

    def local_g(pack, half):
        return local_rows(cot_hbm, g_in, g_sem, pack, half)

    weights = (
        pltpu.make_async_copy(project_hbm.at[0], project, weight_sem.at[0]),
        pltpu.make_async_copy(out_hbm.at[0], out_weight, weight_sem.at[1]),
        pltpu.make_async_copy(up_hbm.at[0], up_weight, weight_sem.at[2]),
        pltpu.make_async_copy(down_hbm.at[0], down_weight, weight_sem.at[3]),
    )

    @pl.when(section == 0)
    def _():
        for pack in range(packs):
            for half in range(2):
                local_x(pack, half).start()

    weights[0].start()

    @pl.when(section == last)
    def _():
        for pack in range(packs):
            for half in range(2):
                local_g(pack, half).start()

    barrier = pltpu.get_barrier_semaphore()
    pl.semaphore_signal(barrier, inc=1, device_id=partner, device_id_type=MESH)
    pl.semaphore_wait(barrier, 1)

    sums[...] = jnp.zeros_like(sums)
    up_sums[...] = jnp.zeros_like(up_sums)

    def hop(way, source, target, sems, pack, half):
        rows = half_of(half)
        return pltpu.make_async_remote_copy(
            src_ref=source.at[rows],
            dst_ref=target.at[pack, rows],
            send_sem=send_sem.at[way, pack, half],
            recv_sem=sems.at[pack, half],
            device_id=partner,
            device_id_type=MESH,
        )

    def hop_forward(pack, half):
        return hop(0, result, x_in, x_sem, pack, half)

    def hop_backward(pack, half):
        return hop(1, grad_low, g_in, g_sem, pack, half)

    kept = (
        (result, result_hbm),
        (normed, normed_hbm),
        (attended, attended_hbm),
        (second_normed, second_hbm),
        (hidden, hidden_hbm),
        (mixed, mixed_hbm),
        (branch, branch_hbm),
        (slope, upper_hbm),
        (g_in, output_hbm),
        (input_grad, input_grad_hbm),
    )

    def store(index, pack):
        source, target = kept[index]
        source = source if len(source.shape) == 2 else source.at[pack]
        return pltpu.make_async_copy(source, rows_of(target, pack), out_sem.at[index, pack])

    lane = lax.broadcasted_iota(jnp.int32, (SEQ, PAIR), 1)

    def heads_of(pack, pair):
        start = pl.multiple_of(pair * PAIR, PAIR)
        return [mixed[pack, :, pl.ds(third * width + start, PAIR)] for third in range(3)]

    def forward(pack):
        first = pack == 0

        gain = first_gain[...].astype(F32)
        shift = first_shift[...].astype(F32)

        @pl.when(pack > 0)
        def _():
            store(1, pack - 1).wait()

        places = lax.broadcasted_iota(jnp.int32, (1, SEQ), 1) + SEQ
        fill_bias(jnp.where(valid_ref[pack] == 1, segment_ref[pack], places).astype(F32), bias)

        @pl.when(first)
        def _():
            weights[0].wait()
            for copy in weights[1:]:
                copy.start()

        def project_half(half):
            @pl.when(section == 0)
            def _():
                local_x(pack, half).wait()

            @pl.when(section == last)
            def _():
                hop_forward(pack, half).wait_recv()

            def norm_step(block):
                rows = pl.ds(pl.multiple_of(half * HALF + block * ROWS, ROWS), ROWS)
                white, _ = norm_rows(x_in[pack, rows].astype(F32))
                normed[rows] = (white * gain + shift).astype(LOW)

            loop(HALF // ROWS, norm_step)
            rows = half_of(half)
            for third, offset_ref in enumerate((query_bias, None, value_bias)):
                there = slice(third * width, (third + 1) * width)
                value = times(normed[rows], project[:, there])
                if offset_ref is not None:
                    value = value + offset_ref[...].astype(F32)
                mixed[pack, rows, there] = value.astype(LOW)

        loop(2, project_half)
        store(1, pack).start()

        def scores_of(pair, slot):
            query, key, _ = heads_of(pack, pair)
            for side in range(2):
                own = (lane < HEAD_DIM) == (side == 0)
                one = jnp.where(own, query * SCORE_SCALE, 0.0).astype(LOW)
                score_buf[slot, side] = times_t(key, one) + bias[...]

        def attend(pair, slot):
            value_across = jnp.transpose(heads_of(pack, pair)[2])
            ones = jnp.ones((16, SEQ), LOW)
            outs = []
            for side in range(2):
                heads = slice(side * HEAD_DIM, (side + 1) * HEAD_DIM)
                scores = score_buf[slot, side]
                key_max = jnp.max(scores, axis=0, keepdims=True)
                exponent = jnp.exp(scores - key_max).astype(LOW)
                exponents[pack, 2 * pair + side] = exponent
                sums_too = times(jnp.concatenate([value_across[heads], ones], axis=0), exponent)
                inverse = 1.0 / sums_too[HEAD_DIM : HEAD_DIM + 1]
                inv_sums[pack, 2 * pair + side] = jnp.broadcast_to(inverse, (8, SEQ))
                outs.append(sums_too[:HEAD_DIM] * inverse)
                outputs_across[pack, 2 * pair + side] = outs[side]
            attended[:, part(pair, PAIR)] = jnp.transpose(jnp.concatenate(outs, axis=0)).astype(LOW)

        @pl.when(pack > 0)
        def _():
            store(2, pack - 1).wait()

        scores_of(0, 0)

        def attend_step(index):
            for slot in range(2):
                pair = 2 * index + slot
                scores_of(jnp.minimum(pair + 1, PAIRS - 1), 1 - slot)
                attend(pair, slot)

        loop(PAIRS // 2, attend_step)
        store(2, pack).start()

        @pl.when(first)
        def _():
            weights[1].wait()

        middle[pack] = x_in[pack].astype(F32) + (
            times(attended[...], out_weight[...]) + out_bias[...].astype(F32)
        )
        gain2 = second_gain[...].astype(F32)
        shift2 = second_shift[...].astype(F32)

        @pl.when(pack > 0)
        def _():
            store(3, pack - 1).wait()
            store(4, pack - 1).wait()
            store(0, pack - 1).wait()

        @pl.when(first)
        def _():
            weights[2].wait()
            weights[3].wait()

        def feed_half(half):
            def second_step(block):
                rows = pl.ds(pl.multiple_of(half * HALF + block * ROWS, ROWS), ROWS)
                white, _ = norm_rows(middle[pack, rows])
                second_normed[rows] = (white * gain2 + shift2).astype(LOW)

            loop(HALF // ROWS, second_step)
            rows = half_of(half)

            def up_step(tile):
                here = part(tile, width)
                upper = times(second_normed[rows], up_weight[:, here]) + up_bias[:, here].astype(F32)
                act, act_slope = gelu_both(upper)
                hidden[rows, here] = act.astype(LOW)
                slope[pack, rows, here] = act_slope.astype(LOW)

            loop(hidden_width // width, up_step)

            @pl.when((pack > 0) & (section == 0))
            def _():
                hop_forward(pack - 1, half).wait_send()

            value = middle[pack, rows] + (times(hidden[rows], down_weight[...]) + down_bias[...].astype(F32))
            result[rows] = value.astype(LOW)

            @pl.when(section == 0)
            def _():
                hop_forward(pack, half).start()

        loop(2, feed_half)
        store(3, pack).start()
        store(4, pack).start()
        store(0, pack).start()

    def backward(order):
        pack = packs - 1 - order

        def hidden_half(half):
            @pl.when(section == last)
            def _():
                local_g(pack, half).wait()

            @pl.when(section == 0)
            def _():
                hop_backward(pack, half).wait_recv()

            rows = half_of(half)
            sums[7] += fold_rows(g_in[pack, rows].astype(F32))

            def hidden_step(tile):
                here = part(tile, WIDE)
                value = times_t(g_in[pack, rows], down_weight[here]).astype(LOW).astype(F32)
                low = (value * slope[pack, rows, here].astype(F32)).astype(LOW)
                slope[pack, rows, here] = low
                up_sums[:, here] += fold_rows(low.astype(F32))

            loop(hidden_width // WIDE, hidden_step)

        loop(2, hidden_half)
        store(8, pack).start()
        store(7, pack).start()

        @pl.when(order > 0)
        def _():
            store(9, pack + 1).wait()
            store(6, pack + 1).wait()

        @pl.when(order == 0)
        def _():
            store(1, pack).wait()
            store(2, pack).wait()

        wide[...] = times_t(slope[pack], up_weight[...])
        gain2 = second_gain[...].astype(F32)

        def second_back(block):
            rows = part(block, ROWS)
            grad = wide[rows]
            white, scale = norm_rows(middle[pack, rows])
            total = g_in[pack, rows].astype(F32) + norm_back(grad, white, scale, gain2)
            sums[5] += fold_rows(grad * white)
            sums[6] += fold_rows(grad)
            middle[pack, rows] = total
            low = total.astype(LOW)
            branch[rows] = low
            sums[4] += fold_rows(low.astype(F32))

        loop(SEQ // ROWS, second_back)
        store(6, pack).start()

        attended_low[...] = times_t(branch[...], out_weight[...]).astype(LOW)

        def attend_back(pair):
            here = part(pair, PAIR)
            query, key, value = heads_of(pack, pair)
            key_across, up_across = jnp.transpose(key), jnp.transpose(attended_low[:, here])
            empty = jnp.zeros((HEAD_DIM, SEQ), LOW)
            query_across, value_across, key_grad = [], [], 0.0
            for side in range(2):
                head = 2 * pair + side
                heads = slice(side * HEAD_DIM, (side + 1) * HEAD_DIM)
                own = (lane < HEAD_DIM) == (side == 0)
                one_query = jnp.where(own, query * SCORE_SCALE, 0.0).astype(LOW)
                one_up = (up_across[heads].astype(F32) * inv_sums[pack, head, 0:1]).astype(LOW)
                inner = jnp.sum(one_up.astype(F32) * outputs_across[pack, head], axis=0, keepdims=True)
                soft_grad = times(value, jnp.concatenate([one_up, empty][:: 1 - 2 * side], axis=0))
                score_low[side] = (exponents[pack, head].astype(F32) * (soft_grad - inner)).astype(LOW)
                value_across.append(times_t(one_up, exponents[pack, head]))
                key_grad += times(score_low[side], one_query)
                query_across.append(times(key_across[heads], score_low[side]))
            query_grad = (jnp.transpose(jnp.concatenate(query_across, axis=0)) * SCORE_SCALE).astype(LOW)
            value_grad = jnp.transpose(jnp.concatenate(value_across, axis=0)).astype(LOW)
            sums[2, :, here] += fold_rows(query_grad.astype(F32))
            sums[3, :, here] += fold_rows(value_grad.astype(F32))
            for third, grad in enumerate((query_grad, key_grad.astype(LOW), value_grad)):
                start = pl.multiple_of(third * width + pair * PAIR, PAIR)
                mixed[pack, :, pl.ds(start, PAIR)] = grad

        loop(PAIRS, attend_back)
        store(5, pack).start()

        gain = first_gain[...].astype(F32)

        def first_half(half):
            rows = half_of(half)
            wide[rows] = times_t(mixed[pack, rows], project[...])

            @pl.when((order > 0) & (section == last))
            def _():
                hop_backward(pack + 1, half).wait_send()

            def first_back(block):
                rows = pl.ds(pl.multiple_of(half * HALF + block * ROWS, ROWS), ROWS)
                grad = wide[rows]
                white, scale = norm_rows(x_in[pack, rows].astype(F32))
                total = middle[pack, rows] + norm_back(grad, white, scale, gain)
                sums[0] += fold_rows(grad * white)
                sums[1] += fold_rows(grad)
                input_grad[rows] = total
                grad_low[rows] = total.astype(LOW)

            loop(HALF // ROWS, first_back)

            @pl.when(section == last)
            def _():
                hop_backward(pack, half).start()

        loop(2, first_half)
        store(9, pack).start()

    loop(packs, forward)
    loop(packs, backward)

    count = sums.shape[0]
    vector_ref[count:] = jnp.zeros((vector_ref.shape[0] - count, width), F32)
    for index in range(count):
        vector_ref[index : index + 1] = jnp.sum(sums[index], axis=0, keepdims=True)
    for index in range(hidden_width // width):
        lanes = slice(index * width, (index + 1) * width)
        vector_ref[count + index : count + index + 1] = jnp.sum(up_sums[:, lanes], axis=0, keepdims=True)

    for index in (0, 3, 4):
        store(index, packs - 1).wait()
    for index in (6, 9):
        store(index, 0).wait()
    for pack in range(packs):
        for index in (5, 7, 8):
            store(index, pack).wait()

    @pl.when(section == 0)
    def _():
        for half in range(2):
            hop_forward(packs - 1, half).wait_send()

    @pl.when(section == last)
    def _():
        for half in range(2):
            hop_backward(0, half).wait_send()


def relay(arrays):
    inputs, cotangent, segments, valid_flags = arrays[:4]
    rows, width = inputs.shape
    hidden_width = arrays[13].shape[2]
    packs = rows // SEQ
    anywhere = pl.BlockSpec(memory_space=pl.ANY)
    vmem = pl.BlockSpec(memory_space=pltpu.VMEM)

    def low(columns):
        return jax.ShapeDtypeStruct((rows, columns), LOW)

    outs = (
        low(width),
        jax.ShapeDtypeStruct((rows, width), F32),
        jax.ShapeDtypeStruct((16, width), F32),
        low(width),
        low(width),
        low(width),
        low(hidden_width),
        low(3 * width),
        low(width),
        low(hidden_width),
        low(width),
    )

    def held(columns, kind=LOW):
        return pltpu.VMEM((packs, SEQ, columns), kind)

    scratch = [
        pltpu.VMEM((width, 3 * width), LOW),
        pltpu.VMEM((width, width), LOW),
        pltpu.VMEM((width, hidden_width), LOW),
        pltpu.VMEM((hidden_width, width), LOW),
        held(width),
        held(width),
        pltpu.VMEM((SEQ, width), LOW),
        held(3 * width),
        pltpu.VMEM((SEQ, width), LOW),
        held(width, F32),
        pltpu.VMEM((SEQ, width), LOW),
        pltpu.VMEM((SEQ, hidden_width), LOW),
        held(hidden_width),
        pltpu.VMEM((SEQ, width), LOW),
        pltpu.VMEM((SEQ, width), F32),
        pltpu.VMEM((SEQ, width), LOW),
        pltpu.VMEM((SEQ, SEQ), F32),
        pltpu.VMEM((packs, HEADS, 8, SEQ), F32),
        pltpu.VMEM((2, 2, SEQ, SEQ), F32),
        pltpu.VMEM((2, SEQ, SEQ), LOW),
        pltpu.VMEM((packs, HEADS, SEQ, SEQ), LOW),
        pltpu.VMEM((packs, HEADS, HEAD_DIM, SEQ), F32),
        pltpu.VMEM((8, 8, width), F32),
        pltpu.VMEM((8, hidden_width), F32),
        pltpu.SemaphoreType.DMA((4,)),
        pltpu.SemaphoreType.DMA((packs, 2)),
        pltpu.SemaphoreType.DMA((packs, 2)),
        pltpu.SemaphoreType.DMA((2, packs, 2)),
        pltpu.SemaphoreType.DMA((10, packs)),
    ]
    return pl.pallas_call(
        relay_kernel,
        out_shape=outs,
        in_specs=[
            anywhere, anywhere, vmem, vmem,
            vmem, vmem, anywhere, vmem, vmem, anywhere, vmem,
            vmem, vmem, anywhere, vmem, anywhere, vmem,
        ],
        out_specs=[anywhere, anywhere, vmem] + [anywhere] * 8,
        scratch_shapes=scratch,
        name="relay",
        compiler_params=pltpu.CompilerParams(
            collective_id=0, has_side_effects=True, vmem_limit_bytes=67043328
        ),
    )(
        inputs,
        cotangent,
        segments.reshape(packs, 1, SEQ),
        valid_flags.reshape(packs, 1, SEQ),
        *arrays[4:],
    )


def reduce_kernel(
    vector_ref,
    branch_hbm,
    output_hbm,
    upper_hbm,
    mixed_hbm,
    attended_hbm,
    hidden_hbm,
    second_hbm,
    normed_hbm,
    total_ref,
    whole_ref,
    rights,
    loaded,
    lefts,
    send_core,
    take_core,
    send_x,
    take_x,
    send_z,
    take_z,
    own,
    vectors,
    take_vector,
    right_sem,
    load_sem,
    core_sems,
    x_sems,
    z_sems,
    vector_sems,
):
    units, unit, width = total_ref.shape
    rows = rights.shape[1]
    shards = lax.axis_size("dp")
    levels = shards // 4
    ups = upper_hbm.shape[1] // width
    me = lax.axis_index("dp")
    core, x, z = me % 2, (me // 2) % 2, me // 4
    sibling = {"dp": me + 1 - 2 * core}
    across = {"dp": me + 2 - 4 * x}

    def level_peer(step):
        return {"dp": ((z + step) % levels) * 4 + x * 2 + core}

    first_up = 1 + ups
    first_mixed = first_up + ups

    sources = (
        [attended_hbm]
        + [hidden_hbm.at[:, pl.ds(block * width, width)] for block in range(ups)]
        + [second_hbm, normed_hbm]
    )

    def right_copy(index):
        return pltpu.make_async_copy(sources[index], rights.at[index], right_sem.at[index])

    chunks = [(branch_hbm, 0), (output_hbm, 0)]
    chunks += [(upper_hbm, block) for block in range(ups)]
    chunks += [(mixed_hbm, block) for block in range(3)]

    def left_copy(index):
        source, block = chunks[index]
        return pltpu.make_async_copy(
            source.at[:, pl.ds(block * width, width)], loaded.at[index % 2], load_sem.at[index % 2]
        )

    left_copy(0).start()
    right_copy(0).start()
    left_copy(1).start()

    barrier = pltpu.get_barrier_semaphore()
    peers = [sibling, across] + [level_peer(step) for step in range(1, levels)]
    for peer in peers:
        pl.semaphore_signal(barrier, inc=1, device_id=peer, device_id_type=MESH)

    def send(source, target, sems, index, peer):
        return pltpu.make_async_remote_copy(
            src_ref=source,
            dst_ref=target,
            send_sem=sems.at[(0,) + index],
            recv_sem=sems.at[(1,) + index],
            device_id=peer,
            device_id_type=MESH,
        )

    def to_core(j):
        return send(send_core.at[j], take_core.at[j], core_sems, (j,), sibling)

    def to_x(j):
        return send(send_x.at[j], take_x.at[j], x_sems, (j,), across)

    def to_z(j, step):
        return send(send_z.at[j, step - 1], take_z.at[j, step - 1], z_sems, (j, step - 1), level_peer(step))

    def vector_hop(index):
        peer = (sibling, across)[index] if index < 2 else level_peer(index - 1)
        return send(vectors.at[min(index, 2)], take_vector.at[index], vector_sems, (index,), peer)

    vectors[0] = vector_ref[...]

    def turn(index, group, first_left):
        left_copy(index).wait()
        block = chunks[index][1]
        source = loaded.at[index % 2]
        pieces = unit // 16

        def step(lane_block):
            turned = jnp.transpose(source[:, part(lane_block, 128)])
            for piece in range(8):
                place = block * (width // 16) + lane_block * 8 + piece
                shard, inner = lax.div(place, group), lax.rem(place, group)
                order = (
                    2 * levels * (1 - lax.rem(shard + core, 2))
                    + levels * (1 - lax.rem(lax.div(shard, 2) + x, 2))
                    + lax.div(shard, 4)
                )
                row = pl.multiple_of(order * unit + lax.rem(inner, pieces) * 16, 16)
                lefts[first_left + lax.div(inner, pieces), pl.ds(row, 16)] = turned[piece * 16 : (piece + 1) * 16]

        loop(width // 128, step)
        if index + 2 < len(chunks):
            left_copy(index + 2).start()

    half = 2 * levels * unit
    quarter = levels * unit

    span = width // CUT
    steps = units * CUT

    def left_of(u):
        return jnp.maximum(jnp.minimum(u, 1), u + 1 - ups)

    def right_of(u):
        return jnp.minimum(u, first_up) + jnp.where(u >= first_mixed, 1, 0)

    def product(j, start, count):
        u = lax.div(j, CUT)
        return times(lefts[left_of(u), start : start + count], rights[right_of(u), :, part(lax.rem(j, CUT), span)])

    def stage_core(j):
        send_core[j] = product(j, 0, half).astype(LOW)
        to_core(j).start()

    def stage_x(j):
        to_core(j).wait_recv()
        value = product(j, half, quarter) + take_core[j, :quarter].astype(F32)
        send_x[j] = value.astype(LOW)
        to_x(j).start()

    def stage_z(j):
        to_x(j).wait_recv()
        value = product(j, half + quarter, quarter) + take_core[j, quarter:].astype(F32) + take_x[j].astype(F32)
        own[...] = value.reshape(levels, unit, span)
        for hop in range(1, levels):
            send_z[j, hop - 1] = own[(z + hop) % levels].astype(LOW)
            to_z(j, hop).start()
        total_ref[lax.div(j, CUT), :, part(lax.rem(j, CUT), span)] = own[z]

    def finish(j):
        u, here = lax.div(j, CUT), part(lax.rem(j, CUT), span)
        value = total_ref[u, :, here]
        for hop in range(1, levels):
            to_z(j, hop).wait_recv()
            value = value + take_z[j, hop - 1].astype(F32)
        total_ref[u, :, here] = value

    def feed(j):
        @pl.when(j == 1)
        def _():
            turn(1, unit // 16, 1)
            for index in range(1 + ups, 3 + ups):
                right_copy(index).start()

        for block in range(ups):

            @pl.when(j == CUT * block + 2)
            def _(block=block):
                turn(2 + block, ups * unit // 16, 2)

        for block in range(3):

            @pl.when(j == CUT * (block + ups) + 2)
            def _(block=block):
                turn(2 + ups + block, 3 * unit // 16, 2 + ups)

    def need_right(j):
        for index, when in [(block, block) for block in range(1, 1 + ups)] + [
            (1 + ups, first_up),
            (2 + ups, first_mixed),
        ]:

            @pl.when(j == CUT * when)
            def _(index=index):
                right_copy(index).wait()

    turn(0, unit // 16, 0)
    for index in range(1, 1 + ups):
        right_copy(index).start()
    right_copy(0).wait()
    pl.semaphore_wait(barrier, len(peers))
    vector_hop(0).start()

    def advance(j):
        feed(j)

        @pl.when((j >= 1) & (j < steps + 1))
        def _():
            stage_x(j - 1)

        need_right(j)

        @pl.when(j < steps)
        def _():
            stage_core(j)

        @pl.when((j >= LAG) & (j < steps + LAG))
        def _():
            stage_z(j - LAG)

        @pl.when(j >= 2 * LAG)
        def _():
            finish(j - 2 * LAG)

        @pl.when(j == 2)
        def _():
            vector_hop(0).wait_recv()
            vectors[1] = vectors[0] + take_vector[0]
            vector_hop(1).start()

        @pl.when(j == 4)
        def _():
            vector_hop(1).wait_recv()
            vectors[2] = vectors[1] + take_vector[1]
            for hop in range(1, levels):
                vector_hop(hop + 1).start()

    loop(steps + 2 * LAG, advance)
    whole = vectors[2]
    for hop in range(1, levels):
        vector_hop(hop + 1).wait_recv()
        whole = whole + take_vector[hop + 1]
    whole_ref[...] = whole

    def drain(j):
        to_core(j).wait_send()
        to_x(j).wait_send()
        for hop in range(1, levels):
            to_z(j, hop).wait_send()

    loop(steps, drain)
    for hop in range(levels + 1):
        vector_hop(hop).wait_send()


def reduce_parts(vector, lefts, rights):
    shards = lax.axis_size("dp")
    branch, output_low, upper_low, mixed = lefts
    attended, hidden, second_normed, normed = rights
    rows, width = branch.shape
    ups = hidden.shape[1] // width
    unit, levels = width // shards, shards // 4
    units = 1 + 2 * ups + 3
    steps, span = units * CUT, width // CUT
    anywhere = pl.BlockSpec(memory_space=pl.ANY)
    vmem = pl.BlockSpec(memory_space=pltpu.VMEM)
    total, whole = pl.pallas_call(
        reduce_kernel,
        out_shape=(
            jax.ShapeDtypeStruct((units, unit, width), F32),
            jax.ShapeDtypeStruct(vector.shape, F32),
        ),
        in_specs=[vmem] + [anywhere] * 8,
        out_specs=[vmem, vmem],
        scratch_shapes=[
            pltpu.VMEM((3 + ups, rows, width), LOW),
            pltpu.VMEM((2, rows, width), LOW),
            pltpu.VMEM((5 + ups, width, rows), LOW),
            pltpu.VMEM((steps, 2 * levels * unit, span), LOW),
            pltpu.VMEM((steps, 2 * levels * unit, span), LOW),
            pltpu.VMEM((steps, levels * unit, span), LOW),
            pltpu.VMEM((steps, levels * unit, span), LOW),
            pltpu.VMEM((steps, levels - 1, unit, span), LOW),
            pltpu.VMEM((steps, levels - 1, unit, span), LOW),
            pltpu.VMEM((levels, unit, span), F32),
            pltpu.VMEM((3,) + vector.shape, F32),
            pltpu.VMEM((levels + 1,) + vector.shape, F32),
            pltpu.SemaphoreType.DMA((3 + ups,)),
            pltpu.SemaphoreType.DMA((2,)),
            pltpu.SemaphoreType.DMA((2, steps)),
            pltpu.SemaphoreType.DMA((2, steps)),
            pltpu.SemaphoreType.DMA((2, steps, levels - 1)),
            pltpu.SemaphoreType.DMA((2, levels + 1)),
        ],
        name="reduce",
        compiler_params=pltpu.CompilerParams(
            collective_id=1, has_side_effects=True, vmem_limit_bytes=67043328
        ),
    )(vector, branch, output_low, upper_low, mixed, attended, hidden, second_normed, normed)
    return whole, total


def finish_kernel(
    whole_ref,
    total_hbm,
    result_hbm,
    input_grad_hbm,
    result_out,
    input_grad_out,
    first_gain_out,
    first_shift_out,
    project_out,
    query_bias_out,
    value_bias_out,
    out_weight_out,
    out_bias_out,
    second_gain_out,
    second_shift_out,
    up_out,
    up_bias_out,
    down_out,
    down_bias_out,
    total,
    rows_low,
    rows_wide,
    in_sem,
    out_sem,
):
    units, unit, width = total.shape
    ups = down_out.shape[1] // width
    blocks = rows_low.shape[0]
    me = lax.axis_index("dp")
    shards = lax.axis_size("dp")
    first_up, first_mixed = 1 + ups, 1 + 2 * ups
    take = pltpu.make_async_copy(total_hbm, total, in_sem.at[2 * blocks])
    take.start()

    def block_of(ref, block):
        size = rows_low.shape[1]
        return ref.at[pl.ds(block * size, size)]

    pairs = []
    for block in range(blocks):
        for index, (source, middle, target) in enumerate(
            ((result_hbm, rows_low, result_out), (input_grad_hbm, rows_wide, input_grad_out))
        ):
            slot = 2 * block + index
            load = pltpu.make_async_copy(block_of(source, block), middle.at[block], in_sem.at[slot])
            save = pltpu.make_async_copy(middle.at[block], block_of(target, block), out_sem.at[slot])
            load.start()
            pairs.append((load, save))

    pieces = [(0, out_weight_out)]
    pieces += [(1 + block, down_out.at[:, pl.ds(block * width, width)]) for block in range(ups)]
    pieces += [(first_up + block, up_out.at[pl.ds(block * unit, unit)]) for block in range(ups)]
    pieces += [(first_mixed + block, project_out.at[pl.ds(block * unit, unit)]) for block in range(3)]
    take.wait()
    for index, (source, target) in enumerate(pieces):
        save = pltpu.make_async_copy(total.at[source], target, out_sem.at[2 * blocks + index])
        save.start()
        pieces[index] = save
    for load, save in pairs:
        load.wait()
        save.start()
    rolled = pltpu.roll(whole_ref[:8], lax.rem(shards - me, shards) * unit, 1)
    small_outs = (
        first_gain_out, first_shift_out, query_bias_out, value_bias_out,
        out_bias_out, second_gain_out, second_shift_out, down_bias_out,
    )
    for index, small in enumerate(small_outs):
        small[...] = rolled[index : index + 1, :unit]
    span = ups * unit
    inner = width // span
    wide_rolled = pltpu.roll(whole_ref[8:16], lax.rem(inner - lax.rem(me, inner), inner) * span, 1)
    mine = lax.broadcasted_iota(jnp.int32, (8, width), 0) == lax.div(me, inner)
    up_bias_out[...] = jnp.sum(jnp.where(mine, wide_rolled, 0.0), axis=0, keepdims=True)[:, :span]
    for _, save in pairs:
        save.wait()
    for save in pieces:
        save.wait()


def finish(whole, total, result, input_grad, ups):
    units, unit, width = total.shape
    rows = result.shape[0]
    anywhere = pl.BlockSpec(memory_space=pl.ANY)
    vmem = pl.BlockSpec(memory_space=pltpu.VMEM)

    def wide(*shape):
        return jax.ShapeDtypeStruct(shape, F32)

    small, matrix = wide(1, unit), wide(unit, width)
    blocks = 4
    outs = pl.pallas_call(
        finish_kernel,
        out_shape=(
            jax.ShapeDtypeStruct(result.shape, LOW), wide(rows, width), small, small,
            wide(3 * unit, width), small, small, matrix, small, small, small,
            wide(ups * unit, width), wide(1, ups * unit), wide(unit, ups * width), small,
        ),
        in_specs=[vmem] + [anywhere] * 3,
        out_specs=[
            anywhere, anywhere, vmem, vmem, anywhere, vmem, vmem, anywhere,
            vmem, vmem, vmem, anywhere, vmem, anywhere, vmem,
        ],
        scratch_shapes=[
            pltpu.VMEM(total.shape, F32),
            pltpu.VMEM((blocks, rows // blocks, width), LOW),
            pltpu.VMEM((blocks, rows // blocks, width), F32),
            pltpu.SemaphoreType.DMA((2 * blocks + 1,)),
            pltpu.SemaphoreType.DMA((2 * blocks + units,)),
        ],
        name="finish",
        compiler_params=pltpu.CompilerParams(vmem_limit_bytes=67043328),
    )(whole, total, result, input_grad)
    result, input_grad = outs[0][None], outs[1][None]
    turned = [outs[index].T[None] for index in (4, 7, 11, 13)]
    return (
        result, input_grad, outs[2], outs[3], turned[0], outs[5], outs[6], turned[1],
        outs[8], outs[9], outs[10], turned[2], outs[12], turned[3], outs[14],
    )


def contract_rows(left, right):
    return lax.dot_general(left, right, (((0,), (0,)), ((), ())), preferred_element_type=F32)


def scatter_parts(vector, lefts, rights):
    def reduce_rows(left, right):
        piece = lax.psum_scatter(contract_rows(left, right), "dp", scatter_dimension=0, tiled=True)
        return piece.T

    branch, output_low, upper_low, mixed = lefts
    attended, hidden, second_normed, normed = rights
    return (
        lax.psum(vector, "dp"),
        reduce_rows(mixed, normed),
        reduce_rows(branch, attended),
        reduce_rows(upper_low, second_normed),
        reduce_rows(output_low, hidden),
    )


def on_device(*arrays):
    shards = lax.axis_size("dp")
    me = lax.axis_index("dp")
    (
        result, input_grad, vector,
        normed, attended, second_normed, hidden, mixed, branch, upper_low, output_low,
    ) = relay(arrays)
    lefts = (branch, output_low, upper_low, mixed)
    rights = (attended, hidden, second_normed, normed)
    width = branch.shape[1]
    if shards % 4 == 0 and width % (16 * shards) == 0:
        whole, total = reduce_parts(vector, lefts, rights)
        return finish(whole, total, result, input_grad, hidden.shape[1] // width)
    whole, project_grad, out_grad, up_grad, down_grad = scatter_parts(vector, lefts, rights)
    size = width // shards
    small = lax.dynamic_slice_in_dim(whole[:8], me * size, size, 1)
    up_size = hidden.shape[1] // shards
    up_small = lax.dynamic_slice_in_dim(whole[8:].reshape(1, -1), me * up_size, up_size, 1)
    return (
        result[None],
        input_grad[None],
        small[0:1],
        small[1:2],
        project_grad[None],
        small[2:3],
        small[3:4],
        out_grad[None],
        small[4:5],
        small[5:6],
        small[6:7],
        up_grad[None],
        up_small,
        down_grad[None],
        small[7:8],
    )


def solution(mesh):
    stack1 = P("section", None)
    stack2 = P("section", None, None)
    in_specs = (
        P("dp", None), P("dp", None), P("dp"), P("dp"),
        stack1, stack1, stack2, stack1, stack1, stack2, stack1,
        stack1, stack1, stack2, stack1, stack2, stack1,
    )
    row = P("section", "dp")
    matrix = P("section", None, "dp")
    rows = P("section", "dp", None)
    out_specs = (
        rows, rows, row, row, matrix, row, row, matrix, row, row, row, matrix, row, matrix, row,
    )
    return jax.shard_map(
        on_device, mesh=mesh, in_specs=in_specs, out_specs=out_specs, check_vma=False
    )
```

```python
import functools

import jax
import jax.numpy as jnp
from jax import lax
from jax.experimental import pallas as pl
from jax.experimental.pallas import tpu as pltpu
from jax.sharding import PartitionSpec as P

HEADS = 12
HEAD_DIM = 64
SEQ = 512
PAIR = 2 * HEAD_DIM
PAIRS = HEADS // 2
TILE = 256
WIDE = 1024
HALF = 256
CUT = 2
RING = 6
LATE = 16
LAG = 3
ROWS = 128
EPSILON = 1e-06
SCORE_SCALE = 0.125
FAR = -1e30
F32 = jnp.float32
LOW = jnp.bfloat16
MESH = pl.DeviceIdType.MESH


def times(left, right):
    return lax.dot_general(left, right, (((1,), (0,)), ((), ())), preferred_element_type=F32)


def times_t(left, right):
    return lax.dot_general(left, right, (((1,), (1,)), ((), ())), preferred_element_type=F32)


def loop(count, body):
    def step(index, carry):
        body(index)
        return carry

    lax.fori_loop(0, count, step, 0)


def part(index, size):
    return pl.ds(pl.multiple_of(index * size, size), size)


def norm_rows(values):
    average = jnp.mean(values, axis=-1, keepdims=True)
    centred = values - average
    inv_scale = lax.rsqrt(jnp.mean(centred * centred, axis=-1, keepdims=True) + EPSILON)
    return centred * inv_scale, inv_scale


def norm_back(normed_grad, whitened, inv_scale, gain):
    scaled = normed_grad * gain
    return inv_scale * (
        scaled
        - jnp.mean(scaled, axis=-1, keepdims=True)
        - whitened * jnp.mean(scaled * whitened, axis=-1, keepdims=True)
    )


def fold_rows(values):
    rows, width = values.shape
    return jnp.sum(values.reshape(rows // 8, 8, width), axis=0)


def fill_bias(code_row, bias):
    across = jnp.transpose(jnp.broadcast_to(code_row, (128, SEQ)))
    for block in range(SEQ // 128):
        lanes = slice(block * 128, (block + 1) * 128)
        bias[:, lanes] = jnp.where(across == code_row[:, lanes], 0.0, FAR)


def gelu_both(upper):
    cumulative = 0.5 * (1.0 + lax.erf(upper * (0.5**0.5)))
    density = jnp.exp2((upper * upper) * -0.7213475204444817) * 0.3989422804014327
    return upper * cumulative, cumulative + upper * density


def relay_kernel(
    defer,
    x_hbm,
    cot_hbm,
    segment_ref,
    valid_ref,
    first_gain,
    first_shift,
    project_hbm,
    query_bias,
    value_bias,
    out_hbm,
    out_bias,
    second_gain,
    second_shift,
    up_hbm,
    up_bias,
    down_hbm,
    down_bias,
    result_hbm,
    input_grad_hbm,
    vector_ref,
    normed_hbm,
    attended_hbm,
    second_hbm,
    hidden_hbm,
    mixed_hbm,
    branch_hbm,
    upper_hbm,
    output_hbm,
    late_exponents,
    late_outputs,
    late_inverse,
    late_upstream,
    late_middle,
    project,
    out_weight,
    up_weight,
    down_weight,
    x_in,
    g_in,
    normed,
    mixed,
    attended,
    middle,
    second_normed,
    hidden,
    slope,
    result,
    wide,
    grad_low,
    bias,
    inv_sums,
    score_buf,
    score_low,
    exponents,
    outputs_across,
    sums,
    up_sums,
    weight_sem,
    x_sem,
    g_sem,
    send_sem,
    out_sem,
    late_sem,
):
    section = lax.axis_index("section")
    width = x_in.shape[2]
    hidden_width = hidden.shape[1]
    packs = x_in.shape[0]
    last = lax.axis_size("section") - 1
    partner = {"section": 1 - section}
    branch, attended_low, input_grad = normed, attended, wide

    def rows_of(ref, pack):
        return ref.at[pl.ds(pl.multiple_of(pack * SEQ, SEQ), SEQ)]

    def half_of(half):
        return pl.ds(pl.multiple_of(half * HALF, HALF), HALF)

    def local_rows(source, target, sems, pack, half):
        there = pl.ds(pl.multiple_of(pack * SEQ + half * HALF, HALF), HALF)
        return pltpu.make_async_copy(source.at[there], target.at[pack, half_of(half)], sems.at[pack, half])

    def local_x(pack, half):
        return local_rows(x_hbm, x_in, x_sem, pack, half)

    def local_g(pack, half):
        return local_rows(cot_hbm, g_in, g_sem, pack, half)

    weights = (
        pltpu.make_async_copy(project_hbm.at[0], project, weight_sem.at[0]),
        pltpu.make_async_copy(out_hbm.at[0], out_weight, weight_sem.at[1]),
        pltpu.make_async_copy(up_hbm.at[0], up_weight, weight_sem.at[2]),
        pltpu.make_async_copy(down_hbm.at[0], down_weight, weight_sem.at[3]),
    )

    @pl.when(section == 0)
    def _():
        for pack in range(packs):
            for half in range(2):
                local_x(pack, half).start()

    weights[0].start()

    @pl.when(section == last)
    def _():
        for pack in range(packs):
            for half in range(2):
                local_g(pack, half).start()

    barrier = pltpu.get_barrier_semaphore()
    pl.semaphore_signal(barrier, inc=1, device_id=partner, device_id_type=MESH)
    pl.semaphore_wait(barrier, 1)

    sums[...] = jnp.zeros_like(sums)
    up_sums[...] = jnp.zeros_like(up_sums)

    def hop(way, source, target, sems, pack, half):
        rows = half_of(half)
        return pltpu.make_async_remote_copy(
            src_ref=source.at[rows],
            dst_ref=target.at[pack, rows],
            send_sem=send_sem.at[way, pack, half],
            recv_sem=sems.at[pack, half],
            device_id=partner,
            device_id_type=MESH,
        )

    def hop_forward(pack, half):
        return hop(0, result, x_in, x_sem, pack, half)

    def hop_backward(pack, half):
        return hop(1, grad_low, g_in, g_sem, pack, half)

    kept = (
        (result, result_hbm),
        (normed, normed_hbm),
        (attended, attended_hbm),
        (second_normed, second_hbm),
        (hidden, hidden_hbm),
        (mixed, mixed_hbm),
        (branch, branch_hbm),
        (slope, upper_hbm),
        (g_in, output_hbm),
        (input_grad, input_grad_hbm),
    )

    def store(index, pack):
        source, target = kept[index]
        source = source if len(source.shape) == 2 else source.at[pack]
        return pltpu.make_async_copy(source, rows_of(target, pack), out_sem.at[index, pack])

    lane = lax.broadcasted_iota(jnp.int32, (SEQ, PAIR), 1)

    def heads_of(pack, pair):
        start = pl.multiple_of(pair * PAIR, PAIR)
        return [mixed[pack, :, pl.ds(third * width + start, PAIR)] for third in range(3)]

    late = (
        pltpu.make_async_copy(exponents.at[0], late_exponents, late_sem.at[0]),
        pltpu.make_async_copy(outputs_across.at[0], late_outputs, late_sem.at[1]),
        pltpu.make_async_copy(inv_sums.at[0], late_inverse, late_sem.at[2]),
        pltpu.make_async_copy(attended_low, late_upstream, late_sem.at[3]),
        pltpu.make_async_copy(middle.at[0], late_middle, late_sem.at[4]),
    )

    def forward(pack):
        first = pack == 0

        gain = first_gain[...].astype(F32)
        shift = first_shift[...].astype(F32)

        @pl.when(pack > 0)
        def _():
            store(1, pack - 1).wait()

        places = lax.broadcasted_iota(jnp.int32, (1, SEQ), 1) + SEQ
        fill_bias(jnp.where(valid_ref[pack] == 1, segment_ref[pack], places).astype(F32), bias)

        @pl.when(first)
        def _():
            weights[0].wait()
            for copy in weights[1:]:
                copy.start()

        def project_half(half):
            @pl.when(section == 0)
            def _():
                local_x(pack, half).wait()

            @pl.when(section == last)
            def _():
                hop_forward(pack, half).wait_recv()

            def norm_step(block):
                rows = pl.ds(pl.multiple_of(half * HALF + block * ROWS, ROWS), ROWS)
                white, _ = norm_rows(x_in[pack, rows].astype(F32))
                normed[rows] = (white * gain + shift).astype(LOW)

            loop(HALF // ROWS, norm_step)
            rows = half_of(half)
            for third, offset_ref in enumerate((query_bias, None, value_bias)):
                there = slice(third * width, (third + 1) * width)
                value = times(normed[rows], project[:, there])
                if offset_ref is not None:
                    value = value + offset_ref[...].astype(F32)
                mixed[pack, rows, there] = value.astype(LOW)

        loop(2, project_half)
        store(1, pack).start()

        def scores_of(pair, slot):
            query, key, _ = heads_of(pack, pair)
            for side in range(2):
                own = (lane < HEAD_DIM) == (side == 0)
                one = jnp.where(own, query * SCORE_SCALE, 0.0).astype(LOW)
                score_buf[slot, side] = times_t(key, one) + bias[...]

        def attend(pair, slot):
            value_across = jnp.transpose(heads_of(pack, pair)[2])
            ones = jnp.ones((16, SEQ), LOW)
            outs = []
            for side in range(2):
                heads = slice(side * HEAD_DIM, (side + 1) * HEAD_DIM)
                scores = score_buf[slot, side]
                key_max = jnp.max(scores, axis=0, keepdims=True)
                exponent = jnp.exp(scores - key_max).astype(LOW)
                exponents[pack, 2 * pair + side] = exponent
                sums_too = times(jnp.concatenate([value_across[heads], ones], axis=0), exponent)
                inverse = 1.0 / sums_too[HEAD_DIM : HEAD_DIM + 1]
                inv_sums[pack, 2 * pair + side] = jnp.broadcast_to(inverse, (8, SEQ))
                outs.append(sums_too[:HEAD_DIM] * inverse)
                outputs_across[pack, 2 * pair + side] = outs[side]
            attended[:, part(pair, PAIR)] = jnp.transpose(jnp.concatenate(outs, axis=0)).astype(LOW)

        @pl.when(pack > 0)
        def _():
            store(2, pack - 1).wait()

        scores_of(0, 0)

        def attend_step(index):
            for slot in range(2):
                pair = 2 * index + slot
                scores_of(jnp.minimum(pair + 1, PAIRS - 1), 1 - slot)
                attend(pair, slot)

        loop(PAIRS // 2, attend_step)
        store(2, pack).start()

        @pl.when(first)
        def _():
            weights[1].wait()

        middle[pack] = x_in[pack].astype(F32) + (
            times(attended[...], out_weight[...]) + out_bias[...].astype(F32)
        )
        gain2 = second_gain[...].astype(F32)
        shift2 = second_shift[...].astype(F32)

        @pl.when(pack > 0)
        def _():
            store(3, pack - 1).wait()
            store(4, pack - 1).wait()
            store(0, pack - 1).wait()

        @pl.when(first)
        def _():
            weights[2].wait()
            weights[3].wait()

        def feed_half(half):
            def second_step(block):
                rows = pl.ds(pl.multiple_of(half * HALF + block * ROWS, ROWS), ROWS)
                white, _ = norm_rows(middle[pack, rows])
                second_normed[rows] = (white * gain2 + shift2).astype(LOW)

            loop(HALF // ROWS, second_step)
            rows = half_of(half)

            def up_step(tile):
                here = part(tile, width)
                upper = times(second_normed[rows], up_weight[:, here]) + up_bias[:, here].astype(F32)
                act, act_slope = gelu_both(upper)
                hidden[rows, here] = act.astype(LOW)
                slope[pack, rows, here] = act_slope.astype(LOW)

            loop(hidden_width // width, up_step)

            @pl.when((pack > 0) & (section == 0))
            def _():
                hop_forward(pack - 1, half).wait_send()

            value = middle[pack, rows] + (times(hidden[rows], down_weight[...]) + down_bias[...].astype(F32))
            result[rows] = value.astype(LOW)

            @pl.when(section == 0)
            def _():
                hop_forward(pack, half).start()

        loop(2, feed_half)
        store(3, pack).start()
        store(4, pack).start()
        store(0, pack).start()

    def backward(order):
        pack = packs - 1 - order

        def hidden_half(half):
            @pl.when(section == last)
            def _():
                local_g(pack, half).wait()

            @pl.when(section == 0)
            def _():
                hop_backward(pack, half).wait_recv()

            rows = half_of(half)
            sums[7] += fold_rows(g_in[pack, rows].astype(F32))

            def hidden_step(tile):
                here = part(tile, WIDE)
                value = times_t(g_in[pack, rows], down_weight[here]).astype(LOW).astype(F32)
                low = (value * slope[pack, rows, here].astype(F32)).astype(LOW)
                slope[pack, rows, here] = low
                up_sums[:, here] += fold_rows(low.astype(F32))

            loop(hidden_width // WIDE, hidden_step)

        loop(2, hidden_half)
        store(8, pack).start()
        store(7, pack).start()

        @pl.when(order > 0)
        def _():
            store(9, pack + 1).wait()
            store(6, pack + 1).wait()

        @pl.when(order == 0)
        def _():
            store(1, pack).wait()
            store(2, pack).wait()

        wide[...] = times_t(slope[pack], up_weight[...])
        gain2 = second_gain[...].astype(F32)

        def second_back(block):
            rows = part(block, ROWS)
            grad = wide[rows]
            white, scale = norm_rows(middle[pack, rows])
            total = g_in[pack, rows].astype(F32) + norm_back(grad, white, scale, gain2)
            sums[5] += fold_rows(grad * white)
            sums[6] += fold_rows(grad)
            middle[pack, rows] = total
            low = total.astype(LOW)
            branch[rows] = low
            sums[4] += fold_rows(low.astype(F32))

        loop(SEQ // ROWS, second_back)
        store(6, pack).start()

        attended_low[...] = times_t(branch[...], out_weight[...]).astype(LOW)

        def attend_back(pair):
            here = part(pair, PAIR)
            query, key, value = heads_of(pack, pair)
            key_across, up_across = jnp.transpose(key), jnp.transpose(attended_low[:, here])
            empty = jnp.zeros((HEAD_DIM, SEQ), LOW)
            query_across, value_across, key_grad = [], [], 0.0
            for side in range(2):
                head = 2 * pair + side
                heads = slice(side * HEAD_DIM, (side + 1) * HEAD_DIM)
                own = (lane < HEAD_DIM) == (side == 0)
                one_query = jnp.where(own, query * SCORE_SCALE, 0.0).astype(LOW)
                one_up = (up_across[heads].astype(F32) * inv_sums[pack, head, 0:1]).astype(LOW)
                inner = jnp.sum(one_up.astype(F32) * outputs_across[pack, head], axis=0, keepdims=True)
                soft_grad = times(value, jnp.concatenate([one_up, empty][:: 1 - 2 * side], axis=0))
                score_low[side] = (exponents[pack, head].astype(F32) * (soft_grad - inner)).astype(LOW)
                value_across.append(times_t(one_up, exponents[pack, head]))
                key_grad += times(score_low[side], one_query)
                query_across.append(times(key_across[heads], score_low[side]))
            query_grad = (jnp.transpose(jnp.concatenate(query_across, axis=0)) * SCORE_SCALE).astype(LOW)
            value_grad = jnp.transpose(jnp.concatenate(value_across, axis=0)).astype(LOW)
            sums[2, :, here] += fold_rows(query_grad.astype(F32))
            sums[3, :, here] += fold_rows(value_grad.astype(F32))
            for third, grad in enumerate((query_grad, key_grad.astype(LOW), value_grad)):
                start = pl.multiple_of(third * width + pair * PAIR, PAIR)
                mixed[pack, :, pl.ds(start, PAIR)] = grad

        def attend_all():
            loop(PAIRS, attend_back)
            store(5, pack).start()

        gain = first_gain[...].astype(F32)

        def first_half(half):
            rows = half_of(half)
            wide[rows] = times_t(mixed[pack, rows], project[...])

            @pl.when((order > 0) & (section == last))
            def _():
                hop_backward(pack + 1, half).wait_send()

            def first_back(block):
                rows = pl.ds(pl.multiple_of(half * HALF + block * ROWS, ROWS), ROWS)
                grad = wide[rows]
                white, scale = norm_rows(x_in[pack, rows].astype(F32))
                total = middle[pack, rows] + norm_back(grad, white, scale, gain)
                sums[0] += fold_rows(grad * white)
                sums[1] += fold_rows(grad)
                input_grad[rows] = total
                grad_low[rows] = total.astype(LOW)

            loop(HALF // ROWS, first_back)

            @pl.when(section == last)
            def _():
                hop_backward(pack, half).start()

        def first_all():
            loop(2, first_half)
            store(9, pack).start()

        if not defer:
            attend_all()
            first_all()
        else:
            put_off = (order == packs - 1) & (section == 0)

            @pl.when(put_off)
            def _():
                store(5, pack).start()
                for copy in late[3:]:
                    copy.start()

            @pl.when(jnp.logical_not(put_off))
            def _():
                attend_all()
                first_all()

    loop(packs, forward)
    if defer:

        @pl.when(section == 0)
        def _():
            for copy in late[:3]:
                copy.start()

    loop(packs, backward)

    count = sums.shape[0]
    vector_ref[count:] = jnp.zeros((vector_ref.shape[0] - count, width), F32)
    for index in range(count):
        vector_ref[index : index + 1] = jnp.sum(sums[index], axis=0, keepdims=True)
    for index in range(hidden_width // width):
        lanes = slice(index * width, (index + 1) * width)
        vector_ref[count + index : count + index + 1] = jnp.sum(up_sums[:, lanes], axis=0, keepdims=True)

    for index in (0, 3, 4):
        store(index, packs - 1).wait()
    store(6, 0).wait()
    if not defer:
        store(9, 0).wait()
    else:

        @pl.when(section == last)
        def _():
            store(9, 0).wait()

        @pl.when(section == 0)
        def _():
            for copy in late:
                copy.wait()

    for pack in range(packs):
        for index in (5, 7, 8):
            store(index, pack).wait()

    @pl.when(section == 0)
    def _():
        for half in range(2):
            hop_forward(packs - 1, half).wait_send()

    @pl.when(section == last)
    def _():
        for half in range(2):
            hop_backward(0, half).wait_send()


def relay(arrays, defer):
    inputs, cotangent, segments, valid_flags = arrays[:4]
    rows, width = inputs.shape
    hidden_width = arrays[13].shape[2]
    packs = rows // SEQ
    anywhere = pl.BlockSpec(memory_space=pl.ANY)
    vmem = pl.BlockSpec(memory_space=pltpu.VMEM)

    def low(columns):
        return jax.ShapeDtypeStruct((rows, columns), LOW)

    outs = (
        low(width),
        jax.ShapeDtypeStruct((rows, width), F32),
        jax.ShapeDtypeStruct((16, width), F32),
        low(width),
        low(width),
        low(width),
        low(hidden_width),
        low(3 * width),
        low(width),
        low(hidden_width),
        low(width),
        jax.ShapeDtypeStruct((HEADS, SEQ, SEQ), LOW),
        jax.ShapeDtypeStruct((HEADS, HEAD_DIM, SEQ), F32),
        jax.ShapeDtypeStruct((HEADS, 8, SEQ), F32),
        jax.ShapeDtypeStruct((SEQ, width), LOW),
        jax.ShapeDtypeStruct((SEQ, width), F32),
    )

    def held(columns, kind=LOW):
        return pltpu.VMEM((packs, SEQ, columns), kind)

    scratch = [
        pltpu.VMEM((width, 3 * width), LOW),
        pltpu.VMEM((width, width), LOW),
        pltpu.VMEM((width, hidden_width), LOW),
        pltpu.VMEM((hidden_width, width), LOW),
        held(width),
        held(width),
        pltpu.VMEM((SEQ, width), LOW),
        held(3 * width),
        pltpu.VMEM((SEQ, width), LOW),
        held(width, F32),
        pltpu.VMEM((SEQ, width), LOW),
        pltpu.VMEM((SEQ, hidden_width), LOW),
        held(hidden_width),
        pltpu.VMEM((SEQ, width), LOW),
        pltpu.VMEM((SEQ, width), F32),
        pltpu.VMEM((SEQ, width), LOW),
        pltpu.VMEM((SEQ, SEQ), F32),
        pltpu.VMEM((packs, HEADS, 8, SEQ), F32),
        pltpu.VMEM((2, 2, SEQ, SEQ), F32),
        pltpu.VMEM((2, SEQ, SEQ), LOW),
        pltpu.VMEM((packs, HEADS, SEQ, SEQ), LOW),
        pltpu.VMEM((packs, HEADS, HEAD_DIM, SEQ), F32),
        pltpu.VMEM((8, 8, width), F32),
        pltpu.VMEM((8, hidden_width), F32),
        pltpu.SemaphoreType.DMA((4,)),
        pltpu.SemaphoreType.DMA((packs, 2)),
        pltpu.SemaphoreType.DMA((packs, 2)),
        pltpu.SemaphoreType.DMA((2, packs, 2)),
        pltpu.SemaphoreType.DMA((10, packs)),
        pltpu.SemaphoreType.DMA((5,)),
    ]
    return pl.pallas_call(
        functools.partial(relay_kernel, defer),
        out_shape=outs,
        in_specs=[
            anywhere, anywhere, vmem, vmem,
            vmem, vmem, anywhere, vmem, vmem, anywhere, vmem,
            vmem, vmem, anywhere, vmem, anywhere, vmem,
        ],
        out_specs=[anywhere, anywhere, vmem] + [anywhere] * 13,
        scratch_shapes=scratch,
        name="relay",
        compiler_params=pltpu.CompilerParams(
            collective_id=0, has_side_effects=True, vmem_limit_bytes=67043328
        ),
    )(
        inputs,
        cotangent,
        segments.reshape(packs, 1, SEQ),
        valid_flags.reshape(packs, 1, SEQ),
        *arrays[4:],
    )


def reduce_kernel(
    vector_ref,
    branch_hbm,
    output_hbm,
    upper_hbm,
    mixed_hbm,
    attended_hbm,
    hidden_hbm,
    second_hbm,
    normed_hbm,
    x_hbm,
    project_hbm,
    first_gain,
    late_exponents,
    late_outputs,
    late_inverse,
    late_upstream,
    late_middle,
    total_ref,
    whole_ref,
    late_grad,
    rights,
    loaded,
    lefts,
    send_core,
    take_core,
    send_x,
    take_x,
    send_z,
    take_z,
    own,
    vectors,
    take_vector,
    right_sem,
    load_sem,
    core_sems,
    x_sems,
    z_sems,
    vector_sems,
    mixed,
    exponents,
    outputs_across,
    inverse,
    upstream,
    project,
    score_low,
    middle,
    x_in,
    wide,
    sums,
    late_sems,
    pair_sems,
    half_sems,
):
    units, unit, width = total_ref.shape
    rows = rights.shape[1]
    shards = lax.axis_size("dp")
    levels = shards // 4
    ups = upper_hbm.shape[1] // width
    me = lax.axis_index("dp")
    core, x, z = me % 2, (me // 2) % 2, me // 4
    sibling = {"dp": me + 1 - 2 * core}
    across = {"dp": me + 2 - 4 * x}

    def level_peer(step):
        return {"dp": ((z + step) % levels) * 4 + x * 2 + core}

    first_up = 1 + ups
    first_mixed = first_up + ups

    sources = (
        [attended_hbm]
        + [hidden_hbm.at[:, pl.ds(block * width, width)] for block in range(ups)]
        + [second_hbm, normed_hbm]
    )

    def right_copy(index):
        return pltpu.make_async_copy(sources[index], rights.at[index], right_sem.at[index])

    chunks = [(branch_hbm, 0), (output_hbm, 0)]
    chunks += [(upper_hbm, block) for block in range(ups)]
    chunks += [(mixed_hbm, block) for block in range(3)]

    def left_copy(index):
        source, block = chunks[index]
        columns = pl.ds(block * width, width)
        if index >= 2 + ups:
            behind = pl.ds(SEQ, rows - SEQ)
            return pltpu.make_async_copy(
                source.at[behind, columns], loaded.at[index % 2, behind], load_sem.at[index % 2]
            )
        return pltpu.make_async_copy(source.at[:, columns], loaded.at[index % 2], load_sem.at[index % 2])

    left_copy(0).start()
    right_copy(0).start()
    left_copy(1).start()

    barrier = pltpu.get_barrier_semaphore()
    peers = [sibling, across] + [level_peer(step) for step in range(1, levels)]
    for peer in peers:
        pl.semaphore_signal(barrier, inc=1, device_id=peer, device_id_type=MESH)

    def send(source, target, sems, index, peer):
        return pltpu.make_async_remote_copy(
            src_ref=source,
            dst_ref=target,
            send_sem=sems.at[(0,) + index],
            recv_sem=sems.at[(1,) + index],
            device_id=peer,
            device_id_type=MESH,
        )

    def to_core(j):
        return send(send_core.at[lax.rem(j, RING)], take_core.at[j], core_sems, (j,), sibling)

    def to_x(j):
        return send(send_x.at[lax.rem(j, RING)], take_x.at[j], x_sems, (j,), across)

    def to_z(j, step):
        return send(send_z.at[j, step - 1], take_z.at[j, step - 1], z_sems, (j, step - 1), level_peer(step))

    def vector_hop(index):
        peer = (sibling, across)[index] if index < 2 else level_peer(index - 1)
        return send(vectors.at[min(index, 2)], take_vector.at[index], vector_sems, (index,), peer)

    def turn(index, group, first_left):
        left_copy(index).wait()
        block = chunks[index][1]
        source = loaded.at[index % 2]
        pieces = unit // 16

        def step(lane_block):
            here = part(lane_block, 128)
            if index >= 2 + ups:
                there = pl.ds(pl.multiple_of(block * width + lane_block * 128, 128), 128)
                turned = jnp.concatenate(
                    [jnp.transpose(mixed[:, there]), jnp.transpose(source[SEQ:, here])], axis=1
                )
            else:
                turned = jnp.transpose(source[:, here])
            for piece in range(8):
                place = block * (width // 16) + lane_block * 8 + piece
                shard, inner = lax.div(place, group), lax.rem(place, group)
                order = (
                    2 * levels * (1 - lax.rem(shard + core, 2))
                    + levels * (1 - lax.rem(lax.div(shard, 2) + x, 2))
                    + lax.div(shard, 4)
                )
                row = pl.multiple_of(order * unit + lax.rem(inner, pieces) * 16, 16)
                lefts[first_left + lax.div(inner, pieces), pl.ds(row, 16)] = turned[piece * 16 : (piece + 1) * 16]

        loop(width // 128, step)
        if index + 2 < len(chunks):
            left_copy(index + 2).start()

    half = 2 * levels * unit
    quarter = levels * unit

    span = width // CUT
    steps = units * CUT

    def left_of(u):
        return jnp.maximum(jnp.minimum(u, 1), u + 1 - ups)

    def right_of(u):
        return jnp.minimum(u, first_up) + jnp.where(u >= first_mixed, 1, 0)

    def product(j, start, count):
        u = lax.div(j, CUT)
        return times(lefts[left_of(u), start : start + count], rights[right_of(u), :, part(lax.rem(j, CUT), span)])

    def stage_core(j):
        @pl.when(j >= RING)
        def _():
            to_core(j - RING).wait_send()

        send_core[lax.rem(j, RING)] = product(j, 0, half).astype(LOW)
        to_core(j).start()

    def stage_x(j):
        to_core(j).wait_recv()
        value = product(j, half, quarter) + take_core[j, :quarter].astype(F32)

        @pl.when(j >= RING)
        def _():
            to_x(j - RING).wait_send()

        send_x[lax.rem(j, RING)] = value.astype(LOW)
        to_x(j).start()

    def stage_z(j):
        to_x(j).wait_recv()
        value = product(j, half + quarter, quarter) + take_core[j, quarter:].astype(F32) + take_x[j].astype(F32)
        own[...] = value.reshape(levels, unit, span)
        for hop in range(1, levels):
            send_z[j, hop - 1] = own[(z + hop) % levels].astype(LOW)
            to_z(j, hop).start()
        total_ref[lax.div(j, CUT), :, part(lax.rem(j, CUT), span)] = own[z]

    def finish(j):
        u, here = lax.div(j, CUT), part(lax.rem(j, CUT), span)
        value = total_ref[u, :, here]
        for hop in range(1, levels):
            to_z(j, hop).wait_recv()
            value = value + take_z[j, hop - 1].astype(F32)
        total_ref[u, :, here] = value

    def feed(j):
        @pl.when(j == 1)
        def _():
            turn(1, unit // 16, 1)
            for index in range(1 + ups, 3 + ups):
                right_copy(index).start()

        for block in range(ups):

            @pl.when(j == CUT * block + 2)
            def _(block=block):
                turn(2 + block, ups * unit // 16, 2)

        for block in range(3):

            @pl.when(j == CUT * first_mixed - 4 + block)
            def _(block=block):
                turn(2 + ups + block, 3 * unit // 16, 2 + ups)

    def need_right(j):
        for index, when in [(block, block) for block in range(1, 1 + ups)] + [
            (1 + ups, first_up),
            (2 + ups, first_mixed),
        ]:

            @pl.when(j == CUT * when)
            def _(index=index):
                right_copy(index).wait()

    turn(0, unit // 16, 0)
    for index in range(1, 1 + ups):
        right_copy(index).start()
    right_copy(0).wait()
    pl.semaphore_wait(barrier, len(peers))

    def pair_copies(pair, slot):
        heads = pl.ds(pair * 2, 2)
        return (
            pltpu.make_async_copy(late_exponents.at[heads], exponents.at[slot], pair_sems.at[0, slot]),
            pltpu.make_async_copy(late_outputs.at[heads], outputs_across.at[slot], pair_sems.at[1, slot]),
        )

    def half_copies(half):
        half_rows = pl.ds(pl.multiple_of(half * HALF, HALF), HALF)
        return (
            pltpu.make_async_copy(late_middle.at[half_rows], middle, half_sems.at[0]),
            pltpu.make_async_copy(x_hbm.at[half_rows], x_in, half_sems.at[1]),
            pltpu.make_async_copy(wide, late_grad.at[half_rows], half_sems.at[2]),
        )

    late_loads = (
        pltpu.make_async_copy(late_inverse, inverse, late_sems.at[1]),
        pltpu.make_async_copy(late_upstream, upstream, late_sems.at[2]),
        pltpu.make_async_copy(project_hbm.at[0], project, late_sems.at[3]),
    )
    mixed_load = pltpu.make_async_copy(mixed_hbm.at[pl.ds(0, SEQ)], mixed, late_sems.at[0])
    mixed_load.start()
    sums[...] = jnp.zeros_like(sums)
    lane = lax.broadcasted_iota(jnp.int32, (SEQ, PAIR), 1)
    section = lax.axis_index("section")

    @pl.when(section == 0)
    def _():
        for copy in late_loads:
            copy.start()
        for copy in pair_copies(0, 0) + half_copies(0)[:2]:
            copy.start()

    def attend_late(pair):
        slot = lax.rem(pair, 2)
        for copy in pair_copies(pair, slot):
            copy.wait()

        @pl.when(pair < PAIRS - 1)
        def _():
            for copy in pair_copies(pair + 1, 1 - slot):
                copy.start()

        here = part(pair, PAIR)
        places = [pl.ds(pl.multiple_of(third * width + pair * PAIR, PAIR), PAIR) for third in range(3)]
        query, key, value = [mixed[:, place] for place in places]
        key_across, up_across = jnp.transpose(key), jnp.transpose(upstream[:, here])
        empty = jnp.zeros((HEAD_DIM, SEQ), LOW)
        query_across, value_across, key_grad = [], [], 0.0
        for side in range(2):
            heads = slice(side * HEAD_DIM, (side + 1) * HEAD_DIM)
            own_lanes = (lane < HEAD_DIM) == (side == 0)
            one_query = jnp.where(own_lanes, query * SCORE_SCALE, 0.0).astype(LOW)
            one_up = (up_across[heads].astype(F32) * inverse[2 * pair + side, 0:1]).astype(LOW)
            inner = jnp.sum(one_up.astype(F32) * outputs_across[slot, side], axis=0, keepdims=True)
            soft_grad = times(value, jnp.concatenate([one_up, empty][:: 1 - 2 * side], axis=0))
            score_low[side] = (exponents[slot, side].astype(F32) * (soft_grad - inner)).astype(LOW)
            value_across.append(times_t(one_up, exponents[slot, side]))
            key_grad += times(score_low[side], one_query)
            query_across.append(times(key_across[heads], score_low[side]))
        query_grad = (jnp.transpose(jnp.concatenate(query_across, axis=0)) * SCORE_SCALE).astype(LOW)
        value_grad = jnp.transpose(jnp.concatenate(value_across, axis=0)).astype(LOW)
        sums[2, :, here] += fold_rows(query_grad.astype(F32))
        sums[3, :, here] += fold_rows(value_grad.astype(F32))
        for place, grad in zip(places, (query_grad, key_grad.astype(LOW), value_grad)):
            mixed[:, place] = grad

    def first_late(half):
        loads = half_copies(half)
        for copy in loads[:2]:
            copy.wait()

        @pl.when(half > 0)
        def _():
            half_copies(half - 1)[2].wait()

        wide[...] = times_t(mixed[pl.ds(pl.multiple_of(half * HALF, HALF), HALF)], project[...])
        gain = first_gain[...].astype(F32)

        def back(block):
            some = part(block, ROWS)
            grad = wide[some]
            white, scale = norm_rows(x_in[some].astype(F32))
            sums[0] += fold_rows(grad * white)
            sums[1] += fold_rows(grad)
            wide[some] = middle[some] + norm_back(grad, white, scale, gain)

        loop(HALF // ROWS, back)
        loads[2].start()

        @pl.when(half == 0)
        def _():
            for copy in half_copies(1)[:2]:
                copy.start()

    def late(j):
        pair = lax.div(j - 3, 2)

        @pl.when(j == 3)
        def _():
            mixed_load.wait()

        @pl.when((section == 0) & (j == 3))
        def _():
            for copy in late_loads:
                copy.wait()

        @pl.when((section == 0) & (j >= 3) & (j < 3 + 2 * PAIRS) & (lax.rem(j, 2) == 1))
        def _():
            attend_late(pair)

        @pl.when((section == 0) & (j >= LATE) & (j < LATE + 2))
        def _():
            first_late(j - LATE)

    def advance(j):
        feed(j)

        @pl.when((j >= 1) & (j < steps + 1))
        def _():
            stage_x(j - 1)

        need_right(j)

        @pl.when(j < steps)
        def _():
            stage_core(j)

        @pl.when((j >= LAG) & (j < steps + LAG))
        def _():
            stage_z(j - LAG)

        @pl.when(j >= 2 * LAG)
        def _():
            finish(j - 2 * LAG)

        late(j)

        @pl.when(j == LATE + 2)
        def _():
            vectors[0] = vector_ref[...]
            for index in range(4):
                vectors[0, index : index + 1] += jnp.sum(sums[index], axis=0, keepdims=True)
            vector_hop(0).start()

        @pl.when(j == LATE + 4)
        def _():
            vector_hop(0).wait_recv()
            vectors[1] = vectors[0] + take_vector[0]
            vector_hop(1).start()

        @pl.when(j == LATE + 6)
        def _():
            vector_hop(1).wait_recv()
            vectors[2] = vectors[1] + take_vector[1]
            for hop in range(1, levels):
                vector_hop(hop + 1).start()

    loop(steps + 2 * LAG, advance)
    whole = vectors[2]
    for hop in range(1, levels):
        vector_hop(hop + 1).wait_recv()
        whole = whole + take_vector[hop + 1]
    whole_ref[...] = whole

    def drain(j):
        @pl.when(j >= steps - RING)
        def _():
            to_core(j).wait_send()
            to_x(j).wait_send()

        for hop in range(1, levels):
            to_z(j, hop).wait_send()

    loop(steps, drain)
    for hop in range(levels + 1):
        vector_hop(hop).wait_send()

    @pl.when(section == 0)
    def _():
        half_copies(1)[2].wait()


def reduce_parts(vector, lefts, rights, late):
    shards = lax.axis_size("dp")
    branch, output_low, upper_low, mixed = lefts
    attended, hidden, second_normed, normed = rights
    rows, width = branch.shape
    ups = hidden.shape[1] // width
    unit, levels = width // shards, shards // 4
    units = 1 + 2 * ups + 3
    steps, span = units * CUT, width // CUT
    anywhere = pl.BlockSpec(memory_space=pl.ANY)
    vmem = pl.BlockSpec(memory_space=pltpu.VMEM)
    return pl.pallas_call(
        reduce_kernel,
        out_shape=(
            jax.ShapeDtypeStruct((units, unit, width), F32),
            jax.ShapeDtypeStruct(vector.shape, F32),
            jax.ShapeDtypeStruct((SEQ, width), F32),
        ),
        in_specs=[vmem] + [anywhere] * 10 + [vmem] + [anywhere] * 5,
        out_specs=[vmem, vmem, anywhere],
        scratch_shapes=[
            pltpu.VMEM((3 + ups, rows, width), LOW),
            pltpu.VMEM((2, rows, width), LOW),
            pltpu.VMEM((5 + ups, width, rows), LOW),
            pltpu.VMEM((RING, 2 * levels * unit, span), LOW),
            pltpu.VMEM((steps, 2 * levels * unit, span), LOW),
            pltpu.VMEM((RING, levels * unit, span), LOW),
            pltpu.VMEM((steps, levels * unit, span), LOW),
            pltpu.VMEM((steps, levels - 1, unit, span), LOW),
            pltpu.VMEM((steps, levels - 1, unit, span), LOW),
            pltpu.VMEM((levels, unit, span), F32),
            pltpu.VMEM((3,) + vector.shape, F32),
            pltpu.VMEM((levels + 1,) + vector.shape, F32),
            pltpu.SemaphoreType.DMA((3 + ups,)),
            pltpu.SemaphoreType.DMA((2,)),
            pltpu.SemaphoreType.DMA((2, steps)),
            pltpu.SemaphoreType.DMA((2, steps)),
            pltpu.SemaphoreType.DMA((2, steps, levels - 1)),
            pltpu.SemaphoreType.DMA((2, levels + 1)),
            pltpu.VMEM((SEQ, 3 * width), LOW),
            pltpu.VMEM((2, 2, SEQ, SEQ), LOW),
            pltpu.VMEM((2, 2, HEAD_DIM, SEQ), F32),
            pltpu.VMEM((HEADS, 8, SEQ), F32),
            pltpu.VMEM((SEQ, width), LOW),
            pltpu.VMEM((width, 3 * width), LOW),
            pltpu.VMEM((2, SEQ, SEQ), LOW),
            pltpu.VMEM((HALF, width), F32),
            pltpu.VMEM((HALF, width), LOW),
            pltpu.VMEM((HALF, width), F32),
            pltpu.VMEM((4, 8, width), F32),
            pltpu.SemaphoreType.DMA((4,)),
            pltpu.SemaphoreType.DMA((2, 2)),
            pltpu.SemaphoreType.DMA((3,)),
        ],
        name="reduce",
        compiler_params=pltpu.CompilerParams(
            collective_id=1, has_side_effects=True, vmem_limit_bytes=67043328
        ),
    )(vector, branch, output_low, upper_low, mixed, attended, hidden, second_normed, normed, *late)


def finish_kernel(
    whole_ref,
    total_hbm,
    result_hbm,
    input_grad_hbm,
    late_grad,
    result_out,
    input_grad_out,
    first_gain_out,
    first_shift_out,
    project_out,
    query_bias_out,
    value_bias_out,
    out_weight_out,
    out_bias_out,
    second_gain_out,
    second_shift_out,
    up_out,
    up_bias_out,
    down_out,
    down_bias_out,
    total,
    rows_low,
    rows_wide,
    in_sem,
    out_sem,
):
    units, unit, width = total.shape
    ups = down_out.shape[1] // width
    blocks = rows_low.shape[0]
    me = lax.axis_index("dp")
    shards = lax.axis_size("dp")
    section = lax.axis_index("section")
    first_up, first_mixed = 1 + ups, 1 + 2 * ups
    take = pltpu.make_async_copy(total_hbm, total, in_sem.at[2 * blocks])
    take.start()

    def block_of(ref, block):
        size = rows_low.shape[1]
        return ref.at[pl.ds(block * size, size)]

    pairs = []
    for block in range(blocks):
        for index, (source, middle, target) in enumerate(
            ((result_hbm, rows_low, result_out), (input_grad_hbm, rows_wide, input_grad_out))
        ):
            slot = 2 * block + index
            load = pltpu.make_async_copy(block_of(source, block), middle.at[block], in_sem.at[slot])
            save = pltpu.make_async_copy(middle.at[block], block_of(target, block), out_sem.at[slot])
            pairs.append((load, save))
            if index == 1 and (block + 1) * rows_low.shape[1] <= SEQ:
                other = pltpu.make_async_copy(block_of(late_grad, block), middle.at[block], in_sem.at[slot])
                pl.when(section == 0)(other.start)
                pl.when(section != 0)(load.start)
            else:
                load.start()

    pieces = [(0, out_weight_out)]
    pieces += [(1 + block, down_out.at[:, pl.ds(block * width, width)]) for block in range(ups)]
    pieces += [(first_up + block, up_out.at[pl.ds(block * unit, unit)]) for block in range(ups)]
    pieces += [(first_mixed + block, project_out.at[pl.ds(block * unit, unit)]) for block in range(3)]
    take.wait()
    for index, (source, target) in enumerate(pieces):
        save = pltpu.make_async_copy(total.at[source], target, out_sem.at[2 * blocks + index])
        save.start()
        pieces[index] = save
    for load, save in pairs:
        load.wait()
        save.start()
    rolled = pltpu.roll(whole_ref[:8], lax.rem(shards - me, shards) * unit, 1)
    small_outs = (
        first_gain_out, first_shift_out, query_bias_out, value_bias_out,
        out_bias_out, second_gain_out, second_shift_out, down_bias_out,
    )
    for index, small in enumerate(small_outs):
        small[...] = rolled[index : index + 1, :unit]
    span = ups * unit
    inner = width // span
    wide_rolled = pltpu.roll(whole_ref[8:16], lax.rem(inner - lax.rem(me, inner), inner) * span, 1)
    mine = lax.broadcasted_iota(jnp.int32, (8, width), 0) == lax.div(me, inner)
    up_bias_out[...] = jnp.sum(jnp.where(mine, wide_rolled, 0.0), axis=0, keepdims=True)[:, :span]
    for _, save in pairs:
        save.wait()
    for save in pieces:
        save.wait()


def finish(whole, total, result, input_grad, late_grad, ups):
    units, unit, width = total.shape
    rows = result.shape[0]
    anywhere = pl.BlockSpec(memory_space=pl.ANY)
    vmem = pl.BlockSpec(memory_space=pltpu.VMEM)

    def wide(*shape):
        return jax.ShapeDtypeStruct(shape, F32)

    small, matrix = wide(1, unit), wide(unit, width)
    blocks = 4
    outs = pl.pallas_call(
        finish_kernel,
        out_shape=(
            jax.ShapeDtypeStruct(result.shape, LOW), wide(rows, width), small, small,
            wide(3 * unit, width), small, small, matrix, small, small, small,
            wide(ups * unit, width), wide(1, ups * unit), wide(unit, ups * width), small,
        ),
        in_specs=[vmem] + [anywhere] * 4,
        out_specs=[
            anywhere, anywhere, vmem, vmem, anywhere, vmem, vmem, anywhere,
            vmem, vmem, vmem, anywhere, vmem, anywhere, vmem,
        ],
        scratch_shapes=[
            pltpu.VMEM(total.shape, F32),
            pltpu.VMEM((blocks, rows // blocks, width), LOW),
            pltpu.VMEM((blocks, rows // blocks, width), F32),
            pltpu.SemaphoreType.DMA((2 * blocks + 1,)),
            pltpu.SemaphoreType.DMA((2 * blocks + units,)),
        ],
        name="finish",
        compiler_params=pltpu.CompilerParams(vmem_limit_bytes=67043328),
    )(whole, total, result, input_grad, late_grad)
    result, input_grad = outs[0][None], outs[1][None]
    turned = [outs[index].T[None] for index in (4, 7, 11, 13)]
    return (
        result, input_grad, outs[2], outs[3], turned[0], outs[5], outs[6], turned[1],
        outs[8], outs[9], outs[10], turned[2], outs[12], turned[3], outs[14],
    )


def contract_rows(left, right):
    return lax.dot_general(left, right, (((0,), (0,)), ((), ())), preferred_element_type=F32)


def scatter_parts(vector, lefts, rights):
    def reduce_rows(left, right):
        piece = lax.psum_scatter(contract_rows(left, right), "dp", scatter_dimension=0, tiled=True)
        return piece.T

    branch, output_low, upper_low, mixed = lefts
    attended, hidden, second_normed, normed = rights
    return (
        lax.psum(vector, "dp"),
        reduce_rows(mixed, normed),
        reduce_rows(branch, attended),
        reduce_rows(upper_low, second_normed),
        reduce_rows(output_low, hidden),
    )


def on_device(*arrays):
    shards = lax.axis_size("dp")
    me = lax.axis_index("dp")
    width = arrays[0].shape[1]
    aligned = shards % 4 == 0 and width % (16 * shards) == 0
    (
        result, input_grad, vector,
        normed, attended, second_normed, hidden, mixed, branch, upper_low, output_low,
        *late,
    ) = relay(arrays, aligned)
    lefts = (branch, output_low, upper_low, mixed)
    rights = (attended, hidden, second_normed, normed)
    if aligned:
        late = (arrays[0], arrays[6], arrays[4], *late)
        total, whole, late_grad = reduce_parts(vector, lefts, rights, late)
        return finish(whole, total, result, input_grad, late_grad, hidden.shape[1] // width)
    whole, project_grad, out_grad, up_grad, down_grad = scatter_parts(vector, lefts, rights)
    size = width // shards
    small = lax.dynamic_slice_in_dim(whole[:8], me * size, size, 1)
    up_size = hidden.shape[1] // shards
    up_small = lax.dynamic_slice_in_dim(whole[8:].reshape(1, -1), me * up_size, up_size, 1)
    return (
        result[None],
        input_grad[None],
        small[0:1],
        small[1:2],
        project_grad[None],
        small[2:3],
        small[3:4],
        out_grad[None],
        small[4:5],
        small[5:6],
        small[6:7],
        up_grad[None],
        up_small,
        down_grad[None],
        small[7:8],
    )


def solution(mesh):
    stack1 = P("section", None)
    stack2 = P("section", None, None)
    in_specs = (
        P("dp", None), P("dp", None), P("dp"), P("dp"),
        stack1, stack1, stack2, stack1, stack1, stack2, stack1,
        stack1, stack1, stack2, stack1, stack2, stack1,
    )
    row = P("section", "dp")
    matrix = P("section", None, "dp")
    rows = P("section", "dp", None)
    out_specs = (
        rows, rows, row, row, matrix, row, row, matrix, row, row, row, matrix, row, matrix, row,
    )
    return jax.shard_map(
        on_device, mesh=mesh, in_specs=in_specs, out_specs=out_specs, check_vma=False
    )
```

```python
import functools

import jax
import jax.numpy as jnp
from jax import lax
from jax.experimental import pallas as pl
from jax.experimental.pallas import tpu as pltpu
from jax.sharding import PartitionSpec as P

HEADS = 12
HEAD_DIM = 64
SEQ = 512
PAIR = 2 * HEAD_DIM
PAIRS = HEADS // 2
TILE = 256
WIDE = 3072
HALF = 256
UP_WIDE = 1536
CUT = 2
RING = 6
LATE = 16
LAG = 3
ROWS = 128
EPSILON = 1e-06
SCORE_SCALE = 0.125
FAR = -1e30
F32 = jnp.float32
LOW = jnp.bfloat16
MESH = pl.DeviceIdType.MESH


def times(left, right):
    return lax.dot_general(left, right, (((1,), (0,)), ((), ())), preferred_element_type=F32)


def times_t(left, right):
    return lax.dot_general(left, right, (((1,), (1,)), ((), ())), preferred_element_type=F32)


def loop(count, body):
    def step(index, carry):
        body(index)
        return carry

    lax.fori_loop(0, count, step, 0)


def part(index, size):
    return pl.ds(pl.multiple_of(index * size, size), size)


def norm_rows(values):
    average = jnp.mean(values, axis=-1, keepdims=True)
    centred = values - average
    inv_scale = lax.rsqrt(jnp.mean(centred * centred, axis=-1, keepdims=True) + EPSILON)
    return centred * inv_scale, inv_scale


def norm_back(normed_grad, whitened, inv_scale, gain):
    scaled = normed_grad * gain
    return inv_scale * (
        scaled
        - jnp.mean(scaled, axis=-1, keepdims=True)
        - whitened * jnp.mean(scaled * whitened, axis=-1, keepdims=True)
    )


def fold_rows(values):
    rows, width = values.shape
    return jnp.sum(values.reshape(rows // 8, 8, width), axis=0)


def fill_bias(code_row, bias):
    across = jnp.transpose(jnp.broadcast_to(code_row, (128, SEQ)))
    for block in range(SEQ // 128):
        lanes = slice(block * 128, (block + 1) * 128)
        bias[:, lanes] = jnp.where(across == code_row[:, lanes], 0.0, FAR)


def gelu_both(upper):
    cumulative = 0.5 * (1.0 + lax.erf(upper * (0.5**0.5)))
    density = jnp.exp2((upper * upper) * -0.7213475204444817) * 0.3989422804014327
    return upper * cumulative, cumulative + upper * density


def relay_kernel(
    defer,
    x_hbm,
    cot_hbm,
    segment_ref,
    valid_ref,
    first_gain,
    first_shift,
    project_hbm,
    query_bias,
    value_bias,
    out_hbm,
    out_bias,
    second_gain,
    second_shift,
    up_hbm,
    up_bias,
    down_hbm,
    down_bias,
    result_hbm,
    input_grad_hbm,
    vector_ref,
    normed_hbm,
    attended_hbm,
    second_hbm,
    hidden_hbm,
    mixed_hbm,
    branch_hbm,
    upper_hbm,
    output_hbm,
    late_exponents,
    late_outputs,
    late_inverse,
    late_upstream,
    late_middle,
    project,
    out_weight,
    up_weight,
    down_weight,
    x_in,
    g_in,
    normed,
    mixed,
    attended,
    middle,
    second_normed,
    hidden,
    slope,
    result,
    wide,
    grad_low,
    bias,
    inv_sums,
    score_buf,
    score_low,
    exponents,
    outputs_across,
    sums,
    up_sums,
    weight_sem,
    x_sem,
    g_sem,
    send_sem,
    out_sem,
    late_sem,
):
    section = lax.axis_index("section")
    width = x_in.shape[2]
    hidden_width = hidden.shape[1]
    packs = x_in.shape[0]
    last = lax.axis_size("section") - 1
    partner = {"section": 1 - section}
    branch, attended_low, input_grad = normed, attended, wide

    def rows_of(ref, pack):
        return ref.at[pl.ds(pl.multiple_of(pack * SEQ, SEQ), SEQ)]

    def half_of(half):
        return pl.ds(pl.multiple_of(half * HALF, HALF), HALF)

    def local_rows(source, target, sems, pack, half):
        there = pl.ds(pl.multiple_of(pack * SEQ + half * HALF, HALF), HALF)
        return pltpu.make_async_copy(source.at[there], target.at[pack, half_of(half)], sems.at[pack, half])

    def local_x(pack, half):
        return local_rows(x_hbm, x_in, x_sem, pack, half)

    def local_g(pack, half):
        return local_rows(cot_hbm, g_in, g_sem, pack, half)

    weights = (
        pltpu.make_async_copy(project_hbm.at[0], project, weight_sem.at[0]),
        pltpu.make_async_copy(out_hbm.at[0], out_weight, weight_sem.at[1]),
        pltpu.make_async_copy(up_hbm.at[0], up_weight, weight_sem.at[2]),
        pltpu.make_async_copy(down_hbm.at[0], down_weight, weight_sem.at[3]),
    )

    @pl.when(section == 0)
    def _():
        for pack in range(packs):
            for half in range(2):
                local_x(pack, half).start()

    weights[0].start()

    @pl.when(section == last)
    def _():
        for pack in range(packs):
            for half in range(2):
                local_g(pack, half).start()

    barrier = pltpu.get_barrier_semaphore()
    pl.semaphore_signal(barrier, inc=1, device_id=partner, device_id_type=MESH)
    pl.semaphore_wait(barrier, 1)

    sums[...] = jnp.zeros_like(sums)
    up_sums[...] = jnp.zeros_like(up_sums)

    def hop(way, source, target, sems, pack, half):
        rows = half_of(half)
        return pltpu.make_async_remote_copy(
            src_ref=source.at[rows],
            dst_ref=target.at[pack, rows],
            send_sem=send_sem.at[way, pack, half],
            recv_sem=sems.at[pack, half],
            device_id=partner,
            device_id_type=MESH,
        )

    def hop_forward(pack, half):
        return hop(0, result, x_in, x_sem, pack, half)

    def hop_backward(pack, half):
        return hop(1, grad_low, g_in, g_sem, pack, half)

    kept = (
        (result, result_hbm),
        (normed, normed_hbm),
        (attended, attended_hbm),
        (second_normed, second_hbm),
        (hidden, hidden_hbm),
        (mixed, mixed_hbm),
        (branch, branch_hbm),
        (slope, upper_hbm),
        (g_in, output_hbm),
        (input_grad, input_grad_hbm),
    )

    def store(index, pack):
        source, target = kept[index]
        source = source if len(source.shape) == 2 else source.at[pack]
        return pltpu.make_async_copy(source, rows_of(target, pack), out_sem.at[index, pack])

    lane = lax.broadcasted_iota(jnp.int32, (SEQ, PAIR), 1)

    def heads_of(pack, pair):
        start = pl.multiple_of(pair * PAIR, PAIR)
        return [mixed[pack, :, pl.ds(third * width + start, PAIR)] for third in range(3)]

    late = (
        pltpu.make_async_copy(exponents.at[0], late_exponents, late_sem.at[0]),
        pltpu.make_async_copy(outputs_across.at[0], late_outputs, late_sem.at[1]),
        pltpu.make_async_copy(inv_sums.at[0], late_inverse, late_sem.at[2]),
        pltpu.make_async_copy(attended_low, late_upstream, late_sem.at[3]),
        pltpu.make_async_copy(middle.at[0], late_middle, late_sem.at[4]),
    )

    def forward(pack):
        first = pack == 0

        gain = first_gain[...].astype(F32)
        shift = first_shift[...].astype(F32)

        @pl.when(pack > 0)
        def _():
            store(1, pack - 1).wait()

        places = lax.broadcasted_iota(jnp.int32, (1, SEQ), 1) + SEQ
        fill_bias(jnp.where(valid_ref[pack] == 1, segment_ref[pack], places).astype(F32), bias)

        @pl.when(first)
        def _():
            weights[0].wait()
            for copy in weights[1:]:
                copy.start()

        def project_half(half):
            @pl.when(section == 0)
            def _():
                local_x(pack, half).wait()

            @pl.when(section == last)
            def _():
                hop_forward(pack, half).wait_recv()

            def norm_step(block):
                rows = pl.ds(pl.multiple_of(half * HALF + block * ROWS, ROWS), ROWS)
                white, _ = norm_rows(x_in[pack, rows].astype(F32))
                normed[rows] = (white * gain + shift).astype(LOW)

            loop(HALF // ROWS, norm_step)
            rows = half_of(half)
            for third, offset_ref in enumerate((query_bias, None, value_bias)):
                there = slice(third * width, (third + 1) * width)
                value = times(normed[rows], project[:, there])
                if offset_ref is not None:
                    value = value + offset_ref[...].astype(F32)
                mixed[pack, rows, there] = value.astype(LOW)

        loop(2, project_half)
        store(1, pack).start()

        def scores_of(pair, slot):
            query, key, _ = heads_of(pack, pair)
            for side in range(2):
                own = (lane < HEAD_DIM) == (side == 0)
                one = jnp.where(own, query * SCORE_SCALE, 0.0).astype(LOW)
                score_buf[slot, side] = times_t(key, one) + bias[...]

        def attend(pair, slot):
            value_across = jnp.transpose(heads_of(pack, pair)[2])
            ones = jnp.ones((16, SEQ), LOW)
            outs = []
            for side in range(2):
                heads = slice(side * HEAD_DIM, (side + 1) * HEAD_DIM)
                scores = score_buf[slot, side]
                key_max = jnp.max(scores, axis=0, keepdims=True)
                exponent = jnp.exp(scores - key_max).astype(LOW)
                exponents[pack, 2 * pair + side] = exponent
                sums_too = times(jnp.concatenate([value_across[heads], ones], axis=0), exponent)
                inverse = 1.0 / sums_too[HEAD_DIM : HEAD_DIM + 1]
                inv_sums[pack, 2 * pair + side] = jnp.broadcast_to(inverse, (8, SEQ))
                outs.append(sums_too[:HEAD_DIM] * inverse)
                outputs_across[pack, 2 * pair + side] = outs[side]
            attended[:, part(pair, PAIR)] = jnp.transpose(jnp.concatenate(outs, axis=0)).astype(LOW)

        @pl.when(pack > 0)
        def _():
            store(2, pack - 1).wait()

        scores_of(0, 0)

        def attend_step(index):
            for slot in range(2):
                pair = 2 * index + slot
                scores_of(jnp.minimum(pair + 1, PAIRS - 1), 1 - slot)
                attend(pair, slot)

        loop(PAIRS // 2, attend_step)
        store(2, pack).start()

        @pl.when(first)
        def _():
            weights[1].wait()

        middle[pack] = x_in[pack].astype(F32) + (
            times(attended[...], out_weight[...]) + out_bias[...].astype(F32)
        )
        gain2 = second_gain[...].astype(F32)
        shift2 = second_shift[...].astype(F32)

        @pl.when(pack > 0)
        def _():
            store(3, pack - 1).wait()
            store(4, pack - 1).wait()
            store(0, pack - 1).wait()

        @pl.when(first)
        def _():
            weights[2].wait()
            weights[3].wait()

        def feed_half(half):
            def second_step(block):
                rows = pl.ds(pl.multiple_of(half * HALF + block * ROWS, ROWS), ROWS)
                white, _ = norm_rows(middle[pack, rows])
                second_normed[rows] = (white * gain2 + shift2).astype(LOW)

            loop(HALF // ROWS, second_step)
            rows = half_of(half)

            def up_step(tile):
                here = part(tile, UP_WIDE)
                upper = times(second_normed[rows], up_weight[:, here]) + up_bias[:, here].astype(F32)
                act, act_slope = gelu_both(upper)
                hidden[rows, here] = act.astype(LOW)
                slope[pack, rows, here] = act_slope.astype(LOW)

            loop(hidden_width // UP_WIDE, up_step)

            @pl.when((pack > 0) & (section == 0))
            def _():
                hop_forward(pack - 1, half).wait_send()

            value = middle[pack, rows] + (times(hidden[rows], down_weight[...]) + down_bias[...].astype(F32))
            result[rows] = value.astype(LOW)

            @pl.when(section == 0)
            def _():
                hop_forward(pack, half).start()

        loop(2, feed_half)
        store(3, pack).start()
        store(4, pack).start()
        store(0, pack).start()

    def backward(order):
        pack = packs - 1 - order

        def hidden_half(half):
            @pl.when(section == last)
            def _():
                local_g(pack, half).wait()

            @pl.when(section == 0)
            def _():
                hop_backward(pack, half).wait_recv()

            rows = half_of(half)
            sums[7] += fold_rows(g_in[pack, rows].astype(F32))

            def hidden_step(tile):
                here = part(tile, WIDE)
                value = times_t(g_in[pack, rows], down_weight[here]).astype(LOW).astype(F32)
                low = (value * slope[pack, rows, here].astype(F32)).astype(LOW)
                slope[pack, rows, here] = low
                up_sums[:, here] += fold_rows(low.astype(F32))

            loop(hidden_width // WIDE, hidden_step)

        loop(2, hidden_half)
        store(8, pack).start()
        store(7, pack).start()

        @pl.when(order > 0)
        def _():
            store(9, pack + 1).wait()
            store(6, pack + 1).wait()

        @pl.when(order == 0)
        def _():
            store(1, pack).wait()
            store(2, pack).wait()

        wide[...] = times_t(slope[pack], up_weight[...])
        gain2 = second_gain[...].astype(F32)

        def second_back(block):
            rows = part(block, ROWS)
            grad = wide[rows]
            white, scale = norm_rows(middle[pack, rows])
            total = g_in[pack, rows].astype(F32) + norm_back(grad, white, scale, gain2)
            sums[5] += fold_rows(grad * white)
            sums[6] += fold_rows(grad)
            middle[pack, rows] = total
            low = total.astype(LOW)
            branch[rows] = low
            sums[4] += fold_rows(low.astype(F32))

        loop(SEQ // ROWS, second_back)
        store(6, pack).start()

        attended_low[...] = times_t(branch[...], out_weight[...]).astype(LOW)

        def attend_back(pair):
            here = part(pair, PAIR)
            query, key, value = heads_of(pack, pair)
            key_across, up_across = jnp.transpose(key), jnp.transpose(attended_low[:, here])
            empty = jnp.zeros((HEAD_DIM, SEQ), LOW)
            query_across, value_across, key_grad = [], [], 0.0
            for side in range(2):
                head = 2 * pair + side
                heads = slice(side * HEAD_DIM, (side + 1) * HEAD_DIM)
                own = (lane < HEAD_DIM) == (side == 0)
                one_query = jnp.where(own, query * SCORE_SCALE, 0.0).astype(LOW)
                one_up = (up_across[heads].astype(F32) * inv_sums[pack, head, 0:1]).astype(LOW)
                inner = jnp.sum(one_up.astype(F32) * outputs_across[pack, head], axis=0, keepdims=True)
                soft_grad = times(value, jnp.concatenate([one_up, empty][:: 1 - 2 * side], axis=0))
                score_low[side] = (exponents[pack, head].astype(F32) * (soft_grad - inner)).astype(LOW)
                value_across.append(times_t(one_up, exponents[pack, head]))
                key_grad += times(score_low[side], one_query)
                query_across.append(times(key_across[heads], score_low[side]))
            query_grad = (jnp.transpose(jnp.concatenate(query_across, axis=0)) * SCORE_SCALE).astype(LOW)
            value_grad = jnp.transpose(jnp.concatenate(value_across, axis=0)).astype(LOW)
            sums[2, :, here] += fold_rows(query_grad.astype(F32))
            sums[3, :, here] += fold_rows(value_grad.astype(F32))
            for third, grad in enumerate((query_grad, key_grad.astype(LOW), value_grad)):
                start = pl.multiple_of(third * width + pair * PAIR, PAIR)
                mixed[pack, :, pl.ds(start, PAIR)] = grad

        def attend_all():
            loop(PAIRS, attend_back)
            store(5, pack).start()

        gain = first_gain[...].astype(F32)

        def first_half(half):
            rows = half_of(half)
            wide[rows] = times_t(mixed[pack, rows], project[...])

            @pl.when((order > 0) & (section == last))
            def _():
                hop_backward(pack + 1, half).wait_send()

            def first_back(block):
                rows = pl.ds(pl.multiple_of(half * HALF + block * ROWS, ROWS), ROWS)
                grad = wide[rows]
                white, scale = norm_rows(x_in[pack, rows].astype(F32))
                total = middle[pack, rows] + norm_back(grad, white, scale, gain)
                sums[0] += fold_rows(grad * white)
                sums[1] += fold_rows(grad)
                input_grad[rows] = total
                grad_low[rows] = total.astype(LOW)

            loop(HALF // ROWS, first_back)

            @pl.when(section == last)
            def _():
                hop_backward(pack, half).start()

        def first_all():
            loop(2, first_half)
            store(9, pack).start()

        if not defer:
            attend_all()
            first_all()
        else:
            put_off = (order == packs - 1) & (section == 0)

            @pl.when(put_off)
            def _():
                store(5, pack).start()
                for copy in late[3:]:
                    copy.start()

            @pl.when(jnp.logical_not(put_off))
            def _():
                attend_all()
                first_all()

    loop(packs, forward)
    if defer:

        @pl.when(section == 0)
        def _():
            for copy in late[:3]:
                copy.start()

    loop(packs, backward)

    count = sums.shape[0]
    vector_ref[count:] = jnp.zeros((vector_ref.shape[0] - count, width), F32)
    for index in range(count):
        vector_ref[index : index + 1] = jnp.sum(sums[index], axis=0, keepdims=True)
    for index in range(hidden_width // width):
        lanes = slice(index * width, (index + 1) * width)
        vector_ref[count + index : count + index + 1] = jnp.sum(up_sums[:, lanes], axis=0, keepdims=True)

    for index in (0, 3, 4):
        store(index, packs - 1).wait()
    store(6, 0).wait()
    if not defer:
        store(9, 0).wait()
    else:

        @pl.when(section == last)
        def _():
            store(9, 0).wait()

        @pl.when(section == 0)
        def _():
            for copy in late:
                copy.wait()

    for pack in range(packs):
        for index in (5, 7, 8):
            store(index, pack).wait()

    @pl.when(section == 0)
    def _():
        for half in range(2):
            hop_forward(packs - 1, half).wait_send()

    @pl.when(section == last)
    def _():
        for half in range(2):
            hop_backward(0, half).wait_send()


def relay(arrays, defer):
    inputs, cotangent, segments, valid_flags = arrays[:4]
    rows, width = inputs.shape
    hidden_width = arrays[13].shape[2]
    packs = rows // SEQ
    anywhere = pl.BlockSpec(memory_space=pl.ANY)
    vmem = pl.BlockSpec(memory_space=pltpu.VMEM)

    def low(columns):
        return jax.ShapeDtypeStruct((rows, columns), LOW)

    outs = (
        low(width),
        jax.ShapeDtypeStruct((rows, width), F32),
        jax.ShapeDtypeStruct((16, width), F32),
        low(width),
        low(width),
        low(width),
        low(hidden_width),
        low(3 * width),
        low(width),
        low(hidden_width),
        low(width),
        jax.ShapeDtypeStruct((HEADS, SEQ, SEQ), LOW),
        jax.ShapeDtypeStruct((HEADS, HEAD_DIM, SEQ), F32),
        jax.ShapeDtypeStruct((HEADS, 8, SEQ), F32),
        jax.ShapeDtypeStruct((SEQ, width), LOW),
        jax.ShapeDtypeStruct((SEQ, width), F32),
    )

    def held(columns, kind=LOW):
        return pltpu.VMEM((packs, SEQ, columns), kind)

    scratch = [
        pltpu.VMEM((width, 3 * width), LOW),
        pltpu.VMEM((width, width), LOW),
        pltpu.VMEM((width, hidden_width), LOW),
        pltpu.VMEM((hidden_width, width), LOW),
        held(width),
        held(width),
        pltpu.VMEM((SEQ, width), LOW),
        held(3 * width),
        pltpu.VMEM((SEQ, width), LOW),
        held(width, F32),
        pltpu.VMEM((SEQ, width), LOW),
        pltpu.VMEM((SEQ, hidden_width), LOW),
        held(hidden_width),
        pltpu.VMEM((SEQ, width), LOW),
        pltpu.VMEM((SEQ, width), F32),
        pltpu.VMEM((SEQ, width), LOW),
        pltpu.VMEM((SEQ, SEQ), F32),
        pltpu.VMEM((packs, HEADS, 8, SEQ), F32),
        pltpu.VMEM((2, 2, SEQ, SEQ), F32),
        pltpu.VMEM((2, SEQ, SEQ), LOW),
        pltpu.VMEM((packs, HEADS, SEQ, SEQ), LOW),
        pltpu.VMEM((packs, HEADS, HEAD_DIM, SEQ), F32),
        pltpu.VMEM((8, 8, width), F32),
        pltpu.VMEM((8, hidden_width), F32),
        pltpu.SemaphoreType.DMA((4,)),
        pltpu.SemaphoreType.DMA((packs, 2)),
        pltpu.SemaphoreType.DMA((packs, 2)),
        pltpu.SemaphoreType.DMA((2, packs, 2)),
        pltpu.SemaphoreType.DMA((10, packs)),
        pltpu.SemaphoreType.DMA((5,)),
    ]
    return pl.pallas_call(
        functools.partial(relay_kernel, defer),
        out_shape=outs,
        in_specs=[
            anywhere, anywhere, vmem, vmem,
            vmem, vmem, anywhere, vmem, vmem, anywhere, vmem,
            vmem, vmem, anywhere, vmem, anywhere, vmem,
        ],
        out_specs=[anywhere, anywhere, vmem] + [anywhere] * 13,
        scratch_shapes=scratch,
        name="relay",
        compiler_params=pltpu.CompilerParams(
            collective_id=0, has_side_effects=True, vmem_limit_bytes=67043328
        ),
    )(
        inputs,
        cotangent,
        segments.reshape(packs, 1, SEQ),
        valid_flags.reshape(packs, 1, SEQ),
        *arrays[4:],
    )


def reduce_kernel(
    vector_ref,
    branch_hbm,
    output_hbm,
    upper_hbm,
    mixed_hbm,
    attended_hbm,
    hidden_hbm,
    second_hbm,
    normed_hbm,
    x_hbm,
    project_hbm,
    first_gain,
    late_exponents,
    late_outputs,
    late_inverse,
    late_upstream,
    late_middle,
    total_ref,
    whole_ref,
    late_grad,
    rights,
    loaded,
    lefts,
    send_core,
    take_core,
    send_x,
    take_x,
    send_z,
    take_z,
    own,
    vectors,
    take_vector,
    right_sem,
    load_sem,
    core_sems,
    x_sems,
    z_sems,
    vector_sems,
    mixed,
    exponents,
    outputs_across,
    inverse,
    upstream,
    project,
    score_low,
    middle,
    x_in,
    wide,
    sums,
    late_sems,
    pair_sems,
    half_sems,
):
    units, unit, width = total_ref.shape
    rows = rights.shape[1]
    shards = lax.axis_size("dp")
    levels = shards // 4
    ups = upper_hbm.shape[1] // width
    me = lax.axis_index("dp")
    core, x, z = me % 2, (me // 2) % 2, me // 4
    sibling = {"dp": me + 1 - 2 * core}
    across = {"dp": me + 2 - 4 * x}

    def level_peer(step):
        return {"dp": ((z + step) % levels) * 4 + x * 2 + core}

    first_up = 1 + ups
    first_mixed = first_up + ups

    sources = (
        [attended_hbm]
        + [hidden_hbm.at[:, pl.ds(block * width, width)] for block in range(ups)]
        + [second_hbm, normed_hbm]
    )

    def right_copy(index):
        return pltpu.make_async_copy(sources[index], rights.at[index], right_sem.at[index])

    chunks = [(branch_hbm, 0), (output_hbm, 0)]
    chunks += [(upper_hbm, block) for block in range(ups)]
    chunks += [(mixed_hbm, block) for block in range(3)]

    def left_copy(index):
        source, block = chunks[index]
        columns = pl.ds(block * width, width)
        if index >= 2 + ups:
            behind = pl.ds(SEQ, rows - SEQ)
            return pltpu.make_async_copy(
                source.at[behind, columns], loaded.at[index % 2, behind], load_sem.at[index % 2]
            )
        return pltpu.make_async_copy(source.at[:, columns], loaded.at[index % 2], load_sem.at[index % 2])

    left_copy(0).start()
    right_copy(0).start()
    left_copy(1).start()

    barrier = pltpu.get_barrier_semaphore()
    peers = [sibling, across] + [level_peer(step) for step in range(1, levels)]
    for peer in peers:
        pl.semaphore_signal(barrier, inc=1, device_id=peer, device_id_type=MESH)

    def send(source, target, sems, index, peer):
        return pltpu.make_async_remote_copy(
            src_ref=source,
            dst_ref=target,
            send_sem=sems.at[(0,) + index],
            recv_sem=sems.at[(1,) + index],
            device_id=peer,
            device_id_type=MESH,
        )

    def to_core(j):
        return send(send_core.at[lax.rem(j, RING)], take_core.at[j], core_sems, (j,), sibling)

    def to_x(j):
        return send(send_x.at[lax.rem(j, RING)], take_x.at[j], x_sems, (j,), across)

    def to_z(j, step):
        return send(send_z.at[j, step - 1], take_z.at[j, step - 1], z_sems, (j, step - 1), level_peer(step))

    def vector_hop(index):
        peer = (sibling, across)[index] if index < 2 else level_peer(index - 1)
        return send(vectors.at[min(index, 2)], take_vector.at[index], vector_sems, (index,), peer)

    def turn(index, group, first_left):
        left_copy(index).wait()
        block = chunks[index][1]
        source = loaded.at[index % 2]
        pieces = unit // 16

        def step(lane_block):
            here = part(lane_block, 128)
            if index >= 2 + ups:
                there = pl.ds(pl.multiple_of(block * width + lane_block * 128, 128), 128)
                turned = jnp.concatenate(
                    [jnp.transpose(mixed[:, there]), jnp.transpose(source[SEQ:, here])], axis=1
                )
            else:
                turned = jnp.transpose(source[:, here])
            for piece in range(8):
                place = block * (width // 16) + lane_block * 8 + piece
                shard, inner = lax.div(place, group), lax.rem(place, group)
                order = (
                    2 * levels * (1 - lax.rem(shard + core, 2))
                    + levels * (1 - lax.rem(lax.div(shard, 2) + x, 2))
                    + lax.div(shard, 4)
                )
                row = pl.multiple_of(order * unit + lax.rem(inner, pieces) * 16, 16)
                lefts[first_left + lax.div(inner, pieces), pl.ds(row, 16)] = turned[piece * 16 : (piece + 1) * 16]

        loop(width // 128, step)
        if index + 2 < len(chunks):
            left_copy(index + 2).start()

    half = 2 * levels * unit
    quarter = levels * unit

    span = width // CUT
    steps = units * CUT

    def left_of(u):
        return jnp.maximum(jnp.minimum(u, 1), u + 1 - ups)

    def right_of(u):
        return jnp.minimum(u, first_up) + jnp.where(u >= first_mixed, 1, 0)

    def product(j, start, count):
        u = lax.div(j, CUT)
        return times(lefts[left_of(u), start : start + count], rights[right_of(u), :, part(lax.rem(j, CUT), span)])

    def stage_core(j):
        @pl.when(j >= RING)
        def _():
            to_core(j - RING).wait_send()

        send_core[lax.rem(j, RING)] = product(j, 0, half).astype(LOW)
        to_core(j).start()

    def stage_x(j):
        to_core(j).wait_recv()
        value = product(j, half, quarter) + take_core[j, :quarter].astype(F32)

        @pl.when(j >= RING)
        def _():
            to_x(j - RING).wait_send()

        send_x[lax.rem(j, RING)] = value.astype(LOW)
        to_x(j).start()

    def stage_z(j):
        to_x(j).wait_recv()
        value = product(j, half + quarter, quarter) + take_core[j, quarter:].astype(F32) + take_x[j].astype(F32)
        own[...] = value.reshape(levels, unit, span)
        for hop in range(1, levels):
            send_z[j, hop - 1] = own[(z + hop) % levels].astype(LOW)
            to_z(j, hop).start()
        total_ref[lax.div(j, CUT), :, part(lax.rem(j, CUT), span)] = own[z]

    def finish(j):
        u, here = lax.div(j, CUT), part(lax.rem(j, CUT), span)
        value = total_ref[u, :, here]
        for hop in range(1, levels):
            to_z(j, hop).wait_recv()
            value = value + take_z[j, hop - 1].astype(F32)
        total_ref[u, :, here] = value

    def feed(j):
        @pl.when(j == 1)
        def _():
            turn(1, unit // 16, 1)
            for index in range(1 + ups, 3 + ups):
                right_copy(index).start()

        for block in range(ups):

            @pl.when(j == CUT * block + 2)
            def _(block=block):
                turn(2 + block, ups * unit // 16, 2)

        for block in range(3):

            @pl.when(j == CUT * first_mixed - 4 + block)
            def _(block=block):
                turn(2 + ups + block, 3 * unit // 16, 2 + ups)

    def need_right(j):
        for index, when in [(block, block) for block in range(1, 1 + ups)] + [
            (1 + ups, first_up),
            (2 + ups, first_mixed),
        ]:

            @pl.when(j == CUT * when)
            def _(index=index):
                right_copy(index).wait()

    turn(0, unit // 16, 0)
    for index in range(1, 1 + ups):
        right_copy(index).start()
    right_copy(0).wait()
    pl.semaphore_wait(barrier, len(peers))

    def pair_copies(pair, slot):
        heads = pl.ds(pair * 2, 2)
        return (
            pltpu.make_async_copy(late_exponents.at[heads], exponents.at[slot], pair_sems.at[0, slot]),
            pltpu.make_async_copy(late_outputs.at[heads], outputs_across.at[slot], pair_sems.at[1, slot]),
        )

    def half_copies(half):
        half_rows = pl.ds(pl.multiple_of(half * HALF, HALF), HALF)
        return (
            pltpu.make_async_copy(late_middle.at[half_rows], middle, half_sems.at[0]),
            pltpu.make_async_copy(x_hbm.at[half_rows], x_in, half_sems.at[1]),
            pltpu.make_async_copy(wide, late_grad.at[half_rows], half_sems.at[2]),
        )

    late_loads = (
        pltpu.make_async_copy(late_inverse, inverse, late_sems.at[1]),
        pltpu.make_async_copy(late_upstream, upstream, late_sems.at[2]),
        pltpu.make_async_copy(project_hbm.at[0], project, late_sems.at[3]),
    )
    mixed_load = pltpu.make_async_copy(mixed_hbm.at[pl.ds(0, SEQ)], mixed, late_sems.at[0])
    mixed_load.start()
    sums[...] = jnp.zeros_like(sums)
    lane = lax.broadcasted_iota(jnp.int32, (SEQ, PAIR), 1)
    section = lax.axis_index("section")

    @pl.when(section == 0)
    def _():
        for copy in late_loads:
            copy.start()
        for copy in pair_copies(0, 0) + half_copies(0)[:2]:
            copy.start()

    def attend_late(pair):
        slot = lax.rem(pair, 2)
        for copy in pair_copies(pair, slot):
            copy.wait()

        @pl.when(pair < PAIRS - 1)
        def _():
            for copy in pair_copies(pair + 1, 1 - slot):
                copy.start()

        here = part(pair, PAIR)
        places = [pl.ds(pl.multiple_of(third * width + pair * PAIR, PAIR), PAIR) for third in range(3)]
        query, key, value = [mixed[:, place] for place in places]
        key_across, up_across = jnp.transpose(key), jnp.transpose(upstream[:, here])
        empty = jnp.zeros((HEAD_DIM, SEQ), LOW)
        query_across, value_across, key_grad = [], [], 0.0
        for side in range(2):
            heads = slice(side * HEAD_DIM, (side + 1) * HEAD_DIM)
            own_lanes = (lane < HEAD_DIM) == (side == 0)
            one_query = jnp.where(own_lanes, query * SCORE_SCALE, 0.0).astype(LOW)
            one_up = (up_across[heads].astype(F32) * inverse[2 * pair + side, 0:1]).astype(LOW)
            inner = jnp.sum(one_up.astype(F32) * outputs_across[slot, side], axis=0, keepdims=True)
            soft_grad = times(value, jnp.concatenate([one_up, empty][:: 1 - 2 * side], axis=0))
            score_low[side] = (exponents[slot, side].astype(F32) * (soft_grad - inner)).astype(LOW)
            value_across.append(times_t(one_up, exponents[slot, side]))
            key_grad += times(score_low[side], one_query)
            query_across.append(times(key_across[heads], score_low[side]))
        query_grad = (jnp.transpose(jnp.concatenate(query_across, axis=0)) * SCORE_SCALE).astype(LOW)
        value_grad = jnp.transpose(jnp.concatenate(value_across, axis=0)).astype(LOW)
        sums[2, :, here] += fold_rows(query_grad.astype(F32))
        sums[3, :, here] += fold_rows(value_grad.astype(F32))
        for place, grad in zip(places, (query_grad, key_grad.astype(LOW), value_grad)):
            mixed[:, place] = grad

    def first_late(half):
        loads = half_copies(half)
        for copy in loads[:2]:
            copy.wait()

        @pl.when(half > 0)
        def _():
            half_copies(half - 1)[2].wait()

        wide[...] = times_t(mixed[pl.ds(pl.multiple_of(half * HALF, HALF), HALF)], project[...])
        gain = first_gain[...].astype(F32)

        def back(block):
            some = part(block, ROWS)
            grad = wide[some]
            white, scale = norm_rows(x_in[some].astype(F32))
            sums[0] += fold_rows(grad * white)
            sums[1] += fold_rows(grad)
            wide[some] = middle[some] + norm_back(grad, white, scale, gain)

        loop(HALF // ROWS, back)
        loads[2].start()

        @pl.when(half == 0)
        def _():
            for copy in half_copies(1)[:2]:
                copy.start()

    def late(j):
        pair = lax.div(j - 3, 2)

        @pl.when(j == 3)
        def _():
            mixed_load.wait()

        @pl.when((section == 0) & (j == 3))
        def _():
            for copy in late_loads:
                copy.wait()

        @pl.when((section == 0) & (j >= 3) & (j < 3 + 2 * PAIRS) & (lax.rem(j, 2) == 1))
        def _():
            attend_late(pair)

        @pl.when((section == 0) & (j >= LATE) & (j < LATE + 2))
        def _():
            first_late(j - LATE)

    def advance(j):
        feed(j)

        @pl.when((j >= 1) & (j < steps + 1))
        def _():
            stage_x(j - 1)

        need_right(j)

        @pl.when(j < steps)
        def _():
            stage_core(j)

        @pl.when((j >= LAG) & (j < steps + LAG))
        def _():
            stage_z(j - LAG)

        @pl.when(j >= 2 * LAG)
        def _():
            finish(j - 2 * LAG)

        late(j)

        @pl.when(j == LATE + 2)
        def _():
            vectors[0] = vector_ref[...]
            for index in range(4):
                vectors[0, index : index + 1] += jnp.sum(sums[index], axis=0, keepdims=True)
            vector_hop(0).start()

        @pl.when(j == LATE + 4)
        def _():
            vector_hop(0).wait_recv()
            vectors[1] = vectors[0] + take_vector[0]
            vector_hop(1).start()

        @pl.when(j == LATE + 6)
        def _():
            vector_hop(1).wait_recv()
            vectors[2] = vectors[1] + take_vector[1]
            for hop in range(1, levels):
                vector_hop(hop + 1).start()

    loop(steps + 2 * LAG, advance)
    whole = vectors[2]
    for hop in range(1, levels):
        vector_hop(hop + 1).wait_recv()
        whole = whole + take_vector[hop + 1]
    whole_ref[...] = whole

    def drain(j):
        @pl.when(j >= steps - RING)
        def _():
            to_core(j).wait_send()
            to_x(j).wait_send()

        for hop in range(1, levels):
            to_z(j, hop).wait_send()

    loop(steps, drain)
    for hop in range(levels + 1):
        vector_hop(hop).wait_send()

    @pl.when(section == 0)
    def _():
        half_copies(1)[2].wait()


def reduce_parts(vector, lefts, rights, late):
    shards = lax.axis_size("dp")
    branch, output_low, upper_low, mixed = lefts
    attended, hidden, second_normed, normed = rights
    rows, width = branch.shape
    ups = hidden.shape[1] // width
    unit, levels = width // shards, shards // 4
    units = 1 + 2 * ups + 3
    steps, span = units * CUT, width // CUT
    anywhere = pl.BlockSpec(memory_space=pl.ANY)
    vmem = pl.BlockSpec(memory_space=pltpu.VMEM)
    return pl.pallas_call(
        reduce_kernel,
        out_shape=(
            jax.ShapeDtypeStruct((units, unit, width), F32),
            jax.ShapeDtypeStruct(vector.shape, F32),
            jax.ShapeDtypeStruct((SEQ, width), F32),
        ),
        in_specs=[vmem] + [anywhere] * 10 + [vmem] + [anywhere] * 5,
        out_specs=[vmem, vmem, anywhere],
        scratch_shapes=[
            pltpu.VMEM((3 + ups, rows, width), LOW),
            pltpu.VMEM((2, rows, width), LOW),
            pltpu.VMEM((5 + ups, width, rows), LOW),
            pltpu.VMEM((RING, 2 * levels * unit, span), LOW),
            pltpu.VMEM((steps, 2 * levels * unit, span), LOW),
            pltpu.VMEM((RING, levels * unit, span), LOW),
            pltpu.VMEM((steps, levels * unit, span), LOW),
            pltpu.VMEM((steps, levels - 1, unit, span), LOW),
            pltpu.VMEM((steps, levels - 1, unit, span), LOW),
            pltpu.VMEM((levels, unit, span), F32),
            pltpu.VMEM((3,) + vector.shape, F32),
            pltpu.VMEM((levels + 1,) + vector.shape, F32),
            pltpu.SemaphoreType.DMA((3 + ups,)),
            pltpu.SemaphoreType.DMA((2,)),
            pltpu.SemaphoreType.DMA((2, steps)),
            pltpu.SemaphoreType.DMA((2, steps)),
            pltpu.SemaphoreType.DMA((2, steps, levels - 1)),
            pltpu.SemaphoreType.DMA((2, levels + 1)),
            pltpu.VMEM((SEQ, 3 * width), LOW),
            pltpu.VMEM((2, 2, SEQ, SEQ), LOW),
            pltpu.VMEM((2, 2, HEAD_DIM, SEQ), F32),
            pltpu.VMEM((HEADS, 8, SEQ), F32),
            pltpu.VMEM((SEQ, width), LOW),
            pltpu.VMEM((width, 3 * width), LOW),
            pltpu.VMEM((2, SEQ, SEQ), LOW),
            pltpu.VMEM((HALF, width), F32),
            pltpu.VMEM((HALF, width), LOW),
            pltpu.VMEM((HALF, width), F32),
            pltpu.VMEM((4, 8, width), F32),
            pltpu.SemaphoreType.DMA((4,)),
            pltpu.SemaphoreType.DMA((2, 2)),
            pltpu.SemaphoreType.DMA((3,)),
        ],
        name="reduce",
        compiler_params=pltpu.CompilerParams(
            collective_id=1, has_side_effects=True, vmem_limit_bytes=67043328
        ),
    )(vector, branch, output_low, upper_low, mixed, attended, hidden, second_normed, normed, *late)


def finish_kernel(
    whole_ref,
    total_hbm,
    result_hbm,
    input_grad_hbm,
    late_grad,
    result_out,
    input_grad_out,
    first_gain_out,
    first_shift_out,
    project_out,
    query_bias_out,
    value_bias_out,
    out_weight_out,
    out_bias_out,
    second_gain_out,
    second_shift_out,
    up_out,
    up_bias_out,
    down_out,
    down_bias_out,
    total,
    rows_low,
    rows_wide,
    in_sem,
    out_sem,
):
    units, unit, width = total.shape
    ups = down_out.shape[1] // width
    blocks = rows_low.shape[0]
    me = lax.axis_index("dp")
    shards = lax.axis_size("dp")
    section = lax.axis_index("section")
    first_up, first_mixed = 1 + ups, 1 + 2 * ups
    take = pltpu.make_async_copy(total_hbm, total, in_sem.at[2 * blocks])
    take.start()

    def block_of(ref, block):
        size = rows_low.shape[1]
        return ref.at[pl.ds(block * size, size)]

    pairs = []
    for block in range(blocks):
        for index, (source, middle, target) in enumerate(
            ((result_hbm, rows_low, result_out), (input_grad_hbm, rows_wide, input_grad_out))
        ):
            slot = 2 * block + index
            load = pltpu.make_async_copy(block_of(source, block), middle.at[block], in_sem.at[slot])
            save = pltpu.make_async_copy(middle.at[block], block_of(target, block), out_sem.at[slot])
            pairs.append((load, save))
            if index == 1 and (block + 1) * rows_low.shape[1] <= SEQ:
                other = pltpu.make_async_copy(block_of(late_grad, block), middle.at[block], in_sem.at[slot])
                pl.when(section == 0)(other.start)
                pl.when(section != 0)(load.start)
            else:
                load.start()

    pieces = [(0, out_weight_out)]
    pieces += [(1 + block, down_out.at[:, pl.ds(block * width, width)]) for block in range(ups)]
    pieces += [(first_up + block, up_out.at[pl.ds(block * unit, unit)]) for block in range(ups)]
    pieces += [(first_mixed + block, project_out.at[pl.ds(block * unit, unit)]) for block in range(3)]
    take.wait()
    for index, (source, target) in enumerate(pieces):
        save = pltpu.make_async_copy(total.at[source], target, out_sem.at[2 * blocks + index])
        save.start()
        pieces[index] = save
    for load, save in pairs:
        load.wait()
        save.start()
    rolled = pltpu.roll(whole_ref[:8], lax.rem(shards - me, shards) * unit, 1)
    small_outs = (
        first_gain_out, first_shift_out, query_bias_out, value_bias_out,
        out_bias_out, second_gain_out, second_shift_out, down_bias_out,
    )
    for index, small in enumerate(small_outs):
        small[...] = rolled[index : index + 1, :unit]
    span = ups * unit
    inner = width // span
    wide_rolled = pltpu.roll(whole_ref[8:16], lax.rem(inner - lax.rem(me, inner), inner) * span, 1)
    mine = lax.broadcasted_iota(jnp.int32, (8, width), 0) == lax.div(me, inner)
    up_bias_out[...] = jnp.sum(jnp.where(mine, wide_rolled, 0.0), axis=0, keepdims=True)[:, :span]
    for _, save in pairs:
        save.wait()
    for save in pieces:
        save.wait()


def finish(whole, total, result, input_grad, late_grad, ups):
    units, unit, width = total.shape
    rows = result.shape[0]
    anywhere = pl.BlockSpec(memory_space=pl.ANY)
    vmem = pl.BlockSpec(memory_space=pltpu.VMEM)

    def wide(*shape):
        return jax.ShapeDtypeStruct(shape, F32)

    small, matrix = wide(1, unit), wide(unit, width)
    blocks = 4
    outs = pl.pallas_call(
        finish_kernel,
        out_shape=(
            jax.ShapeDtypeStruct(result.shape, LOW), wide(rows, width), small, small,
            wide(3 * unit, width), small, small, matrix, small, small, small,
            wide(ups * unit, width), wide(1, ups * unit), wide(unit, ups * width), small,
        ),
        in_specs=[vmem] + [anywhere] * 4,
        out_specs=[
            anywhere, anywhere, vmem, vmem, anywhere, vmem, vmem, anywhere,
            vmem, vmem, vmem, anywhere, vmem, anywhere, vmem,
        ],
        scratch_shapes=[
            pltpu.VMEM(total.shape, F32),
            pltpu.VMEM((blocks, rows // blocks, width), LOW),
            pltpu.VMEM((blocks, rows // blocks, width), F32),
            pltpu.SemaphoreType.DMA((2 * blocks + 1,)),
            pltpu.SemaphoreType.DMA((2 * blocks + units,)),
        ],
        name="finish",
        compiler_params=pltpu.CompilerParams(vmem_limit_bytes=67043328),
    )(whole, total, result, input_grad, late_grad)
    result, input_grad = outs[0][None], outs[1][None]
    turned = [outs[index].T[None] for index in (4, 7, 11, 13)]
    return (
        result, input_grad, outs[2], outs[3], turned[0], outs[5], outs[6], turned[1],
        outs[8], outs[9], outs[10], turned[2], outs[12], turned[3], outs[14],
    )


def contract_rows(left, right):
    return lax.dot_general(left, right, (((0,), (0,)), ((), ())), preferred_element_type=F32)


def scatter_parts(vector, lefts, rights):
    def reduce_rows(left, right):
        piece = lax.psum_scatter(contract_rows(left, right), "dp", scatter_dimension=0, tiled=True)
        return piece.T

    branch, output_low, upper_low, mixed = lefts
    attended, hidden, second_normed, normed = rights
    return (
        lax.psum(vector, "dp"),
        reduce_rows(mixed, normed),
        reduce_rows(branch, attended),
        reduce_rows(upper_low, second_normed),
        reduce_rows(output_low, hidden),
    )


def on_device(*arrays):
    shards = lax.axis_size("dp")
    me = lax.axis_index("dp")
    width = arrays[0].shape[1]
    aligned = shards % 4 == 0 and width % (16 * shards) == 0
    (
        result, input_grad, vector,
        normed, attended, second_normed, hidden, mixed, branch, upper_low, output_low,
        *late,
    ) = relay(arrays, aligned)
    lefts = (branch, output_low, upper_low, mixed)
    rights = (attended, hidden, second_normed, normed)
    if aligned:
        late = (arrays[0], arrays[6], arrays[4], *late)
        total, whole, late_grad = reduce_parts(vector, lefts, rights, late)
        return finish(whole, total, result, input_grad, late_grad, hidden.shape[1] // width)
    whole, project_grad, out_grad, up_grad, down_grad = scatter_parts(vector, lefts, rights)
    size = width // shards
    small = lax.dynamic_slice_in_dim(whole[:8], me * size, size, 1)
    up_size = hidden.shape[1] // shards
    up_small = lax.dynamic_slice_in_dim(whole[8:].reshape(1, -1), me * up_size, up_size, 1)
    return (
        result[None],
        input_grad[None],
        small[0:1],
        small[1:2],
        project_grad[None],
        small[2:3],
        small[3:4],
        out_grad[None],
        small[4:5],
        small[5:6],
        small[6:7],
        up_grad[None],
        up_small,
        down_grad[None],
        small[7:8],
    )


def solution(mesh):
    stack1 = P("section", None)
    stack2 = P("section", None, None)
    in_specs = (
        P("dp", None), P("dp", None), P("dp"), P("dp"),
        stack1, stack1, stack2, stack1, stack1, stack2, stack1,
        stack1, stack1, stack2, stack1, stack2, stack1,
    )
    row = P("section", "dp")
    matrix = P("section", None, "dp")
    rows = P("section", "dp", None)
    out_specs = (
        rows, rows, row, row, matrix, row, row, matrix, row, row, row, matrix, row, matrix, row,
    )
    return jax.shard_map(
        on_device, mesh=mesh, in_specs=in_specs, out_specs=out_specs, check_vma=False
    )
```

```python
import functools

import jax
import jax.numpy as jnp
from jax import lax
from jax.experimental import pallas as pl
from jax.experimental.pallas import tpu as pltpu
from jax.sharding import PartitionSpec as P

HEADS = 12
HEAD_DIM = 64
SEQ = 512
PAIR = 2 * HEAD_DIM
PAIRS = HEADS // 2
TILE = 256
WIDE = 3072
HALF = 256
UP_WIDE = 1536
CUT = 2
RING = 6
LATE = 16
LAG = 3
ROWS = 128
EPSILON = 1e-06
SCORE_SCALE = 0.125
FAR = -1e30
F32 = jnp.float32
LOW = jnp.bfloat16
MESH = pl.DeviceIdType.MESH


def times(left, right):
    return lax.dot_general(left, right, (((1,), (0,)), ((), ())), preferred_element_type=F32)


def times_t(left, right):
    return lax.dot_general(left, right, (((1,), (1,)), ((), ())), preferred_element_type=F32)


def loop(count, body):
    def step(index, carry):
        body(index)
        return carry

    lax.fori_loop(0, count, step, 0)


def part(index, size):
    return pl.ds(pl.multiple_of(index * size, size), size)


def norm_rows(values):
    average = jnp.mean(values, axis=-1, keepdims=True)
    centred = values - average
    inv_scale = lax.rsqrt(jnp.mean(centred * centred, axis=-1, keepdims=True) + EPSILON)
    return centred * inv_scale, inv_scale


def norm_back(normed_grad, whitened, inv_scale, gain):
    scaled = normed_grad * gain
    return inv_scale * (
        scaled
        - jnp.mean(scaled, axis=-1, keepdims=True)
        - whitened * jnp.mean(scaled * whitened, axis=-1, keepdims=True)
    )


def fold_rows(values):
    rows, width = values.shape
    return jnp.sum(values.reshape(rows // 8, 8, width), axis=0)


def fill_bias(code_row, bias):
    across = jnp.transpose(jnp.broadcast_to(code_row, (128, SEQ)))
    for block in range(SEQ // 128):
        lanes = slice(block * 128, (block + 1) * 128)
        bias[:, lanes] = jnp.where(across == code_row[:, lanes], 0.0, FAR)


def gelu_both(upper):
    cumulative = 0.5 * (1.0 + lax.erf(upper * (0.5**0.5)))
    density = jnp.exp2((upper * upper) * -0.7213475204444817) * 0.3989422804014327
    return upper * cumulative, cumulative + upper * density


def relay_kernel(
    defer,
    x_hbm,
    cot_hbm,
    segment_ref,
    valid_ref,
    first_gain,
    first_shift,
    project_hbm,
    query_bias,
    value_bias,
    out_hbm,
    out_bias,
    second_gain,
    second_shift,
    up_hbm,
    up_bias,
    down_hbm,
    down_bias,
    result_hbm,
    input_grad_hbm,
    vector_ref,
    normed_hbm,
    attended_hbm,
    second_hbm,
    hidden_hbm,
    mixed_hbm,
    branch_hbm,
    upper_hbm,
    output_hbm,
    late_exponents,
    late_outputs,
    late_inverse,
    late_upstream,
    late_middle,
    project,
    out_weight,
    up_weight,
    down_weight,
    x_in,
    g_in,
    normed,
    mixed,
    attended,
    middle,
    second_normed,
    hidden,
    slope,
    result,
    wide,
    bias,
    inv_sums,
    score_buf,
    score_low,
    exponents,
    outputs_across,
    sums,
    up_sums,
    weight_sem,
    x_sem,
    g_sem,
    send_sem,
    out_sem,
    late_sem,
):
    section = lax.axis_index("section")
    width = x_in.shape[2]
    hidden_width = hidden.shape[1]
    packs = x_in.shape[0]
    last = lax.axis_size("section") - 1
    partner = {"section": 1 - section}
    branch, attended_low, input_grad, grad_low = normed, attended, wide, result

    def rows_of(ref, pack):
        return ref.at[pl.ds(pl.multiple_of(pack * SEQ, SEQ), SEQ)]

    def half_of(half):
        return pl.ds(pl.multiple_of(half * HALF, HALF), HALF)

    def local_rows(source, target, sems, pack, half):
        there = pl.ds(pl.multiple_of(pack * SEQ + half * HALF, HALF), HALF)
        return pltpu.make_async_copy(source.at[there], target.at[pack, half_of(half)], sems.at[pack, half])

    def local_x(pack, half):
        return local_rows(x_hbm, x_in, x_sem, pack, half)

    def local_g(pack, half):
        return local_rows(cot_hbm, g_in, g_sem, pack, half)

    weights = (
        pltpu.make_async_copy(project_hbm.at[0], project, weight_sem.at[0]),
        pltpu.make_async_copy(out_hbm.at[0], out_weight, weight_sem.at[1]),
        pltpu.make_async_copy(up_hbm.at[0], up_weight, weight_sem.at[2]),
        pltpu.make_async_copy(down_hbm.at[0], down_weight, weight_sem.at[3]),
    )

    @pl.when(section == 0)
    def _():
        for pack in range(packs):
            for half in range(2):
                local_x(pack, half).start()

    weights[0].start()

    @pl.when(section == last)
    def _():
        for pack in range(packs):
            for half in range(2):
                local_g(pack, half).start()

    barrier = pltpu.get_barrier_semaphore()
    pl.semaphore_signal(barrier, inc=1, device_id=partner, device_id_type=MESH)
    pl.semaphore_wait(barrier, 1)

    sums[...] = jnp.zeros_like(sums)
    up_sums[...] = jnp.zeros_like(up_sums)

    def hop(way, source, target, sems, pack, half):
        rows = half_of(half)
        return pltpu.make_async_remote_copy(
            src_ref=source.at[rows],
            dst_ref=target.at[pack, rows],
            send_sem=send_sem.at[way, pack, half],
            recv_sem=sems.at[pack, half],
            device_id=partner,
            device_id_type=MESH,
        )

    def hop_forward(pack, half):
        return hop(0, result, x_in, x_sem, pack, half)

    def hop_backward(pack, half):
        return hop(1, grad_low, g_in, g_sem, pack, half)

    kept = (
        (result, result_hbm),
        (normed, normed_hbm),
        (attended, attended_hbm),
        (second_normed, second_hbm),
        (hidden, hidden_hbm),
        (mixed, mixed_hbm),
        (branch, branch_hbm),
        (slope, upper_hbm),
        (g_in, output_hbm),
        (input_grad, input_grad_hbm),
    )

    def store(index, pack):
        source, target = kept[index]
        source = source if len(source.shape) == 2 else source.at[pack]
        return pltpu.make_async_copy(source, rows_of(target, pack), out_sem.at[index, pack])

    lane = lax.broadcasted_iota(jnp.int32, (SEQ, PAIR), 1)

    def heads_of(pack, pair):
        start = pl.multiple_of(pair * PAIR, PAIR)
        return [mixed[pack, :, pl.ds(third * width + start, PAIR)] for third in range(3)]

    late = (
        pltpu.make_async_copy(exponents.at[0], late_exponents, late_sem.at[0]),
        pltpu.make_async_copy(outputs_across.at[0], late_outputs, late_sem.at[1]),
        pltpu.make_async_copy(inv_sums.at[0], late_inverse, late_sem.at[2]),
        pltpu.make_async_copy(attended_low, late_upstream, late_sem.at[3]),
        pltpu.make_async_copy(middle.at[0], late_middle, late_sem.at[4]),
    )

    def forward(pack):
        first = pack == 0

        gain = first_gain[...].astype(F32)
        shift = first_shift[...].astype(F32)

        @pl.when(pack > 0)
        def _():
            store(1, pack - 1).wait()

        places = lax.broadcasted_iota(jnp.int32, (1, SEQ), 1) + SEQ
        fill_bias(jnp.where(valid_ref[pack] == 1, segment_ref[pack], places).astype(F32), bias)

        @pl.when(first)
        def _():
            weights[0].wait()
            for copy in weights[1:]:
                copy.start()

        def project_half(half):
            @pl.when(section == 0)
            def _():
                local_x(pack, half).wait()

            @pl.when(section == last)
            def _():
                hop_forward(pack, half).wait_recv()

            def norm_step(block):
                rows = pl.ds(pl.multiple_of(half * HALF + block * HALF, HALF), HALF)
                white, _ = norm_rows(x_in[pack, rows].astype(F32))
                normed[rows] = (white * gain + shift).astype(LOW)

            loop(HALF // HALF, norm_step)
            rows = half_of(half)
            for third, offset_ref in enumerate((query_bias, None, value_bias)):
                there = slice(third * width, (third + 1) * width)
                value = times(normed[rows], project[:, there])
                if offset_ref is not None:
                    value = value + offset_ref[...].astype(F32)
                mixed[pack, rows, there] = value.astype(LOW)

        loop(2, project_half)
        store(1, pack).start()

        def scores_of(pair, slot):
            query, key, _ = heads_of(pack, pair)
            for side in range(2):
                own = (lane < HEAD_DIM) == (side == 0)
                one = jnp.where(own, query * SCORE_SCALE, 0.0).astype(LOW)
                score_buf[slot, side] = times_t(key, one) + bias[...]

        def attend(pair, slot):
            value_across = jnp.transpose(heads_of(pack, pair)[2])
            ones = jnp.ones((16, SEQ), LOW)
            outs = []
            for side in range(2):
                heads = slice(side * HEAD_DIM, (side + 1) * HEAD_DIM)
                scores = score_buf[slot, side]
                key_max = jnp.max(scores, axis=0, keepdims=True)
                exponent = jnp.exp(scores - key_max).astype(LOW)
                exponents[pack, 2 * pair + side] = exponent
                sums_too = times(jnp.concatenate([value_across[heads], ones], axis=0), exponent)
                inverse = 1.0 / sums_too[HEAD_DIM : HEAD_DIM + 1]
                inv_sums[pack, 2 * pair + side] = jnp.broadcast_to(inverse, (8, SEQ))
                outs.append(sums_too[:HEAD_DIM] * inverse)
                outputs_across[pack, 2 * pair + side] = outs[side]
            attended[:, part(pair, PAIR)] = jnp.transpose(jnp.concatenate(outs, axis=0)).astype(LOW)

        @pl.when(pack > 0)
        def _():
            store(2, pack - 1).wait()

        scores_of(0, 0)

        def attend_step(index):
            for slot in range(2):
                pair = 2 * index + slot
                scores_of(jnp.minimum(pair + 1, PAIRS - 1), 1 - slot)
                attend(pair, slot)

        loop(PAIRS // 2, attend_step)
        store(2, pack).start()

        @pl.when(first)
        def _():
            weights[1].wait()

        middle[pack] = x_in[pack].astype(F32) + (
            times(attended[...], out_weight[...]) + out_bias[...].astype(F32)
        )
        gain2 = second_gain[...].astype(F32)
        shift2 = second_shift[...].astype(F32)

        @pl.when(pack > 0)
        def _():
            store(3, pack - 1).wait()
            store(4, pack - 1).wait()
            store(0, pack - 1).wait()

        @pl.when(first)
        def _():
            weights[2].wait()
            weights[3].wait()

        def feed_half(half):
            def second_step(block):
                rows = pl.ds(pl.multiple_of(half * HALF + block * HALF, HALF), HALF)
                white, _ = norm_rows(middle[pack, rows])
                second_normed[rows] = (white * gain2 + shift2).astype(LOW)

            loop(HALF // HALF, second_step)
            rows = half_of(half)

            def up_step(tile):
                here = part(tile, UP_WIDE)
                upper = times(second_normed[rows], up_weight[:, here]) + up_bias[:, here].astype(F32)
                act, act_slope = gelu_both(upper)
                hidden[rows, here] = act.astype(LOW)
                slope[pack, rows, here] = act_slope.astype(LOW)

            loop(hidden_width // UP_WIDE, up_step)

            @pl.when((pack > 0) & (section == 0))
            def _():
                hop_forward(pack - 1, half).wait_send()

            value = middle[pack, rows] + (times(hidden[rows], down_weight[...]) + down_bias[...].astype(F32))
            result[rows] = value.astype(LOW)

            @pl.when(section == 0)
            def _():
                hop_forward(pack, half).start()

        loop(2, feed_half)
        store(3, pack).start()
        store(4, pack).start()
        store(0, pack).start()

    def backward(order):
        pack = packs - 1 - order

        def hidden_half(half):
            @pl.when(section == last)
            def _():
                local_g(pack, half).wait()

            @pl.when(section == 0)
            def _():
                hop_backward(pack, half).wait_recv()

            rows = half_of(half)
            sums[7] += fold_rows(g_in[pack, rows].astype(F32))

            def hidden_step(tile):
                here = part(tile, WIDE)
                value = times_t(g_in[pack, rows], down_weight[here]).astype(LOW).astype(F32)
                low = (value * slope[pack, rows, here].astype(F32)).astype(LOW)
                slope[pack, rows, here] = low
                up_sums[:, here] += fold_rows(low.astype(F32))

            loop(hidden_width // WIDE, hidden_step)

        loop(2, hidden_half)
        store(8, pack).start()
        store(7, pack).start()

        @pl.when(order > 0)
        def _():
            store(9, pack + 1).wait()
            store(6, pack + 1).wait()

        @pl.when(order == 0)
        def _():
            store(0, pack).wait()
            store(1, pack).wait()
            store(2, pack).wait()

        @pl.when((order == 0) & (section == 0))
        def _():
            for half in range(2):
                hop_forward(pack, half).wait_send()

        wide[...] = times_t(slope[pack], up_weight[...])
        gain2 = second_gain[...].astype(F32)

        def second_back(block):
            rows = part(block, HALF)
            grad = wide[rows]
            white, scale = norm_rows(middle[pack, rows])
            total = g_in[pack, rows].astype(F32) + norm_back(grad, white, scale, gain2)
            sums[5] += fold_rows(grad * white)
            sums[6] += fold_rows(grad)
            middle[pack, rows] = total
            low = total.astype(LOW)
            branch[rows] = low
            sums[4] += fold_rows(low.astype(F32))

        loop(SEQ // HALF, second_back)
        store(6, pack).start()

        attended_low[...] = times_t(branch[...], out_weight[...]).astype(LOW)

        def attend_back(pair):
            here = part(pair, PAIR)
            query, key, value = heads_of(pack, pair)
            key_across, up_across = jnp.transpose(key), jnp.transpose(attended_low[:, here])
            empty = jnp.zeros((HEAD_DIM, SEQ), LOW)
            query_across, value_across, key_grad = [], [], 0.0
            for side in range(2):
                head = 2 * pair + side
                heads = slice(side * HEAD_DIM, (side + 1) * HEAD_DIM)
                own = (lane < HEAD_DIM) == (side == 0)
                one_query = jnp.where(own, query * SCORE_SCALE, 0.0).astype(LOW)
                one_up = (up_across[heads].astype(F32) * inv_sums[pack, head, 0:1]).astype(LOW)
                inner = jnp.sum(one_up.astype(F32) * outputs_across[pack, head], axis=0, keepdims=True)
                soft_grad = times(value, jnp.concatenate([one_up, empty][:: 1 - 2 * side], axis=0))
                score_low[side] = (exponents[pack, head].astype(F32) * (soft_grad - inner)).astype(LOW)
                value_across.append(times_t(one_up, exponents[pack, head]))
                key_grad += times(score_low[side], one_query)
                query_across.append(times(key_across[heads], score_low[side]))
            query_grad = (jnp.transpose(jnp.concatenate(query_across, axis=0)) * SCORE_SCALE).astype(LOW)
            value_grad = jnp.transpose(jnp.concatenate(value_across, axis=0)).astype(LOW)
            sums[2, :, here] += fold_rows(query_grad.astype(F32))
            sums[3, :, here] += fold_rows(value_grad.astype(F32))
            for third, grad in enumerate((query_grad, key_grad.astype(LOW), value_grad)):
                start = pl.multiple_of(third * width + pair * PAIR, PAIR)
                mixed[pack, :, pl.ds(start, PAIR)] = grad

        def attend_all():
            loop(PAIRS, attend_back)
            store(5, pack).start()

        gain = first_gain[...].astype(F32)

        def first_half(half):
            rows = half_of(half)
            wide[rows] = times_t(mixed[pack, rows], project[...])

            @pl.when((order > 0) & (section == last))
            def _():
                hop_backward(pack + 1, half).wait_send()

            def first_back(block):
                rows = pl.ds(pl.multiple_of(half * HALF + block * HALF, HALF), HALF)
                grad = wide[rows]
                white, scale = norm_rows(x_in[pack, rows].astype(F32))
                total = middle[pack, rows] + norm_back(grad, white, scale, gain)
                sums[0] += fold_rows(grad * white)
                sums[1] += fold_rows(grad)
                input_grad[rows] = total
                grad_low[rows] = total.astype(LOW)

            loop(HALF // HALF, first_back)

            @pl.when(section == last)
            def _():
                hop_backward(pack, half).start()

        def first_all():
            loop(2, first_half)
            store(9, pack).start()

        if not defer:
            attend_all()
            first_all()
        else:
            put_off = (order == packs - 1) & (section == 0)

            @pl.when(put_off)
            def _():
                store(5, pack).start()
                for copy in late[3:]:
                    copy.start()

            @pl.when(jnp.logical_not(put_off))
            def _():
                attend_all()
                first_all()

    loop(packs, forward)
    if defer:

        @pl.when(section == 0)
        def _():
            for copy in late[:3]:
                copy.start()

    loop(packs, backward)

    count = sums.shape[0]
    vector_ref[count:] = jnp.zeros((vector_ref.shape[0] - count, width), F32)
    for index in range(count):
        vector_ref[index : index + 1] = jnp.sum(sums[index], axis=0, keepdims=True)
    for index in range(hidden_width // width):
        lanes = slice(index * width, (index + 1) * width)
        vector_ref[count + index : count + index + 1] = jnp.sum(up_sums[:, lanes], axis=0, keepdims=True)

    for index in (3, 4):
        store(index, packs - 1).wait()
    store(6, 0).wait()
    if not defer:
        store(9, 0).wait()
    else:

        @pl.when(section == last)
        def _():
            store(9, 0).wait()

        @pl.when(section == 0)
        def _():
            for copy in late:
                copy.wait()

    for pack in range(packs):
        for index in (5, 7, 8):
            store(index, pack).wait()

    @pl.when(section == last)
    def _():
        for half in range(2):
            hop_backward(0, half).wait_send()


def relay(arrays, defer):
    inputs, cotangent, segments, valid_flags = arrays[:4]
    rows, width = inputs.shape
    hidden_width = arrays[13].shape[2]
    packs = rows // SEQ
    anywhere = pl.BlockSpec(memory_space=pl.ANY)
    vmem = pl.BlockSpec(memory_space=pltpu.VMEM)

    def low(columns):
        return jax.ShapeDtypeStruct((rows, columns), LOW)

    outs = (
        low(width),
        jax.ShapeDtypeStruct((rows, width), F32),
        jax.ShapeDtypeStruct((16, width), F32),
        low(width),
        low(width),
        low(width),
        low(hidden_width),
        low(3 * width),
        low(width),
        low(hidden_width),
        low(width),
        jax.ShapeDtypeStruct((HEADS, SEQ, SEQ), LOW),
        jax.ShapeDtypeStruct((HEADS, HEAD_DIM, SEQ), F32),
        jax.ShapeDtypeStruct((HEADS, 8, SEQ), F32),
        jax.ShapeDtypeStruct((SEQ, width), LOW),
        jax.ShapeDtypeStruct((SEQ, width), F32),
    )

    def held(columns, kind=LOW):
        return pltpu.VMEM((packs, SEQ, columns), kind)

    scratch = [
        pltpu.VMEM((width, 3 * width), LOW),
        pltpu.VMEM((width, width), LOW),
        pltpu.VMEM((width, hidden_width), LOW),
        pltpu.VMEM((hidden_width, width), LOW),
        held(width),
        held(width),
        pltpu.VMEM((SEQ, width), LOW),
        held(3 * width),
        pltpu.VMEM((SEQ, width), LOW),
        held(width, F32),
        pltpu.VMEM((SEQ, width), LOW),
        pltpu.VMEM((SEQ, hidden_width), LOW),
        held(hidden_width),
        pltpu.VMEM((SEQ, width), LOW),
        pltpu.VMEM((SEQ, width), F32),
        pltpu.VMEM((SEQ, SEQ), F32),
        pltpu.VMEM((packs, HEADS, 8, SEQ), F32),
        pltpu.VMEM((2, 2, SEQ, SEQ), F32),
        pltpu.VMEM((2, SEQ, SEQ), LOW),
        pltpu.VMEM((packs, HEADS, SEQ, SEQ), LOW),
        pltpu.VMEM((packs, HEADS, HEAD_DIM, SEQ), F32),
        pltpu.VMEM((8, 8, width), F32),
        pltpu.VMEM((8, hidden_width), F32),
        pltpu.SemaphoreType.DMA((4,)),
        pltpu.SemaphoreType.DMA((packs, 2)),
        pltpu.SemaphoreType.DMA((packs, 2)),
        pltpu.SemaphoreType.DMA((2, packs, 2)),
        pltpu.SemaphoreType.DMA((10, packs)),
        pltpu.SemaphoreType.DMA((5,)),
    ]
    return pl.pallas_call(
        functools.partial(relay_kernel, defer),
        out_shape=outs,
        in_specs=[
            anywhere, anywhere, vmem, vmem,
            vmem, vmem, anywhere, vmem, vmem, anywhere, vmem,
            vmem, vmem, anywhere, vmem, anywhere, vmem,
        ],
        out_specs=[anywhere, anywhere, vmem] + [anywhere] * 13,
        scratch_shapes=scratch,
        name="relay",
        compiler_params=pltpu.CompilerParams(
            collective_id=0, has_side_effects=True, vmem_limit_bytes=67043328
        ),
    )(
        inputs,
        cotangent,
        segments.reshape(packs, 1, SEQ),
        valid_flags.reshape(packs, 1, SEQ),
        *arrays[4:],
    )


def reduce_kernel(
    vector_ref,
    branch_hbm,
    output_hbm,
    upper_hbm,
    mixed_hbm,
    attended_hbm,
    hidden_hbm,
    second_hbm,
    normed_hbm,
    x_hbm,
    project_hbm,
    first_gain,
    late_exponents,
    late_outputs,
    late_inverse,
    late_upstream,
    late_middle,
    total_ref,
    whole_ref,
    late_grad,
    rights,
    loaded,
    lefts,
    send_core,
    take_core,
    send_x,
    take_x,
    send_z,
    take_z,
    own,
    vectors,
    take_vector,
    right_sem,
    load_sem,
    core_sems,
    x_sems,
    z_sems,
    vector_sems,
    mixed,
    exponents,
    outputs_across,
    inverse,
    upstream,
    project,
    score_low,
    middle,
    x_in,
    wide,
    sums,
    late_sems,
    pair_sems,
    half_sems,
):
    units, unit, width = total_ref.shape
    rows = rights.shape[1]
    shards = lax.axis_size("dp")
    levels = shards // 4
    ups = upper_hbm.shape[1] // width
    me = lax.axis_index("dp")
    core, x, z = me % 2, (me // 2) % 2, me // 4
    sibling = {"dp": me + 1 - 2 * core}
    across = {"dp": me + 2 - 4 * x}

    def level_peer(step):
        return {"dp": ((z + step) % levels) * 4 + x * 2 + core}

    first_up = 1 + ups
    first_mixed = first_up + ups

    sources = (
        [attended_hbm]
        + [hidden_hbm.at[:, pl.ds(block * width, width)] for block in range(ups)]
        + [second_hbm, normed_hbm]
    )

    def right_copy(index):
        return pltpu.make_async_copy(sources[index], rights.at[index], right_sem.at[index])

    chunks = [(branch_hbm, 0), (output_hbm, 0)]
    chunks += [(upper_hbm, block) for block in range(ups)]
    chunks += [(mixed_hbm, block) for block in range(3)]

    def left_copy(index):
        source, block = chunks[index]
        columns = pl.ds(block * width, width)
        if index >= 2 + ups:
            behind = pl.ds(SEQ, rows - SEQ)
            return pltpu.make_async_copy(
                source.at[behind, columns], loaded.at[index % 2, behind], load_sem.at[index % 2]
            )
        return pltpu.make_async_copy(source.at[:, columns], loaded.at[index % 2], load_sem.at[index % 2])

    left_copy(0).start()
    right_copy(0).start()
    left_copy(1).start()

    barrier = pltpu.get_barrier_semaphore()
    peers = [sibling, across] + [level_peer(step) for step in range(1, levels)]
    for peer in peers:
        pl.semaphore_signal(barrier, inc=1, device_id=peer, device_id_type=MESH)

    def send(source, target, sems, index, peer):
        return pltpu.make_async_remote_copy(
            src_ref=source,
            dst_ref=target,
            send_sem=sems.at[(0,) + index],
            recv_sem=sems.at[(1,) + index],
            device_id=peer,
            device_id_type=MESH,
        )

    def to_core(j):
        return send(send_core.at[lax.rem(j, RING)], take_core.at[j], core_sems, (j,), sibling)

    def to_x(j):
        return send(send_x.at[lax.rem(j, RING)], take_x.at[j], x_sems, (j,), across)

    def to_z(j, step):
        return send(send_z.at[j, step - 1], take_z.at[j, step - 1], z_sems, (j, step - 1), level_peer(step))

    def vector_hop(index):
        peer = (sibling, across)[index] if index < 2 else level_peer(index - 1)
        return send(vectors.at[min(index, 2)], take_vector.at[index], vector_sems, (index,), peer)

    def turn(index, group, first_left):
        left_copy(index).wait()
        block = chunks[index][1]
        source = loaded.at[index % 2]
        pieces = unit // 16

        def step(lane_block):
            here = part(lane_block, 128)
            if index >= 2 + ups:
                there = pl.ds(pl.multiple_of(block * width + lane_block * 128, 128), 128)
                turned = jnp.concatenate(
                    [jnp.transpose(mixed[:, there]), jnp.transpose(source[SEQ:, here])], axis=1
                )
            else:
                turned = jnp.transpose(source[:, here])
            for piece in range(8):
                place = block * (width // 16) + lane_block * 8 + piece
                shard, inner = lax.div(place, group), lax.rem(place, group)
                order = (
                    2 * levels * (1 - lax.rem(shard + core, 2))
                    + levels * (1 - lax.rem(lax.div(shard, 2) + x, 2))
                    + lax.div(shard, 4)
                )
                row = pl.multiple_of(order * unit + lax.rem(inner, pieces) * 16, 16)
                lefts[first_left + lax.div(inner, pieces), pl.ds(row, 16)] = turned[piece * 16 : (piece + 1) * 16]

        loop(width // 128, step)
        if index + 2 < len(chunks):
            left_copy(index + 2).start()

    half = 2 * levels * unit
    quarter = levels * unit

    span = width // CUT
    steps = units * CUT

    def left_of(u):
        return jnp.maximum(jnp.minimum(u, 1), u + 1 - ups)

    def right_of(u):
        return jnp.minimum(u, first_up) + jnp.where(u >= first_mixed, 1, 0)

    def product(j, start, count):
        u = lax.div(j, CUT)
        return times(lefts[left_of(u), start : start + count], rights[right_of(u), :, part(lax.rem(j, CUT), span)])

    def stage_core(j):
        @pl.when(j >= RING)
        def _():
            to_core(j - RING).wait_send()

        send_core[lax.rem(j, RING)] = product(j, 0, half).astype(LOW)
        to_core(j).start()

    def stage_x(j):
        to_core(j).wait_recv()
        value = product(j, half, quarter) + take_core[j, :quarter].astype(F32)

        @pl.when(j >= RING)
        def _():
            to_x(j - RING).wait_send()

        send_x[lax.rem(j, RING)] = value.astype(LOW)
        to_x(j).start()

    def stage_z(j):
        to_x(j).wait_recv()
        value = product(j, half + quarter, quarter) + take_core[j, quarter:].astype(F32) + take_x[j].astype(F32)
        own[...] = value.reshape(levels, unit, span)
        for hop in range(1, levels):
            send_z[j, hop - 1] = own[(z + hop) % levels].astype(LOW)
            to_z(j, hop).start()
        total_ref[lax.div(j, CUT), :, part(lax.rem(j, CUT), span)] = own[z]

    def finish(j):
        u, here = lax.div(j, CUT), part(lax.rem(j, CUT), span)
        value = total_ref[u, :, here]
        for hop in range(1, levels):
            to_z(j, hop).wait_recv()
            value = value + take_z[j, hop - 1].astype(F32)
        total_ref[u, :, here] = value

    def feed(j):
        @pl.when(j == 1)
        def _():
            turn(1, unit // 16, 1)
            for index in range(1 + ups, 3 + ups):
                right_copy(index).start()

        for block in range(ups):

            @pl.when(j == CUT * block + 2)
            def _(block=block):
                turn(2 + block, ups * unit // 16, 2)

        for block in range(3):

            @pl.when(j == CUT * first_mixed - 4 + block)
            def _(block=block):
                turn(2 + ups + block, 3 * unit // 16, 2 + ups)

    def need_right(j):
        for index, when in [(block, block) for block in range(1, 1 + ups)] + [
            (1 + ups, first_up),
            (2 + ups, first_mixed),
        ]:

            @pl.when(j == CUT * when)
            def _(index=index):
                right_copy(index).wait()

    turn(0, unit // 16, 0)
    for index in range(1, 1 + ups):
        right_copy(index).start()
    right_copy(0).wait()
    pl.semaphore_wait(barrier, len(peers))

    def pair_copies(pair, slot):
        heads = pl.ds(pair * 2, 2)
        return (
            pltpu.make_async_copy(late_exponents.at[heads], exponents.at[slot], pair_sems.at[0, slot]),
            pltpu.make_async_copy(late_outputs.at[heads], outputs_across.at[slot], pair_sems.at[1, slot]),
        )

    def half_copies(half):
        half_rows = pl.ds(pl.multiple_of(half * HALF, HALF), HALF)
        return (
            pltpu.make_async_copy(late_middle.at[half_rows], middle, half_sems.at[0]),
            pltpu.make_async_copy(x_hbm.at[half_rows], x_in, half_sems.at[1]),
            pltpu.make_async_copy(wide, late_grad.at[half_rows], half_sems.at[2]),
        )

    late_loads = (
        pltpu.make_async_copy(late_inverse, inverse, late_sems.at[1]),
        pltpu.make_async_copy(late_upstream, upstream, late_sems.at[2]),
        pltpu.make_async_copy(project_hbm.at[0], project, late_sems.at[3]),
    )
    mixed_load = pltpu.make_async_copy(mixed_hbm.at[pl.ds(0, SEQ)], mixed, late_sems.at[0])
    mixed_load.start()
    sums[...] = jnp.zeros_like(sums)
    lane = lax.broadcasted_iota(jnp.int32, (SEQ, PAIR), 1)
    section = lax.axis_index("section")

    @pl.when(section == 0)
    def _():
        for copy in late_loads:
            copy.start()
        for copy in pair_copies(0, 0) + half_copies(0)[:2]:
            copy.start()

    def attend_late(pair):
        slot = lax.rem(pair, 2)
        for copy in pair_copies(pair, slot):
            copy.wait()

        @pl.when(pair < PAIRS - 1)
        def _():
            for copy in pair_copies(pair + 1, 1 - slot):
                copy.start()

        here = part(pair, PAIR)
        places = [pl.ds(pl.multiple_of(third * width + pair * PAIR, PAIR), PAIR) for third in range(3)]
        query, key, value = [mixed[:, place] for place in places]
        key_across, up_across = jnp.transpose(key), jnp.transpose(upstream[:, here])
        empty = jnp.zeros((HEAD_DIM, SEQ), LOW)
        query_across, value_across, key_grad = [], [], 0.0
        for side in range(2):
            heads = slice(side * HEAD_DIM, (side + 1) * HEAD_DIM)
            own_lanes = (lane < HEAD_DIM) == (side == 0)
            one_query = jnp.where(own_lanes, query * SCORE_SCALE, 0.0).astype(LOW)
            one_up = (up_across[heads].astype(F32) * inverse[2 * pair + side, 0:1]).astype(LOW)
            inner = jnp.sum(one_up.astype(F32) * outputs_across[slot, side], axis=0, keepdims=True)
            soft_grad = times(value, jnp.concatenate([one_up, empty][:: 1 - 2 * side], axis=0))
            score_low[side] = (exponents[slot, side].astype(F32) * (soft_grad - inner)).astype(LOW)
            value_across.append(times_t(one_up, exponents[slot, side]))
            key_grad += times(score_low[side], one_query)
            query_across.append(times(key_across[heads], score_low[side]))
        query_grad = (jnp.transpose(jnp.concatenate(query_across, axis=0)) * SCORE_SCALE).astype(LOW)
        value_grad = jnp.transpose(jnp.concatenate(value_across, axis=0)).astype(LOW)
        sums[2, :, here] += fold_rows(query_grad.astype(F32))
        sums[3, :, here] += fold_rows(value_grad.astype(F32))
        for place, grad in zip(places, (query_grad, key_grad.astype(LOW), value_grad)):
            mixed[:, place] = grad

    def first_late(half):
        loads = half_copies(half)
        for copy in loads[:2]:
            copy.wait()

        @pl.when(half > 0)
        def _():
            half_copies(half - 1)[2].wait()

        wide[...] = times_t(mixed[pl.ds(pl.multiple_of(half * HALF, HALF), HALF)], project[...])
        gain = first_gain[...].astype(F32)

        def back(block):
            some = part(block, ROWS)
            grad = wide[some]
            white, scale = norm_rows(x_in[some].astype(F32))
            sums[0] += fold_rows(grad * white)
            sums[1] += fold_rows(grad)
            wide[some] = middle[some] + norm_back(grad, white, scale, gain)

        loop(HALF // ROWS, back)
        loads[2].start()

        @pl.when(half == 0)
        def _():
            for copy in half_copies(1)[:2]:
                copy.start()

    def late(j):
        pair = lax.div(j - 3, 2)

        @pl.when(j == 3)
        def _():
            mixed_load.wait()

        @pl.when((section == 0) & (j == 3))
        def _():
            for copy in late_loads:
                copy.wait()

        @pl.when((section == 0) & (j >= 3) & (j < 3 + 2 * PAIRS) & (lax.rem(j, 2) == 1))
        def _():
            attend_late(pair)

        @pl.when((section == 0) & (j >= LATE) & (j < LATE + 2))
        def _():
            first_late(j - LATE)

    def advance(j):
        feed(j)

        @pl.when((j >= 1) & (j < steps + 1))
        def _():
            stage_x(j - 1)

        need_right(j)

        @pl.when(j < steps)
        def _():
            stage_core(j)

        @pl.when((j >= LAG) & (j < steps + LAG))
        def _():
            stage_z(j - LAG)

        @pl.when(j >= 2 * LAG)
        def _():
            finish(j - 2 * LAG)

        late(j)

        @pl.when(j == LATE + 2)
        def _():
            vectors[0] = vector_ref[...]
            for index in range(4):
                vectors[0, index : index + 1] += jnp.sum(sums[index], axis=0, keepdims=True)
            vector_hop(0).start()

        @pl.when(j == LATE + 4)
        def _():
            vector_hop(0).wait_recv()
            vectors[1] = vectors[0] + take_vector[0]
            vector_hop(1).start()

        @pl.when(j == LATE + 6)
        def _():
            vector_hop(1).wait_recv()
            vectors[2] = vectors[1] + take_vector[1]
            for hop in range(1, levels):
                vector_hop(hop + 1).start()

    loop(steps + 2 * LAG, advance)
    whole = vectors[2]
    for hop in range(1, levels):
        vector_hop(hop + 1).wait_recv()
        whole = whole + take_vector[hop + 1]
    whole_ref[...] = whole

    def drain(j):
        @pl.when(j >= steps - RING)
        def _():
            to_core(j).wait_send()
            to_x(j).wait_send()

        for hop in range(1, levels):
            to_z(j, hop).wait_send()

    loop(steps, drain)
    for hop in range(levels + 1):
        vector_hop(hop).wait_send()

    @pl.when(section == 0)
    def _():
        half_copies(1)[2].wait()


def reduce_parts(vector, lefts, rights, late):
    shards = lax.axis_size("dp")
    branch, output_low, upper_low, mixed = lefts
    attended, hidden, second_normed, normed = rights
    rows, width = branch.shape
    ups = hidden.shape[1] // width
    unit, levels = width // shards, shards // 4
    units = 1 + 2 * ups + 3
    steps, span = units * CUT, width // CUT
    anywhere = pl.BlockSpec(memory_space=pl.ANY)
    vmem = pl.BlockSpec(memory_space=pltpu.VMEM)
    return pl.pallas_call(
        reduce_kernel,
        out_shape=(
            jax.ShapeDtypeStruct((units, unit, width), F32),
            jax.ShapeDtypeStruct(vector.shape, F32),
            jax.ShapeDtypeStruct((SEQ, width), F32),
        ),
        in_specs=[vmem] + [anywhere] * 10 + [vmem] + [anywhere] * 5,
        out_specs=[vmem, vmem, anywhere],
        scratch_shapes=[
            pltpu.VMEM((3 + ups, rows, width), LOW),
            pltpu.VMEM((2, rows, width), LOW),
            pltpu.VMEM((5 + ups, width, rows), LOW),
            pltpu.VMEM((RING, 2 * levels * unit, span), LOW),
            pltpu.VMEM((steps, 2 * levels * unit, span), LOW),
            pltpu.VMEM((RING, levels * unit, span), LOW),
            pltpu.VMEM((steps, levels * unit, span), LOW),
            pltpu.VMEM((steps, levels - 1, unit, span), LOW),
            pltpu.VMEM((steps, levels - 1, unit, span), LOW),
            pltpu.VMEM((levels, unit, span), F32),
            pltpu.VMEM((3,) + vector.shape, F32),
            pltpu.VMEM((levels + 1,) + vector.shape, F32),
            pltpu.SemaphoreType.DMA((3 + ups,)),
            pltpu.SemaphoreType.DMA((2,)),
            pltpu.SemaphoreType.DMA((2, steps)),
            pltpu.SemaphoreType.DMA((2, steps)),
            pltpu.SemaphoreType.DMA((2, steps, levels - 1)),
            pltpu.SemaphoreType.DMA((2, levels + 1)),
            pltpu.VMEM((SEQ, 3 * width), LOW),
            pltpu.VMEM((2, 2, SEQ, SEQ), LOW),
            pltpu.VMEM((2, 2, HEAD_DIM, SEQ), F32),
            pltpu.VMEM((HEADS, 8, SEQ), F32),
            pltpu.VMEM((SEQ, width), LOW),
            pltpu.VMEM((width, 3 * width), LOW),
            pltpu.VMEM((2, SEQ, SEQ), LOW),
            pltpu.VMEM((HALF, width), F32),
            pltpu.VMEM((HALF, width), LOW),
            pltpu.VMEM((HALF, width), F32),
            pltpu.VMEM((4, 8, width), F32),
            pltpu.SemaphoreType.DMA((4,)),
            pltpu.SemaphoreType.DMA((2, 2)),
            pltpu.SemaphoreType.DMA((3,)),
        ],
        name="reduce",
        compiler_params=pltpu.CompilerParams(
            collective_id=1, has_side_effects=True, vmem_limit_bytes=67043328
        ),
    )(vector, branch, output_low, upper_low, mixed, attended, hidden, second_normed, normed, *late)


def finish_kernel(
    whole_ref,
    total_hbm,
    result_hbm,
    input_grad_hbm,
    late_grad,
    result_out,
    input_grad_out,
    first_gain_out,
    first_shift_out,
    project_out,
    query_bias_out,
    value_bias_out,
    out_weight_out,
    out_bias_out,
    second_gain_out,
    second_shift_out,
    up_out,
    up_bias_out,
    down_out,
    down_bias_out,
    total,
    rows_low,
    rows_wide,
    in_sem,
    out_sem,
):
    units, unit, width = total.shape
    ups = down_out.shape[1] // width
    blocks = rows_low.shape[0]
    me = lax.axis_index("dp")
    shards = lax.axis_size("dp")
    section = lax.axis_index("section")
    first_up, first_mixed = 1 + ups, 1 + 2 * ups
    take = pltpu.make_async_copy(total_hbm, total, in_sem.at[2 * blocks])
    take.start()

    def block_of(ref, block):
        size = rows_low.shape[1]
        return ref.at[pl.ds(block * size, size)]

    pairs = []
    for block in range(blocks):
        for index, (source, middle, target) in enumerate(
            ((result_hbm, rows_low, result_out), (input_grad_hbm, rows_wide, input_grad_out))
        ):
            slot = 2 * block + index
            load = pltpu.make_async_copy(block_of(source, block), middle.at[block], in_sem.at[slot])
            save = pltpu.make_async_copy(middle.at[block], block_of(target, block), out_sem.at[slot])
            pairs.append((load, save))
            if index == 1 and (block + 1) * rows_low.shape[1] <= SEQ:
                other = pltpu.make_async_copy(block_of(late_grad, block), middle.at[block], in_sem.at[slot])
                pl.when(section == 0)(other.start)
                pl.when(section != 0)(load.start)
            else:
                load.start()

    pieces = [(0, out_weight_out)]
    pieces += [(1 + block, down_out.at[:, pl.ds(block * width, width)]) for block in range(ups)]
    pieces += [(first_up + block, up_out.at[pl.ds(block * unit, unit)]) for block in range(ups)]
    pieces += [(first_mixed + block, project_out.at[pl.ds(block * unit, unit)]) for block in range(3)]
    take.wait()
    for index, (source, target) in enumerate(pieces):
        save = pltpu.make_async_copy(total.at[source], target, out_sem.at[2 * blocks + index])
        save.start()
        pieces[index] = save
    for load, save in pairs:
        load.wait()
        save.start()
    rolled = pltpu.roll(whole_ref[:8], lax.rem(shards - me, shards) * unit, 1)
    small_outs = (
        first_gain_out, first_shift_out, query_bias_out, value_bias_out,
        out_bias_out, second_gain_out, second_shift_out, down_bias_out,
    )
    for index, small in enumerate(small_outs):
        small[...] = rolled[index : index + 1, :unit]
    span = ups * unit
    inner = width // span
    wide_rolled = pltpu.roll(whole_ref[8:16], lax.rem(inner - lax.rem(me, inner), inner) * span, 1)
    mine = lax.broadcasted_iota(jnp.int32, (8, width), 0) == lax.div(me, inner)
    up_bias_out[...] = jnp.sum(jnp.where(mine, wide_rolled, 0.0), axis=0, keepdims=True)[:, :span]
    for _, save in pairs:
        save.wait()
    for save in pieces:
        save.wait()


def finish(whole, total, result, input_grad, late_grad, ups):
    units, unit, width = total.shape
    rows = result.shape[0]
    anywhere = pl.BlockSpec(memory_space=pl.ANY)
    vmem = pl.BlockSpec(memory_space=pltpu.VMEM)

    def wide(*shape):
        return jax.ShapeDtypeStruct(shape, F32)

    small, matrix = wide(1, unit), wide(unit, width)
    blocks = 4
    outs = pl.pallas_call(
        finish_kernel,
        out_shape=(
            jax.ShapeDtypeStruct(result.shape, LOW), wide(rows, width), small, small,
            wide(3 * unit, width), small, small, matrix, small, small, small,
            wide(ups * unit, width), wide(1, ups * unit), wide(unit, ups * width), small,
        ),
        in_specs=[vmem] + [anywhere] * 4,
        out_specs=[
            anywhere, anywhere, vmem, vmem, anywhere, vmem, vmem, anywhere,
            vmem, vmem, vmem, anywhere, vmem, anywhere, vmem,
        ],
        scratch_shapes=[
            pltpu.VMEM(total.shape, F32),
            pltpu.VMEM((blocks, rows // blocks, width), LOW),
            pltpu.VMEM((blocks, rows // blocks, width), F32),
            pltpu.SemaphoreType.DMA((2 * blocks + 1,)),
            pltpu.SemaphoreType.DMA((2 * blocks + units,)),
        ],
        name="finish",
        compiler_params=pltpu.CompilerParams(vmem_limit_bytes=67043328),
    )(whole, total, result, input_grad, late_grad)
    result, input_grad = outs[0][None], outs[1][None]
    turned = [outs[index].T[None] for index in (4, 7, 11, 13)]
    return (
        result, input_grad, outs[2], outs[3], turned[0], outs[5], outs[6], turned[1],
        outs[8], outs[9], outs[10], turned[2], outs[12], turned[3], outs[14],
    )


def contract_rows(left, right):
    return lax.dot_general(left, right, (((0,), (0,)), ((), ())), preferred_element_type=F32)


def scatter_parts(vector, lefts, rights):
    def reduce_rows(left, right):
        piece = lax.psum_scatter(contract_rows(left, right), "dp", scatter_dimension=0, tiled=True)
        return piece.T

    branch, output_low, upper_low, mixed = lefts
    attended, hidden, second_normed, normed = rights
    return (
        lax.psum(vector, "dp"),
        reduce_rows(mixed, normed),
        reduce_rows(branch, attended),
        reduce_rows(upper_low, second_normed),
        reduce_rows(output_low, hidden),
    )


def on_device(*arrays):
    shards = lax.axis_size("dp")
    me = lax.axis_index("dp")
    width = arrays[0].shape[1]
    aligned = shards % 4 == 0 and width % (16 * shards) == 0
    (
        result, input_grad, vector,
        normed, attended, second_normed, hidden, mixed, branch, upper_low, output_low,
        *late,
    ) = relay(arrays, aligned)
    lefts = (branch, output_low, upper_low, mixed)
    rights = (attended, hidden, second_normed, normed)
    if aligned:
        late = (arrays[0], arrays[6], arrays[4], *late)
        total, whole, late_grad = reduce_parts(vector, lefts, rights, late)
        return finish(whole, total, result, input_grad, late_grad, hidden.shape[1] // width)
    whole, project_grad, out_grad, up_grad, down_grad = scatter_parts(vector, lefts, rights)
    size = width // shards
    small = lax.dynamic_slice_in_dim(whole[:8], me * size, size, 1)
    up_size = hidden.shape[1] // shards
    up_small = lax.dynamic_slice_in_dim(whole[8:].reshape(1, -1), me * up_size, up_size, 1)
    return (
        result[None],
        input_grad[None],
        small[0:1],
        small[1:2],
        project_grad[None],
        small[2:3],
        small[3:4],
        out_grad[None],
        small[4:5],
        small[5:6],
        small[6:7],
        up_grad[None],
        up_small,
        down_grad[None],
        small[7:8],
    )


def solution(mesh):
    stack1 = P("section", None)
    stack2 = P("section", None, None)
    in_specs = (
        P("dp", None), P("dp", None), P("dp"), P("dp"),
        stack1, stack1, stack2, stack1, stack1, stack2, stack1,
        stack1, stack1, stack2, stack1, stack2, stack1,
    )
    row = P("section", "dp")
    matrix = P("section", None, "dp")
    rows = P("section", "dp", None)
    out_specs = (
        rows, rows, row, row, matrix, row, row, matrix, row, row, row, matrix, row, matrix, row,
    )
    return jax.shard_map(
        on_device, mesh=mesh, in_specs=in_specs, out_specs=out_specs, check_vma=False
    )
```

```python
import functools

import jax
import jax.numpy as jnp
from jax import lax
from jax.experimental import pallas as pl
from jax.experimental.pallas import tpu as pltpu
from jax.sharding import PartitionSpec as P

HEADS = 12
HEAD_DIM = 64
SEQ = 512
PAIR = 2 * HEAD_DIM
PAIRS = HEADS // 2
TILE = 256
WIDE = 3072
HALF = 256
UP_WIDE = 1536
CUT = 2
RING = 6
LATE = 16
LAG = 3
ROWS = 128
EPSILON = 1e-06
SCORE_SCALE = 0.125
FAR = -1e30
F32 = jnp.float32
LOW = jnp.bfloat16
MESH = pl.DeviceIdType.MESH


def times(left, right):
    return lax.dot_general(left, right, (((1,), (0,)), ((), ())), preferred_element_type=F32)


def times_t(left, right):
    return lax.dot_general(left, right, (((1,), (1,)), ((), ())), preferred_element_type=F32)


def loop(count, body):
    def step(index, carry):
        body(index)
        return carry

    lax.fori_loop(0, count, step, 0)


def part(index, size):
    return pl.ds(pl.multiple_of(index * size, size), size)


def norm_rows(values):
    average = jnp.mean(values, axis=-1, keepdims=True)
    centred = values - average
    inv_scale = lax.rsqrt(jnp.mean(centred * centred, axis=-1, keepdims=True) + EPSILON)
    return centred * inv_scale, inv_scale


def norm_back(normed_grad, whitened, inv_scale, gain):
    scaled = normed_grad * gain
    return inv_scale * (
        scaled
        - jnp.mean(scaled, axis=-1, keepdims=True)
        - whitened * jnp.mean(scaled * whitened, axis=-1, keepdims=True)
    )


def fold_rows(values):
    rows, width = values.shape
    return jnp.sum(values.reshape(rows // 8, 8, width), axis=0)


def fill_bias(code_row, bias):
    across = jnp.transpose(jnp.broadcast_to(code_row, (128, SEQ)))
    for block in range(SEQ // 128):
        lanes = slice(block * 128, (block + 1) * 128)
        bias[:, lanes] = jnp.where(across == code_row[:, lanes], 0.0, FAR)


def gelu_both(upper):
    cumulative = 0.5 * (1.0 + lax.erf(upper * (0.5**0.5)))
    density = jnp.exp2((upper * upper) * -0.7213475204444817) * 0.3989422804014327
    return upper * cumulative, cumulative + upper * density


def relay_kernel(
    defer,
    x_hbm,
    cot_hbm,
    segment_ref,
    valid_ref,
    first_gain,
    first_shift,
    project_hbm,
    query_bias,
    value_bias,
    out_hbm,
    out_bias,
    second_gain,
    second_shift,
    up_hbm,
    up_bias,
    down_hbm,
    down_bias,
    result_hbm,
    input_grad_hbm,
    vector_ref,
    normed_hbm,
    attended_hbm,
    second_hbm,
    hidden_hbm,
    mixed_hbm,
    branch_hbm,
    upper_hbm,
    output_hbm,
    late_exponents,
    late_outputs,
    late_inverse,
    late_upstream,
    late_middle,
    project,
    out_weight,
    up_weight,
    down_weight,
    x_in,
    g_in,
    normed,
    mixed,
    attended,
    middle,
    second_normed,
    hidden,
    slope,
    result,
    wide,
    bias,
    inv_sums,
    score_buf,
    score_low,
    exponents,
    outputs_across,
    sums,
    up_sums,
    weight_sem,
    x_sem,
    g_sem,
    send_sem,
    out_sem,
    late_sem,
):
    section = lax.axis_index("section")
    width = x_in.shape[2]
    hidden_width = hidden.shape[1]
    packs = x_in.shape[0]
    last = lax.axis_size("section") - 1
    partner = {"section": 1 - section}
    branch, attended_low, input_grad, grad_low = normed, attended, wide, result

    def rows_of(ref, pack):
        return ref.at[pl.ds(pl.multiple_of(pack * SEQ, SEQ), SEQ)]

    def half_of(half):
        return pl.ds(pl.multiple_of(half * HALF, HALF), HALF)

    def local_rows(source, target, sems, pack, half):
        there = pl.ds(pl.multiple_of(pack * SEQ + half * HALF, HALF), HALF)
        return pltpu.make_async_copy(source.at[there], target.at[pack, half_of(half)], sems.at[pack, half])

    def local_x(pack, half):
        return local_rows(x_hbm, x_in, x_sem, pack, half)

    def local_g(pack, half):
        return local_rows(cot_hbm, g_in, g_sem, pack, half)

    weights = (
        pltpu.make_async_copy(project_hbm.at[0], project, weight_sem.at[0]),
        pltpu.make_async_copy(out_hbm.at[0], out_weight, weight_sem.at[1]),
        pltpu.make_async_copy(up_hbm.at[0], up_weight, weight_sem.at[2]),
        pltpu.make_async_copy(down_hbm.at[0], down_weight, weight_sem.at[3]),
    )

    @pl.when(section == 0)
    def _():
        for pack in range(packs):
            for half in range(2):
                local_x(pack, half).start()

    weights[0].start()

    @pl.when(section == last)
    def _():
        for pack in range(packs):
            for half in range(2):
                local_g(pack, half).start()

    barrier = pltpu.get_barrier_semaphore()
    pl.semaphore_signal(barrier, inc=1, device_id=partner, device_id_type=MESH)
    pl.semaphore_wait(barrier, 1)

    sums[...] = jnp.zeros_like(sums)
    up_sums[...] = jnp.zeros_like(up_sums)

    def hop(way, source, target, sems, pack, half):
        rows = half_of(half)
        return pltpu.make_async_remote_copy(
            src_ref=source.at[rows],
            dst_ref=target.at[pack, rows],
            send_sem=send_sem.at[way, pack, half],
            recv_sem=sems.at[pack, half],
            device_id=partner,
            device_id_type=MESH,
        )

    def hop_forward(pack, half):
        return hop(0, result, x_in, x_sem, pack, half)

    def hop_backward(pack, half):
        return hop(1, grad_low, g_in, g_sem, pack, half)

    kept = (
        (result, result_hbm),
        (normed, normed_hbm),
        (attended, attended_hbm),
        (second_normed, second_hbm),
        (hidden, hidden_hbm),
        (mixed, mixed_hbm),
        (branch, branch_hbm),
        (slope, upper_hbm),
        (g_in, output_hbm),
        (input_grad, input_grad_hbm),
    )

    def store(index, pack):
        source, target = kept[index]
        source = source if len(source.shape) == 2 else source.at[pack]
        return pltpu.make_async_copy(source, rows_of(target, pack), out_sem.at[index, pack])

    lane = lax.broadcasted_iota(jnp.int32, (SEQ, PAIR), 1)

    def heads_of(pack, pair):
        start = pl.multiple_of(pair * PAIR, PAIR)
        return [mixed[pack, :, pl.ds(third * width + start, PAIR)] for third in range(3)]

    late = (
        pltpu.make_async_copy(exponents.at[0], late_exponents, late_sem.at[0]),
        pltpu.make_async_copy(outputs_across.at[0], late_outputs, late_sem.at[1]),
        pltpu.make_async_copy(inv_sums.at[0], late_inverse, late_sem.at[2]),
        pltpu.make_async_copy(attended_low, late_upstream, late_sem.at[3]),
        pltpu.make_async_copy(middle.at[0], late_middle, late_sem.at[4]),
    )

    def forward(pack):
        first = pack == 0

        gain = first_gain[...].astype(F32)
        shift = first_shift[...].astype(F32)

        @pl.when(pack > 0)
        def _():
            store(1, pack - 1).wait()

        places = lax.broadcasted_iota(jnp.int32, (1, SEQ), 1) + SEQ
        fill_bias(jnp.where(valid_ref[pack] == 1, segment_ref[pack], places).astype(F32), bias)

        def project_half(half):
            @pl.when(section == 0)
            def _():
                local_x(pack, half).wait()

            @pl.when(section == last)
            def _():
                hop_forward(pack, half).wait_recv()

            def norm_step(block):
                rows = pl.ds(pl.multiple_of(half * HALF + block * HALF, HALF), HALF)
                white, _ = norm_rows(x_in[pack, rows].astype(F32))
                normed[rows] = (white * gain + shift).astype(LOW)

            loop(HALF // HALF, norm_step)

            @pl.when(first & (half == 0))
            def _():
                weights[0].wait()
                for copy in weights[1:]:
                    copy.start()

            rows = half_of(half)
            for third, offset_ref in enumerate((query_bias, None, value_bias)):
                there = slice(third * width, (third + 1) * width)
                value = times(normed[rows], project[:, there])
                if offset_ref is not None:
                    value = value + offset_ref[...].astype(F32)
                mixed[pack, rows, there] = value.astype(LOW)

        loop(2, project_half)
        store(1, pack).start()

        def scores_of(pair, slot):
            query, key, _ = heads_of(pack, pair)
            for side in range(2):
                own = (lane < HEAD_DIM) == (side == 0)
                one = jnp.where(own, query * SCORE_SCALE, 0.0).astype(LOW)
                score_buf[slot, side] = times_t(key, one) + bias[...]

        def attend(pair, slot):
            value_across = jnp.transpose(heads_of(pack, pair)[2])
            ones = jnp.ones((16, SEQ), LOW)
            outs = []
            for side in range(2):
                heads = slice(side * HEAD_DIM, (side + 1) * HEAD_DIM)
                scores = score_buf[slot, side]
                key_max = jnp.max(scores, axis=0, keepdims=True)
                exponent = jnp.exp(scores - key_max).astype(LOW)
                exponents[pack, 2 * pair + side] = exponent
                sums_too = times(jnp.concatenate([value_across[heads], ones], axis=0), exponent)
                inverse = 1.0 / sums_too[HEAD_DIM : HEAD_DIM + 1]
                inv_sums[pack, 2 * pair + side] = jnp.broadcast_to(inverse, (8, SEQ))
                outs.append(sums_too[:HEAD_DIM] * inverse)
                outputs_across[pack, 2 * pair + side] = outs[side]
            attended[:, part(pair, PAIR)] = jnp.transpose(jnp.concatenate(outs, axis=0)).astype(LOW)

        @pl.when(pack > 0)
        def _():
            store(2, pack - 1).wait()

        scores_of(0, 0)

        def attend_step(index):
            for slot in range(2):
                pair = 2 * index + slot
                scores_of(jnp.minimum(pair + 1, PAIRS - 1), 1 - slot)
                attend(pair, slot)

        loop(PAIRS // 2, attend_step)
        store(2, pack).start()

        @pl.when(first)
        def _():
            weights[1].wait()

        middle[pack] = x_in[pack].astype(F32) + (
            times(attended[...], out_weight[...]) + out_bias[...].astype(F32)
        )
        gain2 = second_gain[...].astype(F32)
        shift2 = second_shift[...].astype(F32)

        @pl.when(pack > 0)
        def _():
            store(3, pack - 1).wait()
            store(4, pack - 1).wait()
            store(0, pack - 1).wait()

        @pl.when(first)
        def _():
            weights[2].wait()
            weights[3].wait()

        def feed_half(half):
            def second_step(block):
                rows = pl.ds(pl.multiple_of(half * HALF + block * HALF, HALF), HALF)
                white, _ = norm_rows(middle[pack, rows])
                second_normed[rows] = (white * gain2 + shift2).astype(LOW)

            loop(HALF // HALF, second_step)
            rows = half_of(half)

            def up_step(tile):
                here = part(tile, UP_WIDE)
                upper = times(second_normed[rows], up_weight[:, here]) + up_bias[:, here].astype(F32)
                act, act_slope = gelu_both(upper)
                hidden[rows, here] = act.astype(LOW)
                slope[pack, rows, here] = act_slope.astype(LOW)

            loop(hidden_width // UP_WIDE, up_step)

            @pl.when((pack > 0) & (section == 0))
            def _():
                hop_forward(pack - 1, half).wait_send()

            value = middle[pack, rows] + (times(hidden[rows], down_weight[...]) + down_bias[...].astype(F32))
            result[rows] = value.astype(LOW)

            @pl.when(section == 0)
            def _():
                hop_forward(pack, half).start()

        loop(2, feed_half)
        store(3, pack).start()
        store(4, pack).start()
        store(0, pack).start()

    def backward(order):
        pack = packs - 1 - order

        def hidden_half(half):
            @pl.when(section == last)
            def _():
                local_g(pack, half).wait()

            @pl.when(section == 0)
            def _():
                hop_backward(pack, half).wait_recv()

            rows = half_of(half)
            sums[7] += fold_rows(g_in[pack, rows].astype(F32))

            def hidden_step(tile):
                here = part(tile, WIDE)
                value = times_t(g_in[pack, rows], down_weight[here]).astype(LOW).astype(F32)
                low = (value * slope[pack, rows, here].astype(F32)).astype(LOW)
                slope[pack, rows, here] = low
                up_sums[:, here] += fold_rows(low.astype(F32))

            loop(hidden_width // WIDE, hidden_step)

        loop(2, hidden_half)
        store(8, pack).start()
        store(7, pack).start()

        @pl.when(order > 0)
        def _():
            store(9, pack + 1).wait()
            store(6, pack + 1).wait()

        @pl.when(order == 0)
        def _():
            store(0, pack).wait()
            store(1, pack).wait()
            store(2, pack).wait()

        @pl.when((order == 0) & (section == 0))
        def _():
            for half in range(2):
                hop_forward(pack, half).wait_send()

        wide[...] = times_t(slope[pack], up_weight[...])
        gain2 = second_gain[...].astype(F32)

        def second_back(block):
            rows = part(block, HALF)
            grad = wide[rows]
            white, scale = norm_rows(middle[pack, rows])
            total = g_in[pack, rows].astype(F32) + norm_back(grad, white, scale, gain2)
            sums[5] += fold_rows(grad * white)
            sums[6] += fold_rows(grad)
            middle[pack, rows] = total
            low = total.astype(LOW)
            branch[rows] = low
            sums[4] += fold_rows(low.astype(F32))

        loop(SEQ // HALF, second_back)
        store(6, pack).start()

        attended_low[...] = times_t(branch[...], out_weight[...]).astype(LOW)

        def attend_back(pair):
            here = part(pair, PAIR)
            query, key, value = heads_of(pack, pair)
            key_across, up_across = jnp.transpose(key), jnp.transpose(attended_low[:, here])
            empty = jnp.zeros((HEAD_DIM, SEQ), LOW)
            query_across, value_across, key_grad = [], [], 0.0
            for side in range(2):
                head = 2 * pair + side
                heads = slice(side * HEAD_DIM, (side + 1) * HEAD_DIM)
                own = (lane < HEAD_DIM) == (side == 0)
                one_query = jnp.where(own, query * SCORE_SCALE, 0.0).astype(LOW)
                one_up = (up_across[heads].astype(F32) * inv_sums[pack, head, 0:1]).astype(LOW)
                inner = jnp.sum(one_up.astype(F32) * outputs_across[pack, head], axis=0, keepdims=True)
                soft_grad = times(value, jnp.concatenate([one_up, empty][:: 1 - 2 * side], axis=0))
                score_low[side] = (exponents[pack, head].astype(F32) * (soft_grad - inner)).astype(LOW)
                value_across.append(times_t(one_up, exponents[pack, head]))
                key_grad += times(score_low[side], one_query)
                query_across.append(times(key_across[heads], score_low[side]))
            query_grad = (jnp.transpose(jnp.concatenate(query_across, axis=0)) * SCORE_SCALE).astype(LOW)
            value_grad = jnp.transpose(jnp.concatenate(value_across, axis=0)).astype(LOW)
            sums[2, :, here] += fold_rows(query_grad.astype(F32))
            sums[3, :, here] += fold_rows(value_grad.astype(F32))
            for third, grad in enumerate((query_grad, key_grad.astype(LOW), value_grad)):
                start = pl.multiple_of(third * width + pair * PAIR, PAIR)
                mixed[pack, :, pl.ds(start, PAIR)] = grad

        def attend_all():
            loop(PAIRS, attend_back)
            store(5, pack).start()

        gain = first_gain[...].astype(F32)

        def first_half(half):
            rows = half_of(half)
            wide[rows] = times_t(mixed[pack, rows], project[...])

            @pl.when((order > 0) & (section == last))
            def _():
                hop_backward(pack + 1, half).wait_send()

            def first_back(block):
                rows = pl.ds(pl.multiple_of(half * HALF + block * HALF, HALF), HALF)
                grad = wide[rows]
                white, scale = norm_rows(x_in[pack, rows].astype(F32))
                total = middle[pack, rows] + norm_back(grad, white, scale, gain)
                sums[0] += fold_rows(grad * white)
                sums[1] += fold_rows(grad)
                input_grad[rows] = total
                grad_low[rows] = total.astype(LOW)

            loop(HALF // HALF, first_back)

            @pl.when(section == last)
            def _():
                hop_backward(pack, half).start()

        def first_all():
            loop(2, first_half)
            store(9, pack).start()

        if not defer:
            attend_all()
            first_all()
        else:
            put_off = (order == packs - 1) & (section == 0)

            @pl.when(put_off)
            def _():
                store(5, pack).start()
                for copy in late[3:]:
                    copy.start()

            @pl.when(jnp.logical_not(put_off))
            def _():
                attend_all()
                first_all()

    loop(packs, forward)
    if defer:

        @pl.when(section == 0)
        def _():
            for copy in late[:3]:
                copy.start()

    loop(packs, backward)

    count = sums.shape[0]
    vector_ref[count:] = jnp.zeros((vector_ref.shape[0] - count, width), F32)
    for index in range(count):
        vector_ref[index : index + 1] = jnp.sum(sums[index], axis=0, keepdims=True)
    for index in range(hidden_width // width):
        lanes = slice(index * width, (index + 1) * width)
        vector_ref[count + index : count + index + 1] = jnp.sum(up_sums[:, lanes], axis=0, keepdims=True)

    for index in (3, 4):
        store(index, packs - 1).wait()
    store(6, 0).wait()
    if not defer:
        store(9, 0).wait()
    else:

        @pl.when(section == last)
        def _():
            store(9, 0).wait()

        @pl.when(section == 0)
        def _():
            for copy in late:
                copy.wait()

    for pack in range(packs):
        for index in (5, 7, 8):
            store(index, pack).wait()

    @pl.when(section == last)
    def _():
        for half in range(2):
            hop_backward(0, half).wait_send()


def relay(arrays, defer):
    inputs, cotangent, segments, valid_flags = arrays[:4]
    rows, width = inputs.shape
    hidden_width = arrays[13].shape[2]
    packs = rows // SEQ
    anywhere = pl.BlockSpec(memory_space=pl.ANY)
    vmem = pl.BlockSpec(memory_space=pltpu.VMEM)

    def low(columns):
        return jax.ShapeDtypeStruct((rows, columns), LOW)

    outs = (
        low(width),
        jax.ShapeDtypeStruct((rows, width), F32),
        jax.ShapeDtypeStruct((16, width), F32),
        low(width),
        low(width),
        low(width),
        low(hidden_width),
        low(3 * width),
        low(width),
        low(hidden_width),
        low(width),
        jax.ShapeDtypeStruct((HEADS, SEQ, SEQ), LOW),
        jax.ShapeDtypeStruct((HEADS, HEAD_DIM, SEQ), F32),
        jax.ShapeDtypeStruct((HEADS, 8, SEQ), F32),
        jax.ShapeDtypeStruct((SEQ, width), LOW),
        jax.ShapeDtypeStruct((SEQ, width), F32),
    )

    def held(columns, kind=LOW):
        return pltpu.VMEM((packs, SEQ, columns), kind)

    scratch = [
        pltpu.VMEM((width, 3 * width), LOW),
        pltpu.VMEM((width, width), LOW),
        pltpu.VMEM((width, hidden_width), LOW),
        pltpu.VMEM((hidden_width, width), LOW),
        held(width),
        held(width),
        pltpu.VMEM((SEQ, width), LOW),
        held(3 * width),
        pltpu.VMEM((SEQ, width), LOW),
        held(width, F32),
        pltpu.VMEM((SEQ, width), LOW),
        pltpu.VMEM((SEQ, hidden_width), LOW),
        held(hidden_width),
        pltpu.VMEM((SEQ, width), LOW),
        pltpu.VMEM((SEQ, width), F32),
        pltpu.VMEM((SEQ, SEQ), F32),
        pltpu.VMEM((packs, HEADS, 8, SEQ), F32),
        pltpu.VMEM((2, 2, SEQ, SEQ), F32),
        pltpu.VMEM((2, SEQ, SEQ), LOW),
        pltpu.VMEM((packs, HEADS, SEQ, SEQ), LOW),
        pltpu.VMEM((packs, HEADS, HEAD_DIM, SEQ), F32),
        pltpu.VMEM((8, 8, width), F32),
        pltpu.VMEM((8, hidden_width), F32),
        pltpu.SemaphoreType.DMA((4,)),
        pltpu.SemaphoreType.DMA((packs, 2)),
        pltpu.SemaphoreType.DMA((packs, 2)),
        pltpu.SemaphoreType.DMA((2, packs, 2)),
        pltpu.SemaphoreType.DMA((10, packs)),
        pltpu.SemaphoreType.DMA((5,)),
    ]
    return pl.pallas_call(
        functools.partial(relay_kernel, defer),
        out_shape=outs,
        in_specs=[
            anywhere, anywhere, vmem, vmem,
            vmem, vmem, anywhere, vmem, vmem, anywhere, vmem,
            vmem, vmem, anywhere, vmem, anywhere, vmem,
        ],
        out_specs=[anywhere, anywhere, vmem] + [anywhere] * 13,
        scratch_shapes=scratch,
        name="relay",
        compiler_params=pltpu.CompilerParams(
            collective_id=0, has_side_effects=True, vmem_limit_bytes=67043328
        ),
    )(
        inputs,
        cotangent,
        segments.reshape(packs, 1, SEQ),
        valid_flags.reshape(packs, 1, SEQ),
        *arrays[4:],
    )


def reduce_kernel(
    vector_ref,
    branch_hbm,
    output_hbm,
    upper_hbm,
    mixed_hbm,
    attended_hbm,
    hidden_hbm,
    second_hbm,
    normed_hbm,
    x_hbm,
    project_hbm,
    first_gain,
    late_exponents,
    late_outputs,
    late_inverse,
    late_upstream,
    late_middle,
    total_ref,
    whole_ref,
    late_grad,
    rights,
    loaded,
    lefts,
    send_core,
    take_core,
    send_x,
    take_x,
    send_z,
    take_z,
    own,
    vectors,
    take_vector,
    right_sem,
    load_sem,
    core_sems,
    x_sems,
    z_sems,
    vector_sems,
    mixed,
    exponents,
    outputs_across,
    inverse,
    upstream,
    project,
    score_low,
    middle,
    x_in,
    wide,
    sums,
    late_sems,
    pair_sems,
    half_sems,
):
    units, unit, width = total_ref.shape
    rows = rights.shape[1]
    shards = lax.axis_size("dp")
    levels = shards // 4
    ups = upper_hbm.shape[1] // width
    me = lax.axis_index("dp")
    core, x, z = me % 2, (me // 2) % 2, me // 4
    sibling = {"dp": me + 1 - 2 * core}
    across = {"dp": me + 2 - 4 * x}

    def level_peer(step):
        return {"dp": ((z + step) % levels) * 4 + x * 2 + core}

    first_up = 1 + ups
    first_mixed = first_up + ups

    sources = (
        [attended_hbm]
        + [hidden_hbm.at[:, pl.ds(block * width, width)] for block in range(ups)]
        + [second_hbm, normed_hbm]
    )

    def right_copy(index):
        return pltpu.make_async_copy(sources[index], rights.at[index], right_sem.at[index])

    chunks = [(branch_hbm, 0), (output_hbm, 0)]
    chunks += [(upper_hbm, block) for block in range(ups)]
    chunks += [(mixed_hbm, block) for block in range(3)]

    def left_copy(index):
        source, block = chunks[index]
        columns = pl.ds(block * width, width)
        if index >= 2 + ups:
            behind = pl.ds(SEQ, rows - SEQ)
            return pltpu.make_async_copy(
                source.at[behind, columns], loaded.at[index % 2, behind], load_sem.at[index % 2]
            )
        return pltpu.make_async_copy(source.at[:, columns], loaded.at[index % 2], load_sem.at[index % 2])

    left_copy(0).start()
    right_copy(0).start()
    left_copy(1).start()

    barrier = pltpu.get_barrier_semaphore()
    peers = [sibling, across] + [level_peer(step) for step in range(1, levels)]
    for peer in peers:
        pl.semaphore_signal(barrier, inc=1, device_id=peer, device_id_type=MESH)

    def send(source, target, sems, index, peer):
        return pltpu.make_async_remote_copy(
            src_ref=source,
            dst_ref=target,
            send_sem=sems.at[(0,) + index],
            recv_sem=sems.at[(1,) + index],
            device_id=peer,
            device_id_type=MESH,
        )

    def to_core(j):
        return send(send_core.at[lax.rem(j, RING)], take_core.at[j], core_sems, (j,), sibling)

    def to_x(j):
        return send(send_x.at[lax.rem(j, RING)], take_x.at[j], x_sems, (j,), across)

    def to_z(j, step):
        return send(send_z.at[j, step - 1], take_z.at[j, step - 1], z_sems, (j, step - 1), level_peer(step))

    def vector_hop(index):
        peer = (sibling, across)[index] if index < 2 else level_peer(index - 1)
        return send(vectors.at[min(index, 2)], take_vector.at[index], vector_sems, (index,), peer)

    def turn(index, group, first_left):
        left_copy(index).wait()
        block = chunks[index][1]
        source = loaded.at[index % 2]
        pieces = unit // 16

        def step(lane_block):
            here = part(lane_block, 128)
            if index >= 2 + ups:
                there = pl.ds(pl.multiple_of(block * width + lane_block * 128, 128), 128)
                turned = jnp.concatenate(
                    [jnp.transpose(mixed[:, there]), jnp.transpose(source[SEQ:, here])], axis=1
                )
            else:
                turned = jnp.transpose(source[:, here])
            for piece in range(8):
                place = block * (width // 16) + lane_block * 8 + piece
                shard, inner = lax.div(place, group), lax.rem(place, group)
                order = (
                    2 * levels * (1 - lax.rem(shard + core, 2))
                    + levels * (1 - lax.rem(lax.div(shard, 2) + x, 2))
                    + lax.div(shard, 4)
                )
                row = pl.multiple_of(order * unit + lax.rem(inner, pieces) * 16, 16)
                lefts[first_left + lax.div(inner, pieces), pl.ds(row, 16)] = turned[piece * 16 : (piece + 1) * 16]

        loop(width // 128, step)
        if index + 2 < len(chunks):
            left_copy(index + 2).start()

    half = 2 * levels * unit
    quarter = levels * unit

    span = width // CUT
    steps = units * CUT

    def left_of(u):
        return jnp.maximum(jnp.minimum(u, 1), u + 1 - ups)

    def right_of(u):
        return jnp.minimum(u, first_up) + jnp.where(u >= first_mixed, 1, 0)

    def product(j, start, count):
        u = lax.div(j, CUT)
        return times(lefts[left_of(u), start : start + count], rights[right_of(u), :, part(lax.rem(j, CUT), span)])

    def stage_core(j):
        @pl.when(j >= RING)
        def _():
            to_core(j - RING).wait_send()

        send_core[lax.rem(j, RING)] = product(j, 0, half).astype(LOW)
        to_core(j).start()

    def stage_x(j):
        to_core(j).wait_recv()
        value = product(j, half, quarter) + take_core[j, :quarter].astype(F32)

        @pl.when(j >= RING)
        def _():
            to_x(j - RING).wait_send()

        send_x[lax.rem(j, RING)] = value.astype(LOW)
        to_x(j).start()

    def stage_z(j):
        to_x(j).wait_recv()
        value = product(j, half + quarter, quarter) + take_core[j, quarter:].astype(F32) + take_x[j].astype(F32)
        own[...] = value.reshape(levels, unit, span)
        for hop in range(1, levels):
            send_z[j, hop - 1] = own[(z + hop) % levels].astype(LOW)
            to_z(j, hop).start()
        total_ref[lax.div(j, CUT), :, part(lax.rem(j, CUT), span)] = own[z]

    def finish(j):
        u, here = lax.div(j, CUT), part(lax.rem(j, CUT), span)
        value = total_ref[u, :, here]
        for hop in range(1, levels):
            to_z(j, hop).wait_recv()
            value = value + take_z[j, hop - 1].astype(F32)
        total_ref[u, :, here] = value

    def feed(j):
        @pl.when(j == 1)
        def _():
            turn(1, unit // 16, 1)
            for index in range(1 + ups, 3 + ups):
                right_copy(index).start()

        for block in range(ups):

            @pl.when(j == CUT * block + 2)
            def _(block=block):
                turn(2 + block, ups * unit // 16, 2)

        for block in range(3):

            @pl.when(j == CUT * first_mixed - 4 + block)
            def _(block=block):
                turn(2 + ups + block, 3 * unit // 16, 2 + ups)

    def need_right(j):
        for index, when in [(block, block) for block in range(1, 1 + ups)] + [
            (1 + ups, first_up),
            (2 + ups, first_mixed),
        ]:

            @pl.when(j == CUT * when)
            def _(index=index):
                right_copy(index).wait()

    turn(0, unit // 16, 0)
    for index in range(1, 1 + ups):
        right_copy(index).start()
    right_copy(0).wait()
    pl.semaphore_wait(barrier, len(peers))

    def pair_copies(pair, slot):
        heads = pl.ds(pair * 2, 2)
        return (
            pltpu.make_async_copy(late_exponents.at[heads], exponents.at[slot], pair_sems.at[0, slot]),
            pltpu.make_async_copy(late_outputs.at[heads], outputs_across.at[slot], pair_sems.at[1, slot]),
        )

    def half_copies(half):
        half_rows = pl.ds(pl.multiple_of(half * HALF, HALF), HALF)
        return (
            pltpu.make_async_copy(late_middle.at[half_rows], middle, half_sems.at[0]),
            pltpu.make_async_copy(x_hbm.at[half_rows], x_in, half_sems.at[1]),
            pltpu.make_async_copy(wide, late_grad.at[half_rows], half_sems.at[2]),
        )

    late_loads = (
        pltpu.make_async_copy(late_inverse, inverse, late_sems.at[1]),
        pltpu.make_async_copy(late_upstream, upstream, late_sems.at[2]),
        pltpu.make_async_copy(project_hbm.at[0], project, late_sems.at[3]),
    )
    mixed_load = pltpu.make_async_copy(mixed_hbm.at[pl.ds(0, SEQ)], mixed, late_sems.at[0])
    mixed_load.start()
    sums[...] = jnp.zeros_like(sums)
    lane = lax.broadcasted_iota(jnp.int32, (SEQ, PAIR), 1)
    section = lax.axis_index("section")

    @pl.when(section == 0)
    def _():
        for copy in late_loads:
            copy.start()
        for copy in pair_copies(0, 0) + half_copies(0)[:2]:
            copy.start()

    def attend_late(pair):
        slot = lax.rem(pair, 2)
        for copy in pair_copies(pair, slot):
            copy.wait()

        @pl.when(pair < PAIRS - 1)
        def _():
            for copy in pair_copies(pair + 1, 1 - slot):
                copy.start()

        here = part(pair, PAIR)
        places = [pl.ds(pl.multiple_of(third * width + pair * PAIR, PAIR), PAIR) for third in range(3)]
        query, key, value = [mixed[:, place] for place in places]
        key_across, up_across = jnp.transpose(key), jnp.transpose(upstream[:, here])
        empty = jnp.zeros((HEAD_DIM, SEQ), LOW)
        query_across, value_across, key_grad = [], [], 0.0
        for side in range(2):
            heads = slice(side * HEAD_DIM, (side + 1) * HEAD_DIM)
            own_lanes = (lane < HEAD_DIM) == (side == 0)
            one_query = jnp.where(own_lanes, query * SCORE_SCALE, 0.0).astype(LOW)
            one_up = (up_across[heads].astype(F32) * inverse[2 * pair + side, 0:1]).astype(LOW)
            inner = jnp.sum(one_up.astype(F32) * outputs_across[slot, side], axis=0, keepdims=True)
            soft_grad = times(value, jnp.concatenate([one_up, empty][:: 1 - 2 * side], axis=0))
            score_low[side] = (exponents[slot, side].astype(F32) * (soft_grad - inner)).astype(LOW)
            value_across.append(times_t(one_up, exponents[slot, side]))
            key_grad += times(score_low[side], one_query)
            query_across.append(times(key_across[heads], score_low[side]))
        query_grad = (jnp.transpose(jnp.concatenate(query_across, axis=0)) * SCORE_SCALE).astype(LOW)
        value_grad = jnp.transpose(jnp.concatenate(value_across, axis=0)).astype(LOW)
        sums[2, :, here] += fold_rows(query_grad.astype(F32))
        sums[3, :, here] += fold_rows(value_grad.astype(F32))
        for place, grad in zip(places, (query_grad, key_grad.astype(LOW), value_grad)):
            mixed[:, place] = grad

    def first_late(half):
        loads = half_copies(half)
        for copy in loads[:2]:
            copy.wait()

        @pl.when(half > 0)
        def _():
            half_copies(half - 1)[2].wait()

        wide[...] = times_t(mixed[pl.ds(pl.multiple_of(half * HALF, HALF), HALF)], project[...])
        gain = first_gain[...].astype(F32)

        def back(block):
            some = part(block, ROWS)
            grad = wide[some]
            white, scale = norm_rows(x_in[some].astype(F32))
            sums[0] += fold_rows(grad * white)
            sums[1] += fold_rows(grad)
            wide[some] = middle[some] + norm_back(grad, white, scale, gain)

        loop(HALF // ROWS, back)
        loads[2].start()

        @pl.when(half == 0)
        def _():
            for copy in half_copies(1)[:2]:
                copy.start()

    def late(j):
        pair = lax.div(j - 3, 2)

        @pl.when(j == 3)
        def _():
            mixed_load.wait()

        @pl.when((section == 0) & (j == 3))
        def _():
            for copy in late_loads:
                copy.wait()

        @pl.when((section == 0) & (j >= 3) & (j < 3 + 2 * PAIRS) & (lax.rem(j, 2) == 1))
        def _():
            attend_late(pair)

        @pl.when((section == 0) & (j >= LATE) & (j < LATE + 2))
        def _():
            first_late(j - LATE)

    def advance(j):
        feed(j)

        @pl.when((j >= 1) & (j < steps + 1))
        def _():
            stage_x(j - 1)

        need_right(j)

        @pl.when(j < steps)
        def _():
            stage_core(j)

        @pl.when((j >= LAG) & (j < steps + LAG))
        def _():
            stage_z(j - LAG)

        @pl.when(j >= 2 * LAG)
        def _():
            finish(j - 2 * LAG)

        late(j)

        @pl.when(j == LATE + 2)
        def _():
            vectors[0] = vector_ref[...]
            for index in range(4):
                vectors[0, index : index + 1] += jnp.sum(sums[index], axis=0, keepdims=True)
            vector_hop(0).start()

        @pl.when(j == LATE + 4)
        def _():
            vector_hop(0).wait_recv()
            vectors[1] = vectors[0] + take_vector[0]
            vector_hop(1).start()

        @pl.when(j == LATE + 6)
        def _():
            vector_hop(1).wait_recv()
            vectors[2] = vectors[1] + take_vector[1]
            for hop in range(1, levels):
                vector_hop(hop + 1).start()

    loop(steps + 2 * LAG, advance)
    whole = vectors[2]
    for hop in range(1, levels):
        vector_hop(hop + 1).wait_recv()
        whole = whole + take_vector[hop + 1]
    whole_ref[...] = whole

    def drain(j):
        @pl.when(j >= steps - RING)
        def _():
            to_core(j).wait_send()
            to_x(j).wait_send()

        for hop in range(1, levels):
            to_z(j, hop).wait_send()

    loop(steps, drain)
    for hop in range(levels + 1):
        vector_hop(hop).wait_send()

    @pl.when(section == 0)
    def _():
        half_copies(1)[2].wait()


def reduce_parts(vector, lefts, rights, late):
    shards = lax.axis_size("dp")
    branch, output_low, upper_low, mixed = lefts
    attended, hidden, second_normed, normed = rights
    rows, width = branch.shape
    ups = hidden.shape[1] // width
    unit, levels = width // shards, shards // 4
    units = 1 + 2 * ups + 3
    steps, span = units * CUT, width // CUT
    anywhere = pl.BlockSpec(memory_space=pl.ANY)
    vmem = pl.BlockSpec(memory_space=pltpu.VMEM)
    return pl.pallas_call(
        reduce_kernel,
        out_shape=(
            jax.ShapeDtypeStruct((units, unit, width), F32),
            jax.ShapeDtypeStruct(vector.shape, F32),
            jax.ShapeDtypeStruct((SEQ, width), F32),
        ),
        in_specs=[vmem] + [anywhere] * 10 + [vmem] + [anywhere] * 5,
        out_specs=[vmem, vmem, anywhere],
        scratch_shapes=[
            pltpu.VMEM((3 + ups, rows, width), LOW),
            pltpu.VMEM((2, rows, width), LOW),
            pltpu.VMEM((5 + ups, width, rows), LOW),
            pltpu.VMEM((RING, 2 * levels * unit, span), LOW),
            pltpu.VMEM((steps, 2 * levels * unit, span), LOW),
            pltpu.VMEM((RING, levels * unit, span), LOW),
            pltpu.VMEM((steps, levels * unit, span), LOW),
            pltpu.VMEM((steps, levels - 1, unit, span), LOW),
            pltpu.VMEM((steps, levels - 1, unit, span), LOW),
            pltpu.VMEM((levels, unit, span), F32),
            pltpu.VMEM((3,) + vector.shape, F32),
            pltpu.VMEM((levels + 1,) + vector.shape, F32),
            pltpu.SemaphoreType.DMA((3 + ups,)),
            pltpu.SemaphoreType.DMA((2,)),
            pltpu.SemaphoreType.DMA((2, steps)),
            pltpu.SemaphoreType.DMA((2, steps)),
            pltpu.SemaphoreType.DMA((2, steps, levels - 1)),
            pltpu.SemaphoreType.DMA((2, levels + 1)),
            pltpu.VMEM((SEQ, 3 * width), LOW),
            pltpu.VMEM((2, 2, SEQ, SEQ), LOW),
            pltpu.VMEM((2, 2, HEAD_DIM, SEQ), F32),
            pltpu.VMEM((HEADS, 8, SEQ), F32),
            pltpu.VMEM((SEQ, width), LOW),
            pltpu.VMEM((width, 3 * width), LOW),
            pltpu.VMEM((2, SEQ, SEQ), LOW),
            pltpu.VMEM((HALF, width), F32),
            pltpu.VMEM((HALF, width), LOW),
            pltpu.VMEM((HALF, width), F32),
            pltpu.VMEM((4, 8, width), F32),
            pltpu.SemaphoreType.DMA((4,)),
            pltpu.SemaphoreType.DMA((2, 2)),
            pltpu.SemaphoreType.DMA((3,)),
        ],
        name="reduce",
        compiler_params=pltpu.CompilerParams(
            collective_id=1, has_side_effects=True, vmem_limit_bytes=67043328
        ),
    )(vector, branch, output_low, upper_low, mixed, attended, hidden, second_normed, normed, *late)


def finish_kernel(
    whole_ref,
    total_hbm,
    result_hbm,
    input_grad_hbm,
    late_grad,
    result_out,
    input_grad_out,
    first_gain_out,
    first_shift_out,
    project_out,
    query_bias_out,
    value_bias_out,
    out_weight_out,
    out_bias_out,
    second_gain_out,
    second_shift_out,
    up_out,
    up_bias_out,
    down_out,
    down_bias_out,
    total,
    rows_low,
    rows_wide,
    in_sem,
    out_sem,
):
    units, unit, width = total.shape
    ups = down_out.shape[1] // width
    blocks = rows_low.shape[0]
    me = lax.axis_index("dp")
    shards = lax.axis_size("dp")
    section = lax.axis_index("section")
    first_up, first_mixed = 1 + ups, 1 + 2 * ups
    take = pltpu.make_async_copy(total_hbm, total, in_sem.at[2 * blocks])
    take.start()

    def block_of(ref, block):
        size = rows_low.shape[1]
        return ref.at[pl.ds(block * size, size)]

    pairs = []
    for block in range(blocks):
        for index, (source, middle, target) in enumerate(
            ((result_hbm, rows_low, result_out), (input_grad_hbm, rows_wide, input_grad_out))
        ):
            slot = 2 * block + index
            load = pltpu.make_async_copy(block_of(source, block), middle.at[block], in_sem.at[slot])
            save = pltpu.make_async_copy(middle.at[block], block_of(target, block), out_sem.at[slot])
            pairs.append((load, save))
            if index == 1 and (block + 1) * rows_low.shape[1] <= SEQ:
                other = pltpu.make_async_copy(block_of(late_grad, block), middle.at[block], in_sem.at[slot])
                pl.when(section == 0)(other.start)
                pl.when(section != 0)(load.start)
            else:
                load.start()

    pieces = [(0, out_weight_out)]
    pieces += [(1 + block, down_out.at[:, pl.ds(block * width, width)]) for block in range(ups)]
    pieces += [(first_up + block, up_out.at[pl.ds(block * unit, unit)]) for block in range(ups)]
    pieces += [(first_mixed + block, project_out.at[pl.ds(block * unit, unit)]) for block in range(3)]
    take.wait()
    for index, (source, target) in enumerate(pieces):
        save = pltpu.make_async_copy(total.at[source], target, out_sem.at[2 * blocks + index])
        save.start()
        pieces[index] = save
    for load, save in pairs:
        load.wait()
        save.start()
    rolled = pltpu.roll(whole_ref[:8], lax.rem(shards - me, shards) * unit, 1)
    small_outs = (
        first_gain_out, first_shift_out, query_bias_out, value_bias_out,
        out_bias_out, second_gain_out, second_shift_out, down_bias_out,
    )
    for index, small in enumerate(small_outs):
        small[...] = rolled[index : index + 1, :unit]
    span = ups * unit
    inner = width // span
    wide_rolled = pltpu.roll(whole_ref[8:16], lax.rem(inner - lax.rem(me, inner), inner) * span, 1)
    mine = lax.broadcasted_iota(jnp.int32, (8, width), 0) == lax.div(me, inner)
    up_bias_out[...] = jnp.sum(jnp.where(mine, wide_rolled, 0.0), axis=0, keepdims=True)[:, :span]
    for _, save in pairs:
        save.wait()
    for save in pieces:
        save.wait()


def finish(whole, total, result, input_grad, late_grad, ups):
    units, unit, width = total.shape
    rows = result.shape[0]
    anywhere = pl.BlockSpec(memory_space=pl.ANY)
    vmem = pl.BlockSpec(memory_space=pltpu.VMEM)

    def wide(*shape):
        return jax.ShapeDtypeStruct(shape, F32)

    small, matrix = wide(1, unit), wide(unit, width)
    blocks = 4
    outs = pl.pallas_call(
        finish_kernel,
        out_shape=(
            jax.ShapeDtypeStruct(result.shape, LOW), wide(rows, width), small, small,
            wide(3 * unit, width), small, small, matrix, small, small, small,
            wide(ups * unit, width), wide(1, ups * unit), wide(unit, ups * width), small,
        ),
        in_specs=[vmem] + [anywhere] * 4,
        out_specs=[
            anywhere, anywhere, vmem, vmem, anywhere, vmem, vmem, anywhere,
            vmem, vmem, vmem, anywhere, vmem, anywhere, vmem,
        ],
        scratch_shapes=[
            pltpu.VMEM(total.shape, F32),
            pltpu.VMEM((blocks, rows // blocks, width), LOW),
            pltpu.VMEM((blocks, rows // blocks, width), F32),
            pltpu.SemaphoreType.DMA((2 * blocks + 1,)),
            pltpu.SemaphoreType.DMA((2 * blocks + units,)),
        ],
        name="finish",
        compiler_params=pltpu.CompilerParams(vmem_limit_bytes=67043328),
    )(whole, total, result, input_grad, late_grad)
    result, input_grad = outs[0][None], outs[1][None]
    turned = [outs[index].T[None] for index in (4, 7, 11, 13)]
    return (
        result, input_grad, outs[2], outs[3], turned[0], outs[5], outs[6], turned[1],
        outs[8], outs[9], outs[10], turned[2], outs[12], turned[3], outs[14],
    )


def contract_rows(left, right):
    return lax.dot_general(left, right, (((0,), (0,)), ((), ())), preferred_element_type=F32)


def scatter_parts(vector, lefts, rights):
    def reduce_rows(left, right):
        piece = lax.psum_scatter(contract_rows(left, right), "dp", scatter_dimension=0, tiled=True)
        return piece.T

    branch, output_low, upper_low, mixed = lefts
    attended, hidden, second_normed, normed = rights
    return (
        lax.psum(vector, "dp"),
        reduce_rows(mixed, normed),
        reduce_rows(branch, attended),
        reduce_rows(upper_low, second_normed),
        reduce_rows(output_low, hidden),
    )


def on_device(*arrays):
    shards = lax.axis_size("dp")
    me = lax.axis_index("dp")
    width = arrays[0].shape[1]
    aligned = shards % 4 == 0 and width % (16 * shards) == 0
    (
        result, input_grad, vector,
        normed, attended, second_normed, hidden, mixed, branch, upper_low, output_low,
        *late,
    ) = relay(arrays, aligned)
    lefts = (branch, output_low, upper_low, mixed)
    rights = (attended, hidden, second_normed, normed)
    if aligned:
        late = (arrays[0], arrays[6], arrays[4], *late)
        total, whole, late_grad = reduce_parts(vector, lefts, rights, late)
        return finish(whole, total, result, input_grad, late_grad, hidden.shape[1] // width)
    whole, project_grad, out_grad, up_grad, down_grad = scatter_parts(vector, lefts, rights)
    size = width // shards
    small = lax.dynamic_slice_in_dim(whole[:8], me * size, size, 1)
    up_size = hidden.shape[1] // shards
    up_small = lax.dynamic_slice_in_dim(whole[8:].reshape(1, -1), me * up_size, up_size, 1)
    return (
        result[None],
        input_grad[None],
        small[0:1],
        small[1:2],
        project_grad[None],
        small[2:3],
        small[3:4],
        out_grad[None],
        small[4:5],
        small[5:6],
        small[6:7],
        up_grad[None],
        up_small,
        down_grad[None],
        small[7:8],
    )


def solution(mesh):
    stack1 = P("section", None)
    stack2 = P("section", None, None)
    in_specs = (
        P("dp", None), P("dp", None), P("dp"), P("dp"),
        stack1, stack1, stack2, stack1, stack1, stack2, stack1,
        stack1, stack1, stack2, stack1, stack2, stack1,
    )
    row = P("section", "dp")
    matrix = P("section", None, "dp")
    rows = P("section", "dp", None)
    out_specs = (
        rows, rows, row, row, matrix, row, row, matrix, row, row, row, matrix, row, matrix, row,
    )
    return jax.shard_map(
        on_device, mesh=mesh, in_specs=in_specs, out_specs=out_specs, check_vma=False
    )
```
